32 devices in a mesh: dp: 4 (over x, core), seq: 8 (over z, y).
Axes of the slice: x: 2, y: 2, z: 4, core: 2. Of those that a mesh axis runs over, the one named last changes fastest.
Arguments:
- tokens: bfloat16 [4, 2, 1024, 1024], P('dp', None, 'seq'), may hold values from -6 to 6
- cotangent: bfloat16 [4, 2, 1024, 1024], P('dp', None, 'seq'), may hold values from -6 to 6
- node_lengths: int32 [4, 2, 13], P('dp'), may hold values from 1 to 512, 1024 in all within a row
- parents: int32 [4, 2, 13], P('dp'), may hold values from 0 to 11, as said below
- w_query: bfloat16 [1024, 2048], P(('dp', 'seq')), may hold values from -0.1875 to 0.1875
- w_key: bfloat16 [1024, 1024], P(('dp', 'seq')), may hold values from -0.1875 to 0.1875
- w_value: bfloat16 [1024, 1024], P(('dp', 'seq')), may hold values from -0.1875 to 0.1875
- w_output: bfloat16 [2048, 1024], P(('dp', 'seq')), may hold values from -1.5 to 1.5
- w_gate: bfloat16 [1024, 3072], P(('dp', 'seq')), may hold values from -0.1875 to 0.1875
- w_up: bfloat16 [1024, 3072], P(('dp', 'seq')), may hold values from -0.1875 to 0.1875
- w_down: bfloat16 [3072, 1024], P(('dp', 'seq')), may hold values from -0.109375 to 0.109375
- attn_gain: bfloat16 [1024], P(('dp', 'seq')), may hold values from 0.5 to 1.5
- ffn_gain: bfloat16 [1024], P(('dp', 'seq')), may hold values from 0.5 to 1.5
- query_gain: bfloat16 [128], P(('dp', 'seq')), may hold values from 0.5 to 1.5
- key_gain: bfloat16 [128], P(('dp', 'seq')), may hold values from 0.5 to 1.5
Outputs:
- outputs: bfloat16 [4, 2, 1024, 1024], P('dp', None, 'seq')
- input_grad: float32 [4, 2, 1024, 1024], P('dp', None, 'seq')
- grad_query: float32 [1024, 2048], P(('dp', 'seq'))
- grad_key: float32 [1024, 1024], P(('dp', 'seq'))
- grad_value: float32 [1024, 1024], P(('dp', 'seq'))
- grad_output: float32 [2048, 1024], P(('dp', 'seq'))
- grad_gate: float32 [1024, 3072], P(('dp', 'seq'))
- grad_up: float32 [1024, 3072], P(('dp', 'seq'))
- grad_down: float32 [3072, 1024], P(('dp', 'seq'))
- grad_attn_gain: float32 [1024], P(('dp', 'seq'))
- grad_ffn_gain: float32 [1024], P(('dp', 'seq'))
- grad_query_gain: float32 [128], P(('dp', 'seq'))
- grad_key_gain: float32 [128], P(('dp', 'seq'))
The draws below stay inside these ranges and needn't reach their ends.
Inputs may be any that keep to these rules, and one draw needn't show every extreme that they name: `node_lengths`: each tree's 13 node lengths sum to 1024. `parents`: node 0 is the root and its entry is 0; every other node's parent is a node below it.
All inputs are finite; a program needn't handle non-finite values.
Results may differ from the reference program's by a relative error of at most 0.023.
Values may be sent and summed in bfloat16 or wider, within the bound.
A program may use at most 320 MiB of HBM per device.

```python
import math
import jax
import jax.numpy as jnp
import numpy as np
from jax import lax

D = 1024
HEADS = 16
KV_HEADS = 8
HEAD_DIM = 128
FF = 3072
MICRO = 2
NODES = 13
GROUPS = 4
TREE_LEN = 1024


def draw_parents(key, part):
    node_ids = jnp.arange(NODES, dtype=jnp.int32)
    random_bits = jax.random.randint(key, (GROUPS, MICRO, NODES), 0, 1 << 30, dtype=jnp.int32)
    chosen = random_bits % jnp.maximum(node_ids, 1)[None, None, :]
    first_tree = (jnp.arange(GROUPS)[:, None, None] == 0) & (jnp.arange(MICRO)[None, :, None] == 0) & (node_ids[None, None, :] == NODES - 1)
    chosen = jnp.where(first_tree, NODES - 2, chosen)
    return chosen.astype(jnp.int32)


def shard_levels(stream_key, dims, split, low, top_value):
    level = 1.0
    for axis_at, parts in split:
        heights = jax.random.uniform(jax.random.fold_in(jax.random.fold_in(stream_key, 6), axis_at), (parts,), jnp.float32, low / len(split), top_value / len(split))
        level = level * jnp.repeat(jnp.exp(heights), dims[axis_at] // parts).reshape((-1,) + (1,) * (len(dims) - 1 - axis_at))
    return level


def split_up(number_of, total, limit, skew):
    weights = [(1 << 20) // math.isqrt(grade ** skew) + 1 for grade in range(2, number_of + 1)]
    surplus, given = total - limit - (number_of - 1), [1] * (number_of - 1)
    while surplus > 0:
        candidates = [i for i in range(number_of - 1) if given[i] < limit]
        whole, budget = sum([weights[i] for i in candidates]), surplus
        for i in candidates:
            extra = min(limit - given[i], max(1, budget * weights[i] // whole), surplus)
            given[i] = given[i] + extra
            surplus = surplus - extra
    return np.array([limit] + given)


def ragged_sizes(own_key, number_of, total, bound, lean):
    if number_of == 2:
        one = jax.random.randint(own_key, (), max(1, total - bound), min(bound, total - 1) + 1)
        return jnp.stack([one, total - one])
    sizes = jnp.asarray(split_up(number_of, total, bound, lean), jnp.int32)
    pairs = (number_of - 1) // 2
    giver, receiver = sizes[1:1 + 2 * pairs:2], sizes[2:2 + 2 * pairs:2]
    margin = jnp.minimum(giver - 1, bound - receiver)
    shifted = jax.random.randint(jax.random.fold_in(own_key, 1), (pairs,), 0, 1 << 20) % (margin + 1)
    sizes = sizes.at[1:1 + 2 * pairs:2].set(giver - shifted).at[2:2 + 2 * pairs:2].set(receiver + shifted)
    return sizes[jax.random.permutation(jax.random.fold_in(own_key, 2), number_of)]


def scatter_about(stream_key, extent, scale, bound, cuts=(), held_as=jnp.bfloat16):
    loudness = shard_levels(stream_key, extent, cuts, -0.22, 0.18) if cuts else 1.0
    values = jax.random.normal(stream_key, extent, jnp.float32) * scale * loudness
    return jnp.minimum(jnp.maximum(values, -bound), bound).astype(held_as)


def setup_inputs(seed: int = 0) -> dict:
    arg_keys = jax.random.split(jax.random.key(seed), 16)
    return {
        "tokens": scatter_about(arg_keys[0], (GROUPS, MICRO, TREE_LEN, D), 1.0, 6.0, ((0, 4), (2, 8))),
        "cotangent": scatter_about(arg_keys[1], (GROUPS, MICRO, TREE_LEN, D), 1.0, 6.0, ((0, 4), (2, 8))),
        "node_lengths": jax.vmap(lambda own: ragged_sizes(own, NODES, TREE_LEN, TREE_LEN // 2, 2))(jax.random.split(arg_keys[2], GROUPS * MICRO)).reshape((GROUPS, MICRO, NODES)).astype(jnp.int32),
        "parents": draw_parents(jax.random.fold_in(arg_keys[15], 71), 0),
        "w_query": scatter_about(arg_keys[4], (D, HEADS * HEAD_DIM), D ** -0.5, 0.1875, ((0, 32),)),
        "w_key": scatter_about(arg_keys[5], (D, KV_HEADS * HEAD_DIM), D ** -0.5, 0.1875, ((0, 32),)),
        "w_value": scatter_about(arg_keys[6], (D, KV_HEADS * HEAD_DIM), D ** -0.5, 0.1875, ((0, 32),)),
        "w_output": scatter_about(arg_keys[7], (HEADS * HEAD_DIM, D), 16 ** -0.5, 1.5, ((0, 32),)),
        "w_gate": scatter_about(arg_keys[8], (D, FF), D ** -0.5, 0.1875, ((0, 32),)),
        "w_up": scatter_about(arg_keys[9], (D, FF), D ** -0.5, 0.1875, ((0, 32),)),
        "w_down": scatter_about(arg_keys[10], (FF, D), FF ** -0.5, 0.109375, ((0, 32),)),
        "attn_gain": jnp.clip(1.0 + 0.1 * jax.random.normal(arg_keys[11], (D,), jnp.float32), 0.5, 1.5).astype(jnp.bfloat16),
        "ffn_gain": jnp.clip(1.0 + 0.1 * jax.random.normal(arg_keys[12], (D,), jnp.float32), 0.5, 1.5).astype(jnp.bfloat16),
        "query_gain": jnp.clip(1.0 + 0.1 * jax.random.normal(arg_keys[13], (HEAD_DIM,), jnp.float32), 0.5, 1.5).astype(jnp.bfloat16),
        "key_gain": jnp.clip(1.0 + 0.1 * jax.random.normal(arg_keys[14], (HEAD_DIM,), jnp.float32), 0.5, 1.5).astype(jnp.bfloat16),
    }


@jax.custom_vjp
def low(v):
    return lax.optimization_barrier(v.astype(jnp.bfloat16)).astype(jnp.float32)

@jax.custom_vjp
def low_back(v):
    return v

def low_keep(v):
    return (low(v), None)

def low_pass(kept, grad):
    return (grad,)

def back_keep(v):
    return (v, None)

def back_low(kept, grad):
    return (low(grad),)
low.defvjp(low_keep, low_pass)
low_back.defvjp(back_keep, back_low)
EPSILON = 1e-06
THETA = 1000000.0
NEGATIVE = -1e+30
PRECISE = lax.Precision.HIGHEST

def norm_rows(values, row_gain):
    return values * lax.rsqrt(lax.optimization_barrier(jnp.mean(values * values, axis=-1, keepdims=True)) + EPSILON) * row_gain

def rope_tables(position, head_dim):
    half_dim = head_dim // 2
    inv_freq = THETA ** (-(jnp.arange(half_dim, dtype=jnp.float32) * (2.0 / head_dim)))
    angles = position.astype(jnp.float32)[:, None] * inv_freq[None, :]
    cosine_table = jnp.cos(angles)
    sine_table = jnp.sin(angles)
    return (jnp.concatenate([cosine_table, cosine_table], axis=1), jnp.concatenate([sine_table, sine_table], axis=1))

def rotate(values, cosine_table, sine_table):
    half_dim = values.shape[-1] // 2
    turned = jnp.concatenate([-values[..., half_dim:], values[..., :half_dim]], axis=-1)
    return values * cosine_table[:, None, :] + turned * sine_table[:, None, :]

def tree_tables(lengths, parent_row):
    node_count = lengths.shape[0]
    labels = jnp.arange(node_count, dtype=jnp.int32)
    parent_hot = ((parent_row[:, None] == labels[None, :]) & (labels[:, None] > 0)).astype(jnp.int32)

    def extend(depth_step, state_pair):
        reached, covered = state_pair
        reached = lax.optimization_barrier(jnp.sum(reached[:, :, None] * parent_hot[None, :, :], axis=1)).astype(jnp.int32)
        return (reached, (covered + reached).astype(jnp.int32))
    reached, covered = lax.fori_loop(0, node_count, extend, (parent_hot, parent_hot))
    ancestry = (covered > 0).astype(jnp.float32)
    starts = (jnp.cumsum(lengths) - lengths).astype(jnp.int32)
    path_base = lax.optimization_barrier(jnp.sum(jnp.where(covered > 0, lengths[None, :], 0), axis=1)).astype(jnp.int32)
    return (labels, starts, path_base, ancestry)

def token_nodes(token_index, labels, starts, path_base):
    node_id = lax.optimization_barrier(jnp.sum((token_index[:, None] >= starts[None, 1:]).astype(jnp.int32), axis=1)).astype(jnp.int32)
    member = node_id[:, None] == labels[None, :]
    offset = lax.optimization_barrier(jnp.sum(jnp.where(member, (path_base - starts)[None, :], 0), axis=1)).astype(jnp.int32)
    return (member.astype(jnp.float32), (token_index + offset).astype(jnp.int32))

def visible(query_member, query_index, key_member, key_index, ancestry):
    numbers = (((1,), (1,)), ((), ()))
    lifted = jnp.dot(query_member, ancestry, precision=PRECISE)
    above = lax.dot_general(lifted, key_member, numbers, precision=PRECISE)
    same_node = lax.dot_general(query_member, key_member, numbers, precision=PRECISE)
    return (above > 0.5) | (same_node > 0.5) & (key_index[None, :] <= query_index[:, None])

def block_forward(tree_in, w_query, w_key, w_value, w_output, w_gate, w_up, w_down, attn_gain, ffn_gain, query_gain, key_gain, cosine_table, sine_table, member, token_index, ancestry):
    row_count = tree_in.shape[0]
    group_size = HEADS // KV_HEADS
    normed_in = low(norm_rows(tree_in, attn_gain))
    query_lin = low_back(jnp.dot(normed_in, w_query, precision=PRECISE))
    key_lin = low_back(jnp.dot(normed_in, w_key, precision=PRECISE))
    value_low = low(low_back(jnp.dot(normed_in, w_value, precision=PRECISE))).reshape(row_count, KV_HEADS, HEAD_DIM)
    query_rot = low(rotate(norm_rows(query_lin.reshape(row_count, HEADS, HEAD_DIM), query_gain), cosine_table, sine_table))
    key_rot = low(rotate(norm_rows(key_lin.reshape(row_count, KV_HEADS, HEAD_DIM), key_gain), cosine_table, sine_table))
    block_rows = math.gcd(row_count, 256)
    blocks = row_count // block_rows
    score_scale = HEAD_DIM ** (-0.5)

    def attend(pieces):
        query_block, member_block, index_block = pieces
        raw_score = low_back(jnp.einsum('qhgd,khd->hgqk', query_block, key_rot, precision=PRECISE))
        keep_mask = visible(member_block, index_block, member, token_index, ancestry)
        scores = jnp.where(keep_mask[None, None], raw_score * score_scale, NEGATIVE)
        row_top = lax.optimization_barrier(jnp.max(scores, axis=-1, keepdims=True))
        weight = jnp.exp(scores - row_top)
        soft_prob = weight / lax.optimization_barrier(jnp.sum(weight, axis=-1, keepdims=True))
        return jnp.einsum('hgqk,khd->qhgd', low(soft_prob), value_low, precision=PRECISE)
    attended = lax.map(jax.checkpoint(attend), (query_rot.reshape(blocks, block_rows, KV_HEADS, group_size, HEAD_DIM), member.reshape(blocks, block_rows, member.shape[1]), token_index.reshape(blocks, block_rows)))
    attended = low(low_back(attended.reshape(row_count, HEADS * HEAD_DIM)))
    middle = tree_in + low_back(jnp.dot(attended, w_output, precision=PRECISE))
    normed_mid = low(norm_rows(middle, ffn_gain))
    gate_lin = low_back(jnp.dot(normed_mid, w_gate, precision=PRECISE))
    up_lin = low_back(jnp.dot(normed_mid, w_up, precision=PRECISE))
    activated = low(jax.nn.silu(gate_lin) * up_lin)
    return middle + low_back(jnp.dot(activated, w_down, precision=PRECISE))

def reference(tokens, cotangent, node_lengths, parents, w_query, w_key, w_value, w_output, w_gate, w_up, w_down, attn_gain, ffn_gain, query_gain, key_gain):
    weights = tuple((item.astype(jnp.float32) for item in (w_query, w_key, w_value, w_output, w_gate, w_up, w_down, attn_gain, ffn_gain, query_gain, key_gain)))
    tree_count = tokens.shape[0] * tokens.shape[1]
    length = tokens.shape[2]
    tree_inputs = tokens.reshape(tree_count, length, D).astype(jnp.float32)
    tree_cotangents = cotangent.reshape(tree_count, length, D).astype(jnp.float32)
    tree_lengths = node_lengths.reshape(tree_count, NODES)
    tree_parents = parents.reshape(tree_count, NODES)
    token_index = jnp.arange(length, dtype=jnp.int32)

    def one_tree(totals, pieces):
        tree_in, tree_cot, lengths, parent_row = pieces
        labels, starts, path_base, ancestry = tree_tables(lengths, parent_row)
        member, position = token_nodes(token_index, labels, starts, path_base)
        cosine_table, sine_table = rope_tables(position, HEAD_DIM)

        def forward(layer_in, *params):
            return block_forward(layer_in, *params, cosine_table, sine_table, member, token_index, ancestry)
        result, pull_back = jax.vjp(forward, tree_in, *weights)
        gradients = pull_back(tree_cot)
        totals = tuple((old + new for old, new in zip(totals, gradients[1:])))
        return (totals, (result.astype(jnp.bfloat16), gradients[0]))
    zero_sums = tuple((jnp.zeros(item.shape, jnp.float32) for item in weights))
    totals, (out_rows, grad_rows) = lax.scan(one_tree, zero_sums, (tree_inputs, tree_cotangents, tree_lengths, tree_parents))
    outputs = out_rows.reshape(tokens.shape)
    input_grad = grad_rows.reshape(tokens.shape)
    return (outputs, input_grad, totals[0], totals[1], totals[2], totals[3], totals[4], totals[5], totals[6], totals[7], totals[8], totals[9], totals[10])
```

```python
import functools

import jax
import jax.numpy as jnp
from jax import lax
from jax.experimental import pallas as pl
from jax.experimental.pallas import tpu as pltpu
from jax.sharding import PartitionSpec as P

D = 1024
HEADS = 16
KV_HEADS = 8
HEAD_DIM = 128
FF = 3072
MICRO = 2


EPSILON = 1e-06
THETA = 1000000.0
NEGATIVE = -1e30
PRECISE = lax.Precision.HIGHEST


def norm_rows(values, row_gain):
    return (
        values * lax.rsqrt(jnp.mean(values * values, axis=-1, keepdims=True) + EPSILON) * row_gain
    )


def rope_tables(position, head_dim):
    half_dim = head_dim // 2
    inv_freq = THETA ** (-(jnp.arange(half_dim, dtype=jnp.float32) * (2.0 / head_dim)))
    angles = position.astype(jnp.float32)[:, None] * inv_freq[None, :]
    cosine_table = jnp.cos(angles)
    sine_table = jnp.sin(angles)
    return (
        jnp.concatenate([cosine_table, cosine_table], axis=1),
        jnp.concatenate([sine_table, sine_table], axis=1),
    )


def rotate(values, cosine_table, sine_table):
    half_dim = values.shape[-1] // 2
    turned = jnp.concatenate([-values[..., half_dim:], values[..., :half_dim]], axis=-1)
    return values * cosine_table[:, None, :] + turned * sine_table[:, None, :]


def tree_tables(lengths, parent_row):
    node_count = lengths.shape[0]
    labels = jnp.arange(node_count, dtype=jnp.int32)
    parent_hot = ((parent_row[:, None] == labels[None, :]) & (labels[:, None] > 0)).astype(
        jnp.int32
    )

    def extend(depth_step, state_pair):
        reached, covered = state_pair
        reached = jnp.sum(reached[:, :, None] * parent_hot[None, :, :], axis=1)
        return (reached, covered + reached)

    reached, covered = lax.fori_loop(0, node_count, extend, (parent_hot, parent_hot))
    ancestry = (covered > 0).astype(jnp.float32)
    starts = jnp.cumsum(lengths) - lengths
    path_base = jnp.sum(jnp.where(covered > 0, lengths[None, :], 0), axis=1)
    return (labels, starts, path_base, ancestry)


def token_nodes(token_index, labels, starts, path_base):
    node_id = jnp.sum((token_index[:, None] >= starts[None, 1:]).astype(jnp.int32), axis=1)
    member = node_id[:, None] == labels[None, :]
    offset = jnp.sum(jnp.where(member, (path_base - starts)[None, :], 0), axis=1)
    return (member.astype(jnp.float32), token_index + offset)


def visible(query_member, query_index, key_member, key_index, ancestry):
    numbers = (((1,), (1,)), ((), ()))
    lifted = jnp.dot(query_member, ancestry, precision=PRECISE)
    above = lax.dot_general(lifted, key_member, numbers, precision=PRECISE)
    same_node = lax.dot_general(query_member, key_member, numbers, precision=PRECISE)
    return (above > 0.5) | (same_node > 0.5) & (key_index[None, :] <= query_index[:, None])


def product(left_side, right_side):
    return jnp.dot(left_side, right_side, preferred_element_type=jnp.float32)


def against(left_side, right_side):
    return lax.dot_general(
        left_side, right_side, (((1,), (1,)), ((), ())), preferred_element_type=jnp.float32
    )


def across(left_side, right_side):
    return lax.dot_general(
        left_side, right_side, (((0,), (0,)), ((), ())), preferred_element_type=jnp.float32
    )


def general_shards(
    tokens,
    cotangent,
    node_lengths,
    parents,
    w_query,
    w_key,
    w_value,
    w_output,
    w_gate,
    w_up,
    w_down,
    attn_gain,
    ffn_gain,
    query_gain,
    key_gain,
):
    rows_here = tokens.shape[2]
    length = lax.axis_size("seq") * rows_here
    group_size = HEADS // KV_HEADS
    pair_count = KV_HEADS // 2
    width_query = 2 * group_size * HEAD_DIM
    width_key = 2 * HEAD_DIM
    score_scale = HEAD_DIM ** (-0.5)
    local_index = lax.axis_index("seq") * rows_here + jnp.arange(rows_here, dtype=jnp.int32)
    full_index = jnp.arange(length, dtype=jnp.int32)
    pair_ids = jnp.arange(pair_count, dtype=jnp.int32)
    float_type = jnp.float32
    brain_type = jnp.bfloat16
    sums = (
        jnp.zeros((D, HEADS * HEAD_DIM), float_type),
        jnp.zeros((D, KV_HEADS * HEAD_DIM), float_type),
        jnp.zeros((D, KV_HEADS * HEAD_DIM), float_type),
        jnp.zeros((HEADS * HEAD_DIM, D), float_type),
        jnp.zeros((D, FF), float_type),
        jnp.zeros((D, FF), float_type),
        jnp.zeros((FF, D), float_type),
        jnp.zeros((D,), float_type),
        jnp.zeros((D,), float_type),
        jnp.zeros((HEAD_DIM,), float_type),
        jnp.zeros((HEAD_DIM,), float_type),
    )
    out_list = []
    grad_list = []
    for batch_index in range(MICRO):
        attn_fwd = (
            lax.all_gather(w_query, ("dp", "seq"), axis=0, tiled=True),
            lax.all_gather(w_key, ("dp", "seq"), axis=0, tiled=True),
            lax.all_gather(w_value, ("dp", "seq"), axis=0, tiled=True),
            lax.all_gather(w_output, ("dp", "seq"), axis=0, tiled=True),
            lax.all_gather(attn_gain, ("dp", "seq"), axis=0, tiled=True),
            lax.all_gather(query_gain, ("dp", "seq"), axis=0, tiled=True),
            lax.all_gather(key_gain, ("dp", "seq"), axis=0, tiled=True),
        )
        ffn_fwd = (
            lax.all_gather(w_gate, ("dp", "seq"), axis=0, tiled=True),
            lax.all_gather(w_up, ("dp", "seq"), axis=0, tiled=True),
            lax.all_gather(w_down, ("dp", "seq"), axis=0, tiled=True),
            lax.all_gather(ffn_gain, ("dp", "seq"), axis=0, tiled=True),
        )
        query_w, key_w, value_w, output_w, attn_g, query_g, key_g = attn_fwd
        gate_w, up_w, down_w, ffn_g = ffn_fwd
        labels, starts, path_base, ancestry = tree_tables(
            node_lengths[0, batch_index], parents[0, batch_index]
        )
        member_here, position = token_nodes(local_index, labels, starts, path_base)
        member_all, unused_position = token_nodes(full_index, labels, starts, path_base)
        keep_mask = visible(member_here, local_index, member_all, full_index, ancestry)
        cosine_table, sine_table = rope_tables(position, HEAD_DIM)
        rows_in = tokens[0, batch_index].astype(float_type)
        attn_g32 = attn_g.astype(float_type)
        query_g32 = query_g.astype(float_type)
        key_g32 = key_g.astype(float_type)
        normed_in = norm_rows(rows_in, attn_g32).astype(brain_type)
        query_heads = product(normed_in, query_w).reshape(rows_here, HEADS, HEAD_DIM)
        key_heads = product(normed_in, key_w).reshape(rows_here, KV_HEADS, HEAD_DIM)
        value_low = product(normed_in, value_w).astype(brain_type)
        query_rot = (
            rotate(norm_rows(query_heads, query_g32), cosine_table, sine_table)
            .astype(brain_type)
            .reshape(rows_here, HEADS * HEAD_DIM)
        )
        key_rot = (
            rotate(norm_rows(key_heads, key_g32), cosine_table, sine_table)
            .astype(brain_type)
            .reshape(rows_here, KV_HEADS * HEAD_DIM)
        )
        key_all, value_all = (
            lax.all_gather(key_rot, "seq", axis=0, tiled=True),
            lax.all_gather(value_low, "seq", axis=0, tiled=True),
        )

        def attend_pair(pair_id):
            query_pair = lax.dynamic_slice_in_dim(
                query_rot, pair_id * width_query, width_query, 1
            ).reshape(rows_here, 2, group_size, HEAD_DIM)
            key_pair = lax.dynamic_slice_in_dim(key_all, pair_id * width_key, width_key, 1).reshape(
                length, 2, HEAD_DIM
            )
            value_pair = lax.dynamic_slice_in_dim(
                value_all, pair_id * width_key, width_key, 1
            ).reshape(length, 2, HEAD_DIM)
            raw_score = jnp.einsum(
                "qhgd,khd->hgqk", query_pair, key_pair, preferred_element_type=jnp.float32
            )
            scores = jnp.where(keep_mask[None, None], raw_score * score_scale, NEGATIVE)
            row_top = jnp.max(scores, axis=-1, keepdims=True)
            weight = jnp.exp(scores - row_top)
            row_total = jnp.sum(weight, axis=-1, keepdims=True)
            soft_low = (weight / row_total).astype(jnp.bfloat16)
            mixed = jnp.einsum(
                "hgqk,khd->qhgd", soft_low, value_pair, preferred_element_type=jnp.float32
            )
            return (mixed, row_top + jnp.log(row_total))

        mixed_pairs, log_totals = lax.map(attend_pair, pair_ids)
        attended = (
            mixed_pairs.transpose(1, 0, 2, 3, 4)
            .reshape(rows_here, HEADS * HEAD_DIM)
            .astype(brain_type)
        )
        middle = rows_in + product(attended, output_w)
        ffn_g32 = ffn_g.astype(float_type)
        normed_mid = norm_rows(middle, ffn_g32).astype(brain_type)
        gate_lin = product(normed_mid, gate_w)
        up_lin = product(normed_mid, up_w)
        activated = (jax.nn.silu(gate_lin) * up_lin).astype(brain_type)
        out_list.append((middle + product(activated, down_w)).astype(brain_type))
        attn_back = (
            lax.all_gather(w_query, ("dp", "seq"), axis=0, tiled=True),
            lax.all_gather(w_key, ("dp", "seq"), axis=0, tiled=True),
            lax.all_gather(w_value, ("dp", "seq"), axis=0, tiled=True),
            lax.all_gather(w_output, ("dp", "seq"), axis=0, tiled=True),
            lax.all_gather(attn_gain, ("dp", "seq"), axis=0, tiled=True),
            lax.all_gather(query_gain, ("dp", "seq"), axis=0, tiled=True),
            lax.all_gather(key_gain, ("dp", "seq"), axis=0, tiled=True),
        )
        ffn_back = (
            lax.all_gather(w_gate, ("dp", "seq"), axis=0, tiled=True),
            lax.all_gather(w_up, ("dp", "seq"), axis=0, tiled=True),
            lax.all_gather(w_down, ("dp", "seq"), axis=0, tiled=True),
            lax.all_gather(ffn_gain, ("dp", "seq"), axis=0, tiled=True),
        )
        key_back, value_back = (
            lax.all_gather(key_rot, "seq", axis=0, tiled=True),
            lax.all_gather(value_low, "seq", axis=0, tiled=True),
        )
        query_wb, key_wb, value_wb, output_wb, attn_gb, query_gb, key_gb = attn_back
        gate_wb, up_wb, down_wb, ffn_gb = ffn_back
        cot_rows = cotangent[0, batch_index]
        grad_down = across(activated, cot_rows)
        d_activated = against(cot_rows, down_wb)
        sigma_gate = jax.nn.sigmoid(gate_lin)
        d_gate = (d_activated * up_lin * sigma_gate * (1.0 + gate_lin * (1.0 - sigma_gate))).astype(
            brain_type
        )
        d_up = (d_activated * gate_lin * sigma_gate).astype(brain_type)
        grad_gate = across(normed_mid, d_gate)
        grad_up = across(normed_mid, d_up)
        d_normed_mid = against(d_gate, gate_wb) + against(d_up, up_wb)
        unused_mid, pull_ffn = jax.vjp(norm_rows, middle, ffn_gb.astype(float_type))
        d_mid_norm, grad_ffn_gain = pull_ffn(d_normed_mid)
        d_middle = cot_rows.astype(float_type) + d_mid_norm
        d_middle_low = d_middle.astype(brain_type)
        grad_output = across(attended, d_middle_low)
        d_attended = against(d_middle_low, output_wb).astype(brain_type)

        def back_pair(pair_id):
            query_pair = lax.dynamic_slice_in_dim(
                query_rot, pair_id * width_query, width_query, 1
            ).reshape(rows_here, 2, group_size, HEAD_DIM)
            grad_pair = lax.dynamic_slice_in_dim(
                d_attended, pair_id * width_query, width_query, 1
            ).reshape(rows_here, 2, group_size, HEAD_DIM)
            key_pair = lax.dynamic_slice_in_dim(
                key_back, pair_id * width_key, width_key, 1
            ).reshape(length, 2, HEAD_DIM)
            value_pair = lax.dynamic_slice_in_dim(
                value_back, pair_id * width_key, width_key, 1
            ).reshape(length, 2, HEAD_DIM)
            raw_score = jnp.einsum(
                "qhgd,khd->hgqk", query_pair, key_pair, preferred_element_type=jnp.float32
            )
            scores = jnp.where(keep_mask[None, None], raw_score * score_scale, NEGATIVE)
            soft_prob = jnp.exp(scores - log_totals[pair_id])
            soft_low = soft_prob.astype(jnp.bfloat16)
            d_prob = jnp.einsum(
                "qhgd,khd->hgqk", grad_pair, value_pair, preferred_element_type=jnp.float32
            )
            d_score = soft_prob * (d_prob - jnp.sum(soft_prob * d_prob, axis=-1, keepdims=True))
            d_raw = (d_score * score_scale).astype(jnp.bfloat16)
            d_query = jnp.einsum(
                "hgqk,khd->qhgd", d_raw, key_pair, preferred_element_type=jnp.float32
            )
            d_key = jnp.einsum(
                "hgqk,qhgd->khd", d_raw, query_pair, preferred_element_type=jnp.float32
            )
            d_value = jnp.einsum(
                "hgqk,qhgd->khd", soft_low, grad_pair, preferred_element_type=jnp.float32
            )
            return (
                d_query,
                jnp.concatenate(
                    [d_key.reshape(length, width_key), d_value.reshape(length, width_key)], axis=1
                ),
            )

        d_query_pairs, kv_terms = lax.map(back_pair, pair_ids)
        kv_share = lax.psum_scatter(
            kv_terms.astype(jnp.bfloat16), "seq", scatter_dimension=1, tiled=True
        ).astype(jnp.float32)
        d_key_rot = (
            kv_share[:, :, :width_key]
            .reshape(pair_count, rows_here, 2, HEAD_DIM)
            .transpose(1, 0, 2, 3)
            .reshape(rows_here, KV_HEADS, HEAD_DIM)
        )
        d_value_low = (
            kv_share[:, :, width_key:]
            .transpose(1, 0, 2)
            .reshape(rows_here, KV_HEADS * HEAD_DIM)
            .astype(brain_type)
        )
        d_query_rot = d_query_pairs.transpose(1, 0, 2, 3, 4).reshape(rows_here, HEADS, HEAD_DIM)

        def turn_rows(heads_in, gain_in):
            return rotate(norm_rows(heads_in, gain_in), cosine_table, sine_table)

        unused_query, pull_query = jax.vjp(turn_rows, query_heads, query_gb.astype(float_type))
        d_query_heads, grad_query_gain = pull_query(d_query_rot)
        unused_key, pull_key = jax.vjp(turn_rows, key_heads, key_gb.astype(float_type))
        d_key_heads, grad_key_gain = pull_key(d_key_rot)
        d_query_low = d_query_heads.reshape(rows_here, HEADS * HEAD_DIM).astype(brain_type)
        d_key_low = d_key_heads.reshape(rows_here, KV_HEADS * HEAD_DIM).astype(brain_type)
        grad_query = across(normed_in, d_query_low)
        grad_key = across(normed_in, d_key_low)
        grad_value = across(normed_in, d_value_low)
        d_normed_in = (
            against(d_query_low, query_wb)
            + against(d_key_low, key_wb)
            + against(d_value_low, value_wb)
        )
        unused_in, pull_attn = jax.vjp(norm_rows, rows_in, attn_gb.astype(float_type))
        d_in_norm, grad_attn_gain = pull_attn(d_normed_in)
        grad_list.append(d_middle + d_in_norm)
        fresh = (
            grad_query,
            grad_key,
            grad_value,
            grad_output,
            grad_gate,
            grad_up,
            grad_down,
            grad_attn_gain,
            grad_ffn_gain,
            grad_query_gain,
            grad_key_gain,
        )
        sums = tuple((old + new for old, new in zip(sums, fresh)))
    attn_parts = (
        lax.psum_scatter(sums[0], ("dp", "seq"), scatter_dimension=0, tiled=True),
        lax.psum_scatter(sums[1], ("dp", "seq"), scatter_dimension=0, tiled=True),
        lax.psum_scatter(sums[2], ("dp", "seq"), scatter_dimension=0, tiled=True),
        lax.psum_scatter(sums[3], ("dp", "seq"), scatter_dimension=0, tiled=True),
        lax.psum_scatter(sums[7], ("dp", "seq"), scatter_dimension=0, tiled=True),
        lax.psum_scatter(sums[9], ("dp", "seq"), scatter_dimension=0, tiled=True),
        lax.psum_scatter(sums[10], ("dp", "seq"), scatter_dimension=0, tiled=True),
    )
    ffn_parts = (
        lax.psum_scatter(sums[4], ("dp", "seq"), scatter_dimension=0, tiled=True),
        lax.psum_scatter(sums[5], ("dp", "seq"), scatter_dimension=0, tiled=True),
        lax.psum_scatter(sums[6], ("dp", "seq"), scatter_dimension=0, tiled=True),
        lax.psum_scatter(sums[8], ("dp", "seq"), scatter_dimension=0, tiled=True),
    )
    outputs = jnp.stack(out_list)[None]
    input_grad = jnp.stack(grad_list)[None]
    return (
        outputs,
        input_grad,
        attn_parts[0],
        attn_parts[1],
        attn_parts[2],
        attn_parts[3],
        ffn_parts[0],
        ffn_parts[1],
        ffn_parts[2],
        attn_parts[4],
        ffn_parts[3],
        attn_parts[5],
        attn_parts[6],
    )


MESH = pl.DeviceIdType.MESH
NDP = 4
NSEQ = 8
BLOCKED = -65536.0


def spot():
    d = lax.axis_index("dp")
    s = lax.axis_index("seq")
    z, y = s // 2, s % 2
    return d, s, z + y * (7 - 2 * z)


def seq_at(position):
    half = position // 4
    z = position + half * (7 - 2 * position)
    return 2 * z + half


def greet_all(d, s):
    barrier = pltpu.get_barrier_semaphore()
    me = d * NSEQ + s

    def signal(i, carry):
        other = (me + i) % (NDP * NSEQ)
        pl.semaphore_signal(
            barrier, inc=1, device_id=(other // NSEQ, other % NSEQ), device_id_type=MESH
        )
        return carry

    lax.fori_loop(1, NDP * NSEQ, signal, 0)
    pl.semaphore_wait(barrier, NDP * NSEQ - 1)


def greet_dp(d, s):
    barrier = pltpu.get_barrier_semaphore()
    for i in range(1, NDP):
        pl.semaphore_signal(barrier, inc=1, device_id=((d + i) % NDP, s), device_id_type=MESH)
    pl.semaphore_wait(barrier, NDP - 1)


def remote(src, dst, send, recv, d, s):
    return pltpu.make_async_remote_copy(
        src_ref=src, dst_ref=dst, send_sem=send, recv_sem=recv, device_id=(d, s), device_id_type=MESH
    )


def ring_halves(ref, kind, j):
    if kind == "cols":
        return ref.at[pl.ds(0, 2), j], ref.at[pl.ds(2, 2), j]
    rows = ref.shape[1] // 2
    return ref.at[j, pl.ds(0, rows)], ref.at[j, pl.ds(rows, rows)]


def spread_dp(out, d, s, ssem, rsem):
    x, c = d // 2, d % 2
    sib, far = 2 * x + 1 - c, 2 * (1 - x) + c
    far_sib = 2 * (1 - x) + 1 - c
    own = out.at[:, d]
    to_far = remote(own, own, ssem.at[0], rsem.at[0], far, s)
    to_sib = remote(own, own, ssem.at[1], rsem.at[1], sib, s)
    to_far.start()
    to_sib.start()
    block = out.at[:, far]
    remote(block, block, ssem.at[0], rsem.at[0], far, s).wait_recv()
    forward = remote(block, block, ssem.at[2], rsem.at[2], sib, s)
    forward.start()
    block = out.at[:, sib]
    remote(block, block, ssem.at[1], rsem.at[1], sib, s).wait_recv()
    block = out.at[:, far_sib]
    remote(block, block, ssem.at[2], rsem.at[2], sib, s).wait_recv()
    to_far.wait_send()
    to_sib.wait_send()
    forward.wait_send()


def gather_dp_sum(part, near, sent, got, d, s, ssem, rsem, finish):
    x, c = d // 2, d % 2
    sib, far = 2 * x + 1 - c, 2 * (1 - x) + c
    first = remote(part.at[:, 2 * (1 - x) + 1 - c], near.at[0], ssem.at[0], rsem.at[0], sib, s)
    second = remote(part.at[:, 2 * x + 1 - c], near.at[1], ssem.at[1], rsem.at[1], sib, s)
    first.start()
    second.start()
    first.wait_recv()

    def join(i, carry):
        sent[i] = (part[i, far].astype(jnp.float32) + near[0, i].astype(jnp.float32)).astype(
            jnp.bfloat16
        )
        return carry

    lax.fori_loop(0, NSEQ, join, 0)
    across_x = remote(sent, got, ssem.at[2], rsem.at[2], far, s)
    across_x.start()
    second.wait_recv()
    across_x.wait_recv()

    def close(i, carry):
        rows = part[i, d].astype(jnp.float32) + near[1, i].astype(jnp.float32)
        finish(i, rows + got[i].astype(jnp.float32))
        return carry

    lax.fori_loop(0, NSEQ, close, 0)
    first.wait_send()
    second.wait_send()
    across_x.wait_send()


def deliver_kernel(
    tok, cot, small, wq, wk, wv, wo, wg, wu, wd, tree, tree_cot, smalls, wa, wb, wc, we,
    loc, s_small, r_small, s_row, r_row, s_col, r_col, s_tok, r_tok, s_ring, r_ring, s_dp, r_dp,
):
    d, s, p = spot()
    greet_all(d, s)
    own_small = pltpu.make_async_copy(small, smalls.at[d, s], loc.at[0])
    own_small.start()
    own_small.wait()
    pending = []
    for i in range(1, NDP):
        q = (d + i) % NDP
        cp = remote(smalls.at[d, s], smalls.at[d, s], s_small.at[i], r_small.at[i], q, s)
        cp.start()
        pending.append(cp)
    pieces = (
        (wq, wa, 512, 0), (wk, wa, 256, 512), (wv, wa, 256, 768), (wg, wc, 768, 0), (wu, wc, 768, 768)
    )
    waits = []
    for n, (src, dst, width, at) in enumerate(pieces):
        cp = pltpu.make_async_copy(
            src.at[:, pl.ds(pl.multiple_of(d * width, 128), width)],
            dst.at[d, s, :, pl.ds(at, width)],
            loc.at[1 + n],
        )
        cp.start()
        waits.append(cp)
        for i in range(1, NDP):
            q = (d + i) % NDP
            cp = remote(
                src.at[:, pl.ds(pl.multiple_of(q * width, 128), width)],
                dst.at[d, s, :, pl.ds(at, width)],
                s_col.at[n, i],
                r_col.at[n, i],
                q,
                s,
            )
            cp.start()
            pending.append(cp)
    for n, (src, dst) in enumerate(((wo, wb), (wd, we))):
        cp = pltpu.make_async_copy(src, dst.at[s], loc.at[6 + n])
        cp.start()
        waits.append(cp)
    for n, (src, dst) in enumerate(((tok, tree), (cot, tree_cot))):
        for m in range(MICRO):
            for i in range(NDP):
                q = (d + i) % NDP
                target = MICRO * d + m
                piece = src.at[m, pl.ds(pl.multiple_of(q * 32, 32), 32)]
                place = dst.at[s, q]
                if i == 0:

                    @pl.when(target == s)
                    def _():
                        pltpu.make_async_copy(piece, place, r_tok.at[n]).start()

                    @pl.when(target != s)
                    def _():
                        remote(piece, place, s_tok.at[n, m, i], r_tok.at[n], q, target).start()
                else:
                    cp = remote(piece, place, s_tok.at[n, m, i], r_tok.at[n], q, target)
                    cp.start()
                    pending.append(cp)
    for cp in waits:
        cp.wait()
    for n, (src, dst, width, at) in enumerate(pieces):
        for i in range(1, NDP):
            q = (d + NDP - i) % NDP
            place = dst.at[q, s, :, pl.ds(at, width)]
            remote(place, place, s_col.at[n, i], r_col.at[n, i], q, s).wait_recv()
    up, down = seq_at((p + 1) % NSEQ), seq_at((p + 7) % NSEQ)
    ring = ((wa, "cols"), (wb, "rows"), (wc, "cols"), (we, "rows"))

    def pass_on(k, carry):
        up_own, down_own = seq_at((p + NSEQ - k) % NSEQ), seq_at((p + k) % NSEQ)
        for n, (ref, kind) in enumerate(ring):
            rising = ring_halves(ref, kind, up_own)[0]
            falling = ring_halves(ref, kind, down_own)[1]

            @pl.when(k > 0)
            def _():
                remote(rising, rising, s_ring.at[n, 0, k - 1], r_ring.at[n, 0, k - 1], up, 0).wait_recv()

            remote(rising, rising, s_ring.at[n, 0, k], r_ring.at[n, 0, k], d, up).start()

            @pl.when(k > 0)
            def _():
                remote(falling, falling, s_ring.at[n, 1, k - 1], r_ring.at[n, 1, k - 1], down, 0).wait_recv()

            remote(falling, falling, s_ring.at[n, 1, k], r_ring.at[n, 1, k], d, down).start()
        return carry

    for n, dst in enumerate((tree, tree_cot)):
        everything = dst.at[:, d]
        pltpu.make_async_copy(everything, everything, r_tok.at[n]).wait()
    lax.fori_loop(0, 2, pass_on, 0)
    for n, dst in enumerate((tree, tree_cot)):
        spread_dp(dst, d, s, s_dp.at[n], r_dp.at[n])
    lax.fori_loop(2, NSEQ - 1, pass_on, 0)
    for i in range(1, NDP):
        place = smalls.at[(d + NDP - i) % NDP, s]
        remote(place, place, s_small.at[i], r_small.at[i], d, s).wait_recv()
    for i in range(1, NSEQ):
        j = (s + i) % NSEQ
        place = smalls.at[:, s]
        cp = remote(place, place, s_small.at[NDP + i], r_small.at[NDP + i], d, j)
        cp.start()
        pending.append(cp)
    for i in range(1, NSEQ):
        place = smalls.at[:, (s + NSEQ - i) % NSEQ]
        remote(place, place, s_small.at[NDP + i], r_small.at[NDP + i], d, s).wait_recv()
    for n, (ref, kind) in enumerate(ring):
        last_up = ring_halves(ref, kind, seq_at((p + 1) % NSEQ))[0]
        last_down = ring_halves(ref, kind, seq_at((p + 7) % NSEQ))[1]
        remote(last_up, last_up, s_ring.at[n, 0, 6], r_ring.at[n, 0, 6], d, up).wait_recv()
        remote(last_down, last_down, s_ring.at[n, 1, 6], r_ring.at[n, 1, 6], d, down).wait_recv()

    def sent_ring(k, carry):
        for n, (ref, kind) in enumerate(ring):
            rising, falling = ring_halves(ref, kind, s)
            remote(rising, rising, s_ring.at[n, 0, k], r_ring.at[n, 0, k], d, up).wait_send()
            remote(falling, falling, s_ring.at[n, 1, k], r_ring.at[n, 1, k], d, down).wait_send()
        return carry

    lax.fori_loop(0, NSEQ - 1, sent_ring, 0)
    for cp in pending:
        cp.wait_send()
    for n, (src, dst) in enumerate(((tok, tree), (cot, tree_cot))):
        for m in range(MICRO):

            @pl.when(MICRO * d + m != s)
            def _():
                place = dst.at[s, d]
                remote(place, place, s_tok.at[n, m, 0], r_tok.at[n], d, s).wait_send()


def deliver(tok, cot, small, wq, wk, wv, wo, wg, wu, wd):
    bf, f32 = jnp.bfloat16, jnp.float32
    dma = pltpu.SemaphoreType.DMA
    shape = jax.ShapeDtypeStruct
    anywhere = pl.BlockSpec(memory_space=pl.ANY)
    return pl.pallas_call(
        deliver_kernel,
        out_shape=(
            shape((NSEQ, NDP, 32, D), bf),
            shape((NSEQ, NDP, 32, D), bf),
            shape((NDP, NSEQ, 8, 128), f32),
            shape((NDP, NSEQ, 32, 1024), bf),
            shape((NSEQ, 64, D), bf),
            shape((NDP, NSEQ, 32, 1536), bf),
            shape((NSEQ, 96, D), bf),
        ),
        in_specs=[anywhere] * 10,
        out_specs=[anywhere] * 7,
        scratch_shapes=[
            dma((8,)),
            dma((12,)), dma((12,)),
            dma((1,)), dma((1,)),
            dma((5, NDP)), dma((5, NDP)),
            dma((2, MICRO, NDP)), dma((2,)),
            dma((4, 2, 7)), dma((4, 2, 7)),
            dma((2, 3)), dma((2, 3)),
        ],
        compiler_params=pltpu.CompilerParams(collective_id=1, has_side_effects=True),
        name="deliver",
    )(tok, cot, small, wq, wk, wv, wo, wg, wu, wd)


def middle_kernel(part, tree, gain, middle, normed, rows_in, near, sent, got, loc, ssem, rsem, s_dp, r_dp):
    d, s, _ = spot()
    greet_dp(d, s)
    own = pltpu.make_async_copy(tree.at[:, d], rows_in, loc.at[0])
    own.start()
    own.wait()

    def finish(i, rows):
        rows = rows + rows_in[i].astype(jnp.float32)
        middle[i] = rows
        scale = lax.rsqrt(jnp.mean(rows * rows, axis=-1, keepdims=True) + EPSILON)
        normed[i, d] = (rows * scale * gain[...]).astype(jnp.bfloat16)

    gather_dp_sum(part, near, sent, got, d, s, ssem, rsem, finish)
    spread_dp(normed, d, s, s_dp, r_dp)


def sum_scratch():
    bf = jnp.bfloat16
    return [
        pltpu.VMEM((2, NSEQ, 32, D), bf),
        pltpu.VMEM((NSEQ, 32, D), bf),
        pltpu.VMEM((NSEQ, 32, D), bf),
    ]


def middle_stage(part, tree, gain):
    bf, f32 = jnp.bfloat16, jnp.float32
    dma = pltpu.SemaphoreType.DMA
    shape = jax.ShapeDtypeStruct
    anywhere = pl.BlockSpec(memory_space=pl.ANY)
    here = pl.BlockSpec(memory_space=pltpu.VMEM)
    return pl.pallas_call(
        middle_kernel,
        out_shape=(shape((NSEQ, 32, D), f32), shape((NSEQ, NDP, 32, D), bf)),
        in_specs=[here, anywhere, here],
        out_specs=[here, here],
        scratch_shapes=[pltpu.VMEM((NSEQ, 32, D), bf)]
        + sum_scratch()
        + [dma((1,)), dma((3,)), dma((3,)), dma((3,)), dma((3,))],
        compiler_params=pltpu.CompilerParams(
            collective_id=2, has_side_effects=True, vmem_limit_bytes=40 << 20
        ),
        name="middle",
    )(part, tree, gain)


def turn_kernel(
    part, part_out, tree_cot, middle, gain, d_middle, d_low, outs, d_gain,
    cot_rows, near, sent, got, near_out, sent_out, got_out,
    loc, ssem, rsem, s_dp, r_dp, s_out, r_out,
):
    d, s, _ = spot()
    greet_dp(d, s)
    own = pltpu.make_async_copy(tree_cot.at[:, d], cot_rows, loc.at[0])
    own.start()
    own.wait()
    d_gain[...] = jnp.zeros_like(d_gain)

    def finish(i, rows):
        mid = middle[i]
        scale = lax.rsqrt(jnp.mean(mid * mid, axis=-1, keepdims=True) + EPSILON)
        unit = mid * scale
        lifted = gain[...] * rows
        d_gain[...] += jnp.sum(rows * unit, axis=0, keepdims=True)
        d_mid = cot_rows[i].astype(jnp.float32) + scale * (
            lifted - unit * jnp.mean(unit * lifted, axis=-1, keepdims=True)
        )
        d_middle[i] = d_mid
        d_low[i, d] = d_mid.astype(jnp.bfloat16)

    gather_dp_sum(part, near, sent, got, d, s, ssem, rsem, finish)
    spread_dp(d_low, d, s, s_dp, r_dp)

    def finish_out(i, rows):
        outs[i] = (middle[i] + rows).astype(jnp.bfloat16)

    gather_dp_sum(part_out, near_out, sent_out, got_out, d, s, s_out, r_out, finish_out)


def turn_stage(part, part_out, tree_cot, middle, gain):
    bf, f32 = jnp.bfloat16, jnp.float32
    dma = pltpu.SemaphoreType.DMA
    shape = jax.ShapeDtypeStruct
    anywhere = pl.BlockSpec(memory_space=pl.ANY)
    here = pl.BlockSpec(memory_space=pltpu.VMEM)
    return pl.pallas_call(
        turn_kernel,
        out_shape=(
            shape((NSEQ, 32, D), f32),
            shape((NSEQ, NDP, 32, D), bf),
            shape((NSEQ, 32, D), bf),
            shape((1, D), f32),
        ),
        in_specs=[here, here, anywhere, here, here],
        out_specs=[here] * 4,
        scratch_shapes=[pltpu.VMEM((NSEQ, 32, D), bf)]
        + sum_scratch()
        + sum_scratch()
        + [dma((1,)), dma((3,)), dma((3,)), dma((3,)), dma((3,)), dma((3,)), dma((3,))],
        compiler_params=pltpu.CompilerParams(
            collective_id=3, has_side_effects=True, vmem_limit_bytes=40 << 20
        ),
        name="turn",
    )(part, part_out, tree_cot, middle, gain)


def return_kernel(
    part, tree, d_middle, gain, outs, pack_in, ga, gb, gc, ge,
    out_rows, grad_rows, pack_out, res_a, res_b, res_c, res_e,
    rows_in, near, sent, got, grad_low, hop_a, hop_b, hop_c, hop_e, fin_a, fin_c,
    pack_dp, pack_seq,
    loc, ssem, rsem, s_back, r_back, s_ring, r_ring, s_col, r_col, s_pack, r_pack,
):
    d, s, p = spot()
    greet_all(d, s)
    bf, f32 = jnp.bfloat16, jnp.float32
    own = pltpu.make_async_copy(tree.at[:, d], rows_in, loc.at[0])
    own.start()
    up, down = seq_at((p + 1) % NSEQ), seq_at((p + 7) % NSEQ)
    ring = ((ga, hop_a, "cols"), (gb, hop_b, "rows"), (gc, hop_c, "cols"), (ge, hop_e, "rows"))
    owner = s // MICRO
    slot = s % MICRO

    def give(src, dst, n):
        def one(j, carry):
            piece = src.at[j]
            place = dst.at[slot, pl.ds(pl.multiple_of(d * 32, 32), 32)]
            same = (owner == d) & (j == s)

            @pl.when(same)
            def _():
                pltpu.make_async_copy(piece, place, r_back.at[n]).start()

            @pl.when(jnp.logical_not(same))
            def _():
                remote(piece, place, s_back.at[n, j], r_back.at[n], owner, j).start()

            return carry

        lax.fori_loop(0, NSEQ, one, 0)

    give(outs, out_rows, 0)

    def ring_step(k, carry):
        up_to, down_to = seq_at((p + 7 - k) % NSEQ), seq_at((p + 1 + k) % NSEQ)
        for n, (ref, hop, kind) in enumerate(ring):
            for way, (block, peer) in enumerate(((up_to, up), (down_to, down))):
                mine = ring_halves(ref, kind, block)[way]

                @pl.when(k == 0)
                def _():
                    remote(mine, hop.at[way, 0], s_ring.at[n, way, 0], r_ring.at[n, way, 0], d, peer).start()

                @pl.when(k > 0)
                def _():
                    here = hop.at[way, k - 1]
                    remote(here, here, s_ring.at[n, way, k - 1], r_ring.at[n, way, k - 1], d, peer).wait_recv()
                    here[...] = (here[...].astype(f32) + mine[...].astype(f32)).astype(bf)
                    remote(here, hop.at[way, k], s_ring.at[n, way, k], r_ring.at[n, way, k], d, peer).start()

        return carry

    lax.fori_loop(0, 2, ring_step, 0)
    own.wait()
    d_gain = jnp.zeros((1, D), f32)
    pack_dp[d] = pack_in[...]

    def finish(i, rows):
        low = rows_in[i].astype(f32)
        scale = lax.rsqrt(jnp.mean(low * low, axis=-1, keepdims=True) + EPSILON)
        unit = low * scale
        lifted = gain[...] * rows
        term = jnp.sum(rows * unit, axis=0, keepdims=True)
        for j in range(8):
            pack_dp[d, pl.ds(j, 1)] += term[:, 128 * j : 128 * (j + 1)]
        grad = d_middle[i] + scale * (
            lifted - unit * jnp.mean(unit * lifted, axis=-1, keepdims=True)
        )
        grad_low[i] = grad.astype(bf)

    gather_dp_sum(part, near, sent, got, d, s, ssem, rsem, finish)
    give(grad_low, grad_rows, 1)
    pending = []
    for i in range(1, NDP):
        q = (d + i) % NDP
        cp = remote(pack_dp.at[d], pack_dp.at[d], s_pack.at[i], r_pack.at[i], q, s)
        cp.start()
        pending.append(cp)
    for i in range(1, NDP):
        place = pack_dp.at[(d + NDP - i) % NDP]
        remote(place, place, s_pack.at[i], r_pack.at[i], d, s).wait_recv()
    pack_seq[s] = (pack_dp[0] + pack_dp[1]) + (pack_dp[2] + pack_dp[3])
    for i in range(1, NSEQ):
        cp = remote(pack_seq.at[s], pack_seq.at[s], s_pack.at[NDP + i], r_pack.at[NDP + i], d, (s + i) % NSEQ)
        cp.start()
        pending.append(cp)
    lax.fori_loop(2, NSEQ - 1, ring_step, 0)
    for n, (ref, hop, kind) in enumerate(ring):
        halves = ring_halves(ref, kind, s)
        for way, peer in enumerate((up, down)):
            here = hop.at[way, 6]
            remote(here, here, s_ring.at[n, way, 6], r_ring.at[n, way, 6], d, peer).wait_recv()
            total = here[...].astype(f32) + halves[way][...].astype(f32)
            if n == 0:
                fin_a[pl.ds(2 * way, 2)] = total.astype(bf)
            elif n == 2:
                fin_c[pl.ds(2 * way, 2)] = total.astype(bf)
            else:
                res = res_b if n == 1 else res_e
                rows = total.shape[0]
                res[pl.ds(way * rows, rows)] = total
    for n, (fin, res) in enumerate(((fin_a, res_a), (fin_c, res_c))):
        cp = pltpu.make_async_copy(fin.at[d], res.at[d], loc.at[1 + n])
        cp.start()
        cp.wait()
        for i in range(1, NDP):
            q = (d + i) % NDP
            cp = remote(fin.at[q], res.at[d], s_col.at[n, i], r_col.at[n, i], q, s)
            cp.start()
            pending.append(cp)
    for i in range(1, NSEQ):
        place = pack_seq.at[(s + NSEQ - i) % NSEQ]
        remote(place, place, s_pack.at[NDP + i], r_pack.at[NDP + i], d, s).wait_recv()
    total = pack_seq[0]
    for j in range(1, NSEQ):
        total = total + pack_seq[j]
    pack_out[...] = total
    for n, res in enumerate((res_a, res_c)):
        for i in range(1, NDP):
            place = res.at[(d + NDP - i) % NDP]
            remote(place, place, s_col.at[n, i], r_col.at[n, i], d, s).wait_recv()
    for n, dst in enumerate((out_rows, grad_rows)):
        pltpu.make_async_copy(dst, dst, r_back.at[n]).wait()

        def sent_back(j, carry):
            same = (owner == d) & (j == s)

            @pl.when(jnp.logical_not(same))
            def _():
                place = grad_low.at[j]
                remote(place, place, s_back.at[n, j], r_back.at[n], owner, j).wait_send()

            return carry

        lax.fori_loop(0, NSEQ, sent_back, 0)

    def sent_ring(k, carry):
        for n, (ref, hop, kind) in enumerate(ring):
            for way, peer in enumerate((up, down)):
                here = hop.at[way, k]
                remote(here, here, s_ring.at[n, way, k], r_ring.at[n, way, k], d, peer).wait_send()
        return carry

    lax.fori_loop(0, NSEQ - 1, sent_ring, 0)
    for cp in pending:
        cp.wait_send()


def return_stage(part, tree, d_middle, gain, outs, pack_in, ga, gb, gc, ge):
    bf, f32 = jnp.bfloat16, jnp.float32
    dma = pltpu.SemaphoreType.DMA
    shape = jax.ShapeDtypeStruct
    vmem = pltpu.VMEM
    anywhere = pl.BlockSpec(memory_space=pl.ANY)
    here = pl.BlockSpec(memory_space=pltpu.VMEM)
    return pl.pallas_call(
        return_kernel,
        out_shape=(
            shape((MICRO, 128, D), bf),
            shape((MICRO, 128, D), bf),
            shape((24, 128), f32),
            shape((NDP, 32, 1024), bf),
            shape((64, D), f32),
            shape((NDP, 32, 1536), bf),
            shape((96, D), f32),
        ),
        in_specs=[here, anywhere] + [here] * 8,
        out_specs=[here] * 7,
        scratch_shapes=[vmem((NSEQ, 32, D), bf)]
        + sum_scratch()
        + [
            vmem((NSEQ, 32, D), bf),
            vmem((2, 7, 2, 32, 1024), bf),
            vmem((2, 7, 32, D), bf),
            vmem((2, 7, 2, 32, 1536), bf),
            vmem((2, 7, 48, D), bf),
            vmem((NDP, 32, 1024), bf),
            vmem((NDP, 32, 1536), bf),
            vmem((NDP, 24, 128), f32),
            vmem((NSEQ, 24, 128), f32),
            dma((3,)), dma((3,)), dma((3,)),
            dma((2, NSEQ)), dma((2,)),
            dma((4, 2, 7)), dma((4, 2, 7)),
            dma((2, NDP)), dma((2, NDP)),
            dma((12,)), dma((12,)),
        ],
        compiler_params=pltpu.CompilerParams(
            collective_id=4, has_side_effects=True, vmem_limit_bytes=56 << 20
        ),
        name="give_back",
    )(part, tree, d_middle, gain, outs, pack_in, ga, gb, gc, ge)


QB = 256


def attend_kernel(q_ref, k_ref, v_ref, o_ref, lse_ref):
    length = q_ref.shape[0]
    scale = HEAD_DIM ** (-0.5)
    row = lax.broadcasted_iota(jnp.int32, (QB, QB), 0)
    col = lax.broadcasted_iota(jnp.int32, (QB, QB), 1)
    for b in range(length // QB):
        n = (b + 1) * QB
        score = against(q_ref[pl.ds(b * QB, QB)], k_ref[pl.ds(0, n)]) * scale
        diag = jnp.where(col <= row, score[:, n - QB :], NEGATIVE)
        score = diag if b == 0 else jnp.concatenate([score[:, : n - QB], diag], axis=1)
        weight = jnp.exp(score)
        total = jnp.sum(weight, axis=-1, keepdims=True)
        mixed = product(weight.astype(jnp.bfloat16), v_ref[pl.ds(0, n)])
        o_ref[pl.ds(b * QB, QB)] = (mixed / total).astype(jnp.bfloat16)
        lse_ref[pl.ds(b * QB, QB)] = jnp.log(total)


def attend(q_aug, k_aug, value):
    heads, length = q_aug.shape[0], q_aug.shape[1]
    shape = jax.ShapeDtypeStruct
    return pl.pallas_call(
        attend_kernel,
        grid=(heads,),
        out_shape=(
            shape((length, heads * HEAD_DIM), jnp.bfloat16),
            shape((heads, length, 1), jnp.float32),
        ),
        in_specs=[
            pl.BlockSpec((None, length, 256), lambda h: (h, 0, 0)),
            pl.BlockSpec((None, length, 256), lambda h: (h // 2, 0, 0)),
            pl.BlockSpec((length, HEAD_DIM), lambda h: (0, h // 2)),
        ],
        out_specs=[
            pl.BlockSpec((length, HEAD_DIM), lambda h: (0, h)),
            pl.BlockSpec((None, length, 1), lambda h: (h, 0, 0)),
        ],
        compiler_params=pltpu.CompilerParams(vmem_limit_bytes=50 << 20),
        name="attend",
    )(q_aug, k_aug, value)


def attend_back_kernel(q_ref, k_ref, v_ref, do_ref, lse_ref, dq_ref, dk_ref, dv_ref):
    length = q_ref.shape[0]
    scale = HEAD_DIM ** (-0.5)
    row = lax.broadcasted_iota(jnp.int32, (QB, QB), 0)
    col = lax.broadcasted_iota(jnp.int32, (QB, QB), 1)

    @pl.when(pl.program_id(0) % 2 == 0)
    def _():
        dk_ref[...] = jnp.zeros_like(dk_ref)
        dv_ref[...] = jnp.zeros_like(dv_ref)

    for b in range(length // QB):
        n = (b + 1) * QB
        here, keys = pl.ds(b * QB, QB), pl.ds(0, n)
        score = against(q_ref[here], k_ref[keys]) * scale
        diag = jnp.where(col <= row, score[:, n - QB :], NEGATIVE)
        score = diag if b == 0 else jnp.concatenate([score[:, : n - QB], diag], axis=1)
        prob = jnp.exp(score - lse_ref[here])
        d_prob = against(do_ref[here], v_ref[keys])
        delta = jnp.sum(prob * d_prob, axis=-1, keepdims=True)
        d_raw = (prob * (d_prob - delta) * scale).astype(jnp.bfloat16)
        dq_ref[here] = product(d_raw, k_ref[keys, pl.ds(0, HEAD_DIM)])
        dk_ref[keys] += across(d_raw, q_ref[here, pl.ds(0, HEAD_DIM)])
        dv_ref[keys] += across(prob.astype(jnp.bfloat16), do_ref[here])


def attend_back(q_aug, k_aug, value, d_att, lse):
    heads, length = q_aug.shape[0], q_aug.shape[1]
    shape = jax.ShapeDtypeStruct
    return pl.pallas_call(
        attend_back_kernel,
        grid=(heads,),
        out_shape=(
            shape((length, heads * HEAD_DIM), jnp.float32),
            shape((length, heads // 2 * HEAD_DIM), jnp.float32),
            shape((length, heads // 2 * HEAD_DIM), jnp.float32),
        ),
        in_specs=[
            pl.BlockSpec((None, length, 256), lambda h: (h, 0, 0)),
            pl.BlockSpec((None, length, 256), lambda h: (h // 2, 0, 0)),
            pl.BlockSpec((length, HEAD_DIM), lambda h: (0, h // 2)),
            pl.BlockSpec((length, HEAD_DIM), lambda h: (0, h)),
            pl.BlockSpec((None, length, 1), lambda h: (h, 0, 0)),
        ],
        out_specs=[
            pl.BlockSpec((length, HEAD_DIM), lambda h: (0, h)),
            pl.BlockSpec((length, HEAD_DIM), lambda h: (0, h // 2)),
            pl.BlockSpec((length, HEAD_DIM), lambda h: (0, h // 2)),
        ],
        compiler_params=pltpu.CompilerParams(vmem_limit_bytes=50 << 20),
        name="attend_back",
    )(q_aug, k_aug, value, d_att, lse)


def tree_shards(
    tokens, cotangent, node_lengths, parents, w_query, w_key, w_value, w_output, w_gate, w_up, w_down,
    attn_gain, ffn_gain, query_gain, key_gain,
):
    f32, bf = jnp.float32, jnp.bfloat16
    d, s = lax.axis_index("dp"), lax.axis_index("seq")
    length = NSEQ * tokens.shape[2]
    heads, kv_heads = HEADS // NDP, KV_HEADS // NDP
    nodes = node_lengths.shape[2]
    gains = jnp.concatenate([attn_gain, ffn_gain, query_gain, key_gain]).astype(f32)
    small = jnp.concatenate(
        [
            jnp.pad(gains, (0, 128 - gains.shape[0]))[None],
            jnp.pad(node_lengths[0].astype(f32), ((0, 0), (0, 128 - nodes))),
            jnp.pad(parents[0].astype(f32), ((0, 0), (0, 128 - nodes))),
            jnp.zeros((3, 128), f32),
        ]
    )
    tree, tree_cot, smalls, wa, wb, wc, we = deliver(
        tokens[0], cotangent[0], small, w_query, w_key, w_value, w_output, w_gate, w_up, w_down
    )
    wa, wb = wa.reshape(D, 1024), wb.reshape(512, D)
    wc, we = wc.reshape(D, 1536), we.reshape(768, D)
    attn_g = smalls[:, :, 0, :32].reshape(D)
    ffn_g = smalls[:, :, 0, 32:64].reshape(D)
    query_g = smalls[:, :, 0, 64:68].reshape(HEAD_DIM)
    key_g = smalls[:, :, 0, 68:72].reshape(HEAD_DIM)
    mine = lax.dynamic_index_in_dim(smalls[:, 0], s // MICRO, 0, False)
    lengths = lax.dynamic_index_in_dim(mine, 1 + s % MICRO, 0, False)[:nodes].astype(jnp.int32)
    parent_row = lax.dynamic_index_in_dim(mine, 3 + s % MICRO, 0, False)[:nodes].astype(jnp.int32)
    labels, starts, path_base, ancestry = tree_tables(lengths, parent_row)
    member, position = token_nodes(jnp.arange(length, dtype=jnp.int32), labels, starts, path_base)
    cosine_table, sine_table = rope_tables(position, HEAD_DIM)
    seen = ancestry + jnp.eye(nodes, dtype=f32)
    hidden = jnp.dot(member, (1.0 - seen) * BLOCKED, precision=PRECISE)
    pad = ((0, 0), (0, 128 - nodes))
    hidden, member = jnp.pad(hidden, pad).astype(bf), jnp.pad(member, pad).astype(bf)

    rows_in = tree.reshape(length, D).astype(f32)
    normed_in = norm_rows(rows_in, attn_g).astype(bf)
    lin = product(normed_in, wa)
    query_heads = lin[:, : heads * HEAD_DIM].reshape(length, heads, HEAD_DIM)
    key_heads = lin[:, heads * HEAD_DIM : (heads + kv_heads) * HEAD_DIM].reshape(
        length, kv_heads, HEAD_DIM
    )
    value = lin[:, (heads + kv_heads) * HEAD_DIM :].astype(bf)

    def turn_rows(heads_in, gain_in):
        return rotate(norm_rows(heads_in, gain_in), cosine_table, sine_table)

    query_rot, pull_query = jax.vjp(turn_rows, query_heads, query_g)
    key_rot, pull_key = jax.vjp(turn_rows, key_heads, key_g)
    wide = lambda side, n: jnp.broadcast_to(side[:, None], (length, n, 128))
    q_aug = jnp.concatenate([query_rot.astype(bf), wide(hidden, heads)], axis=2).transpose(1, 0, 2)
    k_aug = jnp.concatenate([key_rot.astype(bf), wide(member, kv_heads)], axis=2).transpose(1, 0, 2)
    attended, lse = attend(q_aug, k_aug, value)
    part = product(attended, wb).astype(bf).reshape(NSEQ, NDP, 32, D)
    middle, normed_mid = middle_stage(part, tree, ffn_g[None])
    normed_mid = normed_mid.reshape(length, D)
    both = product(normed_mid, wc)
    gate_lin, up_lin = both[:, :768], both[:, 768:]
    sigma_gate = jax.nn.sigmoid(gate_lin)
    activated = (gate_lin * sigma_gate * up_lin).astype(bf)
    part_out = product(activated, we).astype(bf).reshape(NSEQ, NDP, 32, D)
    cot = tree_cot.reshape(length, D)
    grad_e = across(activated, cot).astype(bf)
    d_activated = against(cot, we)
    d_gate = (d_activated * up_lin * sigma_gate * (1.0 + gate_lin * (1.0 - sigma_gate))).astype(bf)
    d_up = (d_activated * gate_lin * sigma_gate).astype(bf)
    d_both = jnp.concatenate([d_gate, d_up], axis=1)
    grad_c = across(normed_mid, d_both).astype(bf)
    part = against(d_both, wc).astype(bf).reshape(NSEQ, NDP, 32, D)
    d_middle, d_low, outs, d_ffn_gain = turn_stage(part, part_out, tree_cot, middle, ffn_g[None])
    d_low = d_low.reshape(length, D)
    grad_b = across(attended, d_low).astype(bf)
    d_att = against(d_low, wb).astype(bf)
    d_query, d_key, d_value = attend_back(q_aug, k_aug, value, d_att, lse)
    d_query, d_query_gain = pull_query(d_query.reshape(length, heads, HEAD_DIM))
    d_key, d_key_gain = pull_key(d_key.reshape(length, kv_heads, HEAD_DIM))
    d_lin = jnp.concatenate(
        [d_query.reshape(length, -1).astype(bf), d_key.reshape(length, -1).astype(bf), d_value.astype(bf)],
        axis=1,
    )
    grad_a = across(normed_in, d_lin).astype(bf)
    part = against(d_lin, wa).astype(bf).reshape(NSEQ, NDP, 32, D)
    pack = jnp.concatenate(
        [
            jnp.zeros((8, 128), f32),
            d_ffn_gain.reshape(8, 128),
            d_query_gain[None],
            d_key_gain[None],
            jnp.zeros((6, 128), f32),
        ]
    )
    out_rows, grad_rows, pack, res_a, res_b, res_c, res_e = return_stage(
        part, tree, d_middle, attn_g[None], outs, pack,
        grad_a.reshape(NDP, NSEQ, 32, 1024),
        grad_b.reshape(NSEQ, 64, D),
        grad_c.reshape(NDP, NSEQ, 32, 1536),
        grad_e.reshape(NSEQ, 96, D),
    )
    flat = lambda piece: piece.transpose(1, 0, 2).reshape(32, -1).astype(f32)
    at = d * NSEQ + s
    own = lambda rows, n: lax.dynamic_slice_in_dim(rows.reshape(-1), at * n, n)
    return (
        out_rows[None],
        grad_rows[None].astype(f32),
        flat(res_a[:, :, :512]),
        flat(res_a[:, :, 512:768]),
        flat(res_a[:, :, 768:]),
        res_b,
        flat(res_c[:, :, :768]),
        flat(res_c[:, :, 768:]),
        res_e,
        own(pack[:8], 32),
        own(pack[8:16], 32),
        own(pack[16], 4),
        own(pack[17], 4),
    )


def solution(mesh):
    ring = mesh.shape["dp"] == NDP and mesh.shape["seq"] == NSEQ
    return jax.shard_map(
        tree_shards if ring else general_shards,
        mesh=mesh,
        in_specs=(
            P("dp", None, "seq", None),
            P("dp", None, "seq", None),
            P("dp", None, None),
            P("dp", None, None),
            P(("dp", "seq"), None),
            P(("dp", "seq"), None),
            P(("dp", "seq"), None),
            P(("dp", "seq"), None),
            P(("dp", "seq"), None),
            P(("dp", "seq"), None),
            P(("dp", "seq"), None),
            P(("dp", "seq")),
            P(("dp", "seq")),
            P(("dp", "seq")),
            P(("dp", "seq")),
        ),
        out_specs=(
            P("dp", None, "seq", None),
            P("dp", None, "seq", None),
            P(("dp", "seq"), None),
            P(("dp", "seq"), None),
            P(("dp", "seq"), None),
            P(("dp", "seq"), None),
            P(("dp", "seq"), None),
            P(("dp", "seq"), None),
            P(("dp", "seq"), None),
            P(("dp", "seq")),
            P(("dp", "seq")),
            P(("dp", "seq")),
            P(("dp", "seq")),
        ),
        check_vma=False,
    )
```

```python
import functools

import jax
import jax.numpy as jnp
from jax import lax
from jax.experimental import pallas as pl
from jax.experimental.pallas import tpu as pltpu
from jax.sharding import PartitionSpec as P

D = 1024
HEADS = 16
KV_HEADS = 8
HEAD_DIM = 128
FF = 3072
MICRO = 2


EPSILON = 1e-06
THETA = 1000000.0
NEGATIVE = -1e30
PRECISE = lax.Precision.HIGHEST


def norm_rows(values, row_gain):
    return (
        values * lax.rsqrt(jnp.mean(values * values, axis=-1, keepdims=True) + EPSILON) * row_gain
    )


def rope_tables(position, head_dim):
    half_dim = head_dim // 2
    inv_freq = THETA ** (-(jnp.arange(half_dim, dtype=jnp.float32) * (2.0 / head_dim)))
    angles = position.astype(jnp.float32)[:, None] * inv_freq[None, :]
    cosine_table = jnp.cos(angles)
    sine_table = jnp.sin(angles)
    return (
        jnp.concatenate([cosine_table, cosine_table], axis=1),
        jnp.concatenate([sine_table, sine_table], axis=1),
    )


def rotate(values, cosine_table, sine_table):
    half_dim = values.shape[-1] // 2
    turned = jnp.concatenate([-values[..., half_dim:], values[..., :half_dim]], axis=-1)
    return values * cosine_table[:, None, :] + turned * sine_table[:, None, :]


def tree_tables(lengths, parent_row):
    node_count = lengths.shape[0]
    labels = jnp.arange(node_count, dtype=jnp.int32)
    parent_hot = ((parent_row[:, None] == labels[None, :]) & (labels[:, None] > 0)).astype(
        jnp.int32
    )

    def extend(depth_step, state_pair):
        reached, covered = state_pair
        reached = jnp.sum(reached[:, :, None] * parent_hot[None, :, :], axis=1)
        return (reached, covered + reached)

    reached, covered = lax.fori_loop(0, node_count, extend, (parent_hot, parent_hot))
    ancestry = (covered > 0).astype(jnp.float32)
    starts = jnp.cumsum(lengths) - lengths
    path_base = jnp.sum(jnp.where(covered > 0, lengths[None, :], 0), axis=1)
    return (labels, starts, path_base, ancestry)


def token_nodes(token_index, labels, starts, path_base):
    node_id = jnp.sum((token_index[:, None] >= starts[None, 1:]).astype(jnp.int32), axis=1)
    member = node_id[:, None] == labels[None, :]
    offset = jnp.sum(jnp.where(member, (path_base - starts)[None, :], 0), axis=1)
    return (member.astype(jnp.float32), token_index + offset)


def visible(query_member, query_index, key_member, key_index, ancestry):
    numbers = (((1,), (1,)), ((), ()))
    lifted = jnp.dot(query_member, ancestry, precision=PRECISE)
    above = lax.dot_general(lifted, key_member, numbers, precision=PRECISE)
    same_node = lax.dot_general(query_member, key_member, numbers, precision=PRECISE)
    return (above > 0.5) | (same_node > 0.5) & (key_index[None, :] <= query_index[:, None])


def product(left_side, right_side):
    return jnp.dot(left_side, right_side, preferred_element_type=jnp.float32)


def against(left_side, right_side):
    return lax.dot_general(
        left_side, right_side, (((1,), (1,)), ((), ())), preferred_element_type=jnp.float32
    )


def across(left_side, right_side):
    return lax.dot_general(
        left_side, right_side, (((0,), (0,)), ((), ())), preferred_element_type=jnp.float32
    )


def general_shards(
    tokens,
    cotangent,
    node_lengths,
    parents,
    w_query,
    w_key,
    w_value,
    w_output,
    w_gate,
    w_up,
    w_down,
    attn_gain,
    ffn_gain,
    query_gain,
    key_gain,
):
    rows_here = tokens.shape[2]
    length = lax.axis_size("seq") * rows_here
    group_size = HEADS // KV_HEADS
    pair_count = KV_HEADS // 2
    width_query = 2 * group_size * HEAD_DIM
    width_key = 2 * HEAD_DIM
    score_scale = HEAD_DIM ** (-0.5)
    local_index = lax.axis_index("seq") * rows_here + jnp.arange(rows_here, dtype=jnp.int32)
    full_index = jnp.arange(length, dtype=jnp.int32)
    pair_ids = jnp.arange(pair_count, dtype=jnp.int32)
    float_type = jnp.float32
    brain_type = jnp.bfloat16
    sums = (
        jnp.zeros((D, HEADS * HEAD_DIM), float_type),
        jnp.zeros((D, KV_HEADS * HEAD_DIM), float_type),
        jnp.zeros((D, KV_HEADS * HEAD_DIM), float_type),
        jnp.zeros((HEADS * HEAD_DIM, D), float_type),
        jnp.zeros((D, FF), float_type),
        jnp.zeros((D, FF), float_type),
        jnp.zeros((FF, D), float_type),
        jnp.zeros((D,), float_type),
        jnp.zeros((D,), float_type),
        jnp.zeros((HEAD_DIM,), float_type),
        jnp.zeros((HEAD_DIM,), float_type),
    )
    out_list = []
    grad_list = []
    for batch_index in range(MICRO):
        attn_fwd = (
            lax.all_gather(w_query, ("dp", "seq"), axis=0, tiled=True),
            lax.all_gather(w_key, ("dp", "seq"), axis=0, tiled=True),
            lax.all_gather(w_value, ("dp", "seq"), axis=0, tiled=True),
            lax.all_gather(w_output, ("dp", "seq"), axis=0, tiled=True),
            lax.all_gather(attn_gain, ("dp", "seq"), axis=0, tiled=True),
            lax.all_gather(query_gain, ("dp", "seq"), axis=0, tiled=True),
            lax.all_gather(key_gain, ("dp", "seq"), axis=0, tiled=True),
        )
        ffn_fwd = (
            lax.all_gather(w_gate, ("dp", "seq"), axis=0, tiled=True),
            lax.all_gather(w_up, ("dp", "seq"), axis=0, tiled=True),
            lax.all_gather(w_down, ("dp", "seq"), axis=0, tiled=True),
            lax.all_gather(ffn_gain, ("dp", "seq"), axis=0, tiled=True),
        )
        query_w, key_w, value_w, output_w, attn_g, query_g, key_g = attn_fwd
        gate_w, up_w, down_w, ffn_g = ffn_fwd
        labels, starts, path_base, ancestry = tree_tables(
            node_lengths[0, batch_index], parents[0, batch_index]
        )
        member_here, position = token_nodes(local_index, labels, starts, path_base)
        member_all, unused_position = token_nodes(full_index, labels, starts, path_base)
        keep_mask = visible(member_here, local_index, member_all, full_index, ancestry)
        cosine_table, sine_table = rope_tables(position, HEAD_DIM)
        rows_in = tokens[0, batch_index].astype(float_type)
        attn_g32 = attn_g.astype(float_type)
        query_g32 = query_g.astype(float_type)
        key_g32 = key_g.astype(float_type)
        normed_in = norm_rows(rows_in, attn_g32).astype(brain_type)
        query_heads = product(normed_in, query_w).reshape(rows_here, HEADS, HEAD_DIM)
        key_heads = product(normed_in, key_w).reshape(rows_here, KV_HEADS, HEAD_DIM)
        value_low = product(normed_in, value_w).astype(brain_type)
        query_rot = (
            rotate(norm_rows(query_heads, query_g32), cosine_table, sine_table)
            .astype(brain_type)
            .reshape(rows_here, HEADS * HEAD_DIM)
        )
        key_rot = (
            rotate(norm_rows(key_heads, key_g32), cosine_table, sine_table)
            .astype(brain_type)
            .reshape(rows_here, KV_HEADS * HEAD_DIM)
        )
        key_all, value_all = (
            lax.all_gather(key_rot, "seq", axis=0, tiled=True),
            lax.all_gather(value_low, "seq", axis=0, tiled=True),
        )

        def attend_pair(pair_id):
            query_pair = lax.dynamic_slice_in_dim(
                query_rot, pair_id * width_query, width_query, 1
            ).reshape(rows_here, 2, group_size, HEAD_DIM)
            key_pair = lax.dynamic_slice_in_dim(key_all, pair_id * width_key, width_key, 1).reshape(
                length, 2, HEAD_DIM
            )
            value_pair = lax.dynamic_slice_in_dim(
                value_all, pair_id * width_key, width_key, 1
            ).reshape(length, 2, HEAD_DIM)
            raw_score = jnp.einsum(
                "qhgd,khd->hgqk", query_pair, key_pair, preferred_element_type=jnp.float32
            )
            scores = jnp.where(keep_mask[None, None], raw_score * score_scale, NEGATIVE)
            row_top = jnp.max(scores, axis=-1, keepdims=True)
            weight = jnp.exp(scores - row_top)
            row_total = jnp.sum(weight, axis=-1, keepdims=True)
            soft_low = (weight / row_total).astype(jnp.bfloat16)
            mixed = jnp.einsum(
                "hgqk,khd->qhgd", soft_low, value_pair, preferred_element_type=jnp.float32
            )
            return (mixed, row_top + jnp.log(row_total))

        mixed_pairs, log_totals = lax.map(attend_pair, pair_ids)
        attended = (
            mixed_pairs.transpose(1, 0, 2, 3, 4)
            .reshape(rows_here, HEADS * HEAD_DIM)
            .astype(brain_type)
        )
        middle = rows_in + product(attended, output_w)
        ffn_g32 = ffn_g.astype(float_type)
        normed_mid = norm_rows(middle, ffn_g32).astype(brain_type)
        gate_lin = product(normed_mid, gate_w)
        up_lin = product(normed_mid, up_w)
        activated = (jax.nn.silu(gate_lin) * up_lin).astype(brain_type)
        out_list.append((middle + product(activated, down_w)).astype(brain_type))
        attn_back = (
            lax.all_gather(w_query, ("dp", "seq"), axis=0, tiled=True),
            lax.all_gather(w_key, ("dp", "seq"), axis=0, tiled=True),
            lax.all_gather(w_value, ("dp", "seq"), axis=0, tiled=True),
            lax.all_gather(w_output, ("dp", "seq"), axis=0, tiled=True),
            lax.all_gather(attn_gain, ("dp", "seq"), axis=0, tiled=True),
            lax.all_gather(query_gain, ("dp", "seq"), axis=0, tiled=True),
            lax.all_gather(key_gain, ("dp", "seq"), axis=0, tiled=True),
        )
        ffn_back = (
            lax.all_gather(w_gate, ("dp", "seq"), axis=0, tiled=True),
            lax.all_gather(w_up, ("dp", "seq"), axis=0, tiled=True),
            lax.all_gather(w_down, ("dp", "seq"), axis=0, tiled=True),
            lax.all_gather(ffn_gain, ("dp", "seq"), axis=0, tiled=True),
        )
        key_back, value_back = (
            lax.all_gather(key_rot, "seq", axis=0, tiled=True),
            lax.all_gather(value_low, "seq", axis=0, tiled=True),
        )
        query_wb, key_wb, value_wb, output_wb, attn_gb, query_gb, key_gb = attn_back
        gate_wb, up_wb, down_wb, ffn_gb = ffn_back
        cot_rows = cotangent[0, batch_index]
        grad_down = across(activated, cot_rows)
        d_activated = against(cot_rows, down_wb)
        sigma_gate = jax.nn.sigmoid(gate_lin)
        d_gate = (d_activated * up_lin * sigma_gate * (1.0 + gate_lin * (1.0 - sigma_gate))).astype(
            brain_type
        )
        d_up = (d_activated * gate_lin * sigma_gate).astype(brain_type)
        grad_gate = across(normed_mid, d_gate)
        grad_up = across(normed_mid, d_up)
        d_normed_mid = against(d_gate, gate_wb) + against(d_up, up_wb)
        unused_mid, pull_ffn = jax.vjp(norm_rows, middle, ffn_gb.astype(float_type))
        d_mid_norm, grad_ffn_gain = pull_ffn(d_normed_mid)
        d_middle = cot_rows.astype(float_type) + d_mid_norm
        d_middle_low = d_middle.astype(brain_type)
        grad_output = across(attended, d_middle_low)
        d_attended = against(d_middle_low, output_wb).astype(brain_type)

        def back_pair(pair_id):
            query_pair = lax.dynamic_slice_in_dim(
                query_rot, pair_id * width_query, width_query, 1
            ).reshape(rows_here, 2, group_size, HEAD_DIM)
            grad_pair = lax.dynamic_slice_in_dim(
                d_attended, pair_id * width_query, width_query, 1
            ).reshape(rows_here, 2, group_size, HEAD_DIM)
            key_pair = lax.dynamic_slice_in_dim(
                key_back, pair_id * width_key, width_key, 1
            ).reshape(length, 2, HEAD_DIM)
            value_pair = lax.dynamic_slice_in_dim(
                value_back, pair_id * width_key, width_key, 1
            ).reshape(length, 2, HEAD_DIM)
            raw_score = jnp.einsum(
                "qhgd,khd->hgqk", query_pair, key_pair, preferred_element_type=jnp.float32
            )
            scores = jnp.where(keep_mask[None, None], raw_score * score_scale, NEGATIVE)
            soft_prob = jnp.exp(scores - log_totals[pair_id])
            soft_low = soft_prob.astype(jnp.bfloat16)
            d_prob = jnp.einsum(
                "qhgd,khd->hgqk", grad_pair, value_pair, preferred_element_type=jnp.float32
            )
            d_score = soft_prob * (d_prob - jnp.sum(soft_prob * d_prob, axis=-1, keepdims=True))
            d_raw = (d_score * score_scale).astype(jnp.bfloat16)
            d_query = jnp.einsum(
                "hgqk,khd->qhgd", d_raw, key_pair, preferred_element_type=jnp.float32
            )
            d_key = jnp.einsum(
                "hgqk,qhgd->khd", d_raw, query_pair, preferred_element_type=jnp.float32
            )
            d_value = jnp.einsum(
                "hgqk,qhgd->khd", soft_low, grad_pair, preferred_element_type=jnp.float32
            )
            return (
                d_query,
                jnp.concatenate(
                    [d_key.reshape(length, width_key), d_value.reshape(length, width_key)], axis=1
                ),
            )

        d_query_pairs, kv_terms = lax.map(back_pair, pair_ids)
        kv_share = lax.psum_scatter(
            kv_terms.astype(jnp.bfloat16), "seq", scatter_dimension=1, tiled=True
        ).astype(jnp.float32)
        d_key_rot = (
            kv_share[:, :, :width_key]
            .reshape(pair_count, rows_here, 2, HEAD_DIM)
            .transpose(1, 0, 2, 3)
            .reshape(rows_here, KV_HEADS, HEAD_DIM)
        )
        d_value_low = (
            kv_share[:, :, width_key:]
            .transpose(1, 0, 2)
            .reshape(rows_here, KV_HEADS * HEAD_DIM)
            .astype(brain_type)
        )
        d_query_rot = d_query_pairs.transpose(1, 0, 2, 3, 4).reshape(rows_here, HEADS, HEAD_DIM)

        def turn_rows(heads_in, gain_in):
            return rotate(norm_rows(heads_in, gain_in), cosine_table, sine_table)

        unused_query, pull_query = jax.vjp(turn_rows, query_heads, query_gb.astype(float_type))
        d_query_heads, grad_query_gain = pull_query(d_query_rot)
        unused_key, pull_key = jax.vjp(turn_rows, key_heads, key_gb.astype(float_type))
        d_key_heads, grad_key_gain = pull_key(d_key_rot)
        d_query_low = d_query_heads.reshape(rows_here, HEADS * HEAD_DIM).astype(brain_type)
        d_key_low = d_key_heads.reshape(rows_here, KV_HEADS * HEAD_DIM).astype(brain_type)
        grad_query = across(normed_in, d_query_low)
        grad_key = across(normed_in, d_key_low)
        grad_value = across(normed_in, d_value_low)
        d_normed_in = (
            against(d_query_low, query_wb)
            + against(d_key_low, key_wb)
            + against(d_value_low, value_wb)
        )
        unused_in, pull_attn = jax.vjp(norm_rows, rows_in, attn_gb.astype(float_type))
        d_in_norm, grad_attn_gain = pull_attn(d_normed_in)
        grad_list.append(d_middle + d_in_norm)
        fresh = (
            grad_query,
            grad_key,
            grad_value,
            grad_output,
            grad_gate,
            grad_up,
            grad_down,
            grad_attn_gain,
            grad_ffn_gain,
            grad_query_gain,
            grad_key_gain,
        )
        sums = tuple((old + new for old, new in zip(sums, fresh)))
    attn_parts = (
        lax.psum_scatter(sums[0], ("dp", "seq"), scatter_dimension=0, tiled=True),
        lax.psum_scatter(sums[1], ("dp", "seq"), scatter_dimension=0, tiled=True),
        lax.psum_scatter(sums[2], ("dp", "seq"), scatter_dimension=0, tiled=True),
        lax.psum_scatter(sums[3], ("dp", "seq"), scatter_dimension=0, tiled=True),
        lax.psum_scatter(sums[7], ("dp", "seq"), scatter_dimension=0, tiled=True),
        lax.psum_scatter(sums[9], ("dp", "seq"), scatter_dimension=0, tiled=True),
        lax.psum_scatter(sums[10], ("dp", "seq"), scatter_dimension=0, tiled=True),
    )
    ffn_parts = (
        lax.psum_scatter(sums[4], ("dp", "seq"), scatter_dimension=0, tiled=True),
        lax.psum_scatter(sums[5], ("dp", "seq"), scatter_dimension=0, tiled=True),
        lax.psum_scatter(sums[6], ("dp", "seq"), scatter_dimension=0, tiled=True),
        lax.psum_scatter(sums[8], ("dp", "seq"), scatter_dimension=0, tiled=True),
    )
    outputs = jnp.stack(out_list)[None]
    input_grad = jnp.stack(grad_list)[None]
    return (
        outputs,
        input_grad,
        attn_parts[0],
        attn_parts[1],
        attn_parts[2],
        attn_parts[3],
        ffn_parts[0],
        ffn_parts[1],
        ffn_parts[2],
        attn_parts[4],
        ffn_parts[3],
        attn_parts[5],
        attn_parts[6],
    )


MESH = pl.DeviceIdType.MESH
NDP = 4
NSEQ = 8
BLOCKED = -65536.0
QB = 256
BLOCKS = (3, 2, 1, 0)
SOFT = HEAD_DIM ** (-0.5) * 1.4426950408889634


def seq_at(position):
    half = position // 4
    z = position + half * (7 - 2 * position)
    return 2 * z + half


def greet_all(d, s):
    barrier = pltpu.get_barrier_semaphore()
    me = d * NSEQ + s

    def signal(i, carry):
        other = (me + i) % (NDP * NSEQ)
        pl.semaphore_signal(
            barrier, inc=1, device_id=(other // NSEQ, other % NSEQ), device_id_type=MESH
        )
        return carry

    lax.fori_loop(1, NDP * NSEQ, signal, 0)
    pl.semaphore_wait(barrier, NDP * NSEQ - 1)


def remote(src, dst, sems, at, d, s):
    send, recv = sems
    return pltpu.make_async_remote_copy(
        src_ref=src,
        dst_ref=dst,
        send_sem=send.at[at],
        recv_sem=recv.at[at],
        device_id=(d, s),
        device_id_type=MESH,
    )


class Sum:
    def __init__(self, part, near, sent, got, sems, n, spot):
        self.part, self.near, self.sent, self.got = part, near, sent, got
        self.sems, self.n = sems, n
        d, self.s = spot
        x, c = d // 2, d % 2
        self.d, self.sib, self.far = d, 2 * x + 1 - c, 2 * (1 - x) + c
        self.far_sib = 2 * (1 - x) + 1 - c

    def copies(self, b):
        rows = pl.ds(2 * b, 2)
        return (
            remote(self.part.at[rows, self.far_sib], self.near.at[0, rows], self.sems, (self.n, 0, b), self.sib, self.s),
            remote(self.part.at[rows, self.sib], self.near.at[1, rows], self.sems, (self.n, 1, b), self.sib, self.s),
            remote(self.sent.at[rows], self.got.at[rows], self.sems, (self.n, 2, b), self.far, self.s),
        )

    def start(self, b):
        first, second, _ = self.copies(b)
        first.start()
        second.start()

    def mid(self, b):
        first, _, across_x = self.copies(b)
        first.wait_recv()
        for i in (2 * b, 2 * b + 1):
            self.sent[i] = (
                self.part[i, self.far].astype(jnp.float32) + self.near[0, i].astype(jnp.float32)
            ).astype(jnp.bfloat16)
        across_x.start()

    def end(self, b, finish):
        first, second, across_x = self.copies(b)
        second.wait_recv()
        across_x.wait_recv()
        for i in (2 * b, 2 * b + 1):
            rows = self.part[i, self.d].astype(jnp.float32) + self.near[1, i].astype(jnp.float32)
            finish(i, rows + self.got[i].astype(jnp.float32))
        first.wait_send()
        second.wait_send()
        across_x.wait_send()


class Spread:
    def __init__(self, out, sems, at, spot):
        self.out, self.sems, self.place = out, sems, at
        d, self.s = spot
        x, c = d // 2, d % 2
        self.d, self.sib, self.far = d, 2 * x + 1 - c, 2 * (1 - x) + c
        self.far_sib = 2 * (1 - x) + 1 - c

    def copy(self, rows, owner, way, to):
        block = self.out.at[rows, owner]
        return remote(block, block, self.sems, self.place(way, rows), to, self.s)

    def start(self, rows):
        self.copy(rows, self.d, 0, self.far).start()
        self.copy(rows, self.d, 1, self.sib).start()

    def mid(self, rows):
        self.copy(rows, self.far, 0, self.far).wait_recv()
        self.copy(rows, self.far, 2, self.sib).start()

    def end(self, rows):
        self.copy(rows, self.sib, 1, self.sib).wait_recv()
        self.copy(rows, self.far_sib, 2, self.sib).wait_recv()

    def sent(self, rows):
        self.copy(rows, self.d, 0, self.far).wait_send()
        self.copy(rows, self.d, 1, self.sib).wait_send()
        self.copy(rows, self.far, 2, self.sib).wait_send()


def layer_kernel(
    nodes,
    tok, cot, small, inv_freq, wq, wk, wv, wo, wg, wu, wd,
    out_rows, grad_rows, pack_out, g_query, g_key, g_value, g_output, g_gate, g_up, g_down,
    smalls, wa, wb, wc, we, ge, hop_a, hop_b, hop_c, hop_e,
    tree, tree_cot, normed_in, normed_mid, d_low, tree_own,
    lin, query, key, value, hidden, member, cosine, sine, att, d_att,
    part, part_out, near, sent, got, near_o, sent_o, got_o,
    middle, d_middle, act, both, d_key, d_value, outs, grad_low,
    fin_a, fin_c, got_a, got_c, attn_g, ffn_g, head_g, pack_dp, pack_seq,
    loc, s_small, r_small, s_col, r_col, s_tok, r_tok, s_ag, r_ag, s_rs, r_rs,
    s_sum, r_sum, s_tree, r_tree, s_spread, r_spread, s_back, r_back, s_fin, r_fin, s_pack, r_pack,
):
    f32, bf = jnp.float32, jnp.bfloat16
    d = lax.axis_index("dp")
    s = lax.axis_index("seq")
    z, y = s // 2, s % 2
    p = z + y * (7 - 2 * z)
    spot = (d, s)
    seat = [seq_at((p + i) % NSEQ) for i in range(NSEQ)]
    up, down = seat[1], seat[7]
    ag_sems, rs_sems = (s_ag, r_ag), (s_rs, r_rs)
    small_sems, col_sems, tok_sems = (s_small, r_small), (s_col, r_col), (s_tok, r_tok)

    def aligned(v, n):
        return pl.multiple_of(v, n)

    def chunk(n, way, j):
        if n in (0, 1, 3, 4):
            return pl.ds(aligned((2 * way + (n + (n > 2)) % 2) * 256 + j * 32, 32), 32)
        if n == 2:
            return pl.ds(aligned(j * 64 + way * 32, 32), 32)
        return pl.ds(aligned(j * 96 + way * 48, 16), 48)

    weight = {0: wa, 1: wa, 2: wb, 3: wc, 4: wc, 5: we}
    grads = {0: wa, 1: wa, 2: wb, 3: wc, 4: wc, 5: ge}
    hops = {0: hop_a.at[0], 1: hop_a.at[1], 2: hop_b, 3: hop_c.at[0], 4: hop_c.at[1], 5: hop_e}

    def owner_at(way, k):
        return seq_at((p + NSEQ - k) % NSEQ) if way == 0 else seq_at((p + k) % NSEQ)

    def gather(n, k):
        for way, peer in enumerate((up, down)):
            block = weight[n].at[chunk(n, way, owner_at(way, k))]
            if not (isinstance(k, int) and k == 0):
                remote(block, block, ag_sems, (n, way, k - 1), d, peer).wait_recv()
            remote(block, block, ag_sems, (n, way, k), d, peer).start()

    def gather_end(n):
        for way, peer in enumerate((up, down)):
            block = weight[n].at[chunk(n, way, owner_at(way, 7))]
            remote(block, block, ag_sems, (n, way, 6), d, peer).wait_recv()

    def gather_sent(n):
        for way, peer in enumerate((up, down)):
            block = weight[n].at[chunk(n, way, s)]
            for k in range(7):
                remote(block, block, ag_sems, (n, way, k), d, peer).wait_send()

    def reduce_(n, k):
        for way, peer in enumerate((up, down)):
            rows = chunk(n, way, seat[(7 - k) % NSEQ] if way == 0 else seat[(1 + k) % NSEQ])
            mine = grads[n].at[rows]
            if k == 0:
                src = mine
            else:
                src = hops[n].at[way, k - 1]
                remote(src, src, rs_sems, (n, way, k - 1), d, peer).wait_recv()
                src[...] = (src[...].astype(f32) + mine[...].astype(f32)).astype(bf)
            remote(src, hops[n].at[way, k], rs_sems, (n, way, k), d, peer).start()

    def reduce_end(n, take):
        for way, peer in enumerate((up, down)):
            src = hops[n].at[way, 6]
            remote(src, src, rs_sems, (n, way, 6), d, peer).wait_recv()
            take(way, src[...].astype(f32) + grads[n][chunk(n, way, s)].astype(f32))

    def reduce_sent(n):
        for way, peer in enumerate((up, down)):
            for k in range(7):
                src = hops[n].at[way, k]
                remote(src, src, rs_sems, (n, way, k), d, peer).wait_send()

    greet_all(d, s)
    pending = []

    def launch(cp):
        cp.start()
        pending.append(cp)

    own_small = pltpu.make_async_copy(small, smalls.at[d, s], loc.at[0])
    own_small.start()
    pieces = (
        (wq, wa, 512, 0), (wk, wa, 256, 512), (wv, wa, 256, 768), (wg, wc, 768, 0), (wu, wc, 768, 768)
    )
    col_rows = lambda q: pl.ds(aligned(q * 256 + s * 32, 32), 32)
    local = []

    def columns(n):
        src, dst, width, at = pieces[n]
        for i in range(1, NDP):
            q = (d + i) % NDP
            launch(
                remote(
                    src.at[:, pl.ds(aligned(q * width, 128), width)],
                    dst.at[col_rows(d), pl.ds(at, width)],
                    col_sems, (n, i), q, s,
                )
            )
        cp = pltpu.make_async_copy(
            src.at[:, pl.ds(aligned(d * width, 128), width)],
            dst.at[col_rows(d), pl.ds(at, width)],
            loc.at[1 + n],
        )
        cp.start()
        local.append(cp)

    def columns_in(n):
        _, dst, width, at = pieces[n]
        local[n].wait()
        for i in range(1, NDP):
            place = dst.at[col_rows((d + NDP - i) % NDP), pl.ds(at, width)]
            remote(place, place, col_sems, (n, i), d, s).wait_recv()

    def rows_out(n, src, dst):
        for m in range(MICRO):
            target = MICRO * d + m
            for i in range(NDP):
                q = (d + i) % NDP
                piece = src.at[m, pl.ds(aligned(q * 32, 32), 32)]
                place = dst.at[s, q]
                cp = pltpu.make_async_remote_copy(
                    src_ref=piece, dst_ref=place, send_sem=s_tok.at[n, m, i], recv_sem=r_tok.at[n],
                    device_id=(q, target), device_id_type=MESH,
                )
                if i == 0:

                    @pl.when(target == s)
                    def _():
                        pltpu.make_async_copy(piece, place, r_tok.at[n]).start()

                    @pl.when(target != s)
                    def _():
                        cp.start()
                else:
                    launch(cp)

    def rows_in(dst, n):
        everything = dst.at[:, d]
        pltpu.make_async_copy(everything, everything, r_tok.at[n]).wait()

    fill_b = pltpu.make_async_copy(wo, wb.at[pl.ds(aligned(s * 64, 64), 64)], loc.at[6])
    fill_e = pltpu.make_async_copy(wd, we.at[pl.ds(aligned(s * 96, 16), 96)], loc.at[7])
    fill_b.start()
    fill_e.start()
    for n in range(3):
        columns(n)
    rows_out(0, tok, tree)
    own_small.wait()
    for i in range(1, NDP):
        launch(remote(smalls.at[d, s], smalls.at[d, s], small_sems, i, (d + i) % NDP, s))
    fill_b.wait()
    gather(2, 0)
    for n in range(3):
        columns_in(n)
    gather(0, 0)
    gather(1, 0)
    for n in range(3, 5):
        columns(n)
    rows_out(1, cot, tree_cot)
    for i in range(1, NDP):
        place = smalls.at[(d + NDP - i) % NDP, s]
        remote(place, place, small_sems, i, d, s).wait_recv()
    for i in range(1, NSEQ):
        launch(remote(smalls.at[:, s], smalls.at[:, s], small_sems, NDP + i, d, (s + i) % NSEQ))

    def gather_ab(k):
        gather(2, k)
        gather(0, k)
        gather(1, k)

    gather_ab(1)
    everything = pl.ds(0, NSEQ)
    spread_tree = Spread(tree, (s_tree, r_tree), lambda way, rows: (0, way), spot)
    spread_cot = Spread(tree_cot, (s_tree, r_tree), lambda way, rows: (1, way), spot)
    rows_in(tree, 0)
    spread_tree.start(everything)
    ir = lax.broadcasted_iota(jnp.int32, (128, 128), 0)
    ic = lax.broadcasted_iota(jnp.int32, (128, 128), 1)
    block = smalls.at[s // MICRO, s]
    length_row = block[pl.ds(4 + s % MICRO, 1), :]
    parent_row = block[pl.ds(6 + s % MICRO, 1), :]
    length_col = jnp.sum(jnp.where(ir == ic, length_row, 0.0), axis=1, keepdims=True)
    over = (parent_row == ir.astype(f32)) & (ic > 0) & (ic < nodes)
    above = jnp.where(over | (ir == ic), 1.0, 0.0)
    for _ in range(4):
        low = above.astype(bf)
        above = jnp.minimum(product(low, low), 1.0)
    start_row = jnp.sum(jnp.where(ir < ic, length_col, 0.0), axis=0, keepdims=True)
    base_row = jnp.sum(
        jnp.where((above > 0.5) & (ir != ic), length_col, 0.0), axis=0, keepdims=True
    )
    shut = jnp.where(above > 0.5, 0.0, BLOCKED).astype(bf)
    gather_ab(2)

    def tables(i, carry):
        rows = pl.ds(aligned(i * QB, QB), QB)
        index = (lax.broadcasted_iota(jnp.int32, (QB, 128), 0) + i * QB).astype(f32)
        inside = (index >= start_row) & (index < start_row + length_row)
        position = index[:, :1] + jnp.sum(
            jnp.where(inside, base_row - start_row, 0.0), axis=1, keepdims=True
        )
        hot = jnp.where(inside, 1.0, 0.0).astype(bf)
        member[rows] = hot
        hidden[rows] = against(hot, shut).astype(bf)
        angle = position * inv_freq[...]
        cosine[rows] = jnp.cos(angle)
        lane = lax.broadcasted_iota(jnp.int32, (QB, 128), 1)
        wave = jnp.sin(angle)
        sine[rows] = jnp.where(lane < 64, -wave, wave)
        return carry

    lax.fori_loop(0, 2, tables, 0)
    gather_ab(3)
    lax.fori_loop(2, 4, tables, 0)
    spread_tree.mid(everything)
    gather_ab(4)
    for i in range(1, NSEQ):
        place = smalls.at[:, (s + NSEQ - i) % NSEQ]
        remote(place, place, small_sems, NDP + i, d, s).wait_recv()
    lane = lax.broadcasted_iota(jnp.int32, (1, 128), 1)
    for row, dst in ((0, attn_g), (1, ffn_g)):
        for j in range(8):
            parts = [smalls[(4 * j + i) // 8, (4 * j + i) % 8, row : row + 1, :] for i in range(4)]
            joined = jnp.where(lane < 64, jnp.where(lane < 32, parts[0], parts[1]), jnp.where(lane < 96, parts[2], parts[3]))
            dst[:, 128 * j : 128 * (j + 1)] = joined
    for row in (2, 3):
        joined = jnp.zeros((1, 128), f32)
        for i in range(32):
            joined = jnp.where(lane // 4 == i, smalls[i // 8, i % 8, row : row + 1, :], joined)
        head_g[row - 2 : row - 1, :] = joined
    pack_dp[d] = jnp.zeros((24, 128), f32)
    spread_tree.end(everything)
    own_rows = pltpu.make_async_copy(tree.at[:, d], tree_own, loc.at[8])
    own_rows.start()

    def norm_in(i, carry):
        rows = tree[i].reshape(128, D).astype(f32)
        scale = lax.rsqrt(jnp.mean(rows * rows, axis=-1, keepdims=True) + EPSILON)
        normed_in[pl.ds(aligned(i * 128, 128), 128)] = (rows * scale * attn_g[...]).astype(bf)
        return carry

    lax.fori_loop(0, 4, norm_in, 0)
    gather_ab(5)
    lax.fori_loop(4, 8, norm_in, 0)
    gather_ab(6)
    for n in range(3, 5):
        columns_in(n)
    gather(3, 0)
    gather(4, 0)
    rows_in(tree_cot, 1)
    spread_cot.start(everything)
    gather_end(0)
    gather_end(1)

    def unit_of(v):
        scale = lax.rsqrt(jnp.mean(v * v, axis=-1, keepdims=True) + EPSILON)
        return v * scale, scale

    def turn(v, gain, cos, sin):
        unit, _ = unit_of(v)
        lifted = unit * gain
        return lifted * cos + pltpu.roll(lifted, 64, 1) * sin

    def turn_back(dr, v, gain, cos, sin):
        d_lift = dr * cos + pltpu.roll(dr * sin, 64, 1)
        unit, scale = unit_of(v)
        d_unit = d_lift * gain
        return (
            scale * (d_unit - unit * jnp.mean(unit * d_unit, axis=-1, keepdims=True)),
            jnp.sum(d_lift * unit, axis=0, keepdims=True),
        )

    def project(i, carry):
        rows = pl.ds(aligned(i * QB, QB), QB)
        normed = normed_in[rows]
        cos, sin = cosine[rows], sine[rows]
        for j in range(3):
            pair = product(normed, wa[:, 256 * j : 256 * (j + 1)])
            lin[rows, 256 * j : 256 * (j + 1)] = pair
            gain = head_g[0:1, :] if j < 2 else head_g[1:2, :]
            for i2 in range(2):
                turned = turn(pair[:, 128 * i2 : 128 * (i2 + 1)], gain, cos, sin).astype(bf)
                if j < 2:
                    query[2 * j + i2, rows] = turned
                else:
                    key[i2, rows] = turned
        value[rows] = product(normed, wa[:, 768:]).astype(bf)
        gather(3, 1 + i)
        gather(4, 1 + i)
        return carry

    lax.fori_loop(0, 4, project, 0)
    gather_end(2)
    spread_cot.mid(everything)
    fill_e.wait()

    def span(b):
        return pl.ds(b * QB, QB), (b + 1) * QB

    def weights_of(b, h, n):
        here = pl.ds(b * QB, QB)
        q = jnp.concatenate([query[h, here], hidden[here]], axis=1)
        k = jnp.concatenate([key[h // 2, pl.ds(0, n)], member[pl.ds(0, n)]], axis=1)
        score = against(q, k) * SOFT
        row = lax.broadcasted_iota(jnp.int32, (QB, QB), 0)
        col = lax.broadcasted_iota(jnp.int32, (QB, QB), 1)
        diag = jnp.where(col <= row, score[:, n - QB :], NEGATIVE)
        score = diag if b == 0 else jnp.concatenate([score[:, : n - QB], diag], axis=1)
        grown = jnp.exp2(score)
        return grown, 1.0 / jnp.sum(grown, axis=-1, keepdims=True)

    def head_lanes(h):
        return pl.ds(aligned(h * HEAD_DIM, HEAD_DIM), HEAD_DIM)

    def attend(b):
        here, n = span(b)

        def one(h, carry):
            grown, inverse = weights_of(b, h, n)
            mixed = product(grown.astype(bf), value[pl.ds(0, n), head_lanes(h // 2)])
            att[here, head_lanes(h)] = (mixed * inverse).astype(bf)
            return carry

        lax.fori_loop(0, HEADS // NDP, one, 0)
        rows = product(att[here], wb[...]).astype(bf)
        part[pl.ds(2 * b, 2)] = rows.reshape(2, NDP, 32, D)

    sum_sems, spread_sems = (s_sum, r_sum), (s_spread, r_spread)
    mixed_sum = Sum(part, near, sent, got, sum_sems, 0, spot)
    mid_sum = Sum(part, near, sent, got, sum_sems, 1, spot)
    out_sum = Sum(part_out, near_o, sent_o, got_o, sum_sems, 2, spot)
    in_sum = Sum(part, near, sent, got, sum_sems, 3, spot)
    pair_of = {b: pl.ds(2 * b, 2) for b in BLOCKS}
    spread_mid = Spread(normed_mid, spread_sems, lambda way, rows: (0, way, rows.start // 2), spot)
    spread_low = Spread(d_low, spread_sems, lambda way, rows: (1, way, rows.start // 2), spot)

    def to_middle(i, rows):
        rows = rows + tree_own[i].astype(f32)
        middle[i] = rows
        scale = lax.rsqrt(jnp.mean(rows * rows, axis=-1, keepdims=True) + EPSILON)
        normed_mid[i, d] = (rows * scale * ffn_g[...]).astype(bf)

    own_rows.wait()
    attend(3)
    mixed_sum.start(3)
    gather(3, 5)
    gather(4, 5)
    attend(2)
    mixed_sum.mid(3)
    mixed_sum.start(2)
    gather(3, 6)
    gather(4, 6)
    gather(5, 0)
    attend(1)
    mixed_sum.end(3, to_middle)
    spread_mid.start(pair_of[3])
    mixed_sum.mid(2)
    mixed_sum.start(1)
    gather(5, 1)
    attend(0)
    spread_mid.mid(pair_of[3])
    mixed_sum.end(2, to_middle)
    spread_mid.start(pair_of[2])
    mixed_sum.mid(1)
    mixed_sum.start(0)
    spread_cot.end(everything)
    gather_end(3)
    gather_end(4)
    gather(5, 2)

    def lift(b):
        here = pl.ds(b * QB, QB)
        rows = normed_mid[pl.ds(2 * b, 2)].reshape(QB, D)

        def one(t, carry):
            left = pl.ds(aligned(t * 256, 256), 256)
            right = pl.ds(aligned(768 + t * 256, 256), 256)
            gate = product(rows, wc[:, left])
            wide = product(rows, wc[:, right])
            sigma = 1.0 / (1.0 + jnp.exp(-gate))
            silu = gate * sigma
            act[here, left] = (silu * wide).astype(bf)
            both[here, left] = (wide * sigma * (1.0 + gate * (1.0 - sigma))).astype(bf)
            both[here, right] = silu.astype(bf)
            return carry

        lax.fori_loop(0, 3, one, 0)

    spread_mid.end(pair_of[3])
    lift(3)
    spread_mid.mid(pair_of[2])
    mixed_sum.end(1, to_middle)
    spread_mid.start(pair_of[1])
    mixed_sum.mid(0)
    gather(5, 3)
    spread_mid.end(pair_of[2])
    lift(2)
    spread_mid.mid(pair_of[1])
    mixed_sum.end(0, to_middle)
    spread_mid.start(pair_of[0])
    gather(5, 4)
    spread_mid.end(pair_of[1])
    lift(1)
    spread_mid.mid(pair_of[0])
    gather(5, 5)
    spread_mid.end(pair_of[0])
    lift(0)
    gather(5, 6)

    def grad_down(i, carry):
        cols = pl.ds(aligned(i * 256, 256), 256)
        ge[cols] = across(act[:, cols], tree_cot[...].reshape(NSEQ * 128, D)).astype(bf)
        return carry

    lax.fori_loop(0, 3, grad_down, 0)
    reduce_(5, 0)
    gather_end(5)

    def sink(b):
        here = pl.ds(b * QB, QB)
        cots = tree_cot[pl.ds(2 * b, 2)].reshape(QB, D)

        def one(t, carry):
            left = pl.ds(aligned(t * 256, 256), 256)
            right = pl.ds(aligned(768 + t * 256, 256), 256)
            d_act = against(cots, we[left])
            both[here, left] = (d_act * both[here, left].astype(f32)).astype(bf)
            both[here, right] = (d_act * both[here, right].astype(f32)).astype(bf)
            return carry

        lax.fori_loop(0, 3, one, 0)
        part[pl.ds(2 * b, 2)] = against(both[here], wc[...]).astype(bf).reshape(2, NDP, 32, D)
        mid_sum.start(b)
        part_out[pl.ds(2 * b, 2)] = product(act[here], we[...]).astype(bf).reshape(2, NDP, 32, D)
        out_sum.start(b)

    def to_turn(i, rows):
        unit, scale = unit_of(middle[i])
        lifted = ffn_g[...] * rows
        term = jnp.sum(rows * unit, axis=0, keepdims=True)
        for j in range(8):
            pack_dp[d, 8 + j : 9 + j] += term[:, 128 * j : 128 * (j + 1)]
        d_mid = tree_cot[i, d].astype(f32) + scale * (
            lifted - unit * jnp.mean(unit * lifted, axis=-1, keepdims=True)
        )
        d_middle[i] = d_mid
        d_low[i, d] = d_mid.astype(bf)

    def to_outs(i, rows):
        outs[i] = (middle[i] + rows).astype(bf)

    back_owner, back_slot = s // MICRO, s % MICRO

    def give(n, src, dst, j, begin):
        place = dst.at[back_slot, pl.ds(aligned(d * 32, 32), 32)]
        same = (back_owner == d) & (s == j)
        cp = pltpu.make_async_remote_copy(
            src_ref=src.at[j], dst_ref=place, send_sem=s_back.at[n, j], recv_sem=r_back.at[n],
            device_id=(back_owner, j), device_id_type=MESH,
        )

        @pl.when(same)
        def _():
            if begin:
                pltpu.make_async_copy(src.at[j], place, r_back.at[n]).start()

        @pl.when(jnp.logical_not(same))
        def _():
            if begin:
                cp.start()
            else:
                cp.wait_send()

    sink(3)
    reduce_(5, 1)
    sink(2)
    mid_sum.mid(3)
    reduce_(5, 2)
    sink(1)
    mid_sum.end(3, to_turn)
    spread_low.start(pair_of[3])
    mid_sum.mid(2)
    reduce_(5, 3)
    sink(0)
    spread_low.mid(pair_of[3])
    mid_sum.end(2, to_turn)
    spread_low.start(pair_of[2])
    mid_sum.mid(1)
    reduce_(5, 4)
    gather_sent(3)
    gather_sent(4)

    def grad_wide(i):
        cols = pl.ds(i * 256, 256)
        for t in range(3):
            lanes = pl.ds(512 * t, 512)
            wc[cols, lanes] = across(
                normed_mid[:, :, :, cols].reshape(NSEQ * 128, 256), both[:, lanes]
            ).astype(bf)

    grad_wide(0)
    grad_wide(2)
    reduce_(3, 0)
    spread_low.mid(pair_of[2])
    mid_sum.end(1, to_turn)
    spread_low.start(pair_of[1])
    mid_sum.mid(0)
    reduce_(5, 5)
    grad_wide(1)
    grad_wide(3)
    reduce_(4, 0)
    spread_low.mid(pair_of[1])
    mid_sum.end(0, to_turn)
    spread_low.start(pair_of[0])
    reduce_(5, 6)

    d_key[...] = jnp.zeros_like(d_key)
    d_value[...] = jnp.zeros_like(d_value)
    d_lin = tree

    def open_low(b):
        here = pl.ds(b * QB, QB)
        rows = d_low[pl.ds(2 * b, 2)].reshape(QB, D)
        d_att[here] = against(rows, wb[...]).astype(bf)

    def attend_back(b):
        here, n = span(b)
        keys = pl.ds(0, n)

        def one(h, carry):
            kv = h // 2
            grown, inverse = weights_of(b, h, n)
            prob = grown * inverse
            d_out = d_att[here, head_lanes(h)]
            d_prob = against(d_out, value[keys, head_lanes(kv)])
            delta = jnp.sum(prob * d_prob, axis=-1, keepdims=True)
            d_raw = (prob * (d_prob - delta) * HEAD_DIM ** (-0.5)).astype(bf)
            d_rot = product(d_raw, key[kv, keys])
            d_key[kv, keys] += across(d_raw, query[h, here])
            d_value[kv, keys] += across(prob.astype(bf), d_out)
            back, d_gain = turn_back(
                d_rot, lin[here, head_lanes(h)], head_g[0:1, :], cosine[here], sine[here]
            )
            pack_dp[d, 16:17] += d_gain
            d_lin[pl.ds(2 * b, 2), :, :, head_lanes(h)] = back.astype(bf).reshape(2, NDP, 32, HEAD_DIM)
            return carry

        lax.fori_loop(0, HEADS // NDP, one, 0)
        for kv in range(KV_HEADS // NDP):
            back, d_gain = turn_back(
                d_key[kv, here], lin[here, pl.ds(512 + 128 * kv, 128)], head_g[1:2, :], cosine[here], sine[here]
            )
            pack_dp[d, 17:18] += d_gain
            d_lin[pl.ds(2 * b, 2), :, :, pl.ds(512 + 128 * kv, 128)] = back.astype(bf).reshape(2, NDP, 32, 128)
            d_lin[pl.ds(2 * b, 2), :, :, pl.ds(768 + 128 * kv, 128)] = (
                d_value[kv, here].astype(bf).reshape(2, NDP, 32, 128)
            )
        rows = against(d_lin[pl.ds(2 * b, 2)].reshape(QB, 1024), wa[...])
        part[pl.ds(2 * b, 2)] = rows.astype(bf).reshape(2, NDP, 32, D)
        in_sum.start(b)

    spread_tree.sent(everything)
    gather_sent(0)
    gather_sent(1)
    gather_sent(2)
    spread_low.end(pair_of[3])
    open_low(3)
    attend_back(3)
    reduce_(3, 1)
    reduce_(4, 1)
    spread_low.mid(pair_of[0])
    for b in (2, 1, 0):
        spread_low.end(pair_of[b])
        open_low(b)
    for i in range(2):
        cols = pl.ds(256 * i, 256)
        wb[cols] = across(att[:, cols], d_low[...].reshape(NSEQ * 128, D)).astype(bf)
    reduce_(2, 0)
    for b in BLOCKS:
        out_sum.mid(b)
    attend_back(2)
    in_sum.mid(3)
    reduce_(3, 2)
    reduce_(4, 2)
    reduce_(2, 1)
    for b in BLOCKS:
        out_sum.end(b, to_outs)
    for j in range(NSEQ):
        give(0, outs, out_rows, j, True)

    def to_grad(i, rows):
        unit, scale = unit_of(tree_own[i].astype(f32))
        lifted = attn_g[...] * rows
        term = jnp.sum(rows * unit, axis=0, keepdims=True)
        for j in range(8):
            pack_dp[d, j : j + 1] += term[:, 128 * j : 128 * (j + 1)]
        grad = d_middle[i] + scale * (
            lifted - unit * jnp.mean(unit * lifted, axis=-1, keepdims=True)
        )
        grad_low[i] = grad.astype(bf)

    def close_in(b):
        in_sum.end(b, to_grad)
        give(1, grad_low, grad_rows, 2 * b, True)
        give(1, grad_low, grad_rows, 2 * b + 1, True)

    attend_back(1)
    close_in(3)
    in_sum.mid(2)
    reduce_(3, 3)
    reduce_(4, 3)
    reduce_(2, 2)
    attend_back(0)
    close_in(2)
    in_sum.mid(1)
    reduce_(3, 4)
    reduce_(4, 4)
    reduce_(2, 3)

    def grad_attn(i):
        cols = pl.ds(i * 256, 256)
        for t in range(2):
            lanes = pl.ds(512 * t, 512)
            wa[cols, lanes] = across(
                normed_in[:, cols], d_lin[:, :, :, lanes].reshape(NSEQ * 128, 512)
            ).astype(bf)

    grad_attn(0)
    grad_attn(2)
    reduce_(0, 0)
    in_sum.mid(0)
    close_in(1)
    grad_attn(1)
    grad_attn(3)
    reduce_(1, 0)
    close_in(0)

    pack_sems, fin_sems = (s_pack, r_pack), (s_fin, r_fin)
    for i in range(1, NDP):
        launch(remote(pack_dp.at[d], pack_dp.at[d], pack_sems, i, (d + i) % NDP, s))

    def close_cols(n, fin, landed, which):
        sub = (n + (n > 2)) % 2

        def take(way, total):
            fin[2 * way + sub] = total.astype(bf)

        reduce_end(n, take)
        for way in range(2):
            q = 2 * way + sub

            @pl.when(q == d)
            def _():
                landed[d] = fin[q]

            @pl.when(q != d)
            def _():
                remote(fin.at[q], landed.at[d], fin_sems, (which, d), q, s).start()

    def land(fin, landed, which, cuts):
        for i in range(1, NDP):
            q = (d + i) % NDP
            remote(landed.at[q], landed.at[q], fin_sems, (which, q), q, s).wait_recv()
        for q in range(NDP):
            for at, width, dst in cuts:
                dst[:, width * q : width * (q + 1)] = landed[q, :, at : at + width].astype(f32)

    reduce_(2, 4)
    reduce_(3, 5)
    reduce_(4, 5)
    reduce_(0, 1)
    reduce_(1, 1)
    for i in range(1, NDP):
        place = pack_dp.at[(d + NDP - i) % NDP]
        remote(place, place, pack_sems, i, d, s).wait_recv()
    pack_seq[s] = (pack_dp[0] + pack_dp[1]) + (pack_dp[2] + pack_dp[3])
    for i in range(1, NSEQ):
        launch(remote(pack_seq.at[s], pack_seq.at[s], pack_sems, NDP + i, d, (s + i) % NSEQ))
    reduce_(2, 5)
    reduce_(3, 6)
    reduce_(4, 6)
    reduce_(0, 2)
    reduce_(1, 2)
    reduce_(2, 6)
    reduce_(0, 3)
    reduce_(1, 3)
    close_cols(3, fin_c, got_c, 1)
    close_cols(4, fin_c, got_c, 1)

    def take_down(way, total):
        g_down[48 * way : 48 * (way + 1)] = total

    def take_output(way, total):
        g_output[32 * way : 32 * (way + 1)] = total

    reduce_(0, 4)
    reduce_(1, 4)
    reduce_end(5, take_down)
    reduce_end(2, take_output)
    reduce_(0, 5)
    reduce_(1, 5)
    land(fin_c, got_c, 1, ((0, 768, g_gate), (768, 768, g_up)))
    reduce_(0, 6)
    reduce_(1, 6)
    for i in range(1, NSEQ):
        place = pack_seq.at[(s + NSEQ - i) % NSEQ]
        remote(place, place, pack_sems, NDP + i, d, s).wait_recv()
    total = pack_seq[0]
    for j in range(1, NSEQ):
        total = total + pack_seq[j]
    pack_out[...] = total
    close_cols(0, fin_a, got_a, 0)
    close_cols(1, fin_a, got_a, 0)
    land(fin_a, got_a, 0, ((0, 512, g_query), (512, 256, g_key), (768, 256, g_value)))

    for n, dst in enumerate((out_rows, grad_rows)):
        pltpu.make_async_copy(dst, dst, r_back.at[n]).wait()
    for j in range(NSEQ):
        give(0, outs, out_rows, j, False)
        give(1, grad_low, grad_rows, j, False)
    for n, (fin, landed) in enumerate(((fin_a, got_a), (fin_c, got_c))):
        for i in range(1, NDP):
            q = (d + i) % NDP
            remote(fin.at[q], landed.at[d], fin_sems, (n, d), q, s).wait_send()
    gather_sent(5)
    for n in range(6):
        reduce_sent(n)
    spread_cot.sent(everything)
    for b in BLOCKS:
        spread_mid.sent(pair_of[b])
        spread_low.sent(pair_of[b])
    for cp in pending:
        cp.wait_send()
    for n in range(2):
        for m in range(MICRO):

            @pl.when(MICRO * d + m != s)
            def _():
                place = tree.at[s, d]
                pltpu.make_async_remote_copy(
                    src_ref=place, dst_ref=place, send_sem=s_tok.at[n, m, 0], recv_sem=r_tok.at[n],
                    device_id=(d, s), device_id_type=MESH,
                ).wait_send()


def tree_shards(
    tokens, cotangent, node_lengths, parents, w_query, w_key, w_value, w_output, w_gate, w_up, w_down,
    attn_gain, ffn_gain, query_gain, key_gain,
):
    f32, bf = jnp.float32, jnp.bfloat16
    d, s = lax.axis_index("dp"), lax.axis_index("seq")
    nodes = node_lengths.shape[2]
    wide = ((0, 0), (0, 128 - nodes))
    small = jnp.concatenate(
        [
            jnp.tile(attn_gain.astype(f32), 4)[None],
            jnp.tile(ffn_gain.astype(f32), 4)[None],
            jnp.tile(query_gain.astype(f32), 32)[None],
            jnp.tile(key_gain.astype(f32), 32)[None],
            jnp.pad(node_lengths[0].astype(f32), wide),
            jnp.pad(parents[0].astype(f32), wide),
        ]
    )
    half = jnp.arange(HEAD_DIM // 2, dtype=f32)
    inv_freq = THETA ** (-(half * (2.0 / HEAD_DIM)))
    inv_freq = jnp.concatenate([inv_freq, inv_freq])[None]
    shape, vmem, dma = jax.ShapeDtypeStruct, pltpu.VMEM, pltpu.SemaphoreType.DMA
    anywhere = pl.BlockSpec(memory_space=pl.ANY)
    here = pl.BlockSpec(memory_space=pltpu.VMEM)
    rows = NSEQ * 128
    quarter = (NSEQ, 32, D)
    twice = lambda *dims: [dma(dims), dma(dims)]
    results = pl.pallas_call(
        functools.partial(layer_kernel, nodes),
        out_shape=(
            shape((MICRO, 128, D), bf),
            shape((MICRO, 128, D), bf),
            shape((24, 128), f32),
            shape((32, 2048), f32),
            shape((32, 1024), f32),
            shape((32, 1024), f32),
            shape((64, D), f32),
            shape((32, FF), f32),
            shape((32, FF), f32),
            shape((96, D), f32),
        ),
        in_specs=[anywhere] * 3 + [here] + [anywhere] * 7,
        out_specs=[anywhere] * 2 + [here] * 8,
        scratch_shapes=[
            vmem((NDP, NSEQ, 8, 128), f32),
            vmem((D, 1024), bf), vmem((512, D), bf), vmem((D, 1536), bf), vmem((768, D), bf),
            vmem((768, D), bf),
            vmem((2, 2, 7, 32, 1024), bf), vmem((2, 7, 32, D), bf),
            vmem((2, 2, 7, 32, 1536), bf), vmem((2, 7, 48, D), bf),
            vmem((NSEQ, NDP, 32, D), bf), vmem((NSEQ, NDP, 32, D), bf), vmem((rows, D), bf),
            vmem((NSEQ, NDP, 32, D), bf), vmem((NSEQ, NDP, 32, D), bf), vmem(quarter, bf),
            vmem((rows, 768), f32), vmem((4, rows, 128), bf), vmem((2, rows, 128), bf),
            vmem((rows, 256), bf), vmem((rows, 128), bf), vmem((rows, 128), bf),
            vmem((rows, 128), f32), vmem((rows, 128), f32), vmem((rows, 512), bf), vmem((rows, 512), bf),
            vmem((NSEQ, NDP, 32, D), bf), vmem((NSEQ, NDP, 32, D), bf),
            vmem((2,) + quarter, bf), vmem(quarter, bf), vmem(quarter, bf),
            vmem((2,) + quarter, bf), vmem(quarter, bf), vmem(quarter, bf),
            vmem(quarter, f32), vmem(quarter, f32), vmem((rows, 768), bf), vmem((rows, 1536), bf),
            vmem((2, rows, 128), f32), vmem((2, rows, 128), f32), vmem(quarter, bf), vmem(quarter, bf),
            vmem((NDP, 32, 1024), bf), vmem((NDP, 32, 1536), bf),
            vmem((NDP, 32, 1024), bf), vmem((NDP, 32, 1536), bf),
            vmem((1, D), f32), vmem((1, D), f32), vmem((8, 128), f32),
            vmem((NDP, 24, 128), f32), vmem((NSEQ, 24, 128), f32),
            dma((9,)),
            *twice(12), *twice(5, NDP), dma((2, MICRO, NDP)), dma((2,)),
            *twice(6, 2, 7), *twice(6, 2, 7),
            *twice(4, 3, 4), *twice(2, 3), *twice(2, 3, 4),
            dma((2, NSEQ)), dma((2,)), *twice(2, NDP), *twice(12),
        ],
        compiler_params=pltpu.CompilerParams(
            collective_id=1, has_side_effects=True, vmem_limit_bytes=61 << 20
        ),
        name="layer",
    )(
        tokens[0], cotangent[0], small, inv_freq,
        w_query, w_key, w_value, w_output, w_gate, w_up, w_down,
    )
    out_rows, grad_rows, pack, g_query, g_key, g_value, g_output, g_gate, g_up, g_down = results
    at = d * NSEQ + s
    own = lambda piece, n: lax.dynamic_slice_in_dim(piece.reshape(-1), at * n, n)
    return (
        out_rows[None],
        grad_rows[None].astype(f32),
        g_query, g_key, g_value, g_output, g_gate, g_up, g_down,
        own(pack[:8], 32),
        own(pack[8:16], 32),
        own(pack[16], 4),
        own(pack[17], 4),
    )


def solution(mesh):
    ring = mesh.shape["dp"] == NDP and mesh.shape["seq"] == NSEQ
    return jax.shard_map(
        tree_shards if ring else general_shards,
        mesh=mesh,
        in_specs=(
            P("dp", None, "seq", None),
            P("dp", None, "seq", None),
            P("dp", None, None),
            P("dp", None, None),
            P(("dp", "seq"), None),
            P(("dp", "seq"), None),
            P(("dp", "seq"), None),
            P(("dp", "seq"), None),
            P(("dp", "seq"), None),
            P(("dp", "seq"), None),
            P(("dp", "seq"), None),
            P(("dp", "seq")),
            P(("dp", "seq")),
            P(("dp", "seq")),
            P(("dp", "seq")),
        ),
        out_specs=(
            P("dp", None, "seq", None),
            P("dp", None, "seq", None),
            P(("dp", "seq"), None),
            P(("dp", "seq"), None),
            P(("dp", "seq"), None),
            P(("dp", "seq"), None),
            P(("dp", "seq"), None),
            P(("dp", "seq"), None),
            P(("dp", "seq"), None),
            P(("dp", "seq")),
            P(("dp", "seq")),
            P(("dp", "seq")),
            P(("dp", "seq")),
        ),
        check_vma=False,
    )
```

```python
import functools

import jax
import jax.numpy as jnp
import numpy as np
from jax import lax
from jax.experimental import pallas as pl
from jax.experimental.pallas import tpu as pltpu
from jax.sharding import PartitionSpec as P

D = 1024
HEADS = 16
KV_HEADS = 8
HEAD_DIM = 128
FF = 3072
MICRO = 2


EPSILON = 1e-06
THETA = 1000000.0
NEGATIVE = -1e30
PRECISE = lax.Precision.HIGHEST


def norm_rows(values, row_gain):
    return (
        values * lax.rsqrt(jnp.mean(values * values, axis=-1, keepdims=True) + EPSILON) * row_gain
    )


def rope_tables(position, head_dim):
    half_dim = head_dim // 2
    inv_freq = THETA ** (-(jnp.arange(half_dim, dtype=jnp.float32) * (2.0 / head_dim)))
    angles = position.astype(jnp.float32)[:, None] * inv_freq[None, :]
    cosine_table = jnp.cos(angles)
    sine_table = jnp.sin(angles)
    return (
        jnp.concatenate([cosine_table, cosine_table], axis=1),
        jnp.concatenate([sine_table, sine_table], axis=1),
    )


def rotate(values, cosine_table, sine_table):
    half_dim = values.shape[-1] // 2
    turned = jnp.concatenate([-values[..., half_dim:], values[..., :half_dim]], axis=-1)
    return values * cosine_table[:, None, :] + turned * sine_table[:, None, :]


def tree_tables(lengths, parent_row):
    node_count = lengths.shape[0]
    labels = jnp.arange(node_count, dtype=jnp.int32)
    parent_hot = ((parent_row[:, None] == labels[None, :]) & (labels[:, None] > 0)).astype(
        jnp.int32
    )

    def extend(depth_step, state_pair):
        reached, covered = state_pair
        reached = jnp.sum(reached[:, :, None] * parent_hot[None, :, :], axis=1)
        return (reached, covered + reached)

    reached, covered = lax.fori_loop(0, node_count, extend, (parent_hot, parent_hot))
    ancestry = (covered > 0).astype(jnp.float32)
    starts = jnp.cumsum(lengths) - lengths
    path_base = jnp.sum(jnp.where(covered > 0, lengths[None, :], 0), axis=1)
    return (labels, starts, path_base, ancestry)


def token_nodes(token_index, labels, starts, path_base):
    node_id = jnp.sum((token_index[:, None] >= starts[None, 1:]).astype(jnp.int32), axis=1)
    member = node_id[:, None] == labels[None, :]
    offset = jnp.sum(jnp.where(member, (path_base - starts)[None, :], 0), axis=1)
    return (member.astype(jnp.float32), token_index + offset)


def visible(query_member, query_index, key_member, key_index, ancestry):
    numbers = (((1,), (1,)), ((), ()))
    lifted = jnp.dot(query_member, ancestry, precision=PRECISE)
    above = lax.dot_general(lifted, key_member, numbers, precision=PRECISE)
    same_node = lax.dot_general(query_member, key_member, numbers, precision=PRECISE)
    return (above > 0.5) | (same_node > 0.5) & (key_index[None, :] <= query_index[:, None])


def product(left_side, right_side):
    return jnp.dot(left_side, right_side, preferred_element_type=jnp.float32)


def against(left_side, right_side):
    return lax.dot_general(
        left_side, right_side, (((1,), (1,)), ((), ())), preferred_element_type=jnp.float32
    )


def across(left_side, right_side):
    return lax.dot_general(
        left_side, right_side, (((0,), (0,)), ((), ())), preferred_element_type=jnp.float32
    )


def general_shards(
    tokens,
    cotangent,
    node_lengths,
    parents,
    w_query,
    w_key,
    w_value,
    w_output,
    w_gate,
    w_up,
    w_down,
    attn_gain,
    ffn_gain,
    query_gain,
    key_gain,
):
    rows_here = tokens.shape[2]
    length = lax.axis_size("seq") * rows_here
    group_size = HEADS // KV_HEADS
    pair_count = KV_HEADS // 2
    width_query = 2 * group_size * HEAD_DIM
    width_key = 2 * HEAD_DIM
    score_scale = HEAD_DIM ** (-0.5)
    local_index = lax.axis_index("seq") * rows_here + jnp.arange(rows_here, dtype=jnp.int32)
    full_index = jnp.arange(length, dtype=jnp.int32)
    pair_ids = jnp.arange(pair_count, dtype=jnp.int32)
    float_type = jnp.float32
    brain_type = jnp.bfloat16
    sums = (
        jnp.zeros((D, HEADS * HEAD_DIM), float_type),
        jnp.zeros((D, KV_HEADS * HEAD_DIM), float_type),
        jnp.zeros((D, KV_HEADS * HEAD_DIM), float_type),
        jnp.zeros((HEADS * HEAD_DIM, D), float_type),
        jnp.zeros((D, FF), float_type),
        jnp.zeros((D, FF), float_type),
        jnp.zeros((FF, D), float_type),
        jnp.zeros((D,), float_type),
        jnp.zeros((D,), float_type),
        jnp.zeros((HEAD_DIM,), float_type),
        jnp.zeros((HEAD_DIM,), float_type),
    )
    out_list = []
    grad_list = []
    for batch_index in range(MICRO):
        attn_fwd = (
            lax.all_gather(w_query, ("dp", "seq"), axis=0, tiled=True),
            lax.all_gather(w_key, ("dp", "seq"), axis=0, tiled=True),
            lax.all_gather(w_value, ("dp", "seq"), axis=0, tiled=True),
            lax.all_gather(w_output, ("dp", "seq"), axis=0, tiled=True),
            lax.all_gather(attn_gain, ("dp", "seq"), axis=0, tiled=True),
            lax.all_gather(query_gain, ("dp", "seq"), axis=0, tiled=True),
            lax.all_gather(key_gain, ("dp", "seq"), axis=0, tiled=True),
        )
        ffn_fwd = (
            lax.all_gather(w_gate, ("dp", "seq"), axis=0, tiled=True),
            lax.all_gather(w_up, ("dp", "seq"), axis=0, tiled=True),
            lax.all_gather(w_down, ("dp", "seq"), axis=0, tiled=True),
            lax.all_gather(ffn_gain, ("dp", "seq"), axis=0, tiled=True),
        )
        query_w, key_w, value_w, output_w, attn_g, query_g, key_g = attn_fwd
        gate_w, up_w, down_w, ffn_g = ffn_fwd
        labels, starts, path_base, ancestry = tree_tables(
            node_lengths[0, batch_index], parents[0, batch_index]
        )
        member_here, position = token_nodes(local_index, labels, starts, path_base)
        member_all, unused_position = token_nodes(full_index, labels, starts, path_base)
        keep_mask = visible(member_here, local_index, member_all, full_index, ancestry)
        cosine_table, sine_table = rope_tables(position, HEAD_DIM)
        rows_in = tokens[0, batch_index].astype(float_type)
        attn_g32 = attn_g.astype(float_type)
        query_g32 = query_g.astype(float_type)
        key_g32 = key_g.astype(float_type)
        normed_in = norm_rows(rows_in, attn_g32).astype(brain_type)
        query_heads = product(normed_in, query_w).reshape(rows_here, HEADS, HEAD_DIM)
        key_heads = product(normed_in, key_w).reshape(rows_here, KV_HEADS, HEAD_DIM)
        value_low = product(normed_in, value_w).astype(brain_type)
        query_rot = (
            rotate(norm_rows(query_heads, query_g32), cosine_table, sine_table)
            .astype(brain_type)
            .reshape(rows_here, HEADS * HEAD_DIM)
        )
        key_rot = (
            rotate(norm_rows(key_heads, key_g32), cosine_table, sine_table)
            .astype(brain_type)
            .reshape(rows_here, KV_HEADS * HEAD_DIM)
        )
        key_all, value_all = (
            lax.all_gather(key_rot, "seq", axis=0, tiled=True),
            lax.all_gather(value_low, "seq", axis=0, tiled=True),
        )

        def attend_pair(pair_id):
            query_pair = lax.dynamic_slice_in_dim(
                query_rot, pair_id * width_query, width_query, 1
            ).reshape(rows_here, 2, group_size, HEAD_DIM)
            key_pair = lax.dynamic_slice_in_dim(key_all, pair_id * width_key, width_key, 1).reshape(
                length, 2, HEAD_DIM
            )
            value_pair = lax.dynamic_slice_in_dim(
                value_all, pair_id * width_key, width_key, 1
            ).reshape(length, 2, HEAD_DIM)
            raw_score = jnp.einsum(
                "qhgd,khd->hgqk", query_pair, key_pair, preferred_element_type=jnp.float32
            )
            scores = jnp.where(keep_mask[None, None], raw_score * score_scale, NEGATIVE)
            row_top = jnp.max(scores, axis=-1, keepdims=True)
            weight = jnp.exp(scores - row_top)
            row_total = jnp.sum(weight, axis=-1, keepdims=True)
            soft_low = (weight / row_total).astype(jnp.bfloat16)
            mixed = jnp.einsum(
                "hgqk,khd->qhgd", soft_low, value_pair, preferred_element_type=jnp.float32
            )
            return (mixed, row_top + jnp.log(row_total))

        mixed_pairs, log_totals = lax.map(attend_pair, pair_ids)
        attended = (
            mixed_pairs.transpose(1, 0, 2, 3, 4)
            .reshape(rows_here, HEADS * HEAD_DIM)
            .astype(brain_type)
        )
        middle = rows_in + product(attended, output_w)
        ffn_g32 = ffn_g.astype(float_type)
        normed_mid = norm_rows(middle, ffn_g32).astype(brain_type)
        gate_lin = product(normed_mid, gate_w)
        up_lin = product(normed_mid, up_w)
        activated = (jax.nn.silu(gate_lin) * up_lin).astype(brain_type)
        out_list.append((middle + product(activated, down_w)).astype(brain_type))
        attn_back = (
            lax.all_gather(w_query, ("dp", "seq"), axis=0, tiled=True),
            lax.all_gather(w_key, ("dp", "seq"), axis=0, tiled=True),
            lax.all_gather(w_value, ("dp", "seq"), axis=0, tiled=True),
            lax.all_gather(w_output, ("dp", "seq"), axis=0, tiled=True),
            lax.all_gather(attn_gain, ("dp", "seq"), axis=0, tiled=True),
            lax.all_gather(query_gain, ("dp", "seq"), axis=0, tiled=True),
            lax.all_gather(key_gain, ("dp", "seq"), axis=0, tiled=True),
        )
        ffn_back = (
            lax.all_gather(w_gate, ("dp", "seq"), axis=0, tiled=True),
            lax.all_gather(w_up, ("dp", "seq"), axis=0, tiled=True),
            lax.all_gather(w_down, ("dp", "seq"), axis=0, tiled=True),
            lax.all_gather(ffn_gain, ("dp", "seq"), axis=0, tiled=True),
        )
        key_back, value_back = (
            lax.all_gather(key_rot, "seq", axis=0, tiled=True),
            lax.all_gather(value_low, "seq", axis=0, tiled=True),
        )
        query_wb, key_wb, value_wb, output_wb, attn_gb, query_gb, key_gb = attn_back
        gate_wb, up_wb, down_wb, ffn_gb = ffn_back
        cot_rows = cotangent[0, batch_index]
        grad_down = across(activated, cot_rows)
        d_activated = against(cot_rows, down_wb)
        sigma_gate = jax.nn.sigmoid(gate_lin)
        d_gate = (d_activated * up_lin * sigma_gate * (1.0 + gate_lin * (1.0 - sigma_gate))).astype(
            brain_type
        )
        d_up = (d_activated * gate_lin * sigma_gate).astype(brain_type)
        grad_gate = across(normed_mid, d_gate)
        grad_up = across(normed_mid, d_up)
        d_normed_mid = against(d_gate, gate_wb) + against(d_up, up_wb)
        unused_mid, pull_ffn = jax.vjp(norm_rows, middle, ffn_gb.astype(float_type))
        d_mid_norm, grad_ffn_gain = pull_ffn(d_normed_mid)
        d_middle = cot_rows.astype(float_type) + d_mid_norm
        d_middle_low = d_middle.astype(brain_type)
        grad_output = across(attended, d_middle_low)
        d_attended = against(d_middle_low, output_wb).astype(brain_type)

        def back_pair(pair_id):
            query_pair = lax.dynamic_slice_in_dim(
                query_rot, pair_id * width_query, width_query, 1
            ).reshape(rows_here, 2, group_size, HEAD_DIM)
            grad_pair = lax.dynamic_slice_in_dim(
                d_attended, pair_id * width_query, width_query, 1
            ).reshape(rows_here, 2, group_size, HEAD_DIM)
            key_pair = lax.dynamic_slice_in_dim(
                key_back, pair_id * width_key, width_key, 1
            ).reshape(length, 2, HEAD_DIM)
            value_pair = lax.dynamic_slice_in_dim(
                value_back, pair_id * width_key, width_key, 1
            ).reshape(length, 2, HEAD_DIM)
            raw_score = jnp.einsum(
                "qhgd,khd->hgqk", query_pair, key_pair, preferred_element_type=jnp.float32
            )
            scores = jnp.where(keep_mask[None, None], raw_score * score_scale, NEGATIVE)
            soft_prob = jnp.exp(scores - log_totals[pair_id])
            soft_low = soft_prob.astype(jnp.bfloat16)
            d_prob = jnp.einsum(
                "qhgd,khd->hgqk", grad_pair, value_pair, preferred_element_type=jnp.float32
            )
            d_score = soft_prob * (d_prob - jnp.sum(soft_prob * d_prob, axis=-1, keepdims=True))
            d_raw = (d_score * score_scale).astype(jnp.bfloat16)
            d_query = jnp.einsum(
                "hgqk,khd->qhgd", d_raw, key_pair, preferred_element_type=jnp.float32
            )
            d_key = jnp.einsum(
                "hgqk,qhgd->khd", d_raw, query_pair, preferred_element_type=jnp.float32
            )
            d_value = jnp.einsum(
                "hgqk,qhgd->khd", soft_low, grad_pair, preferred_element_type=jnp.float32
            )
            return (
                d_query,
                jnp.concatenate(
                    [d_key.reshape(length, width_key), d_value.reshape(length, width_key)], axis=1
                ),
            )

        d_query_pairs, kv_terms = lax.map(back_pair, pair_ids)
        kv_share = lax.psum_scatter(
            kv_terms.astype(jnp.bfloat16), "seq", scatter_dimension=1, tiled=True
        ).astype(jnp.float32)
        d_key_rot = (
            kv_share[:, :, :width_key]
            .reshape(pair_count, rows_here, 2, HEAD_DIM)
            .transpose(1, 0, 2, 3)
            .reshape(rows_here, KV_HEADS, HEAD_DIM)
        )
        d_value_low = (
            kv_share[:, :, width_key:]
            .transpose(1, 0, 2)
            .reshape(rows_here, KV_HEADS * HEAD_DIM)
            .astype(brain_type)
        )
        d_query_rot = d_query_pairs.transpose(1, 0, 2, 3, 4).reshape(rows_here, HEADS, HEAD_DIM)

        def turn_rows(heads_in, gain_in):
            return rotate(norm_rows(heads_in, gain_in), cosine_table, sine_table)

        unused_query, pull_query = jax.vjp(turn_rows, query_heads, query_gb.astype(float_type))
        d_query_heads, grad_query_gain = pull_query(d_query_rot)
        unused_key, pull_key = jax.vjp(turn_rows, key_heads, key_gb.astype(float_type))
        d_key_heads, grad_key_gain = pull_key(d_key_rot)
        d_query_low = d_query_heads.reshape(rows_here, HEADS * HEAD_DIM).astype(brain_type)
        d_key_low = d_key_heads.reshape(rows_here, KV_HEADS * HEAD_DIM).astype(brain_type)
        grad_query = across(normed_in, d_query_low)
        grad_key = across(normed_in, d_key_low)
        grad_value = across(normed_in, d_value_low)
        d_normed_in = (
            against(d_query_low, query_wb)
            + against(d_key_low, key_wb)
            + against(d_value_low, value_wb)
        )
        unused_in, pull_attn = jax.vjp(norm_rows, rows_in, attn_gb.astype(float_type))
        d_in_norm, grad_attn_gain = pull_attn(d_normed_in)
        grad_list.append(d_middle + d_in_norm)
        fresh = (
            grad_query,
            grad_key,
            grad_value,
            grad_output,
            grad_gate,
            grad_up,
            grad_down,
            grad_attn_gain,
            grad_ffn_gain,
            grad_query_gain,
            grad_key_gain,
        )
        sums = tuple((old + new for old, new in zip(sums, fresh)))
    attn_parts = (
        lax.psum_scatter(sums[0], ("dp", "seq"), scatter_dimension=0, tiled=True),
        lax.psum_scatter(sums[1], ("dp", "seq"), scatter_dimension=0, tiled=True),
        lax.psum_scatter(sums[2], ("dp", "seq"), scatter_dimension=0, tiled=True),
        lax.psum_scatter(sums[3], ("dp", "seq"), scatter_dimension=0, tiled=True),
        lax.psum_scatter(sums[7], ("dp", "seq"), scatter_dimension=0, tiled=True),
        lax.psum_scatter(sums[9], ("dp", "seq"), scatter_dimension=0, tiled=True),
        lax.psum_scatter(sums[10], ("dp", "seq"), scatter_dimension=0, tiled=True),
    )
    ffn_parts = (
        lax.psum_scatter(sums[4], ("dp", "seq"), scatter_dimension=0, tiled=True),
        lax.psum_scatter(sums[5], ("dp", "seq"), scatter_dimension=0, tiled=True),
        lax.psum_scatter(sums[6], ("dp", "seq"), scatter_dimension=0, tiled=True),
        lax.psum_scatter(sums[8], ("dp", "seq"), scatter_dimension=0, tiled=True),
    )
    outputs = jnp.stack(out_list)[None]
    input_grad = jnp.stack(grad_list)[None]
    return (
        outputs,
        input_grad,
        attn_parts[0],
        attn_parts[1],
        attn_parts[2],
        attn_parts[3],
        ffn_parts[0],
        ffn_parts[1],
        ffn_parts[2],
        attn_parts[4],
        ffn_parts[3],
        attn_parts[5],
        attn_parts[6],
    )


MESH = pl.DeviceIdType.MESH
NDP = 4
NSEQ = 8
BLOCKED = -65536.0
QB = 256
BLOCKS = (3, 2, 1, 0)
SOFT = HEAD_DIM ** (-0.5) * 1.4426950408889634

A0, A1, B, C0, C1, E = range(0, 60, 10)
R_A0, R_A1, R_B, R_C0, R_C1, R_E = range(60, 120, 10)
(
    ATTEND, MIX_MID, MIX_END, NORM_MID, NORM_END, LIFT, SINK, TURN_MID, TURN_END, LOW_MID, LOW_END,
    OUT_START, OUT_MID, OUT_END, ATTEND_BACK, IN_START, IN_MID, IN_END, PROJECT, GRAD_WIDE,
    GRAD_ATTN, TABLES, NORM_IN,
) = range(200, 430, 10)
(
    START, TOKENS, COTANGENT, SMALL_DP, SMALL_SEQ, A_IN, C_OUT, C_IN, TREE_START, COT_START,
    TREE_MID, COT_MID, COT_END, TREE_END, NODE, GAINS, GRAD_DOWN, GRAD_OUT, PACK_DP, PACK_SEQ,
    PACK_END, LAND_A, LAND_C, DRAIN,
) = range(600, 624, 1)
ORDER = (
    START, B, TOKENS, SMALL_DP, A_IN, A1, B + 1, A0, C_OUT, A1 + 1, C_IN, TREE_START, B + 2, A0 + 1,
    SMALL_SEQ, A1 + 2, NODE, B + 3, TABLES, A0 + 2, A1 + 3, C1, A0 + 3, A1 + 4, B + 4, A0 + 4, TREE_MID,
    A1 + 5, C0, TABLES + 1, A0 + 5, B + 5, TREE_END, GAINS, A1 + 6, A0 + 6, NORM_IN, B + 6, C0 + 1, C1 + 1,
    NORM_IN + 1, A1 + 7, COTANGENT, B + 7, A0 + 7, PROJECT, PROJECT + 1, PROJECT + 2, PROJECT + 3, ATTEND + 3,
    ATTEND + 2, C0 + 2, C1 + 2, MIX_MID + 3, MIX_MID + 2, ATTEND + 1, E, MIX_MID + 1, ATTEND, C0 + 3, C1 + 3,
    MIX_MID, E + 1, MIX_END + 1, MIX_END + 2, C0 + 4, MIX_END + 3, C1 + 4, MIX_END, E + 2, COT_START, C0 + 5,
    NORM_MID + 2, C1 + 5, NORM_MID + 3, E + 3, NORM_MID, NORM_MID + 1, NORM_END + 3, C0 + 6, NORM_END,
    NORM_END + 1, C1 + 6, E + 4, NORM_END + 2, C0 + 7, C1 + 7, LIFT + 2, E + 5, COT_MID, LIFT + 1, LIFT + 3,
    COT_END, E + 6, LIFT, GRAD_DOWN, R_E, E + 7, SINK + 3, OUT_START + 3, SINK + 1, OUT_START + 1, R_E + 1,
    SINK, OUT_START, TURN_MID + 3, SINK + 2, OUT_START + 2, R_E + 2, OUT_MID + 3, GRAD_WIDE, R_C0,
    OUT_MID + 1, GRAD_WIDE + 1, R_C1, TURN_END + 3, R_E + 3, TURN_MID + 2, R_C0 + 1, R_C1 + 1, LOW_MID + 3,
    OUT_END + 1, TURN_MID, LOW_END + 3, TURN_MID + 1, R_C0 + 2, TURN_END + 2, OUT_MID, R_C1 + 2, OUT_END + 3,
    ATTEND_BACK + 3, IN_START + 3, R_C0 + 3, R_C1 + 3, LOW_MID + 2, TURN_END, TURN_END + 1, IN_MID + 3,
    LOW_END + 2, R_E + 4, R_C0 + 4, OUT_END, R_C1 + 4, ATTEND_BACK + 2, IN_START + 2, R_C0 + 5, R_E + 5,
    LOW_MID + 1, LOW_MID, IN_END + 3, IN_MID + 2, R_C1 + 5, LOW_END + 1, ATTEND_BACK + 1, IN_START + 1,
    R_C0 + 6, R_E + 6, LOW_END, GRAD_OUT, IN_END + 2, R_B, ATTEND_BACK, IN_START, IN_MID + 1, GRAD_ATTN + 1,
    R_A1, GRAD_ATTN, R_A0, R_C1 + 6, R_A1 + 1, R_A0 + 1, R_B + 1, R_C0 + 7, OUT_MID + 2, R_A1 + 2, R_A0 + 2,
    IN_END + 1, R_A1 + 3, IN_MID, R_B + 2, R_A0 + 3, R_A1 + 4, R_B + 3, R_A0 + 4, R_C1 + 7, R_A1 + 5, R_E + 7,
    R_B + 4, R_A0 + 5, R_A1 + 6, R_B + 5, LAND_C, R_A0 + 6, IN_END, PACK_DP, R_A1 + 7, R_B + 6, R_A0 + 7,
    PACK_SEQ, OUT_END + 2, PACK_END, R_B + 7, LAND_A, DRAIN,
)


def seq_at(position):
    half = position // 4
    z = position + half * (7 - 2 * position)
    return 2 * z + half


def tree_seat(d, m):
    x, c = d // 2, d % 2
    return 2 * (2 * m + c) + (m + c + x) % 2


def greet_all(d, s):
    barrier = pltpu.get_barrier_semaphore()
    me = d * NSEQ + s

    def signal(i, carry):
        other = (me + i) % (NDP * NSEQ)
        pl.semaphore_signal(
            barrier, inc=1, device_id=(other // NSEQ, other % NSEQ), device_id_type=MESH
        )
        return carry

    lax.fori_loop(1, NDP * NSEQ, signal, 0)
    pl.semaphore_wait(barrier, NDP * NSEQ - 1)


def remote(src, dst, sems, at, d, s):
    send, recv = sems
    return pltpu.make_async_remote_copy(
        src_ref=src,
        dst_ref=dst,
        send_sem=send.at[at],
        recv_sem=recv.at[at],
        device_id=(d, s),
        device_id_type=MESH,
    )


class Sum:
    def __init__(self, part, near, sent, got, sems, n, spot):
        self.part, self.near, self.sent, self.got = part, near, sent, got
        self.sems, self.n = sems, n
        d, self.s = spot
        x, c = d // 2, d % 2
        self.d, self.sib, self.far = d, 2 * x + 1 - c, 2 * (1 - x) + c
        self.far_sib = 2 * (1 - x) + 1 - c

    def copies(self, b):
        rows = pl.ds(2 * b, 2)
        return (
            remote(self.part.at[rows, self.far_sib], self.near.at[0, rows], self.sems, (self.n, 0, b), self.sib, self.s),
            remote(self.part.at[rows, self.sib], self.near.at[1, rows], self.sems, (self.n, 1, b), self.sib, self.s),
            remote(self.sent.at[rows], self.got.at[rows], self.sems, (self.n, 2, b), self.far, self.s),
        )

    def start(self, b):
        first, second, _ = self.copies(b)
        first.start()
        second.start()

    def mid(self, b):
        first, _, across_x = self.copies(b)
        first.wait_recv()

        def join(i, carry):
            self.sent[i] = (
                self.part[i, self.far].astype(jnp.float32) + self.near[0, i].astype(jnp.float32)
            ).astype(jnp.bfloat16)
            return carry

        lax.fori_loop(2 * b, 2 * b + 2, join, 0)
        across_x.start()

    def end(self, b, finish):
        first, second, across_x = self.copies(b)
        second.wait_recv()
        across_x.wait_recv()

        def close(i, carry):
            rows = self.part[i, self.d].astype(jnp.float32) + self.near[1, i].astype(jnp.float32)
            finish(i, rows + self.got[i].astype(jnp.float32))
            return carry

        lax.fori_loop(2 * b, 2 * b + 2, close, 0)
        first.wait_send()
        second.wait_send()
        across_x.wait_send()


class Spread:
    def __init__(self, out, sems, at, spot):
        self.out, self.sems, self.place = out, sems, at
        d, self.s = spot
        x, c = d // 2, d % 2
        self.d, self.sib, self.far = d, 2 * x + 1 - c, 2 * (1 - x) + c
        self.far_sib = 2 * (1 - x) + 1 - c

    def copy(self, rows, owner, way, to):
        block = self.out.at[rows, owner]
        return remote(block, block, self.sems, self.place(way, rows), to, self.s)

    def start(self, rows):
        self.copy(rows, self.d, 0, self.far).start()
        self.copy(rows, self.d, 1, self.sib).start()

    def mid(self, rows):
        self.copy(rows, self.far, 0, self.far).wait_recv()
        self.copy(rows, self.far, 2, self.sib).start()

    def end(self, rows):
        self.copy(rows, self.sib, 1, self.sib).wait_recv()
        self.copy(rows, self.far_sib, 2, self.sib).wait_recv()

    def sent(self, rows):
        self.copy(rows, self.d, 0, self.far).wait_send()
        self.copy(rows, self.d, 1, self.sib).wait_send()
        self.copy(rows, self.far, 2, self.sib).wait_send()


def layer_kernel(
    nodes,
    tok, cot, lengths, parents, gain_a, gain_f, gain_q, gain_k, inv_freq, wq, wk, wv, wo, wg, wu, wd,
    out_rows, grad_rows, res_a, res_c, g_output, g_down, pack_out,
    raw_lengths, raw_parents, raw_a, raw_f, raw_q, raw_k, smalls, wa, wb, wc, we, ge, hop_a, hop_b, hop_c, hop_e,
    tree, tree_cot, normed_in, normed_mid, d_low, tree_own,
    lin, heads, value, hidden, member, cosine, sine, att, d_att,
    part, part_out, near, sent, got, near_o, sent_o, got_o,
    middle, d_middle, act, both, d_key, d_value, outs, grad_low,
    fin_a, fin_c, attn_g, ffn_g, head_g, pack_dp, pack_seq, pack_sum,
    loc, s_small, r_small, s_col, r_col, s_tok, r_tok, s_ag, r_ag, s_rs, r_rs,
    s_sum, r_sum, s_tree, r_tree, s_spread, r_spread, s_back, r_back, s_fin, r_fin, s_pack, r_pack,
):
    f32, bf = jnp.float32, jnp.bfloat16
    d = lax.axis_index("dp")
    s = lax.axis_index("seq")
    z, y = s // 2, s % 2
    p = z + y * (7 - 2 * z)
    spot = (d, s)
    seat = [seq_at((p + i) % NSEQ) for i in range(NSEQ)]
    up, down = seat[1], seat[7]
    ag_sems, rs_sems = (s_ag, r_ag), (s_rs, r_rs)
    small_sems, col_sems, tok_sems = (s_small, r_small), (s_col, r_col), (s_tok, r_tok)

    def aligned(v, n):
        return pl.multiple_of(v, n)

    def chunk(n, way, j):
        if n in (0, 1, 3, 4):
            return pl.ds(aligned((2 * way + (n + (n > 2)) % 2) * 256 + j * 32, 32), 32)
        if n == 2:
            return pl.ds(aligned(j * 64 + way * 32, 32), 32)
        return pl.ds(aligned(j * 96 + way * 48, 16), 48)

    weight = {0: wa, 1: wa, 2: wb, 3: wc, 4: wc, 5: we}
    grads = {0: wa, 1: wa, 2: wb, 3: wc, 4: wc, 5: ge}
    hops = {0: hop_a.at[0], 1: hop_a.at[1], 2: hop_b, 3: hop_c.at[0], 4: hop_c.at[1], 5: hop_e}

    def owner_at(way, k):
        return seq_at((p + NSEQ - k) % NSEQ) if way == 0 else seq_at((p + k) % NSEQ)

    def gather(n, k):
        for way, peer in enumerate((up, down)):
            block = weight[n].at[chunk(n, way, owner_at(way, k))]
            if not (isinstance(k, int) and k == 0):
                remote(block, block, ag_sems, (n, way, k - 1), d, peer).wait_recv()
            remote(block, block, ag_sems, (n, way, k), d, peer).start()

    def gather_end(n):
        for way, peer in enumerate((up, down)):
            block = weight[n].at[chunk(n, way, owner_at(way, 7))]
            remote(block, block, ag_sems, (n, way, 6), d, peer).wait_recv()

    def gather_sent(n):
        for way, peer in enumerate((up, down)):
            block = weight[n].at[chunk(n, way, s)]
            for k in range(7):
                remote(block, block, ag_sems, (n, way, k), d, peer).wait_send()

    def add_rows(into, other):
        def one(i, carry):
            at = pl.ds(aligned(i * 16, 16), 16)
            into[at] = (into[at].astype(f32) + other[at].astype(f32)).astype(bf)
            return carry

        lax.fori_loop(0, into.shape[0] // 16, one, 0)

    def reduce_(n, k):
        for way, peer in enumerate((up, down)):
            rows = chunk(n, way, seat[(7 - k) % NSEQ] if way == 0 else seat[(1 + k) % NSEQ])
            mine = grads[n].at[rows]
            if k == 0:
                src = mine
            else:
                src = hops[n].at[way, k - 1]
                remote(src, src, rs_sems, (n, way, k - 1), d, peer).wait_recv()
                add_rows(src, mine)
            remote(src, hops[n].at[way, k], rs_sems, (n, way, k), d, peer).start()

    def reduce_end(n, take):
        for way, peer in enumerate((up, down)):
            src = hops[n].at[way, 6]
            remote(src, src, rs_sems, (n, way, 6), d, peer).wait_recv()
            take(way, src[...].astype(f32) + grads[n][chunk(n, way, s)].astype(f32))

    def reduce_sent(n):
        for way, peer in enumerate((up, down)):
            for k in range(7):
                src = hops[n].at[way, k]
                remote(src, src, rs_sems, (n, way, k), d, peer).wait_send()

    ops = {}
    tree_slot, tree_core = z // 2, z % 2
    tree_owner = 2 * ((y + tree_slot + tree_core) % 2) + tree_core
    pending = []
    held = {}

    def stage(name):
        def keep(run):
            ops[name] = run
            return run

        return keep

    def launch(cp):
        cp.start()
        pending.append(cp)

    raws = [
        pltpu.make_async_copy(src, dst, loc.at[9 + n])
        for n, (src, dst) in enumerate(
            (
                (lengths, raw_lengths), (parents, raw_parents),
                (gain_a, raw_a), (gain_f, raw_f), (gain_q, raw_q), (gain_k, raw_k),
            )
        )
    ]
    pieces = (
        (wq, wa, 512, 0), (wk, wa, 256, 512), (wv, wa, 256, 768), (wg, wc, 768, 0), (wu, wc, 768, 768)
    )
    col_rows = lambda q: pl.ds(aligned(q * 256 + s * 32, 32), 32)

    def column_copy(n):
        src, dst, width, at = pieces[n]
        return pltpu.make_async_copy(
            src.at[:, pl.ds(aligned(d * width, 128), width)],
            dst.at[col_rows(d), pl.ds(at, width)],
            loc.at[2 + n],
        )

    def columns(n):
        src, dst, width, at = pieces[n]
        for i in range(1, NDP):
            q = (d + i) % NDP
            launch(
                remote(
                    src.at[:, pl.ds(aligned(q * width, 128), width)],
                    dst.at[col_rows(d), pl.ds(at, width)],
                    col_sems, (n, i), q, s,
                )
            )
        column_copy(n).start()

    def columns_in(n):
        _, dst, width, at = pieces[n]
        column_copy(n).wait()
        for i in range(1, NDP):
            place = dst.at[col_rows((d + NDP - i) % NDP), pl.ds(at, width)]
            remote(place, place, col_sems, (n, i), d, s).wait_recv()

    def row_copy(n, m, i):
        src, dst = ((tok, tree), (cot, tree_cot))[n]
        q = (d + i) % NDP
        return pltpu.make_async_remote_copy(
            src_ref=src.at[m, pl.ds(aligned(q * 32, 32), 32)],
            dst_ref=dst.at[s, q],
            send_sem=s_tok.at[n, m, i],
            recv_sem=r_tok.at[n],
            device_id=(q, tree_seat(d, m)),
            device_id_type=MESH,
        )

    def rows_out(n):
        src, dst = ((tok, tree), (cot, tree_cot))[n]
        for m in range(MICRO):
            target = tree_seat(d, m)

            @pl.when(target == s)
            def _():
                piece = src.at[m, pl.ds(aligned(d * 32, 32), 32)]
                pltpu.make_async_copy(piece, dst.at[s, d], r_tok.at[n]).start()

            @pl.when(target != s)
            def _():
                row_copy(n, m, 0).start()

            for i in range(1, NDP):
                row_copy(n, m, i).start()

    def rows_in(dst, n):
        everything = dst.at[:, d]
        pltpu.make_async_copy(everything, everything, r_tok.at[n]).wait()

    fill_b = pltpu.make_async_copy(wo, wb.at[pl.ds(aligned(s * 64, 64), 64)], loc.at[7])
    fill_e = pltpu.make_async_copy(wd, we.at[pl.ds(aligned(s * 96, 16), 96)], loc.at[15])

    @stage(START)
    def _():
        for cp in raws:
            cp.start()
        greet_all(d, s)
        fill_b.start()
        fill_e.start()
        for n in range(3):
            columns(n)

    stage(TOKENS)(lambda: rows_out(0))
    stage(COTANGENT)(lambda: rows_out(1))

    @stage(SMALL_DP)
    def _():
        for cp in raws:
            cp.wait()
        for row, ref in enumerate((raw_a, raw_f, raw_q, raw_k)):
            count = ref.shape[0]
            line = ref[...].astype(f32).reshape(1, count)
            smalls[d, s, row : row + 1, :] = jnp.concatenate([line] * (128 // count), axis=1)
        smalls[d, s, 4:8, :] = jnp.zeros((4, 128), f32)
        smalls[d, s, 4:6, 0:nodes] = raw_lengths[0].astype(f32)
        smalls[d, s, 6:8, 0:nodes] = raw_parents[0].astype(f32)
        for i in range(1, NDP):
            launch(remote(smalls.at[d, s], smalls.at[d, s], small_sems, i, (d + i) % NDP, s))

    @stage(SMALL_SEQ)
    def _():
        for i in range(1, NDP):
            place = smalls.at[(d + NDP - i) % NDP, s]
            remote(place, place, small_sems, i, d, s).wait_recv()
        for i in range(1, NSEQ):
            launch(remote(smalls.at[:, s], smalls.at[:, s], small_sems, NDP + i, d, (s + i) % NSEQ))

    @stage(A_IN)
    def _():
        for n in range(3):
            columns_in(n)

    @stage(C_OUT)
    def _():
        for n in range(3, 5):
            columns(n)

    @stage(C_IN)
    def _():
        for n in range(3, 5):
            columns_in(n)

    streams = ((A0, 0), (A1, 1), (B, 2), (C0, 3), (C1, 4), (E, 5))

    def ring_first(n):
        if n == 2:
            fill_b.wait()
        if n == 5:
            fill_e.wait()
        gather(n, 0)

    for label, n in streams:
        stage(label)(functools.partial(ring_first, n))
        stage(label + 7)(functools.partial(gather_end, n))
        for k in range(1, 7):
            stage(label + k)(functools.partial(gather, n, k))
        for k in range(7):
            stage(R_A0 + label + k)(functools.partial(reduce_, n, k))

    everything = pl.ds(0, NSEQ)
    spread_tree = Spread(tree, (s_tree, r_tree), lambda way, rows: (0, way), spot)
    spread_cot = Spread(tree_cot, (s_tree, r_tree), lambda way, rows: (1, way), spot)

    @stage(TREE_START)
    def _():
        rows_in(tree, 0)
        spread_tree.start(everything)

    @stage(COT_START)
    def _():
        rows_in(tree_cot, 1)
        spread_cot.start(everything)

    stage(TREE_MID)(lambda: spread_tree.mid(everything))
    stage(COT_MID)(lambda: spread_cot.mid(everything))
    stage(COT_END)(lambda: spread_cot.end(everything))
    own_rows = pltpu.make_async_copy(tree.at[:, d], tree_own, loc.at[8])

    @stage(TREE_END)
    def _():
        spread_tree.end(everything)
        own_rows.start()

    @stage(NODE)
    def _():
        ir = lax.broadcasted_iota(jnp.int32, (128, 128), 0)
        ic = lax.broadcasted_iota(jnp.int32, (128, 128), 1)
        block = smalls.at[tree_owner, s]
        length_row = block[pl.ds(4 + tree_slot, 1), :]
        parent_row = block[pl.ds(6 + tree_slot, 1), :]
        length_col = jnp.sum(jnp.where(ir == ic, length_row, 0.0), axis=1, keepdims=True)
        over = (parent_row == ir.astype(f32)) & (ic > 0) & (ic < nodes)
        above = jnp.where(over | (ir == ic), 1.0, 0.0)
        for _ in range(4):
            low = above.astype(bf)
            above = jnp.minimum(product(low, low), 1.0)
        start_row = jnp.sum(jnp.where(ir < ic, length_col, 0.0), axis=0, keepdims=True)
        base_row = jnp.sum(
            jnp.where((above > 0.5) & (ir != ic), length_col, 0.0), axis=0, keepdims=True
        )
        shut = jnp.where(above > 0.5, 0.0, BLOCKED).astype(bf)
        held["node"] = (start_row, start_row + length_row, base_row - start_row, shut)

    def tables(i, carry):
        start_row, end_row, offset_row, shut = held["node"]
        rows = pl.ds(aligned(i * QB, QB), QB)
        index = (lax.broadcasted_iota(jnp.int32, (QB, 128), 0) + i * QB).astype(f32)
        inside = (index >= start_row) & (index < end_row)
        position = index[:, :1] + jnp.sum(
            jnp.where(inside, offset_row, 0.0), axis=1, keepdims=True
        )
        hot = jnp.where(inside, 1.0, 0.0).astype(bf)
        member[rows] = hot
        hidden[rows] = against(hot, shut).astype(bf)
        angle = position * inv_freq[...]
        cosine[rows] = jnp.cos(angle)
        lane = lax.broadcasted_iota(jnp.int32, (QB, 128), 1)
        wave = jnp.sin(angle)
        sine[rows] = jnp.where(lane < 64, -wave, wave)
        return carry

    stage(TABLES + 0)(lambda: lax.fori_loop(0, 2, tables, 0))
    stage(TABLES + 1)(lambda: lax.fori_loop(2, 4, tables, 0))

    @stage(GAINS)
    def _():
        for i in range(1, NSEQ):
            place = smalls.at[:, (s + NSEQ - i) % NSEQ]
            remote(place, place, small_sems, NDP + i, d, s).wait_recv()
        lane = lax.broadcasted_iota(jnp.int32, (1, 128), 1)
        for row, dst in ((0, attn_g), (1, ffn_g)):
            for j in range(8):
                parts = [
                    smalls[(4 * j + i) // 8, (4 * j + i) % 8, row : row + 1, :] for i in range(4)
                ]
                dst[:, 128 * j : 128 * (j + 1)] = jnp.where(
                    lane < 64,
                    jnp.where(lane < 32, parts[0], parts[1]),
                    jnp.where(lane < 96, parts[2], parts[3]),
                )
        for row in (2, 3):
            joined = jnp.zeros((1, 128), f32)
            for i in range(32):
                joined = jnp.where(lane // 4 == i, smalls[i // 8, i % 8, row : row + 1, :], joined)
            head_g[row - 2 : row - 1, :] = joined
        pack_dp[d] = jnp.zeros((24, 128), f32)

    def norm_in(i, carry):
        rows = tree[i].reshape(128, D).astype(f32)
        scale = lax.rsqrt(jnp.mean(rows * rows, axis=-1, keepdims=True) + EPSILON)
        normed_in[pl.ds(aligned(i * 128, 128), 128)] = (rows * scale * attn_g[...]).astype(bf)
        return carry

    stage(NORM_IN + 0)(lambda: lax.fori_loop(0, 4, norm_in, 0))
    stage(NORM_IN + 1)(lambda: lax.fori_loop(4, 8, norm_in, 0))

    def unit_of(v):
        scale = lax.rsqrt(jnp.mean(v * v, axis=-1, keepdims=True) + EPSILON)
        return v * scale, scale

    def turn(v, gain, cos, sin):
        unit, _ = unit_of(v)
        lifted = unit * gain
        return lifted * cos + pltpu.roll(lifted, 64, 1) * sin

    def turn_back(dr, v, gain, cos, sin):
        d_lift = dr * cos + pltpu.roll(dr * sin, 64, 1)
        unit, scale = unit_of(v)
        d_unit = d_lift * gain
        return (
            scale * (d_unit - unit * jnp.mean(unit * d_unit, axis=-1, keepdims=True)),
            jnp.sum(d_lift * unit, axis=0, keepdims=True),
        )

    def project(i):
        rows = pl.ds(i * QB, QB)
        cos, sin = cosine[rows], sine[rows]

        def one(j, carry):
            lanes = pl.ds(aligned(j * 256, 256), 256)
            pair = product(normed_in[rows], wa[:, lanes])
            lin[rows, lanes] = pair
            gain = head_g[pl.ds(j // 2, 1), :]
            for i2 in range(2):
                turned = turn(pair[:, 128 * i2 : 128 * (i2 + 1)], gain, cos, sin)
                heads[2 * j + i2, rows] = turned.astype(bf)
            return carry

        lax.fori_loop(0, 3, one, 0)
        value[rows] = product(normed_in[rows], wa[:, 768:]).astype(bf)

    for i in range(4):
        stage(PROJECT + i)(functools.partial(project, i))

    def span(b):
        return pl.ds(b * QB, QB), (b + 1) * QB

    def weights_of(b, h, n):
        here = pl.ds(b * QB, QB)
        q = jnp.concatenate([heads[h, here], hidden[here]], axis=1)
        k = jnp.concatenate([heads[4 + h // 2, pl.ds(0, n)], member[pl.ds(0, n)]], axis=1)
        score = against(q, k) * SOFT
        row = lax.broadcasted_iota(jnp.int32, (QB, QB), 0)
        col = lax.broadcasted_iota(jnp.int32, (QB, QB), 1)
        diag = jnp.where(col <= row, score[:, n - QB :], NEGATIVE)
        score = diag if b == 0 else jnp.concatenate([score[:, : n - QB], diag], axis=1)
        grown = jnp.exp2(score)
        return grown, 1.0 / jnp.sum(grown, axis=-1, keepdims=True)

    def head_lanes(h):
        return pl.ds(aligned(h * HEAD_DIM, HEAD_DIM), HEAD_DIM)

    sum_sems, spread_sems = (s_sum, r_sum), (s_spread, r_spread)
    mixed_sum = Sum(part, near, sent, got, sum_sems, 0, spot)
    mid_sum = Sum(part, near, sent, got, sum_sems, 1, spot)
    out_sum = Sum(part_out, near_o, sent_o, got_o, sum_sems, 2, spot)
    in_sum = Sum(part, near, sent, got, sum_sems, 3, spot)
    pair_of = {b: pl.ds(2 * b, 2) for b in BLOCKS}
    spread_mid = Spread(normed_mid, spread_sems, lambda way, rows: (0, way, rows.start // 2), spot)
    spread_low = Spread(d_low, spread_sems, lambda way, rows: (1, way, rows.start // 2), spot)

    def attend(b):
        here, n = span(b)
        if b == BLOCKS[0]:
            own_rows.wait()

        def one(h, carry):
            grown, inverse = weights_of(b, h, n)
            mixed = product(grown.astype(bf), value[pl.ds(0, n), head_lanes(h // 2)])
            att[here, head_lanes(h)] = (mixed * inverse).astype(bf)
            return carry

        lax.fori_loop(0, HEADS // NDP, one, 0)
        rows = product(att[here], wb[...]).astype(bf)
        part[pair_of[b]] = rows.reshape(2, NDP, 32, D)
        mixed_sum.start(b)

    def to_middle(i, rows):
        rows = rows + tree_own[i].astype(f32)
        middle[i] = rows
        scale = lax.rsqrt(jnp.mean(rows * rows, axis=-1, keepdims=True) + EPSILON)
        normed_mid[i, d] = (rows * scale * ffn_g[...]).astype(bf)

    def close_mixed(b):
        mixed_sum.end(b, to_middle)
        spread_mid.start(pair_of[b])

    def lift(b):
        here = pl.ds(b * QB, QB)
        rows = normed_mid[pair_of[b]].reshape(QB, D)

        def one(t, carry):
            left = pl.ds(aligned(t * 256, 256), 256)
            right = pl.ds(aligned(768 + t * 256, 256), 256)
            gate = product(rows, wc[:, left])
            wide = product(rows, wc[:, right])
            sigma = 1.0 / (1.0 + jnp.exp(-gate))
            silu = gate * sigma
            act[here, left] = (silu * wide).astype(bf)
            both[here, left] = (wide * sigma * (1.0 + gate * (1.0 - sigma))).astype(bf)
            both[here, right] = silu.astype(bf)
            return carry

        lax.fori_loop(0, 3, one, 0)

    @stage(GRAD_DOWN)
    def _():
        def one(i, carry):
            cols = pl.ds(aligned(i * 256, 256), 256)
            ge[cols] = across(act[:, cols], tree_cot[...].reshape(NSEQ * 128, D)).astype(bf)
            return carry

        lax.fori_loop(0, 3, one, 0)

    def sink(b):
        here = pl.ds(b * QB, QB)
        cots = tree_cot[pair_of[b]].reshape(QB, D)

        def one(t, carry):
            left = pl.ds(aligned(t * 256, 256), 256)
            right = pl.ds(aligned(768 + t * 256, 256), 256)
            d_act = against(cots, we[left])
            both[here, left] = (d_act * both[here, left].astype(f32)).astype(bf)
            both[here, right] = (d_act * both[here, right].astype(f32)).astype(bf)
            return carry

        lax.fori_loop(0, 3, one, 0)
        part[pair_of[b]] = against(both[here], wc[...]).astype(bf).reshape(2, NDP, 32, D)
        mid_sum.start(b)

    def settle(b):
        here = pl.ds(b * QB, QB)
        part_out[pair_of[b]] = product(act[here], we[...]).astype(bf).reshape(2, NDP, 32, D)
        out_sum.start(b)

    def to_turn(i, rows):
        unit, scale = unit_of(middle[i])
        lifted = ffn_g[...] * rows
        term = jnp.sum(rows * unit, axis=0, keepdims=True)
        for j in range(8):
            pack_dp[d, 8 + j : 9 + j] += term[:, 128 * j : 128 * (j + 1)]
        d_mid = tree_cot[i, d].astype(f32) + scale * (
            lifted - unit * jnp.mean(unit * lifted, axis=-1, keepdims=True)
        )
        d_middle[i] = d_mid
        d_low[i, d] = d_mid.astype(bf)

    def close_mid(b):
        mid_sum.end(b, to_turn)
        spread_low.start(pair_of[b])

    def to_outs(i, rows):
        outs[i] = (middle[i] + rows).astype(bf)

    back_owner, back_slot = tree_owner, tree_slot
    back = ((outs, out_rows), (grad_low, grad_rows))

    def give_copy(n, j):
        src, dst = back[n]
        return pltpu.make_async_remote_copy(
            src_ref=src.at[j],
            dst_ref=dst.at[back_slot, pl.ds(aligned(d * 32, 32), 32)],
            send_sem=s_back.at[n, j],
            recv_sem=r_back.at[n],
            device_id=(back_owner, j),
            device_id_type=MESH,
        )

    def give(n, b):
        src, dst = back[n]

        def one(j, carry):
            same = (back_owner == d) & (s == j)

            @pl.when(same)
            def _():
                place = dst.at[back_slot, pl.ds(aligned(d * 32, 32), 32)]
                pltpu.make_async_copy(src.at[j], place, r_back.at[n]).start()

            @pl.when(jnp.logical_not(same))
            def _():
                give_copy(n, j).start()

            return carry

        lax.fori_loop(2 * b, 2 * b + 2, one, 0)

    def close_out(b):
        out_sum.end(b, to_outs)
        give(0, b)

    def grad_wide(sub):
        gather_sent(3 + sub)
        for i in (sub, 2 + sub):
            cols = pl.ds(i * 256, 256)

            def one(t, carry):
                lanes = pl.ds(aligned(512 * t, 512), 512)
                wc[cols, lanes] = across(
                    normed_mid[:, :, :, cols].reshape(NSEQ * 128, 256), both[:, lanes]
                ).astype(bf)
                return carry

            lax.fori_loop(0, 3, one, 0)

    d_lin = tree

    def close_low(b):
        spread_low.end(pair_of[b])
        here = pl.ds(b * QB, QB)
        rows = d_low[pair_of[b]].reshape(QB, D)
        d_att[here] = against(rows, wb[...]).astype(bf)

    def attend_back(b):
        here, n = span(b)
        keys = pl.ds(0, n)
        if b == BLOCKS[0]:
            spread_tree.sent(everything)
            d_key[...] = jnp.zeros_like(d_key)
            d_value[...] = jnp.zeros_like(d_value)

        def one(h, carry):
            kv = h // 2
            grown, inverse = weights_of(b, h, n)
            prob = grown * inverse
            d_out = d_att[here, head_lanes(h)]
            d_prob = against(d_out, value[keys, head_lanes(kv)])
            delta = jnp.sum(prob * d_prob, axis=-1, keepdims=True)
            d_raw = (prob * (d_prob - delta) * HEAD_DIM ** (-0.5)).astype(bf)
            d_rot = product(d_raw, heads[4 + kv, keys])
            d_key[kv, keys] += across(d_raw, heads[h, here])
            d_value[kv, keys] += across(prob.astype(bf), d_out)
            back, d_gain = turn_back(
                d_rot, lin[here, head_lanes(h)], head_g[0:1, :], cosine[here], sine[here]
            )
            pack_dp[d, 16:17] += d_gain
            d_lin[pair_of[b], :, :, head_lanes(h)] = back.astype(bf).reshape(2, NDP, 32, HEAD_DIM)
            return carry

        lax.fori_loop(0, HEADS // NDP, one, 0)
        for kv in range(KV_HEADS // NDP):
            at = 512 + 128 * kv
            back, d_gain = turn_back(
                d_key[kv, here], lin[here, pl.ds(at, 128)], head_g[1:2, :], cosine[here], sine[here]
            )
            pack_dp[d, 17:18] += d_gain
            d_lin[pair_of[b], :, :, pl.ds(at, 128)] = back.astype(bf).reshape(2, NDP, 32, 128)
            d_lin[pair_of[b], :, :, pl.ds(at + 256, 128)] = (
                d_value[kv, here].astype(bf).reshape(2, NDP, 32, 128)
            )

    def sink_in(b):
        rows = against(d_lin[pair_of[b]].reshape(QB, 1024), wa[...])
        part[pair_of[b]] = rows.astype(bf).reshape(2, NDP, 32, D)
        in_sum.start(b)

    @stage(GRAD_OUT)
    def _():
        gather_sent(2)
        for i in range(2):
            cols = pl.ds(256 * i, 256)
            wb[cols] = across(att[:, cols], d_low[...].reshape(NSEQ * 128, D)).astype(bf)

    def grad_attn(sub):
        gather_sent(sub)
        for i in (sub, 2 + sub):
            cols = pl.ds(i * 256, 256)

            def one(t, carry):
                lanes = pl.ds(aligned(512 * t, 512), 512)
                wa[cols, lanes] = across(
                    normed_in[:, cols], d_lin[:, :, :, lanes].reshape(NSEQ * 128, 512)
                ).astype(bf)
                return carry

            lax.fori_loop(0, 2, one, 0)

    def to_grad(i, rows):
        unit, scale = unit_of(tree_own[i].astype(f32))
        lifted = attn_g[...] * rows
        term = jnp.sum(rows * unit, axis=0, keepdims=True)
        for j in range(8):
            pack_dp[d, j : j + 1] += term[:, 128 * j : 128 * (j + 1)]
        grad = d_middle[i] + scale * (
            lifted - unit * jnp.mean(unit * lifted, axis=-1, keepdims=True)
        )
        grad_low[i] = grad.astype(bf)

    def close_in(b):
        in_sum.end(b, to_grad)
        give(1, b)

    per_block = (
        (ATTEND, attend), (MIX_MID, mixed_sum.mid), (MIX_END, close_mixed),
        (NORM_MID, lambda b: spread_mid.mid(pair_of[b])), (NORM_END, lambda b: spread_mid.end(pair_of[b])),
        (LIFT, lift), (SINK, sink), (TURN_MID, mid_sum.mid), (TURN_END, close_mid),
        (LOW_MID, lambda b: spread_low.mid(pair_of[b])), (LOW_END, close_low),
        (OUT_START, settle), (OUT_MID, out_sum.mid), (OUT_END, close_out),
        (ATTEND_BACK, attend_back), (IN_START, sink_in), (IN_MID, in_sum.mid), (IN_END, close_in),
    )
    for label, run in per_block:
        for b in BLOCKS:
            stage(label + b)(functools.partial(run, b))
    for sub in range(2):
        stage(GRAD_WIDE + sub)(functools.partial(grad_wide, sub))
        stage(GRAD_ATTN + sub)(functools.partial(grad_attn, sub))

    pack_sems, fin_sems = (s_pack, r_pack), (s_fin, r_fin)

    @stage(PACK_DP)
    def _():
        for i in range(1, NDP):
            launch(remote(pack_dp.at[d], pack_dp.at[d], pack_sems, i, (d + i) % NDP, s))

    @stage(PACK_SEQ)
    def _():
        for i in range(1, NDP):
            place = pack_dp.at[(d + NDP - i) % NDP]
            remote(place, place, pack_sems, i, d, s).wait_recv()
        pack_seq[s] = (pack_dp[0] + pack_dp[1]) + (pack_dp[2] + pack_dp[3])
        for i in range(1, NSEQ):
            launch(remote(pack_seq.at[s], pack_seq.at[s], pack_sems, NDP + i, d, (s + i) % NSEQ))

    @stage(PACK_END)
    def _():
        for i in range(1, NSEQ):
            place = pack_seq.at[(s + NSEQ - i) % NSEQ]
            remote(place, place, pack_sems, NDP + i, d, s).wait_recv()
        total = pack_seq[0]
        for j in range(1, NSEQ):
            total = total + pack_seq[j]
        pack_sum[...] = total
        at = d * NSEQ + s
        for n, (row, count) in enumerate(
            ((at // 4, 32), (8 + at // 4, 32), (16, 4), (17, 4))
        ):
            line = pack_sum[pl.ds(row, 1), :]
            shift = (128 - (at * count) % 128) % 128
            pack_out[n : n + 1, :] = pltpu.roll(line, shift, 1)

    def close_cols(n, fin, landed, which):
        sub = (n + (n > 2)) % 2

        def take(way, total):
            fin[2 * way + sub] = total.astype(bf)

        reduce_end(n, take)
        for way in range(2):
            q = 2 * way + sub

            @pl.when(q == d)
            def _():
                pltpu.make_async_copy(fin.at[q], landed.at[d], loc.at[which]).start()

            @pl.when(q != d)
            def _():
                remote(fin.at[q], landed.at[d], fin_sems, (which, d), q, s).start()

    for label, n, fin, landed, which in (
        (A0, 0, fin_a, res_a, 0), (A1, 1, fin_a, res_a, 0),
        (C0, 3, fin_c, res_c, 1), (C1, 4, fin_c, res_c, 1),
    ):
        stage(R_A0 + label + 7)(functools.partial(close_cols, n, fin, landed, which))

    def land(landed, which):
        for i in range(1, NDP):
            q = (d + i) % NDP
            remote(landed.at[q], landed.at[q], fin_sems, (which, q), q, s).wait_recv()
        pltpu.make_async_copy(landed.at[d], landed.at[d], loc.at[which]).wait()

    stage(LAND_A)(lambda: land(res_a, 0))
    stage(LAND_C)(lambda: land(res_c, 1))

    def take_rows(dst, rows, way, total):
        dst[rows * way : rows * (way + 1)] = total

    stage(R_B + 7)(lambda: reduce_end(2, functools.partial(take_rows, g_output, 32)))
    stage(R_E + 7)(lambda: reduce_end(5, functools.partial(take_rows, g_down, 48)))

    @stage(DRAIN)
    def _():
        for n, (src, dst) in enumerate(back):
            pltpu.make_async_copy(dst, dst, r_back.at[n]).wait()

            def one(j, carry):
                @pl.when(jnp.logical_not((back_owner == d) & (s == j)))
                def _():
                    give_copy(n, j).wait_send()

                return carry

            lax.fori_loop(0, NSEQ, one, 0)
        for n, (fin, landed) in enumerate(((fin_a, res_a), (fin_c, res_c))):
            for i in range(1, NDP):
                q = (d + i) % NDP
                remote(fin.at[q], landed.at[d], fin_sems, (n, d), q, s).wait_send()
        gather_sent(5)
        for n in range(6):
            reduce_sent(n)
        spread_cot.sent(everything)
        for b in BLOCKS:
            spread_mid.sent(pair_of[b])
            spread_low.sent(pair_of[b])
        for cp in pending:
            cp.wait_send()
        for n in range(2):
            for m in range(MICRO):

                @pl.when(tree_seat(d, m) != s)
                def _():
                    row_copy(n, m, 0).wait_send()

                for i in range(1, NDP):
                    row_copy(n, m, i).wait_send()

    for name in ORDER:
        ops[name]()


def finish_kernel(
    out_rows, grad_rows, res_a, res_c, g_output, g_down, pack,
    outs, grads, g_query, g_key, g_value, out_output, g_gate, g_up, out_down, g_attn, g_ffn, g_qg, g_kg,
    sems,
):
    through = [
        pltpu.make_async_copy(src, dst, sems.at[n])
        for n, (src, dst) in enumerate(
            ((out_rows, outs), (g_output, out_output), (g_down, out_down))
        )
    ]
    for cp in through:
        cp.start()
    grads[...] = grad_rows[...].astype(jnp.float32)
    for src, cuts in (
        (res_a, ((0, 512, g_query), (512, 256, g_key), (768, 256, g_value))),
        (res_c, ((0, 768, g_gate), (768, 768, g_up))),
    ):
        for q in range(NDP):
            for at, width, dst in cuts:
                dst[:, width * q : width * (q + 1)] = src[q, :, at : at + width].astype(jnp.float32)
    for n, dst in enumerate((g_attn, g_ffn, g_qg, g_kg)):
        count = dst.shape[0]
        dst[...] = pack[n : n + 1, 0:count].reshape(count)
    for cp in through:
        cp.wait()


def tree_shards(
    tokens, cotangent, node_lengths, parents, w_query, w_key, w_value, w_output, w_gate, w_up, w_down,
    attn_gain, ffn_gain, query_gain, key_gain,
):
    f32, bf = jnp.float32, jnp.bfloat16
    nodes = node_lengths.shape[2]
    half = np.arange(HEAD_DIM // 2, dtype=np.float64)
    inv_freq = THETA ** (-(half * (2.0 / HEAD_DIM)))
    inv_freq = np.concatenate([inv_freq, inv_freq])[None].astype(np.float32)
    shape, vmem, dma = jax.ShapeDtypeStruct, pltpu.VMEM, pltpu.SemaphoreType.DMA
    anywhere = pl.BlockSpec(memory_space=pl.ANY)
    here = pl.BlockSpec(memory_space=pltpu.VMEM)
    rows = NSEQ * 128
    quarter = (NSEQ, 32, D)
    twice = lambda *dims: [dma(dims), dma(dims)]
    results = pl.pallas_call(
        functools.partial(layer_kernel, nodes),
        out_shape=(
            shape((MICRO, 128, D), bf),
            shape((MICRO, 128, D), bf),
            shape((NDP, 32, 1024), bf),
            shape((NDP, 32, 1536), bf),
            shape((64, D), f32),
            shape((96, D), f32),
            shape((8, 128), f32),
        ),
        in_specs=[anywhere] * 8 + [here] + [anywhere] * 7,
        out_specs=[anywhere] * 4 + [here] * 3,
        scratch_shapes=[
            vmem(node_lengths.shape, jnp.int32), vmem(parents.shape, jnp.int32),
            *[vmem(gain.shape, bf) for gain in (attn_gain, ffn_gain, query_gain, key_gain)],
            vmem((NDP, NSEQ, 8, 128), f32),
            vmem((D, 1024), bf), vmem((512, D), bf), vmem((D, 1536), bf), vmem((768, D), bf),
            vmem((768, D), bf),
            vmem((2, 2, 7, 32, 1024), bf), vmem((2, 7, 32, D), bf),
            vmem((2, 2, 7, 32, 1536), bf), vmem((2, 7, 48, D), bf),
            vmem((NSEQ, NDP, 32, D), bf), vmem((NSEQ, NDP, 32, D), bf), vmem((rows, D), bf),
            vmem((NSEQ, NDP, 32, D), bf), vmem((NSEQ, NDP, 32, D), bf), vmem(quarter, bf),
            vmem((rows, 768), f32), vmem((6, rows, 128), bf),
            vmem((rows, 256), bf), vmem((rows, 128), bf), vmem((rows, 128), bf),
            vmem((rows, 128), f32), vmem((rows, 128), f32), vmem((rows, 512), bf), vmem((rows, 512), bf),
            vmem((NSEQ, NDP, 32, D), bf), vmem((NSEQ, NDP, 32, D), bf),
            vmem((2,) + quarter, bf), vmem(quarter, bf), vmem(quarter, bf),
            vmem((2,) + quarter, bf), vmem(quarter, bf), vmem(quarter, bf),
            vmem(quarter, f32), vmem(quarter, f32), vmem((rows, 768), bf), vmem((rows, 1536), bf),
            vmem((2, rows, 128), f32), vmem((2, rows, 128), f32), vmem(quarter, bf), vmem(quarter, bf),
            vmem((NDP, 32, 1024), bf), vmem((NDP, 32, 1536), bf),
            vmem((1, D), f32), vmem((1, D), f32), vmem((8, 128), f32),
            vmem((NDP, 24, 128), f32), vmem((NSEQ, 24, 128), f32), vmem((24, 128), f32),
            dma((16,)),
            *twice(12), *twice(5, NDP), dma((2, MICRO, NDP)), dma((2,)),
            *twice(6, 2, 7), *twice(6, 2, 7),
            *twice(4, 3, 4), *twice(2, 3), *twice(2, 3, 4),
            dma((2, NSEQ)), dma((2,)), *twice(2, NDP), *twice(12),
        ],
        compiler_params=pltpu.CompilerParams(
            collective_id=1, has_side_effects=True, vmem_limit_bytes=61 << 20
        ),
        name="layer",
    )(
        tokens[0], cotangent[0], node_lengths, parents, attn_gain, ffn_gain, query_gain, key_gain, inv_freq,
        w_query, w_key, w_value, w_output, w_gate, w_up, w_down,
    )
    full = lambda *dims: shape(dims, f32)
    finished = pl.pallas_call(
        finish_kernel,
        out_shape=(
            shape((MICRO, 128, D), bf), full(MICRO, 128, D),
            full(32, 2048), full(32, 1024), full(32, 1024), full(64, D),
            full(32, FF), full(32, FF), full(96, D),
            full(32), full(32), full(4), full(4),
        ),
        in_specs=[anywhere, here, here, here, anywhere, anywhere, here],
        out_specs=[anywhere, here, here, here, here, anywhere, here, here, anywhere] + [here] * 4,
        scratch_shapes=[dma((3,))],
        compiler_params=pltpu.CompilerParams(vmem_limit_bytes=32 << 20),
        name="finish",
    )(*results)
    return (finished[0][None], finished[1][None]) + tuple(finished[2:])


def solution(mesh):
    ring = mesh.shape["dp"] == NDP and mesh.shape["seq"] == NSEQ
    return jax.shard_map(
        tree_shards if ring else general_shards,
        mesh=mesh,
        in_specs=(
            P("dp", None, "seq", None),
            P("dp", None, "seq", None),
            P("dp", None, None),
            P("dp", None, None),
            P(("dp", "seq"), None),
            P(("dp", "seq"), None),
            P(("dp", "seq"), None),
            P(("dp", "seq"), None),
            P(("dp", "seq"), None),
            P(("dp", "seq"), None),
            P(("dp", "seq"), None),
            P(("dp", "seq")),
            P(("dp", "seq")),
            P(("dp", "seq")),
            P(("dp", "seq")),
        ),
        out_specs=(
            P("dp", None, "seq", None),
            P("dp", None, "seq", None),
            P(("dp", "seq"), None),
            P(("dp", "seq"), None),
            P(("dp", "seq"), None),
            P(("dp", "seq"), None),
            P(("dp", "seq"), None),
            P(("dp", "seq"), None),
            P(("dp", "seq"), None),
            P(("dp", "seq")),
            P(("dp", "seq")),
            P(("dp", "seq")),
            P(("dp", "seq")),
        ),
        check_vma=False,
    )
```

```python
import functools

import jax
import jax.numpy as jnp
import numpy as np
from jax import lax
from jax.experimental import pallas as pl
from jax.experimental.pallas import tpu as pltpu
from jax.sharding import PartitionSpec as P

D = 1024
HEADS = 16
KV_HEADS = 8
HEAD_DIM = 128
FF = 3072
MICRO = 2


EPSILON = 1e-06
THETA = 1000000.0
NEGATIVE = -1e30
PRECISE = lax.Precision.HIGHEST


def norm_rows(values, row_gain):
    return (
        values * lax.rsqrt(jnp.mean(values * values, axis=-1, keepdims=True) + EPSILON) * row_gain
    )


def rope_tables(position, head_dim):
    half_dim = head_dim // 2
    inv_freq = THETA ** (-(jnp.arange(half_dim, dtype=jnp.float32) * (2.0 / head_dim)))
    angles = position.astype(jnp.float32)[:, None] * inv_freq[None, :]
    cosine_table = jnp.cos(angles)
    sine_table = jnp.sin(angles)
    return (
        jnp.concatenate([cosine_table, cosine_table], axis=1),
        jnp.concatenate([sine_table, sine_table], axis=1),
    )


def rotate(values, cosine_table, sine_table):
    half_dim = values.shape[-1] // 2
    turned = jnp.concatenate([-values[..., half_dim:], values[..., :half_dim]], axis=-1)
    return values * cosine_table[:, None, :] + turned * sine_table[:, None, :]


def tree_tables(lengths, parent_row):
    node_count = lengths.shape[0]
    labels = jnp.arange(node_count, dtype=jnp.int32)
    parent_hot = ((parent_row[:, None] == labels[None, :]) & (labels[:, None] > 0)).astype(
        jnp.int32
    )

    def extend(depth_step, state_pair):
        reached, covered = state_pair
        reached = jnp.sum(reached[:, :, None] * parent_hot[None, :, :], axis=1)
        return (reached, covered + reached)

    reached, covered = lax.fori_loop(0, node_count, extend, (parent_hot, parent_hot))
    ancestry = (covered > 0).astype(jnp.float32)
    starts = jnp.cumsum(lengths) - lengths
    path_base = jnp.sum(jnp.where(covered > 0, lengths[None, :], 0), axis=1)
    return (labels, starts, path_base, ancestry)


def token_nodes(token_index, labels, starts, path_base):
    node_id = jnp.sum((token_index[:, None] >= starts[None, 1:]).astype(jnp.int32), axis=1)
    member = node_id[:, None] == labels[None, :]
    offset = jnp.sum(jnp.where(member, (path_base - starts)[None, :], 0), axis=1)
    return (member.astype(jnp.float32), token_index + offset)


def visible(query_member, query_index, key_member, key_index, ancestry):
    numbers = (((1,), (1,)), ((), ()))
    lifted = jnp.dot(query_member, ancestry, precision=PRECISE)
    above = lax.dot_general(lifted, key_member, numbers, precision=PRECISE)
    same_node = lax.dot_general(query_member, key_member, numbers, precision=PRECISE)
    return (above > 0.5) | (same_node > 0.5) & (key_index[None, :] <= query_index[:, None])


def product(left_side, right_side):
    return jnp.dot(left_side, right_side, preferred_element_type=jnp.float32)


def against(left_side, right_side):
    return lax.dot_general(
        left_side, right_side, (((1,), (1,)), ((), ())), preferred_element_type=jnp.float32
    )


def across(left_side, right_side):
    return lax.dot_general(
        left_side, right_side, (((0,), (0,)), ((), ())), preferred_element_type=jnp.float32
    )


def general_shards(
    tokens,
    cotangent,
    node_lengths,
    parents,
    w_query,
    w_key,
    w_value,
    w_output,
    w_gate,
    w_up,
    w_down,
    attn_gain,
    ffn_gain,
    query_gain,
    key_gain,
):
    rows_here = tokens.shape[2]
    length = lax.axis_size("seq") * rows_here
    group_size = HEADS // KV_HEADS
    pair_count = KV_HEADS // 2
    width_query = 2 * group_size * HEAD_DIM
    width_key = 2 * HEAD_DIM
    score_scale = HEAD_DIM ** (-0.5)
    local_index = lax.axis_index("seq") * rows_here + jnp.arange(rows_here, dtype=jnp.int32)
    full_index = jnp.arange(length, dtype=jnp.int32)
    pair_ids = jnp.arange(pair_count, dtype=jnp.int32)
    float_type = jnp.float32
    brain_type = jnp.bfloat16
    sums = (
        jnp.zeros((D, HEADS * HEAD_DIM), float_type),
        jnp.zeros((D, KV_HEADS * HEAD_DIM), float_type),
        jnp.zeros((D, KV_HEADS * HEAD_DIM), float_type),
        jnp.zeros((HEADS * HEAD_DIM, D), float_type),
        jnp.zeros((D, FF), float_type),
        jnp.zeros((D, FF), float_type),
        jnp.zeros((FF, D), float_type),
        jnp.zeros((D,), float_type),
        jnp.zeros((D,), float_type),
        jnp.zeros((HEAD_DIM,), float_type),
        jnp.zeros((HEAD_DIM,), float_type),
    )
    out_list = []
    grad_list = []
    for batch_index in range(MICRO):
        attn_fwd = (
            lax.all_gather(w_query, ("dp", "seq"), axis=0, tiled=True),
            lax.all_gather(w_key, ("dp", "seq"), axis=0, tiled=True),
            lax.all_gather(w_value, ("dp", "seq"), axis=0, tiled=True),
            lax.all_gather(w_output, ("dp", "seq"), axis=0, tiled=True),
            lax.all_gather(attn_gain, ("dp", "seq"), axis=0, tiled=True),
            lax.all_gather(query_gain, ("dp", "seq"), axis=0, tiled=True),
            lax.all_gather(key_gain, ("dp", "seq"), axis=0, tiled=True),
        )
        ffn_fwd = (
            lax.all_gather(w_gate, ("dp", "seq"), axis=0, tiled=True),
            lax.all_gather(w_up, ("dp", "seq"), axis=0, tiled=True),
            lax.all_gather(w_down, ("dp", "seq"), axis=0, tiled=True),
            lax.all_gather(ffn_gain, ("dp", "seq"), axis=0, tiled=True),
        )
        query_w, key_w, value_w, output_w, attn_g, query_g, key_g = attn_fwd
        gate_w, up_w, down_w, ffn_g = ffn_fwd
        labels, starts, path_base, ancestry = tree_tables(
            node_lengths[0, batch_index], parents[0, batch_index]
        )
        member_here, position = token_nodes(local_index, labels, starts, path_base)
        member_all, unused_position = token_nodes(full_index, labels, starts, path_base)
        keep_mask = visible(member_here, local_index, member_all, full_index, ancestry)
        cosine_table, sine_table = rope_tables(position, HEAD_DIM)
        rows_in = tokens[0, batch_index].astype(float_type)
        attn_g32 = attn_g.astype(float_type)
        query_g32 = query_g.astype(float_type)
        key_g32 = key_g.astype(float_type)
        normed_in = norm_rows(rows_in, attn_g32).astype(brain_type)
        query_heads = product(normed_in, query_w).reshape(rows_here, HEADS, HEAD_DIM)
        key_heads = product(normed_in, key_w).reshape(rows_here, KV_HEADS, HEAD_DIM)
        value_low = product(normed_in, value_w).astype(brain_type)
        query_rot = (
            rotate(norm_rows(query_heads, query_g32), cosine_table, sine_table)
            .astype(brain_type)
            .reshape(rows_here, HEADS * HEAD_DIM)
        )
        key_rot = (
            rotate(norm_rows(key_heads, key_g32), cosine_table, sine_table)
            .astype(brain_type)
            .reshape(rows_here, KV_HEADS * HEAD_DIM)
        )
        key_all, value_all = (
            lax.all_gather(key_rot, "seq", axis=0, tiled=True),
            lax.all_gather(value_low, "seq", axis=0, tiled=True),
        )

        def attend_pair(pair_id):
            query_pair = lax.dynamic_slice_in_dim(
                query_rot, pair_id * width_query, width_query, 1
            ).reshape(rows_here, 2, group_size, HEAD_DIM)
            key_pair = lax.dynamic_slice_in_dim(key_all, pair_id * width_key, width_key, 1).reshape(
                length, 2, HEAD_DIM
            )
            value_pair = lax.dynamic_slice_in_dim(
                value_all, pair_id * width_key, width_key, 1
            ).reshape(length, 2, HEAD_DIM)
            raw_score = jnp.einsum(
                "qhgd,khd->hgqk", query_pair, key_pair, preferred_element_type=jnp.float32
            )
            scores = jnp.where(keep_mask[None, None], raw_score * score_scale, NEGATIVE)
            row_top = jnp.max(scores, axis=-1, keepdims=True)
            weight = jnp.exp(scores - row_top)
            row_total = jnp.sum(weight, axis=-1, keepdims=True)
            soft_low = (weight / row_total).astype(jnp.bfloat16)
            mixed = jnp.einsum(
                "hgqk,khd->qhgd", soft_low, value_pair, preferred_element_type=jnp.float32
            )
            return (mixed, row_top + jnp.log(row_total))

        mixed_pairs, log_totals = lax.map(attend_pair, pair_ids)
        attended = (
            mixed_pairs.transpose(1, 0, 2, 3, 4)
            .reshape(rows_here, HEADS * HEAD_DIM)
            .astype(brain_type)
        )
        middle = rows_in + product(attended, output_w)
        ffn_g32 = ffn_g.astype(float_type)
        normed_mid = norm_rows(middle, ffn_g32).astype(brain_type)
        gate_lin = product(normed_mid, gate_w)
        up_lin = product(normed_mid, up_w)
        activated = (jax.nn.silu(gate_lin) * up_lin).astype(brain_type)
        out_list.append((middle + product(activated, down_w)).astype(brain_type))
        attn_back = (
            lax.all_gather(w_query, ("dp", "seq"), axis=0, tiled=True),
            lax.all_gather(w_key, ("dp", "seq"), axis=0, tiled=True),
            lax.all_gather(w_value, ("dp", "seq"), axis=0, tiled=True),
            lax.all_gather(w_output, ("dp", "seq"), axis=0, tiled=True),
            lax.all_gather(attn_gain, ("dp", "seq"), axis=0, tiled=True),
            lax.all_gather(query_gain, ("dp", "seq"), axis=0, tiled=True),
            lax.all_gather(key_gain, ("dp", "seq"), axis=0, tiled=True),
        )
        ffn_back = (
            lax.all_gather(w_gate, ("dp", "seq"), axis=0, tiled=True),
            lax.all_gather(w_up, ("dp", "seq"), axis=0, tiled=True),
            lax.all_gather(w_down, ("dp", "seq"), axis=0, tiled=True),
            lax.all_gather(ffn_gain, ("dp", "seq"), axis=0, tiled=True),
        )
        key_back, value_back = (
            lax.all_gather(key_rot, "seq", axis=0, tiled=True),
            lax.all_gather(value_low, "seq", axis=0, tiled=True),
        )
        query_wb, key_wb, value_wb, output_wb, attn_gb, query_gb, key_gb = attn_back
        gate_wb, up_wb, down_wb, ffn_gb = ffn_back
        cot_rows = cotangent[0, batch_index]
        grad_down = across(activated, cot_rows)
        d_activated = against(cot_rows, down_wb)
        sigma_gate = jax.nn.sigmoid(gate_lin)
        d_gate = (d_activated * up_lin * sigma_gate * (1.0 + gate_lin * (1.0 - sigma_gate))).astype(
            brain_type
        )
        d_up = (d_activated * gate_lin * sigma_gate).astype(brain_type)
        grad_gate = across(normed_mid, d_gate)
        grad_up = across(normed_mid, d_up)
        d_normed_mid = against(d_gate, gate_wb) + against(d_up, up_wb)
        unused_mid, pull_ffn = jax.vjp(norm_rows, middle, ffn_gb.astype(float_type))
        d_mid_norm, grad_ffn_gain = pull_ffn(d_normed_mid)
        d_middle = cot_rows.astype(float_type) + d_mid_norm
        d_middle_low = d_middle.astype(brain_type)
        grad_output = across(attended, d_middle_low)
        d_attended = against(d_middle_low, output_wb).astype(brain_type)

        def back_pair(pair_id):
            query_pair = lax.dynamic_slice_in_dim(
                query_rot, pair_id * width_query, width_query, 1
            ).reshape(rows_here, 2, group_size, HEAD_DIM)
            grad_pair = lax.dynamic_slice_in_dim(
                d_attended, pair_id * width_query, width_query, 1
            ).reshape(rows_here, 2, group_size, HEAD_DIM)
            key_pair = lax.dynamic_slice_in_dim(
                key_back, pair_id * width_key, width_key, 1
            ).reshape(length, 2, HEAD_DIM)
            value_pair = lax.dynamic_slice_in_dim(
                value_back, pair_id * width_key, width_key, 1
            ).reshape(length, 2, HEAD_DIM)
            raw_score = jnp.einsum(
                "qhgd,khd->hgqk", query_pair, key_pair, preferred_element_type=jnp.float32
            )
            scores = jnp.where(keep_mask[None, None], raw_score * score_scale, NEGATIVE)
            soft_prob = jnp.exp(scores - log_totals[pair_id])
            soft_low = soft_prob.astype(jnp.bfloat16)
            d_prob = jnp.einsum(
                "qhgd,khd->hgqk", grad_pair, value_pair, preferred_element_type=jnp.float32
            )
            d_score = soft_prob * (d_prob - jnp.sum(soft_prob * d_prob, axis=-1, keepdims=True))
            d_raw = (d_score * score_scale).astype(jnp.bfloat16)
            d_query = jnp.einsum(
                "hgqk,khd->qhgd", d_raw, key_pair, preferred_element_type=jnp.float32
            )
            d_key = jnp.einsum(
                "hgqk,qhgd->khd", d_raw, query_pair, preferred_element_type=jnp.float32
            )
            d_value = jnp.einsum(
                "hgqk,qhgd->khd", soft_low, grad_pair, preferred_element_type=jnp.float32
            )
            return (
                d_query,
                jnp.concatenate(
                    [d_key.reshape(length, width_key), d_value.reshape(length, width_key)], axis=1
                ),
            )

        d_query_pairs, kv_terms = lax.map(back_pair, pair_ids)
        kv_share = lax.psum_scatter(
            kv_terms.astype(jnp.bfloat16), "seq", scatter_dimension=1, tiled=True
        ).astype(jnp.float32)
        d_key_rot = (
            kv_share[:, :, :width_key]
            .reshape(pair_count, rows_here, 2, HEAD_DIM)
            .transpose(1, 0, 2, 3)
            .reshape(rows_here, KV_HEADS, HEAD_DIM)
        )
        d_value_low = (
            kv_share[:, :, width_key:]
            .transpose(1, 0, 2)
            .reshape(rows_here, KV_HEADS * HEAD_DIM)
            .astype(brain_type)
        )
        d_query_rot = d_query_pairs.transpose(1, 0, 2, 3, 4).reshape(rows_here, HEADS, HEAD_DIM)

        def turn_rows(heads_in, gain_in):
            return rotate(norm_rows(heads_in, gain_in), cosine_table, sine_table)

        unused_query, pull_query = jax.vjp(turn_rows, query_heads, query_gb.astype(float_type))
        d_query_heads, grad_query_gain = pull_query(d_query_rot)
        unused_key, pull_key = jax.vjp(turn_rows, key_heads, key_gb.astype(float_type))
        d_key_heads, grad_key_gain = pull_key(d_key_rot)
        d_query_low = d_query_heads.reshape(rows_here, HEADS * HEAD_DIM).astype(brain_type)
        d_key_low = d_key_heads.reshape(rows_here, KV_HEADS * HEAD_DIM).astype(brain_type)
        grad_query = across(normed_in, d_query_low)
        grad_key = across(normed_in, d_key_low)
        grad_value = across(normed_in, d_value_low)
        d_normed_in = (
            against(d_query_low, query_wb)
            + against(d_key_low, key_wb)
            + against(d_value_low, value_wb)
        )
        unused_in, pull_attn = jax.vjp(norm_rows, rows_in, attn_gb.astype(float_type))
        d_in_norm, grad_attn_gain = pull_attn(d_normed_in)
        grad_list.append(d_middle + d_in_norm)
        fresh = (
            grad_query,
            grad_key,
            grad_value,
            grad_output,
            grad_gate,
            grad_up,
            grad_down,
            grad_attn_gain,
            grad_ffn_gain,
            grad_query_gain,
            grad_key_gain,
        )
        sums = tuple((old + new for old, new in zip(sums, fresh)))
    attn_parts = (
        lax.psum_scatter(sums[0], ("dp", "seq"), scatter_dimension=0, tiled=True),
        lax.psum_scatter(sums[1], ("dp", "seq"), scatter_dimension=0, tiled=True),
        lax.psum_scatter(sums[2], ("dp", "seq"), scatter_dimension=0, tiled=True),
        lax.psum_scatter(sums[3], ("dp", "seq"), scatter_dimension=0, tiled=True),
        lax.psum_scatter(sums[7], ("dp", "seq"), scatter_dimension=0, tiled=True),
        lax.psum_scatter(sums[9], ("dp", "seq"), scatter_dimension=0, tiled=True),
        lax.psum_scatter(sums[10], ("dp", "seq"), scatter_dimension=0, tiled=True),
    )
    ffn_parts = (
        lax.psum_scatter(sums[4], ("dp", "seq"), scatter_dimension=0, tiled=True),
        lax.psum_scatter(sums[5], ("dp", "seq"), scatter_dimension=0, tiled=True),
        lax.psum_scatter(sums[6], ("dp", "seq"), scatter_dimension=0, tiled=True),
        lax.psum_scatter(sums[8], ("dp", "seq"), scatter_dimension=0, tiled=True),
    )
    outputs = jnp.stack(out_list)[None]
    input_grad = jnp.stack(grad_list)[None]
    return (
        outputs,
        input_grad,
        attn_parts[0],
        attn_parts[1],
        attn_parts[2],
        attn_parts[3],
        ffn_parts[0],
        ffn_parts[1],
        ffn_parts[2],
        attn_parts[4],
        ffn_parts[3],
        attn_parts[5],
        attn_parts[6],
    )


MESH = pl.DeviceIdType.MESH
NDP = 4
NSEQ = 8
BLOCKED = -65536.0
QB = 256
BLOCKS = (3, 2, 1, 0)
SOFT = HEAD_DIM ** (-0.5) * 1.4426950408889634

A0, A1, B, C0, C1, E = range(0, 60, 10)
R_A0, R_A1, R_B, R_C0, R_C1, R_E = range(60, 120, 10)
(
    ATTEND, MIX_MID, MIX_END, NORM_MID, NORM_END, LIFT, D_ACT, SINK, TURN_MID, TURN_END, LOW_MID,
    LOW_END, OUT_START, OUT_MID, OUT_END, ATTEND_BACK, IN_START, IN_MID, IN_END, PROJECT,
    GRAD_WIDE, GRAD_ATTN, TABLES, NORM_IN, COTANGENT,
) = range(200, 450, 10)
(
    START, TOKENS, SMALL_DP, SMALL_SEQ, A_IN, C_OUT, C_IN, TREE_START, COT_START, TREE_MID,
    COT_MID, COT_END, TREE_END, NODE, GAINS, GRAD_DOWN, GRAD_OUT, PACK_DP, PACK_SEQ, PACK_END,
    LAND_A, LAND_C, GIVE_OUT, GIVE_IN, DRAIN,
) = range(600, 625, 1)
ORDER = (
    START, B, TOKENS, SMALL_DP, C_OUT, A_IN, A1, A0, B + 1, A1 + 1, A0 + 1, TREE_START, B + 2, SMALL_SEQ,
    A1 + 2, C_IN, A0 + 2, B + 3, C1, A0 + 3, A1 + 3, C0, TREE_MID, NODE, B + 4, A0 + 4, TREE_END, A1 + 4,
    TABLES, B + 5, A0 + 5, GAINS, A1 + 5, TABLES + 1, C0 + 1, A0 + 6, NORM_IN, NORM_IN + 1, A1 + 6, C1 + 1,
    C0 + 2, B + 6, COTANGENT, A0 + 7, A1 + 7, PROJECT, E, C1 + 2, PROJECT + 1, COTANGENT + 1, PROJECT + 2,
    PROJECT + 3, B + 7, ATTEND + 3, C0 + 3, ATTEND + 2, MIX_MID + 3, C1 + 3, E + 1, MIX_MID + 2, ATTEND + 1,
    MIX_END + 3, MIX_MID + 1, ATTEND, C0 + 4, MIX_MID, C1 + 4, E + 2, MIX_END + 2, NORM_MID + 3, MIX_END + 1,
    C0 + 5, NORM_END + 3, MIX_END, C1 + 5, E + 3, COT_START, C0 + 6, NORM_MID + 1, NORM_END + 1, C1 + 6,
    E + 4, NORM_MID, NORM_END, NORM_MID + 2, C0 + 7, NORM_END + 2, C1 + 7, LIFT + 3, E + 5, LIFT, LIFT + 1,
    COT_MID, E + 6, LIFT + 2, COT_END, GRAD_DOWN, R_E, E + 7, D_ACT + 3, D_ACT + 2, SINK + 3, D_ACT, R_E + 1,
    TURN_MID + 3, D_ACT + 1, GRAD_WIDE + 1, R_C1, GRAD_WIDE, R_C0, R_E + 2, TURN_END + 3, SINK + 2, R_C1 + 1,
    SINK + 1, TURN_MID + 2, R_C0 + 1, LOW_MID + 3, SINK, TURN_MID + 1, LOW_END + 3, R_E + 3, R_C1 + 2,
    TURN_MID, TURN_END + 2, R_C0 + 2, ATTEND_BACK + 3, R_C1 + 3, TURN_END + 1, IN_START + 3, LOW_MID + 2,
    R_E + 4, R_C0 + 3, TURN_END, LOW_END + 2, R_C1 + 4, ATTEND_BACK + 2, R_C0 + 4, LOW_MID, LOW_MID + 1,
    R_C1 + 5, R_E + 5, LOW_END, LOW_END + 1, GRAD_OUT, R_B, R_C0 + 5, ATTEND_BACK + 1, R_C1 + 6, IN_START + 2,
    IN_START + 1, R_B + 1, R_E + 6, R_C0 + 6, ATTEND_BACK, IN_START, GRAD_ATTN, R_A0, GRAD_ATTN + 1, R_A1,
    R_B + 2, OUT_START + 3, IN_MID, R_A0 + 1, R_A1 + 1, IN_MID + 1, IN_MID + 2, R_B + 3, OUT_START, R_A0 + 2,
    OUT_START + 1, R_A1 + 2, OUT_MID, R_B + 4, R_A0 + 3, IN_MID + 3, R_A1 + 3, OUT_START + 2, R_B + 5, IN_END,
    R_A0 + 4, IN_END + 1, R_A1 + 4, OUT_MID + 3, OUT_MID + 2, R_B + 6, R_A0 + 5, IN_END + 3, R_A1 + 5,
    IN_END + 2, GIVE_IN, OUT_END + 2, PACK_DP, OUT_END + 3, R_E + 7, OUT_MID + 1, R_A1 + 6, R_A0 + 6, OUT_END,
    PACK_SEQ, R_C0 + 7, OUT_END + 1, R_C1 + 7, GIVE_OUT, PACK_END, LAND_C, R_A1 + 7, R_A0 + 7, R_B + 7,
    LAND_A, DRAIN,
)


def seq_at(position):
    half = position // 4
    z = position + half * (7 - 2 * position)
    return 2 * z + half


def tree_seat(d, m):
    x, c = d // 2, d % 2
    return 2 * (2 * m + c) + (m + c + x) % 2


def greet_all(d, s):
    barrier = pltpu.get_barrier_semaphore()
    me = d * NSEQ + s

    def signal(i, carry):
        other = (me + i) % (NDP * NSEQ)
        pl.semaphore_signal(
            barrier, inc=1, device_id=(other // NSEQ, other % NSEQ), device_id_type=MESH
        )
        return carry

    lax.fori_loop(1, NDP * NSEQ, signal, 0)
    pl.semaphore_wait(barrier, NDP * NSEQ - 1)


def remote(src, dst, sems, at, d, s):
    send, recv = sems
    return pltpu.make_async_remote_copy(
        src_ref=src,
        dst_ref=dst,
        send_sem=send.at[at],
        recv_sem=recv.at[at],
        device_id=(d, s),
        device_id_type=MESH,
    )


class Sum:
    def __init__(self, part, near, sent, got, sems, n, spot):
        self.part, self.near, self.sent, self.got = part, near, sent, got
        self.sems, self.n = sems, n
        d, self.s = spot
        x, c = d // 2, d % 2
        self.d, self.sib, self.far = d, 2 * x + 1 - c, 2 * (1 - x) + c
        self.far_sib = 2 * (1 - x) + 1 - c

    def copies(self, b):
        rows = pl.ds(2 * b, 2)
        return (
            remote(self.part.at[rows, self.far_sib], self.near.at[0, rows], self.sems, (self.n, 0, b), self.sib, self.s),
            remote(self.part.at[rows, self.sib], self.near.at[1, rows], self.sems, (self.n, 1, b), self.sib, self.s),
            remote(self.sent.at[rows], self.got.at[rows], self.sems, (self.n, 2, b), self.far, self.s),
        )

    def start(self, b):
        first, second, _ = self.copies(b)
        first.start()
        second.start()

    def mid(self, b):
        first, _, across_x = self.copies(b)
        first.wait_recv()

        def join(i, carry):
            self.sent[i] = (
                self.part[i, self.far].astype(jnp.float32) + self.near[0, i].astype(jnp.float32)
            ).astype(jnp.bfloat16)
            return carry

        lax.fori_loop(2 * b, 2 * b + 2, join, 0)
        across_x.start()

    def end(self, b, finish):
        first, second, across_x = self.copies(b)
        second.wait_recv()
        across_x.wait_recv()

        def close(i, carry):
            rows = self.part[i, self.d].astype(jnp.float32) + self.near[1, i].astype(jnp.float32)
            finish(i, rows + self.got[i].astype(jnp.float32))
            return carry

        lax.fori_loop(2 * b, 2 * b + 2, close, 0)
        first.wait_send()
        second.wait_send()
        across_x.wait_send()


class Spread:
    def __init__(self, out, sems, at, spot):
        self.out, self.sems, self.place = out, sems, at
        d, self.s = spot
        x, c = d // 2, d % 2
        self.d, self.sib, self.far = d, 2 * x + 1 - c, 2 * (1 - x) + c
        self.far_sib = 2 * (1 - x) + 1 - c

    def copy(self, rows, owner, way, to):
        block = self.out.at[rows, owner]
        return remote(block, block, self.sems, self.place(way, rows), to, self.s)

    def start(self, rows):
        self.copy(rows, self.d, 0, self.far).start()
        self.copy(rows, self.d, 1, self.sib).start()

    def mid(self, rows):
        self.copy(rows, self.far, 0, self.far).wait_recv()
        self.copy(rows, self.far, 2, self.sib).start()

    def end(self, rows):
        self.copy(rows, self.sib, 1, self.sib).wait_recv()
        self.copy(rows, self.far_sib, 2, self.sib).wait_recv()

    def sent(self, rows):
        self.copy(rows, self.d, 0, self.far).wait_send()
        self.copy(rows, self.d, 1, self.sib).wait_send()
        self.copy(rows, self.far, 2, self.sib).wait_send()


def layer_kernel(
    nodes,
    tok, cot, lengths, parents, gain_a, gain_f, gain_q, gain_k, inv_freq, wq, wk, wv, wo, wg, wu, wd,
    out_rows, grad_rows, res_a, res_c, g_output, g_down, pack_out,
    raw_lengths, raw_parents, raw_a, raw_f, raw_q, raw_k, smalls, wa, wb, wc, we, gc, ge, hop_a, hop_b, hop_c, hop_e,
    tree, tree_cot, normed_in, normed_mid, d_low, tree_own,
    lin, heads, value, hidden, member, cosine, sine, att, d_att,
    part, part_out, near, sent, got, near_o, sent_o, got_o,
    middle, d_middle, act, both, d_key, d_value, outs, grad_low,
    fin_a, fin_c, attn_g, ffn_g, head_g, pack_dp, pack_seq, pack_sum,
    loc, s_small, r_small, s_col, r_col, s_tok, r_tok, s_ag, r_ag, s_rs, r_rs,
    s_sum, r_sum, s_tree, r_tree, s_spread, r_spread, s_back, r_back, s_fin, r_fin, s_pack, r_pack,
):
    f32, bf = jnp.float32, jnp.bfloat16
    d = lax.axis_index("dp")
    s = lax.axis_index("seq")
    z, y = s // 2, s % 2
    p = z + y * (7 - 2 * z)
    spot = (d, s)
    seat = [seq_at((p + i) % NSEQ) for i in range(NSEQ)]
    up, down = seat[1], seat[7]
    ag_sems, rs_sems = (s_ag, r_ag), (s_rs, r_rs)
    small_sems, col_sems, tok_sems = (s_small, r_small), (s_col, r_col), (s_tok, r_tok)

    def aligned(v, n):
        return pl.multiple_of(v, n)

    def chunk(n, way, j):
        if n in (0, 1, 3, 4):
            return pl.ds(aligned((2 * way + (n + (n > 2)) % 2) * 256 + j * 32, 32), 32)
        if n == 2:
            return pl.ds(aligned(j * 64 + way * 32, 32), 32)
        return pl.ds(aligned(j * 96 + way * 48, 16), 48)

    weight = {0: wa, 1: wa, 2: wb, 3: wc, 4: wc, 5: we}
    grads = {0: wa, 1: wa, 2: wb, 3: gc, 4: gc, 5: ge}
    hops = {0: hop_a.at[0], 1: hop_a.at[1], 2: hop_b, 3: hop_c.at[0], 4: hop_c.at[1], 5: hop_e}

    def owner_at(way, k):
        return seq_at((p + NSEQ - k) % NSEQ) if way == 0 else seq_at((p + k) % NSEQ)

    def gather(n, k):
        for way, peer in enumerate((up, down)):
            block = weight[n].at[chunk(n, way, owner_at(way, k))]
            if not (isinstance(k, int) and k == 0):
                remote(block, block, ag_sems, (n, way, k - 1), d, peer).wait_recv()
            remote(block, block, ag_sems, (n, way, k), d, peer).start()

    def gather_end(n):
        for way, peer in enumerate((up, down)):
            block = weight[n].at[chunk(n, way, owner_at(way, 7))]
            remote(block, block, ag_sems, (n, way, 6), d, peer).wait_recv()

    def gather_sent(n):
        for way, peer in enumerate((up, down)):
            block = weight[n].at[chunk(n, way, s)]
            for k in range(7):
                remote(block, block, ag_sems, (n, way, k), d, peer).wait_send()

    def add_rows(into, other):
        def one(i, carry):
            at = pl.ds(aligned(i * 16, 16), 16)
            into[at] = (into[at].astype(f32) + other[at].astype(f32)).astype(bf)
            return carry

        lax.fori_loop(0, into.shape[0] // 16, one, 0)

    def reduce_(n, k):
        for way, peer in enumerate((up, down)):
            rows = chunk(n, way, seat[(7 - k) % NSEQ] if way == 0 else seat[(1 + k) % NSEQ])
            mine = grads[n].at[rows]
            if k == 0:
                src = mine
            else:
                src = hops[n].at[way, k - 1]
                remote(src, src, rs_sems, (n, way, k - 1), d, peer).wait_recv()
                add_rows(src, mine)
            remote(src, hops[n].at[way, k], rs_sems, (n, way, k), d, peer).start()

    def reduce_end(n, take):
        for way, peer in enumerate((up, down)):
            src = hops[n].at[way, 6]
            remote(src, src, rs_sems, (n, way, 6), d, peer).wait_recv()
            take(way, src[...].astype(f32) + grads[n][chunk(n, way, s)].astype(f32))

    def reduce_sent(n):
        for way, peer in enumerate((up, down)):
            for k in range(7):
                src = hops[n].at[way, k]
                remote(src, src, rs_sems, (n, way, k), d, peer).wait_send()

    ops = {}
    tree_slot, tree_core = z // 2, z % 2
    tree_owner = 2 * ((y + tree_slot + tree_core) % 2) + tree_core
    pending = []
    held = {}

    def stage(name):
        def keep(run):
            ops[name] = run
            return run

        return keep

    def launch(cp):
        cp.start()
        pending.append(cp)

    raws = [
        pltpu.make_async_copy(src, dst, loc.at[9 + n])
        for n, (src, dst) in enumerate(
            (
                (lengths, raw_lengths), (parents, raw_parents),
                (gain_a, raw_a), (gain_f, raw_f), (gain_q, raw_q), (gain_k, raw_k),
            )
        )
    ]
    pieces = (
        (wq, wa, 512, 0), (wk, wa, 256, 512), (wv, wa, 256, 768), (wg, wc, 768, 0), (wu, wc, 768, 768)
    )
    col_rows = lambda q: pl.ds(aligned(q * 256 + s * 32, 32), 32)

    def column_copy(n):
        src, dst, width, at = pieces[n]
        return pltpu.make_async_copy(
            src.at[:, pl.ds(aligned(d * width, 128), width)],
            dst.at[col_rows(d), pl.ds(at, width)],
            loc.at[2 + n],
        )

    def columns(n):
        src, dst, width, at = pieces[n]
        for i in range(1, NDP):
            q = (d + i) % NDP
            launch(
                remote(
                    src.at[:, pl.ds(aligned(q * width, 128), width)],
                    dst.at[col_rows(d), pl.ds(at, width)],
                    col_sems, (n, i), q, s,
                )
            )
        column_copy(n).start()

    def columns_in(n):
        _, dst, width, at = pieces[n]
        column_copy(n).wait()
        for i in range(1, NDP):
            place = dst.at[col_rows((d + NDP - i) % NDP), pl.ds(at, width)]
            remote(place, place, col_sems, (n, i), d, s).wait_recv()

    def row_copy(n, m, i):
        src, dst = ((tok, tree), (cot, tree_cot))[n]
        q = (d + i) % NDP
        return pltpu.make_async_remote_copy(
            src_ref=src.at[m, pl.ds(aligned(q * 32, 32), 32)],
            dst_ref=dst.at[s, q],
            send_sem=s_tok.at[n, m, i],
            recv_sem=r_tok.at[n],
            device_id=(q, tree_seat(d, m)),
            device_id_type=MESH,
        )

    def rows_out(n, half):
        src, dst = ((tok, tree), (cot, tree_cot))[n]
        for m in range(MICRO):
            if half == 0:
                target = tree_seat(d, m)

                @pl.when(target == s)
                def _():
                    piece = src.at[m, pl.ds(aligned(d * 32, 32), 32)]
                    pltpu.make_async_copy(piece, dst.at[s, d], r_tok.at[n]).start()

                @pl.when(target != s)
                def _():
                    row_copy(n, m, 0).start()

                row_copy(n, m, 1).start()
            else:
                row_copy(n, m, 2).start()
                row_copy(n, m, 3).start()

    def rows_in(dst, n):
        everything = dst.at[:, d]
        pltpu.make_async_copy(everything, everything, r_tok.at[n]).wait()

    fill_b = pltpu.make_async_copy(wo, wb.at[pl.ds(aligned(s * 64, 64), 64)], loc.at[7])
    fill_e = pltpu.make_async_copy(wd, we.at[pl.ds(aligned(s * 96, 16), 96)], loc.at[15])

    @stage(START)
    def _():
        for cp in raws:
            cp.start()
        greet_all(d, s)
        fill_b.start()
        fill_e.start()
        for n in range(3):
            columns(n)

    @stage(TOKENS)
    def _():
        rows_out(0, 0)
        rows_out(0, 1)

    for i in range(2):
        stage(COTANGENT + i)(functools.partial(rows_out, 1, i))


    @stage(SMALL_DP)
    def _():
        for cp in raws:
            cp.wait()
        for row, ref in enumerate((raw_a, raw_f, raw_q, raw_k)):
            count = ref.shape[0]
            line = ref[...].astype(f32).reshape(1, count)
            smalls[d, s, row : row + 1, :] = jnp.concatenate([line] * (128 // count), axis=1)
        smalls[d, s, 4:8, :] = jnp.zeros((4, 128), f32)
        smalls[d, s, 4:6, 0:nodes] = raw_lengths[0].astype(f32)
        smalls[d, s, 6:8, 0:nodes] = raw_parents[0].astype(f32)
        for i in range(1, NDP):
            launch(remote(smalls.at[d, s], smalls.at[d, s], small_sems, i, (d + i) % NDP, s))

    @stage(SMALL_SEQ)
    def _():
        for i in range(1, NDP):
            place = smalls.at[(d + NDP - i) % NDP, s]
            remote(place, place, small_sems, i, d, s).wait_recv()
        for i in range(1, NSEQ):
            launch(remote(smalls.at[:, s], smalls.at[:, s], small_sems, NDP + i, d, (s + i) % NSEQ))

    @stage(A_IN)
    def _():
        for n in range(3):
            columns_in(n)

    @stage(C_OUT)
    def _():
        for n in range(3, 5):
            columns(n)

    @stage(C_IN)
    def _():
        for n in range(3, 5):
            columns_in(n)

    streams = ((A0, 0), (A1, 1), (B, 2), (C0, 3), (C1, 4), (E, 5))

    def ring_first(n):
        if n == 2:
            fill_b.wait()
        if n == 5:
            fill_e.wait()
        gather(n, 0)

    for label, n in streams:
        stage(label)(functools.partial(ring_first, n))
        stage(label + 7)(functools.partial(gather_end, n))
        for k in range(1, 7):
            stage(label + k)(functools.partial(gather, n, k))
        for k in range(7):
            stage(R_A0 + label + k)(functools.partial(reduce_, n, k))

    everything = pl.ds(0, NSEQ)
    spread_tree = Spread(tree, (s_tree, r_tree), lambda way, rows: (0, way), spot)
    spread_cot = Spread(tree_cot, (s_tree, r_tree), lambda way, rows: (1, way), spot)

    @stage(TREE_START)
    def _():
        rows_in(tree, 0)
        spread_tree.start(everything)

    @stage(COT_START)
    def _():
        rows_in(tree_cot, 1)
        spread_cot.start(everything)

    stage(TREE_MID)(lambda: spread_tree.mid(everything))
    stage(COT_MID)(lambda: spread_cot.mid(everything))
    stage(COT_END)(lambda: spread_cot.end(everything))
    own_rows = pltpu.make_async_copy(tree.at[:, d], tree_own, loc.at[8])

    @stage(TREE_END)
    def _():
        spread_tree.end(everything)
        own_rows.start()

    @stage(NODE)
    def _():
        ir = lax.broadcasted_iota(jnp.int32, (128, 128), 0)
        ic = lax.broadcasted_iota(jnp.int32, (128, 128), 1)
        block = smalls.at[tree_owner, s]
        length_row = block[pl.ds(4 + tree_slot, 1), :]
        parent_row = block[pl.ds(6 + tree_slot, 1), :]
        length_col = jnp.sum(jnp.where(ir == ic, length_row, 0.0), axis=1, keepdims=True)
        over = (parent_row == ir.astype(f32)) & (ic > 0) & (ic < nodes)
        above = jnp.where(over | (ir == ic), 1.0, 0.0)
        for _ in range(4):
            low = above.astype(bf)
            above = jnp.minimum(product(low, low), 1.0)
        start_row = jnp.sum(jnp.where(ir < ic, length_col, 0.0), axis=0, keepdims=True)
        base_row = jnp.sum(
            jnp.where((above > 0.5) & (ir != ic), length_col, 0.0), axis=0, keepdims=True
        )
        shut = jnp.where(above > 0.5, 0.0, BLOCKED).astype(bf)
        held["node"] = (start_row, start_row + length_row, base_row - start_row, shut)

    def tables(i, carry):
        start_row, end_row, offset_row, shut = held["node"]
        rows = pl.ds(aligned(i * QB, QB), QB)
        index = (lax.broadcasted_iota(jnp.int32, (QB, 128), 0) + i * QB).astype(f32)
        inside = (index >= start_row) & (index < end_row)
        position = index[:, :1] + jnp.sum(
            jnp.where(inside, offset_row, 0.0), axis=1, keepdims=True
        )
        hot = jnp.where(inside, 1.0, 0.0).astype(bf)
        member[rows] = hot
        hidden[rows] = against(hot, shut).astype(bf)
        angle = position * inv_freq[...]
        cosine[rows] = jnp.cos(angle)
        lane = lax.broadcasted_iota(jnp.int32, (QB, 128), 1)
        wave = jnp.sin(angle)
        sine[rows] = jnp.where(lane < 64, -wave, wave)
        return carry

    stage(TABLES + 0)(lambda: lax.fori_loop(0, 2, tables, 0))
    stage(TABLES + 1)(lambda: lax.fori_loop(2, 4, tables, 0))

    @stage(GAINS)
    def _():
        for i in range(1, NSEQ):
            place = smalls.at[:, (s + NSEQ - i) % NSEQ]
            remote(place, place, small_sems, NDP + i, d, s).wait_recv()
        lane = lax.broadcasted_iota(jnp.int32, (1, 128), 1)
        for row, dst in ((0, attn_g), (1, ffn_g)):
            for j in range(8):
                parts = [
                    smalls[(4 * j + i) // 8, (4 * j + i) % 8, row : row + 1, :] for i in range(4)
                ]
                dst[:, 128 * j : 128 * (j + 1)] = jnp.where(
                    lane < 64,
                    jnp.where(lane < 32, parts[0], parts[1]),
                    jnp.where(lane < 96, parts[2], parts[3]),
                )
        for row in (2, 3):
            joined = jnp.zeros((1, 128), f32)
            for i in range(32):
                joined = jnp.where(lane // 4 == i, smalls[i // 8, i % 8, row : row + 1, :], joined)
            head_g[row - 2 : row - 1, :] = joined
        pack_dp[d] = jnp.zeros((24, 128), f32)

    def norm_in(i, carry):
        rows = tree[i].reshape(128, D).astype(f32)
        scale = lax.rsqrt(jnp.mean(rows * rows, axis=-1, keepdims=True) + EPSILON)
        normed_in[pl.ds(aligned(i * 128, 128), 128)] = (rows * scale * attn_g[...]).astype(bf)
        return carry

    stage(NORM_IN + 0)(lambda: lax.fori_loop(0, 4, norm_in, 0))
    stage(NORM_IN + 1)(lambda: lax.fori_loop(4, 8, norm_in, 0))

    def unit_of(v):
        scale = lax.rsqrt(jnp.mean(v * v, axis=-1, keepdims=True) + EPSILON)
        return v * scale, scale

    def turn(v, gain, cos, sin):
        unit, _ = unit_of(v)
        lifted = unit * gain
        return lifted * cos + pltpu.roll(lifted, 64, 1) * sin

    def turn_back(dr, v, gain, cos, sin):
        d_lift = dr * cos + pltpu.roll(dr * sin, 64, 1)
        unit, scale = unit_of(v)
        d_unit = d_lift * gain
        return (
            scale * (d_unit - unit * jnp.mean(unit * d_unit, axis=-1, keepdims=True)),
            jnp.sum(d_lift * unit, axis=0, keepdims=True),
        )

    def project(i):
        rows = pl.ds(i * QB, QB)
        cos, sin = cosine[rows], sine[rows]

        def one(j, carry):
            lanes = pl.ds(aligned(j * 256, 256), 256)
            pair = product(normed_in[rows], wa[:, lanes])
            lin[rows, lanes] = pair
            gain = head_g[pl.ds(j // 2, 1), :]
            for i2 in range(2):
                turned = turn(pair[:, 128 * i2 : 128 * (i2 + 1)], gain, cos, sin)
                heads[2 * j + i2, rows] = turned.astype(bf)
            return carry

        lax.fori_loop(0, 3, one, 0)
        value[rows] = product(normed_in[rows], wa[:, 768:]).astype(bf)

    for i in range(4):
        stage(PROJECT + i)(functools.partial(project, i))

    def span(b):
        return pl.ds(b * QB, QB), (b + 1) * QB

    def weights_of(b, h, n):
        here = pl.ds(b * QB, QB)
        q = jnp.concatenate([heads[h, here], hidden[here]], axis=1)
        k = jnp.concatenate([heads[4 + h // 2, pl.ds(0, n)], member[pl.ds(0, n)]], axis=1)
        score = against(q, k) * SOFT
        row = lax.broadcasted_iota(jnp.int32, (QB, QB), 0)
        col = lax.broadcasted_iota(jnp.int32, (QB, QB), 1)
        diag = jnp.where(col <= row, score[:, n - QB :], NEGATIVE)
        score = diag if b == 0 else jnp.concatenate([score[:, : n - QB], diag], axis=1)
        grown = jnp.exp2(score)
        return grown, 1.0 / jnp.sum(grown, axis=-1, keepdims=True)

    def head_lanes(h):
        return pl.ds(aligned(h * HEAD_DIM, HEAD_DIM), HEAD_DIM)

    sum_sems, spread_sems = (s_sum, r_sum), (s_spread, r_spread)
    mixed_sum = Sum(part, near, sent, got, sum_sems, 0, spot)
    mid_sum = Sum(part, near, sent, got, sum_sems, 1, spot)
    out_sum = Sum(part_out, near_o, sent_o, got_o, sum_sems, 2, spot)
    in_sum = Sum(part, near, sent, got, sum_sems, 3, spot)
    pair_of = {b: pl.ds(2 * b, 2) for b in BLOCKS}
    spread_mid = Spread(normed_mid, spread_sems, lambda way, rows: (0, way, rows.start // 2), spot)
    spread_low = Spread(d_low, spread_sems, lambda way, rows: (1, way, rows.start // 2), spot)

    def attend(b):
        here, n = span(b)
        if b == BLOCKS[0]:
            own_rows.wait()

        def one(h, carry):
            grown, inverse = weights_of(b, h, n)
            mixed = product(grown.astype(bf), value[pl.ds(0, n), head_lanes(h // 2)])
            att[here, head_lanes(h)] = (mixed * inverse).astype(bf)
            return carry

        lax.fori_loop(0, HEADS // NDP, one, 0)
        rows = product(att[here], wb[...]).astype(bf)
        part[pair_of[b]] = rows.reshape(2, NDP, 32, D)
        mixed_sum.start(b)

    def to_middle(i, rows):
        rows = rows + tree_own[i].astype(f32)
        middle[i] = rows
        scale = lax.rsqrt(jnp.mean(rows * rows, axis=-1, keepdims=True) + EPSILON)
        normed_mid[i, d] = (rows * scale * ffn_g[...]).astype(bf)

    def close_mixed(b):
        mixed_sum.end(b, to_middle)
        spread_mid.start(pair_of[b])

    def lift(b):
        here = pl.ds(b * QB, QB)
        rows = normed_mid[pair_of[b]].reshape(QB, D)

        def one(t, carry):
            left = pl.ds(aligned(t * 256, 256), 256)
            right = pl.ds(aligned(768 + t * 256, 256), 256)
            gate = product(rows, wc[:, left])
            wide = product(rows, wc[:, right])
            sigma = 1.0 / (1.0 + jnp.exp(-gate))
            silu = gate * sigma
            act[here, left] = (silu * wide).astype(bf)
            both[here, left] = (wide * sigma * (1.0 + gate * (1.0 - sigma))).astype(bf)
            both[here, right] = silu.astype(bf)
            return carry

        lax.fori_loop(0, 3, one, 0)

    @stage(GRAD_DOWN)
    def _():
        def one(i, carry):
            cols = pl.ds(aligned(i * 256, 256), 256)
            ge[cols] = across(act[:, cols], tree_cot[...].reshape(NSEQ * 128, D)).astype(bf)
            return carry

        lax.fori_loop(0, 3, one, 0)

    def d_activate(b):
        here = pl.ds(b * QB, QB)
        cots = tree_cot[pair_of[b]].reshape(QB, D)

        def one(t, carry):
            left = pl.ds(aligned(t * 256, 256), 256)
            right = pl.ds(aligned(768 + t * 256, 256), 256)
            d_act = against(cots, we[left])
            both[here, left] = (d_act * both[here, left].astype(f32)).astype(bf)
            both[here, right] = (d_act * both[here, right].astype(f32)).astype(bf)
            return carry

        lax.fori_loop(0, 3, one, 0)

    def sink(b):
        here = pl.ds(b * QB, QB)
        part[pair_of[b]] = against(both[here], wc[...]).astype(bf).reshape(2, NDP, 32, D)
        mid_sum.start(b)

    def settle(b):
        here = pl.ds(b * QB, QB)
        part_out[pair_of[b]] = product(act[here], we[...]).astype(bf).reshape(2, NDP, 32, D)
        out_sum.start(b)

    def to_turn(i, rows):
        unit, scale = unit_of(middle[i])
        lifted = ffn_g[...] * rows
        term = jnp.sum(rows * unit, axis=0, keepdims=True)
        for j in range(8):
            pack_dp[d, 8 + j : 9 + j] += term[:, 128 * j : 128 * (j + 1)]
        d_mid = tree_cot[i, d].astype(f32) + scale * (
            lifted - unit * jnp.mean(unit * lifted, axis=-1, keepdims=True)
        )
        d_middle[i] = d_mid
        d_low[i, d] = d_mid.astype(bf)

    def close_mid(b):
        mid_sum.end(b, to_turn)
        spread_low.start(pair_of[b])

    def to_outs(i, rows):
        outs[i] = (middle[i] + rows).astype(bf)

    back_owner, back_slot = tree_owner, tree_slot
    back = ((outs, out_rows), (grad_low, grad_rows))

    def give_copy(n, j):
        src, dst = back[n]
        return pltpu.make_async_remote_copy(
            src_ref=src.at[j],
            dst_ref=dst.at[back_slot, pl.ds(aligned(d * 32, 32), 32)],
            send_sem=s_back.at[n, j],
            recv_sem=r_back.at[n],
            device_id=(back_owner, j),
            device_id_type=MESH,
        )

    def give(n):
        src, dst = back[n]

        def one(j, carry):
            same = (back_owner == d) & (s == j)

            @pl.when(same)
            def _():
                place = dst.at[back_slot, pl.ds(aligned(d * 32, 32), 32)]
                pltpu.make_async_copy(src.at[j], place, r_back.at[n]).start()

            @pl.when(jnp.logical_not(same))
            def _():
                give_copy(n, j).start()

            return carry

        lax.fori_loop(0, NSEQ, one, 0)

    def close_out(b):
        out_sum.end(b, to_outs)

    def grad_wide(sub):
        for i in (sub, 2 + sub):
            cols = pl.ds(i * 256, 256)

            def one(t, carry):
                lanes = pl.ds(aligned(512 * t, 512), 512)
                gc[cols, lanes] = across(
                    normed_mid[:, :, :, cols].reshape(NSEQ * 128, 256), both[:, lanes]
                ).astype(bf)
                return carry

            lax.fori_loop(0, 3, one, 0)

    d_lin = tree

    def close_low(b):
        spread_low.end(pair_of[b])
        here = pl.ds(b * QB, QB)
        rows = d_low[pair_of[b]].reshape(QB, D)
        d_att[here] = against(rows, wb[...]).astype(bf)

    def attend_back(b):
        here, n = span(b)
        keys = pl.ds(0, n)
        if b == BLOCKS[0]:
            spread_tree.sent(everything)
            d_key[...] = jnp.zeros_like(d_key)
            d_value[...] = jnp.zeros_like(d_value)

        def one(h, carry):
            kv = h // 2
            grown, inverse = weights_of(b, h, n)
            prob = grown * inverse
            d_out = d_att[here, head_lanes(h)]
            d_prob = against(d_out, value[keys, head_lanes(kv)])
            delta = jnp.sum(prob * d_prob, axis=-1, keepdims=True)
            d_raw = (prob * (d_prob - delta) * HEAD_DIM ** (-0.5)).astype(bf)
            d_rot = product(d_raw, heads[4 + kv, keys])
            d_key[kv, keys] += across(d_raw, heads[h, here])
            d_value[kv, keys] += across(prob.astype(bf), d_out)
            back, d_gain = turn_back(
                d_rot, lin[here, head_lanes(h)], head_g[0:1, :], cosine[here], sine[here]
            )
            pack_dp[d, 16:17] += d_gain
            d_lin[pair_of[b], :, :, head_lanes(h)] = back.astype(bf).reshape(2, NDP, 32, HEAD_DIM)
            return carry

        lax.fori_loop(0, HEADS // NDP, one, 0)
        for kv in range(KV_HEADS // NDP):
            at = 512 + 128 * kv
            back, d_gain = turn_back(
                d_key[kv, here], lin[here, pl.ds(at, 128)], head_g[1:2, :], cosine[here], sine[here]
            )
            pack_dp[d, 17:18] += d_gain
            d_lin[pair_of[b], :, :, pl.ds(at, 128)] = back.astype(bf).reshape(2, NDP, 32, 128)
            d_lin[pair_of[b], :, :, pl.ds(at + 256, 128)] = (
                d_value[kv, here].astype(bf).reshape(2, NDP, 32, 128)
            )

    def sink_in(b):
        rows = against(d_lin[pair_of[b]].reshape(QB, 1024), wa[...])
        part[pair_of[b]] = rows.astype(bf).reshape(2, NDP, 32, D)
        in_sum.start(b)

    @stage(GRAD_OUT)
    def _():
        gather_sent(2)
        for i in range(2):
            cols = pl.ds(256 * i, 256)
            wb[cols] = across(att[:, cols], d_low[...].reshape(NSEQ * 128, D)).astype(bf)

    def grad_attn(sub):
        gather_sent(sub)
        for i in (sub, 2 + sub):
            cols = pl.ds(i * 256, 256)

            def one(t, carry):
                lanes = pl.ds(aligned(512 * t, 512), 512)
                wa[cols, lanes] = across(
                    normed_in[:, cols], d_lin[:, :, :, lanes].reshape(NSEQ * 128, 512)
                ).astype(bf)
                return carry

            lax.fori_loop(0, 2, one, 0)

    def to_grad(i, rows):
        unit, scale = unit_of(tree_own[i].astype(f32))
        lifted = attn_g[...] * rows
        term = jnp.sum(rows * unit, axis=0, keepdims=True)
        for j in range(8):
            pack_dp[d, j : j + 1] += term[:, 128 * j : 128 * (j + 1)]
        grad = d_middle[i] + scale * (
            lifted - unit * jnp.mean(unit * lifted, axis=-1, keepdims=True)
        )
        grad_low[i] = grad.astype(bf)

    def close_in(b):
        in_sum.end(b, to_grad)

    per_block = (
        (ATTEND, attend), (MIX_MID, mixed_sum.mid), (MIX_END, close_mixed),
        (NORM_MID, lambda b: spread_mid.mid(pair_of[b])), (NORM_END, lambda b: spread_mid.end(pair_of[b])),
        (LIFT, lift), (D_ACT, d_activate), (SINK, sink), (TURN_MID, mid_sum.mid), (TURN_END, close_mid),
        (LOW_MID, lambda b: spread_low.mid(pair_of[b])), (LOW_END, close_low),
        (OUT_START, settle), (OUT_MID, out_sum.mid), (OUT_END, close_out),
        (ATTEND_BACK, attend_back), (IN_START, sink_in), (IN_MID, in_sum.mid), (IN_END, close_in),
    )
    for label, run in per_block:
        for b in BLOCKS:
            stage(label + b)(functools.partial(run, b))
    for sub in range(2):
        stage(GRAD_WIDE + sub)(functools.partial(grad_wide, sub))
        stage(GRAD_ATTN + sub)(functools.partial(grad_attn, sub))

    stage(GIVE_OUT)(functools.partial(give, 0))
    stage(GIVE_IN)(functools.partial(give, 1))

    pack_sems, fin_sems = (s_pack, r_pack), (s_fin, r_fin)

    @stage(PACK_DP)
    def _():
        for i in range(1, NDP):
            launch(remote(pack_dp.at[d], pack_dp.at[d], pack_sems, i, (d + i) % NDP, s))

    @stage(PACK_SEQ)
    def _():
        for i in range(1, NDP):
            place = pack_dp.at[(d + NDP - i) % NDP]
            remote(place, place, pack_sems, i, d, s).wait_recv()
        pack_seq[s] = (pack_dp[0] + pack_dp[1]) + (pack_dp[2] + pack_dp[3])
        for i in range(1, NSEQ):
            launch(remote(pack_seq.at[s], pack_seq.at[s], pack_sems, NDP + i, d, (s + i) % NSEQ))

    @stage(PACK_END)
    def _():
        for i in range(1, NSEQ):
            place = pack_seq.at[(s + NSEQ - i) % NSEQ]
            remote(place, place, pack_sems, NDP + i, d, s).wait_recv()
        total = pack_seq[0]
        for j in range(1, NSEQ):
            total = total + pack_seq[j]
        pack_sum[...] = total
        at = d * NSEQ + s
        for n, (row, count) in enumerate(
            ((at // 4, 32), (8 + at // 4, 32), (16, 4), (17, 4))
        ):
            line = pack_sum[pl.ds(row, 1), :]
            shift = (128 - (at * count) % 128) % 128
            pack_out[n : n + 1, :] = pltpu.roll(line, shift, 1)

    def close_cols(n, fin, landed, which):
        sub = (n + (n > 2)) % 2

        def take(way, total):
            fin[2 * way + sub] = total.astype(bf)

        reduce_end(n, take)
        for way in range(2):
            q = 2 * way + sub

            @pl.when(q == d)
            def _():
                pltpu.make_async_copy(fin.at[q], landed.at[d], loc.at[which]).start()

            @pl.when(q != d)
            def _():
                remote(fin.at[q], landed.at[d], fin_sems, (which, d), q, s).start()

    for label, n, fin, landed, which in (
        (A0, 0, fin_a, res_a, 0), (A1, 1, fin_a, res_a, 0),
        (C0, 3, fin_c, res_c, 1), (C1, 4, fin_c, res_c, 1),
    ):
        stage(R_A0 + label + 7)(functools.partial(close_cols, n, fin, landed, which))

    def land(landed, which):
        for i in range(1, NDP):
            q = (d + i) % NDP
            remote(landed.at[q], landed.at[q], fin_sems, (which, q), q, s).wait_recv()
        pltpu.make_async_copy(landed.at[d], landed.at[d], loc.at[which]).wait()

    stage(LAND_A)(lambda: land(res_a, 0))
    stage(LAND_C)(lambda: land(res_c, 1))

    def take_rows(dst, rows, way, total):
        dst[rows * way : rows * (way + 1)] = total

    stage(R_B + 7)(lambda: reduce_end(2, functools.partial(take_rows, g_output, 32)))
    stage(R_E + 7)(lambda: reduce_end(5, functools.partial(take_rows, g_down, 48)))

    @stage(DRAIN)
    def _():
        for n, (src, dst) in enumerate(back):
            pltpu.make_async_copy(dst, dst, r_back.at[n]).wait()

            def one(j, carry):
                @pl.when(jnp.logical_not((back_owner == d) & (s == j)))
                def _():
                    give_copy(n, j).wait_send()

                return carry

            lax.fori_loop(0, NSEQ, one, 0)
        for n, (fin, landed) in enumerate(((fin_a, res_a), (fin_c, res_c))):
            for i in range(1, NDP):
                q = (d + i) % NDP
                remote(fin.at[q], landed.at[d], fin_sems, (n, d), q, s).wait_send()
        for n in (3, 4, 5):
            gather_sent(n)
        for n in range(6):
            reduce_sent(n)
        spread_cot.sent(everything)
        for b in BLOCKS:
            spread_mid.sent(pair_of[b])
            spread_low.sent(pair_of[b])
        for cp in pending:
            cp.wait_send()
        for n in range(2):
            for m in range(MICRO):

                @pl.when(tree_seat(d, m) != s)
                def _():
                    row_copy(n, m, 0).wait_send()

                for i in range(1, NDP):
                    row_copy(n, m, i).wait_send()

    for name in ORDER:
        ops[name]()


def finish_kernel(
    out_rows, grad_rows, res_a, res_c, g_output, g_down, pack,
    outs, grads, g_query, g_key, g_value, out_output, g_gate, g_up, out_down, g_attn, g_ffn, g_qg, g_kg,
    low_rows, low_a, low_c, small, *rest,
):
    *held, sems = rest
    coming = [
        pltpu.make_async_copy(src, dst, sems.at[n])
        for n, (src, dst) in enumerate(
            (
                (grad_rows, low_rows), (res_a, low_a), (res_c, low_c), (pack, small),
                (out_rows, held[0]), (g_output, held[1]), (g_down, held[2]),
            )
        )
    ]
    for cp in coming:
        cp.start()
    leaving = [
        pltpu.make_async_copy(src, dst, sems.at[7 + n])
        for n, (src, dst) in enumerate(zip(held, (outs, out_output, out_down)))
    ]
    for came, goes in zip(coming[4:], leaving):
        came.wait()
        goes.start()
    coming[0].wait()
    grads[...] = low_rows[...].astype(jnp.float32)
    for cp in coming[1:4]:
        cp.wait()
    for src, cuts in (
        (low_a, ((0, 512, g_query), (512, 256, g_key), (768, 256, g_value))),
        (low_c, ((0, 768, g_gate), (768, 768, g_up))),
    ):
        for q in range(NDP):
            for at, width, dst in cuts:
                dst[:, width * q : width * (q + 1)] = src[q, :, at : at + width].astype(jnp.float32)
    for n, dst in enumerate((g_attn, g_ffn, g_qg, g_kg)):
        count = dst.shape[0]
        dst[...] = small[n : n + 1, 0:count].reshape(count)
    for cp in leaving:
        cp.wait()


def tree_shards(
    tokens, cotangent, node_lengths, parents, w_query, w_key, w_value, w_output, w_gate, w_up, w_down,
    attn_gain, ffn_gain, query_gain, key_gain,
):
    f32, bf = jnp.float32, jnp.bfloat16
    nodes = node_lengths.shape[2]
    half = np.arange(HEAD_DIM // 2, dtype=np.float64)
    inv_freq = THETA ** (-(half * (2.0 / HEAD_DIM)))
    inv_freq = np.concatenate([inv_freq, inv_freq])[None].astype(np.float32)
    shape, vmem, dma = jax.ShapeDtypeStruct, pltpu.VMEM, pltpu.SemaphoreType.DMA
    anywhere = pl.BlockSpec(memory_space=pl.ANY)
    here = pl.BlockSpec(memory_space=pltpu.VMEM)
    rows = NSEQ * 128
    quarter = (NSEQ, 32, D)
    twice = lambda *dims: [dma(dims), dma(dims)]
    results = pl.pallas_call(
        functools.partial(layer_kernel, nodes),
        out_shape=(
            shape((MICRO, 128, D), bf),
            shape((MICRO, 128, D), bf),
            shape((NDP, 32, 1024), bf),
            shape((NDP, 32, 1536), bf),
            shape((64, D), f32),
            shape((96, D), f32),
            shape((8, 128), f32),
        ),
        in_specs=[anywhere] * 8 + [here] + [anywhere] * 7,
        out_specs=[anywhere] * 4 + [here] * 3,
        scratch_shapes=[
            vmem(node_lengths.shape, jnp.int32), vmem(parents.shape, jnp.int32),
            *[vmem(gain.shape, bf) for gain in (attn_gain, ffn_gain, query_gain, key_gain)],
            vmem((NDP, NSEQ, 8, 128), f32),
            vmem((D, 1024), bf), vmem((512, D), bf), vmem((D, 1536), bf), vmem((768, D), bf),
            vmem((D, 1536), bf), vmem((768, D), bf),
            vmem((2, 2, 7, 32, 1024), bf), vmem((2, 7, 32, D), bf),
            vmem((2, 2, 7, 32, 1536), bf), vmem((2, 7, 48, D), bf),
            vmem((NSEQ, NDP, 32, D), bf), vmem((NSEQ, NDP, 32, D), bf), vmem((rows, D), bf),
            vmem((NSEQ, NDP, 32, D), bf), vmem((NSEQ, NDP, 32, D), bf), vmem(quarter, bf),
            vmem((rows, 768), f32), vmem((6, rows, 128), bf),
            vmem((rows, 256), bf), vmem((rows, 128), bf), vmem((rows, 128), bf),
            vmem((rows, 128), f32), vmem((rows, 128), f32), vmem((rows, 512), bf), vmem((rows, 512), bf),
            vmem((NSEQ, NDP, 32, D), bf), vmem((NSEQ, NDP, 32, D), bf),
            vmem((2,) + quarter, bf), vmem(quarter, bf), vmem(quarter, bf),
            vmem((2,) + quarter, bf), vmem(quarter, bf), vmem(quarter, bf),
            vmem(quarter, f32), vmem(quarter, f32), vmem((rows, 768), bf), vmem((rows, 1536), bf),
            vmem((2, rows, 128), f32), vmem((2, rows, 128), f32), vmem(quarter, bf), vmem(quarter, bf),
            vmem((NDP, 32, 1024), bf), vmem((NDP, 32, 1536), bf),
            vmem((1, D), f32), vmem((1, D), f32), vmem((8, 128), f32),
            vmem((NDP, 24, 128), f32), vmem((NSEQ, 24, 128), f32), vmem((24, 128), f32),
            dma((16,)),
            *twice(12), *twice(5, NDP), dma((2, MICRO, NDP)), dma((2,)),
            *twice(6, 2, 7), *twice(6, 2, 7),
            *twice(4, 3, 4), *twice(2, 3), *twice(2, 3, 4),
            dma((2, NSEQ)), dma((2,)), *twice(2, NDP), *twice(12),
        ],
        compiler_params=pltpu.CompilerParams(
            collective_id=1, has_side_effects=True, vmem_limit_bytes=61 << 20
        ),
        name="layer",
    )(
        tokens[0], cotangent[0], node_lengths, parents, attn_gain, ffn_gain, query_gain, key_gain, inv_freq,
        w_query, w_key, w_value, w_output, w_gate, w_up, w_down,
    )
    full = lambda *dims: shape(dims, f32)
    finished = pl.pallas_call(
        finish_kernel,
        out_shape=(
            shape((MICRO, 128, D), bf), full(MICRO, 128, D),
            full(32, 2048), full(32, 1024), full(32, 1024), full(64, D),
            full(32, FF), full(32, FF), full(96, D),
            full(32), full(32), full(4), full(4),
        ),
        in_specs=[pl.BlockSpec(memory_space=pltpu.HBM)] * 7,
        out_specs=[anywhere, here, here, here, here, anywhere, here, here, anywhere] + [here] * 4,
        scratch_shapes=[
            vmem((MICRO, 128, D), bf), vmem((NDP, 32, 1024), bf), vmem((NDP, 32, 1536), bf),
            vmem((8, 128), f32), vmem((MICRO, 128, D), bf), vmem((64, D), f32), vmem((96, D), f32),
            dma((10,)),
        ],
        compiler_params=pltpu.CompilerParams(vmem_limit_bytes=61 << 20),
        name="finish",
    )(*results)
    return (finished[0][None], finished[1][None]) + tuple(finished[2:])


def solution(mesh):
    ring = mesh.shape["dp"] == NDP and mesh.shape["seq"] == NSEQ
    return jax.shard_map(
        tree_shards if ring else general_shards,
        mesh=mesh,
        in_specs=(
            P("dp", None, "seq", None),
            P("dp", None, "seq", None),
            P("dp", None, None),
            P("dp", None, None),
            P(("dp", "seq"), None),
            P(("dp", "seq"), None),
            P(("dp", "seq"), None),
            P(("dp", "seq"), None),
            P(("dp", "seq"), None),
            P(("dp", "seq"), None),
            P(("dp", "seq"), None),
            P(("dp", "seq")),
            P(("dp", "seq")),
            P(("dp", "seq")),
            P(("dp", "seq")),
        ),
        out_specs=(
            P("dp", None, "seq", None),
            P("dp", None, "seq", None),
            P(("dp", "seq"), None),
            P(("dp", "seq"), None),
            P(("dp", "seq"), None),
            P(("dp", "seq"), None),
            P(("dp", "seq"), None),
            P(("dp", "seq"), None),
            P(("dp", "seq"), None),
            P(("dp", "seq")),
            P(("dp", "seq")),
            P(("dp", "seq")),
            P(("dp", "seq")),
        ),
        check_vma=False,
    )
```

```python
import functools

import jax
import jax.numpy as jnp
import numpy as np
from jax import lax
from jax.experimental import pallas as pl
from jax.experimental.pallas import tpu as pltpu
from jax.sharding import PartitionSpec as P

D = 1024
HEADS = 16
KV_HEADS = 8
HEAD_DIM = 128
FF = 3072
MICRO = 2


EPSILON = 1e-06
THETA = 1000000.0
NEGATIVE = -1e30
PRECISE = lax.Precision.HIGHEST


def norm_rows(values, row_gain):
    return (
        values * lax.rsqrt(jnp.mean(values * values, axis=-1, keepdims=True) + EPSILON) * row_gain
    )


def rope_tables(position, head_dim):
    half_dim = head_dim // 2
    inv_freq = THETA ** (-(jnp.arange(half_dim, dtype=jnp.float32) * (2.0 / head_dim)))
    angles = position.astype(jnp.float32)[:, None] * inv_freq[None, :]
    cosine_table = jnp.cos(angles)
    sine_table = jnp.sin(angles)
    return (
        jnp.concatenate([cosine_table, cosine_table], axis=1),
        jnp.concatenate([sine_table, sine_table], axis=1),
    )


def rotate(values, cosine_table, sine_table):
    half_dim = values.shape[-1] // 2
    turned = jnp.concatenate([-values[..., half_dim:], values[..., :half_dim]], axis=-1)
    return values * cosine_table[:, None, :] + turned * sine_table[:, None, :]


def tree_tables(lengths, parent_row):
    node_count = lengths.shape[0]
    labels = jnp.arange(node_count, dtype=jnp.int32)
    parent_hot = ((parent_row[:, None] == labels[None, :]) & (labels[:, None] > 0)).astype(
        jnp.int32
    )

    def extend(depth_step, state_pair):
        reached, covered = state_pair
        reached = jnp.sum(reached[:, :, None] * parent_hot[None, :, :], axis=1)
        return (reached, covered + reached)

    reached, covered = lax.fori_loop(0, node_count, extend, (parent_hot, parent_hot))
    ancestry = (covered > 0).astype(jnp.float32)
    starts = jnp.cumsum(lengths) - lengths
    path_base = jnp.sum(jnp.where(covered > 0, lengths[None, :], 0), axis=1)
    return (labels, starts, path_base, ancestry)


def token_nodes(token_index, labels, starts, path_base):
    node_id = jnp.sum((token_index[:, None] >= starts[None, 1:]).astype(jnp.int32), axis=1)
    member = node_id[:, None] == labels[None, :]
    offset = jnp.sum(jnp.where(member, (path_base - starts)[None, :], 0), axis=1)
    return (member.astype(jnp.float32), token_index + offset)


def visible(query_member, query_index, key_member, key_index, ancestry):
    numbers = (((1,), (1,)), ((), ()))
    lifted = jnp.dot(query_member, ancestry, precision=PRECISE)
    above = lax.dot_general(lifted, key_member, numbers, precision=PRECISE)
    same_node = lax.dot_general(query_member, key_member, numbers, precision=PRECISE)
    return (above > 0.5) | (same_node > 0.5) & (key_index[None, :] <= query_index[:, None])


def product(left_side, right_side):
    return jnp.dot(left_side, right_side, preferred_element_type=jnp.float32)


def against(left_side, right_side):
    return lax.dot_general(
        left_side, right_side, (((1,), (1,)), ((), ())), preferred_element_type=jnp.float32
    )


def across(left_side, right_side):
    return lax.dot_general(
        left_side, right_side, (((0,), (0,)), ((), ())), preferred_element_type=jnp.float32
    )


def general_shards(
    tokens,
    cotangent,
    node_lengths,
    parents,
    w_query,
    w_key,
    w_value,
    w_output,
    w_gate,
    w_up,
    w_down,
    attn_gain,
    ffn_gain,
    query_gain,
    key_gain,
):
    rows_here = tokens.shape[2]
    length = lax.axis_size("seq") * rows_here
    group_size = HEADS // KV_HEADS
    pair_count = KV_HEADS // 2
    width_query = 2 * group_size * HEAD_DIM
    width_key = 2 * HEAD_DIM
    score_scale = HEAD_DIM ** (-0.5)
    local_index = lax.axis_index("seq") * rows_here + jnp.arange(rows_here, dtype=jnp.int32)
    full_index = jnp.arange(length, dtype=jnp.int32)
    pair_ids = jnp.arange(pair_count, dtype=jnp.int32)
    float_type = jnp.float32
    brain_type = jnp.bfloat16
    sums = (
        jnp.zeros((D, HEADS * HEAD_DIM), float_type),
        jnp.zeros((D, KV_HEADS * HEAD_DIM), float_type),
        jnp.zeros((D, KV_HEADS * HEAD_DIM), float_type),
        jnp.zeros((HEADS * HEAD_DIM, D), float_type),
        jnp.zeros((D, FF), float_type),
        jnp.zeros((D, FF), float_type),
        jnp.zeros((FF, D), float_type),
        jnp.zeros((D,), float_type),
        jnp.zeros((D,), float_type),
        jnp.zeros((HEAD_DIM,), float_type),
        jnp.zeros((HEAD_DIM,), float_type),
    )
    out_list = []
    grad_list = []
    for batch_index in range(MICRO):
        attn_fwd = (
            lax.all_gather(w_query, ("dp", "seq"), axis=0, tiled=True),
            lax.all_gather(w_key, ("dp", "seq"), axis=0, tiled=True),
            lax.all_gather(w_value, ("dp", "seq"), axis=0, tiled=True),
            lax.all_gather(w_output, ("dp", "seq"), axis=0, tiled=True),
            lax.all_gather(attn_gain, ("dp", "seq"), axis=0, tiled=True),
            lax.all_gather(query_gain, ("dp", "seq"), axis=0, tiled=True),
            lax.all_gather(key_gain, ("dp", "seq"), axis=0, tiled=True),
        )
        ffn_fwd = (
            lax.all_gather(w_gate, ("dp", "seq"), axis=0, tiled=True),
            lax.all_gather(w_up, ("dp", "seq"), axis=0, tiled=True),
            lax.all_gather(w_down, ("dp", "seq"), axis=0, tiled=True),
            lax.all_gather(ffn_gain, ("dp", "seq"), axis=0, tiled=True),
        )
        query_w, key_w, value_w, output_w, attn_g, query_g, key_g = attn_fwd
        gate_w, up_w, down_w, ffn_g = ffn_fwd
        labels, starts, path_base, ancestry = tree_tables(
            node_lengths[0, batch_index], parents[0, batch_index]
        )
        member_here, position = token_nodes(local_index, labels, starts, path_base)
        member_all, unused_position = token_nodes(full_index, labels, starts, path_base)
        keep_mask = visible(member_here, local_index, member_all, full_index, ancestry)
        cosine_table, sine_table = rope_tables(position, HEAD_DIM)
        rows_in = tokens[0, batch_index].astype(float_type)
        attn_g32 = attn_g.astype(float_type)
        query_g32 = query_g.astype(float_type)
        key_g32 = key_g.astype(float_type)
        normed_in = norm_rows(rows_in, attn_g32).astype(brain_type)
        query_heads = product(normed_in, query_w).reshape(rows_here, HEADS, HEAD_DIM)
        key_heads = product(normed_in, key_w).reshape(rows_here, KV_HEADS, HEAD_DIM)
        value_low = product(normed_in, value_w).astype(brain_type)
        query_rot = (
            rotate(norm_rows(query_heads, query_g32), cosine_table, sine_table)
            .astype(brain_type)
            .reshape(rows_here, HEADS * HEAD_DIM)
        )
        key_rot = (
            rotate(norm_rows(key_heads, key_g32), cosine_table, sine_table)
            .astype(brain_type)
            .reshape(rows_here, KV_HEADS * HEAD_DIM)
        )
        key_all, value_all = (
            lax.all_gather(key_rot, "seq", axis=0, tiled=True),
            lax.all_gather(value_low, "seq", axis=0, tiled=True),
        )

        def attend_pair(pair_id):
            query_pair = lax.dynamic_slice_in_dim(
                query_rot, pair_id * width_query, width_query, 1
            ).reshape(rows_here, 2, group_size, HEAD_DIM)
            key_pair = lax.dynamic_slice_in_dim(key_all, pair_id * width_key, width_key, 1).reshape(
                length, 2, HEAD_DIM
            )
            value_pair = lax.dynamic_slice_in_dim(
                value_all, pair_id * width_key, width_key, 1
            ).reshape(length, 2, HEAD_DIM)
            raw_score = jnp.einsum(
                "qhgd,khd->hgqk", query_pair, key_pair, preferred_element_type=jnp.float32
            )
            scores = jnp.where(keep_mask[None, None], raw_score * score_scale, NEGATIVE)
            row_top = jnp.max(scores, axis=-1, keepdims=True)
            weight = jnp.exp(scores - row_top)
            row_total = jnp.sum(weight, axis=-1, keepdims=True)
            soft_low = (weight / row_total).astype(jnp.bfloat16)
            mixed = jnp.einsum(
                "hgqk,khd->qhgd", soft_low, value_pair, preferred_element_type=jnp.float32
            )
            return (mixed, row_top + jnp.log(row_total))

        mixed_pairs, log_totals = lax.map(attend_pair, pair_ids)
        attended = (
            mixed_pairs.transpose(1, 0, 2, 3, 4)
            .reshape(rows_here, HEADS * HEAD_DIM)
            .astype(brain_type)
        )
        middle = rows_in + product(attended, output_w)
        ffn_g32 = ffn_g.astype(float_type)
        normed_mid = norm_rows(middle, ffn_g32).astype(brain_type)
        gate_lin = product(normed_mid, gate_w)
        up_lin = product(normed_mid, up_w)
        activated = (jax.nn.silu(gate_lin) * up_lin).astype(brain_type)
        out_list.append((middle + product(activated, down_w)).astype(brain_type))
        attn_back = (
            lax.all_gather(w_query, ("dp", "seq"), axis=0, tiled=True),
            lax.all_gather(w_key, ("dp", "seq"), axis=0, tiled=True),
            lax.all_gather(w_value, ("dp", "seq"), axis=0, tiled=True),
            lax.all_gather(w_output, ("dp", "seq"), axis=0, tiled=True),
            lax.all_gather(attn_gain, ("dp", "seq"), axis=0, tiled=True),
            lax.all_gather(query_gain, ("dp", "seq"), axis=0, tiled=True),
            lax.all_gather(key_gain, ("dp", "seq"), axis=0, tiled=True),
        )
        ffn_back = (
            lax.all_gather(w_gate, ("dp", "seq"), axis=0, tiled=True),
            lax.all_gather(w_up, ("dp", "seq"), axis=0, tiled=True),
            lax.all_gather(w_down, ("dp", "seq"), axis=0, tiled=True),
            lax.all_gather(ffn_gain, ("dp", "seq"), axis=0, tiled=True),
        )
        key_back, value_back = (
            lax.all_gather(key_rot, "seq", axis=0, tiled=True),
            lax.all_gather(value_low, "seq", axis=0, tiled=True),
        )
        query_wb, key_wb, value_wb, output_wb, attn_gb, query_gb, key_gb = attn_back
        gate_wb, up_wb, down_wb, ffn_gb = ffn_back
        cot_rows = cotangent[0, batch_index]
        grad_down = across(activated, cot_rows)
        d_activated = against(cot_rows, down_wb)
        sigma_gate = jax.nn.sigmoid(gate_lin)
        d_gate = (d_activated * up_lin * sigma_gate * (1.0 + gate_lin * (1.0 - sigma_gate))).astype(
            brain_type
        )
        d_up = (d_activated * gate_lin * sigma_gate).astype(brain_type)
        grad_gate = across(normed_mid, d_gate)
        grad_up = across(normed_mid, d_up)
        d_normed_mid = against(d_gate, gate_wb) + against(d_up, up_wb)
        unused_mid, pull_ffn = jax.vjp(norm_rows, middle, ffn_gb.astype(float_type))
        d_mid_norm, grad_ffn_gain = pull_ffn(d_normed_mid)
        d_middle = cot_rows.astype(float_type) + d_mid_norm
        d_middle_low = d_middle.astype(brain_type)
        grad_output = across(attended, d_middle_low)
        d_attended = against(d_middle_low, output_wb).astype(brain_type)

        def back_pair(pair_id):
            query_pair = lax.dynamic_slice_in_dim(
                query_rot, pair_id * width_query, width_query, 1
            ).reshape(rows_here, 2, group_size, HEAD_DIM)
            grad_pair = lax.dynamic_slice_in_dim(
                d_attended, pair_id * width_query, width_query, 1
            ).reshape(rows_here, 2, group_size, HEAD_DIM)
            key_pair = lax.dynamic_slice_in_dim(
                key_back, pair_id * width_key, width_key, 1
            ).reshape(length, 2, HEAD_DIM)
            value_pair = lax.dynamic_slice_in_dim(
                value_back, pair_id * width_key, width_key, 1
            ).reshape(length, 2, HEAD_DIM)
            raw_score = jnp.einsum(
                "qhgd,khd->hgqk", query_pair, key_pair, preferred_element_type=jnp.float32
            )
            scores = jnp.where(keep_mask[None, None], raw_score * score_scale, NEGATIVE)
            soft_prob = jnp.exp(scores - log_totals[pair_id])
            soft_low = soft_prob.astype(jnp.bfloat16)
            d_prob = jnp.einsum(
                "qhgd,khd->hgqk", grad_pair, value_pair, preferred_element_type=jnp.float32
            )
            d_score = soft_prob * (d_prob - jnp.sum(soft_prob * d_prob, axis=-1, keepdims=True))
            d_raw = (d_score * score_scale).astype(jnp.bfloat16)
            d_query = jnp.einsum(
                "hgqk,khd->qhgd", d_raw, key_pair, preferred_element_type=jnp.float32
            )
            d_key = jnp.einsum(
                "hgqk,qhgd->khd", d_raw, query_pair, preferred_element_type=jnp.float32
            )
            d_value = jnp.einsum(
                "hgqk,qhgd->khd", soft_low, grad_pair, preferred_element_type=jnp.float32
            )
            return (
                d_query,
                jnp.concatenate(
                    [d_key.reshape(length, width_key), d_value.reshape(length, width_key)], axis=1
                ),
            )

        d_query_pairs, kv_terms = lax.map(back_pair, pair_ids)
        kv_share = lax.psum_scatter(
            kv_terms.astype(jnp.bfloat16), "seq", scatter_dimension=1, tiled=True
        ).astype(jnp.float32)
        d_key_rot = (
            kv_share[:, :, :width_key]
            .reshape(pair_count, rows_here, 2, HEAD_DIM)
            .transpose(1, 0, 2, 3)
            .reshape(rows_here, KV_HEADS, HEAD_DIM)
        )
        d_value_low = (
            kv_share[:, :, width_key:]
            .transpose(1, 0, 2)
            .reshape(rows_here, KV_HEADS * HEAD_DIM)
            .astype(brain_type)
        )
        d_query_rot = d_query_pairs.transpose(1, 0, 2, 3, 4).reshape(rows_here, HEADS, HEAD_DIM)

        def turn_rows(heads_in, gain_in):
            return rotate(norm_rows(heads_in, gain_in), cosine_table, sine_table)

        unused_query, pull_query = jax.vjp(turn_rows, query_heads, query_gb.astype(float_type))
        d_query_heads, grad_query_gain = pull_query(d_query_rot)
        unused_key, pull_key = jax.vjp(turn_rows, key_heads, key_gb.astype(float_type))
        d_key_heads, grad_key_gain = pull_key(d_key_rot)
        d_query_low = d_query_heads.reshape(rows_here, HEADS * HEAD_DIM).astype(brain_type)
        d_key_low = d_key_heads.reshape(rows_here, KV_HEADS * HEAD_DIM).astype(brain_type)
        grad_query = across(normed_in, d_query_low)
        grad_key = across(normed_in, d_key_low)
        grad_value = across(normed_in, d_value_low)
        d_normed_in = (
            against(d_query_low, query_wb)
            + against(d_key_low, key_wb)
            + against(d_value_low, value_wb)
        )
        unused_in, pull_attn = jax.vjp(norm_rows, rows_in, attn_gb.astype(float_type))
        d_in_norm, grad_attn_gain = pull_attn(d_normed_in)
        grad_list.append(d_middle + d_in_norm)
        fresh = (
            grad_query,
            grad_key,
            grad_value,
            grad_output,
            grad_gate,
            grad_up,
            grad_down,
            grad_attn_gain,
            grad_ffn_gain,
            grad_query_gain,
            grad_key_gain,
        )
        sums = tuple((old + new for old, new in zip(sums, fresh)))
    attn_parts = (
        lax.psum_scatter(sums[0], ("dp", "seq"), scatter_dimension=0, tiled=True),
        lax.psum_scatter(sums[1], ("dp", "seq"), scatter_dimension=0, tiled=True),
        lax.psum_scatter(sums[2], ("dp", "seq"), scatter_dimension=0, tiled=True),
        lax.psum_scatter(sums[3], ("dp", "seq"), scatter_dimension=0, tiled=True),
        lax.psum_scatter(sums[7], ("dp", "seq"), scatter_dimension=0, tiled=True),
        lax.psum_scatter(sums[9], ("dp", "seq"), scatter_dimension=0, tiled=True),
        lax.psum_scatter(sums[10], ("dp", "seq"), scatter_dimension=0, tiled=True),
    )
    ffn_parts = (
        lax.psum_scatter(sums[4], ("dp", "seq"), scatter_dimension=0, tiled=True),
        lax.psum_scatter(sums[5], ("dp", "seq"), scatter_dimension=0, tiled=True),
        lax.psum_scatter(sums[6], ("dp", "seq"), scatter_dimension=0, tiled=True),
        lax.psum_scatter(sums[8], ("dp", "seq"), scatter_dimension=0, tiled=True),
    )
    outputs = jnp.stack(out_list)[None]
    input_grad = jnp.stack(grad_list)[None]
    return (
        outputs,
        input_grad,
        attn_parts[0],
        attn_parts[1],
        attn_parts[2],
        attn_parts[3],
        ffn_parts[0],
        ffn_parts[1],
        ffn_parts[2],
        attn_parts[4],
        ffn_parts[3],
        attn_parts[5],
        attn_parts[6],
    )


MESH = pl.DeviceIdType.MESH
NDP = 4
NSEQ = 8
BLOCKED = -65536.0
QB = 256
BLOCKS = (3, 2, 1, 0)
SOFT = HEAD_DIM ** (-0.5) * 1.4426950408889634

A0, A1, B, C0, C1, E0, E1, E2 = range(0, 80, 10)
R_A0, R_A1, R_B, R_C0, R_C1, R_E0, R_E1, R_E2 = range(80, 160, 10)
(
    ATTEND, MIX_MID, MIX_END, NORM_MID, NORM_END, LIFT, D_ACT, SINK, TURN_MID, TURN_END, LOW_MID,
    LOW_END, OUT_START, OUT_MID, OUT_END, ATTEND_BACK, IN_START, IN_MID, IN_END, PROJECT,
    GRAD_WIDE, GRAD_ATTN, TABLES, NORM_IN, COTANGENT,
) = range(200, 450, 10)
(
    START, TOKENS, SMALL_DP, SMALL_SEQ, A_IN, C_OUT, C_IN, TREE_START, COT_START, TREE_MID,
    COT_MID, COT_END, TREE_END, NODE, GAINS, GRAD_DOWN, GRAD_OUT, PACK_DP, PACK_SEQ, PACK_END,
    LAND_A, LAND_C, GIVE_OUT, GIVE_IN, DRAIN,
) = range(600, 625, 1)
ORDER = (
    START, B, E0, E1, E2, B + 1, A_IN, A0, A1, B + 2, A0 + 1, A1 + 1, C_OUT, B + 3, A0 + 2, SMALL_DP, A1 + 2,
    B + 4, TOKENS, A1 + 3, A0 + 3, SMALL_SEQ, TREE_START, C_IN, A1 + 4, A0 + 4, NODE, TABLES, B + 5,
    TABLES + 1, A1 + 5, A0 + 5, C1, A1 + 6, A0 + 6, GAINS, TREE_MID, B + 6, COTANGENT + 1, C0, COTANGENT,
    C1 + 1, A1 + 7, TREE_END, NORM_IN, NORM_IN + 1, A0 + 7, PROJECT, PROJECT + 1, PROJECT + 2, E2 + 1,
    PROJECT + 3, C0 + 1, B + 7, ATTEND + 3, COT_START, E1 + 1, E0 + 1, C1 + 2, ATTEND + 2, C0 + 2, E0 + 2,
    E2 + 2, MIX_MID + 3, MIX_MID + 2, C1 + 3, ATTEND + 1, C0 + 3, ATTEND, E1 + 2, C1 + 4, MIX_MID, C0 + 4,
    E0 + 3, MIX_END + 3, C1 + 5, C0 + 5, E1 + 3, COT_MID, E2 + 3, MIX_END, MIX_MID + 1, C1 + 6, C0 + 6,
    E0 + 4, NORM_MID + 3, MIX_END + 2, E1 + 4, COT_END, NORM_MID, C1 + 7, NORM_END + 3, E2 + 4, NORM_END,
    MIX_END + 1, C0 + 7, LIFT + 3, E0 + 5, E2 + 5, NORM_MID + 2, E1 + 5, LIFT, NORM_MID + 1, NORM_END + 2,
    LIFT + 2, NORM_END + 1, E0 + 6, E1 + 6, E2 + 6, LIFT + 1, GRAD_DOWN, R_E0, R_E2, E0 + 7, R_E1, E1 + 7,
    E2 + 7, D_ACT + 3, SINK + 3, R_E0 + 1, D_ACT + 2, R_E2 + 1, D_ACT, D_ACT + 1, TURN_MID + 3, R_E1 + 1,
    R_E0 + 2, R_E2 + 2, GRAD_WIDE + 1, R_C1, GRAD_WIDE, R_C0, TURN_END + 3, SINK + 2, R_E0 + 3, R_C1 + 1,
    R_E2 + 3, TURN_MID + 2, SINK, R_C0 + 1, OUT_START + 3, LOW_MID + 3, TURN_MID, R_C1 + 2, SINK + 1,
    R_E1 + 2, R_E0 + 4, TURN_END + 2, LOW_END + 3, TURN_MID + 1, R_C0 + 2, R_E2 + 4, TURN_END, R_C1 + 3,
    ATTEND_BACK + 3, R_E1 + 3, R_C0 + 3, LOW_MID + 2, TURN_END + 1, R_E2 + 5, R_E0 + 5, R_C1 + 4, LOW_END + 2,
    ATTEND_BACK + 2, R_C0 + 4, R_E1 + 4, LOW_MID + 1, LOW_MID, IN_START + 3, IN_START + 2, LOW_END, R_C1 + 5,
    LOW_END + 1, GRAD_OUT, R_B, R_C0 + 5, R_E0 + 6, R_E2 + 6, R_E1 + 5, ATTEND_BACK + 1, IN_START + 1,
    R_C1 + 6, R_B + 1, ATTEND_BACK, R_C0 + 6, IN_START, GRAD_ATTN + 1, R_A1, R_B + 2, GRAD_ATTN, R_A0,
    IN_MID + 1, IN_MID + 2, R_A1 + 1, OUT_START, R_B + 3, R_E0 + 7, IN_MID + 3, R_A0 + 1, IN_MID, OUT_MID,
    R_A1 + 2, OUT_MID + 3, R_B + 4, R_A0 + 2, R_C0 + 7, R_A1 + 3, R_B + 5, IN_END + 2, R_A0 + 3, IN_END,
    R_A1 + 4, IN_END + 3, R_B + 6, R_A0 + 4, IN_END + 1, GIVE_IN, PACK_DP, OUT_START + 2, R_A1 + 5,
    OUT_MID + 2, R_A0 + 5, OUT_START + 1, OUT_MID + 1, OUT_END, R_C1 + 7, PACK_SEQ, R_E2 + 7, OUT_END + 2,
    R_E1 + 6, OUT_END + 3, R_B + 7, R_A1 + 6, R_A0 + 6, OUT_END + 1, GIVE_OUT, PACK_END, R_E1 + 7, R_A1 + 7,
    LAND_C, R_A0 + 7, LAND_A, DRAIN,
)


def seq_at(position):
    half = position // 4
    z = position + half * (7 - 2 * position)
    return 2 * z + half


def tree_seat(d, m):
    x, c = d // 2, d % 2
    return 2 * (2 * m + c) + (m + c + x) % 2


def greet_near(d, s, up, down):
    barrier = pltpu.get_barrier_semaphore()
    near = [((d + i) % NDP, s) for i in range(1, NDP)] + [(d, up), (d, down)]
    for other in near:
        pl.semaphore_signal(barrier, inc=1, device_id=other, device_id_type=MESH)
    pl.semaphore_wait(barrier, len(near))


def remote(src, dst, sems, at, d, s):
    send, recv = sems
    return pltpu.make_async_remote_copy(
        src_ref=src,
        dst_ref=dst,
        send_sem=send.at[at],
        recv_sem=recv.at[at],
        device_id=(d, s),
        device_id_type=MESH,
    )


class Sum:
    def __init__(self, part, near, sent, got, sems, n, spot):
        self.part, self.near, self.sent, self.got = part, near, sent, got
        self.sems, self.n = sems, n
        d, self.s = spot
        x, c = d // 2, d % 2
        self.d, self.sib, self.far = d, 2 * x + 1 - c, 2 * (1 - x) + c
        self.far_sib = 2 * (1 - x) + 1 - c

    def copies(self, b):
        rows = pl.ds(2 * b, 2)
        return (
            remote(self.part.at[rows, self.far_sib], self.near.at[0, rows], self.sems, (self.n, 0, b), self.sib, self.s),
            remote(self.part.at[rows, self.sib], self.near.at[1, rows], self.sems, (self.n, 1, b), self.sib, self.s),
            remote(self.sent.at[rows], self.got.at[rows], self.sems, (self.n, 2, b), self.far, self.s),
        )

    def start(self, b):
        first, second, _ = self.copies(b)
        first.start()
        second.start()

    def mid(self, b):
        first, _, across_x = self.copies(b)
        first.wait_recv()

        def join(i, carry):
            self.sent[i] = (
                self.part[i, self.far].astype(jnp.float32) + self.near[0, i].astype(jnp.float32)
            ).astype(jnp.bfloat16)
            return carry

        lax.fori_loop(2 * b, 2 * b + 2, join, 0)
        across_x.start()

    def end(self, b, finish):
        first, second, across_x = self.copies(b)
        second.wait_recv()
        across_x.wait_recv()

        def close(i, carry):
            rows = self.part[i, self.d].astype(jnp.float32) + self.near[1, i].astype(jnp.float32)
            finish(i, rows + self.got[i].astype(jnp.float32))
            return carry

        lax.fori_loop(2 * b, 2 * b + 2, close, 0)
        first.wait_send()
        second.wait_send()
        across_x.wait_send()


class Spread:
    def __init__(self, out, sems, at, spot):
        self.out, self.sems, self.place = out, sems, at
        d, self.s = spot
        x, c = d // 2, d % 2
        self.d, self.sib, self.far = d, 2 * x + 1 - c, 2 * (1 - x) + c
        self.far_sib = 2 * (1 - x) + 1 - c

    def copy(self, rows, owner, way, to):
        block = self.out.at[rows, owner]
        return remote(block, block, self.sems, self.place(way, rows), to, self.s)

    def start(self, rows):
        self.copy(rows, self.d, 0, self.far).start()
        self.copy(rows, self.d, 1, self.sib).start()

    def mid(self, rows):
        self.copy(rows, self.far, 0, self.far).wait_recv()
        self.copy(rows, self.far, 2, self.sib).start()

    def end(self, rows):
        self.copy(rows, self.sib, 1, self.sib).wait_recv()
        self.copy(rows, self.far_sib, 2, self.sib).wait_recv()

    def sent(self, rows):
        self.copy(rows, self.d, 0, self.far).wait_send()
        self.copy(rows, self.d, 1, self.sib).wait_send()
        self.copy(rows, self.far, 2, self.sib).wait_send()


def layer_kernel(
    nodes,
    tok, cot, lengths, parents, gain_a, gain_f, gain_q, gain_k, inv_freq, wq, wk, wv, wo, wg, wu, wd,
    out_rows, grad_rows, res_a, res_c, g_output, g_down, pack_out,
    raw_lengths, raw_parents, raw_a, raw_f, raw_q, raw_k, smalls, wa, wb, wc, we, gc, ge, hop_a, hop_b, hop_c, hop_e,
    tree, tree_cot, normed_in, normed_mid, d_low, tree_own,
    lin, heads, value, hidden, member, cosine, sine, att, d_att,
    part, part_out, near, sent, got, near_o, sent_o, got_o,
    middle, d_middle, act, both, d_key, d_value, outs, grad_low,
    fin_a, fin_c, attn_g, ffn_g, head_g, pack_dp, pack_seq, pack_sum,
    loc, s_small, r_small, s_col, r_col, s_tok, r_tok, s_ag, r_ag, s_rs, r_rs,
    s_sum, r_sum, s_tree, r_tree, s_spread, r_spread, s_back, r_back, s_fin, r_fin, s_pack, r_pack,
):
    f32, bf = jnp.float32, jnp.bfloat16
    d = lax.axis_index("dp")
    s = lax.axis_index("seq")
    z, y = s // 2, s % 2
    p = z + y * (7 - 2 * z)
    spot = (d, s)
    seat = [seq_at((p + i) % NSEQ) for i in range(NSEQ)]
    up, down = seat[1], seat[7]
    ag_sems, rs_sems = (s_ag, r_ag), (s_rs, r_rs)
    small_sems, col_sems, tok_sems = (s_small, r_small), (s_col, r_col), (s_tok, r_tok)

    def aligned(v, n):
        return pl.multiple_of(v, n)

    def chunk(n, way, j):
        if n in (0, 1, 3, 4):
            return pl.ds(aligned((2 * way + (n + (n > 2)) % 2) * 256 + j * 32, 32), 32)
        if n == 2:
            return pl.ds(aligned(j * 64 + way * 32, 32), 32)
        return pl.ds(aligned(j * 96 + way * 48 + (n - 5) * 16, 16), 16)

    weight = {0: wa, 1: wa, 2: wb, 3: wc, 4: wc, 5: we, 6: we, 7: we}
    grads = {0: wa, 1: wa, 2: wb, 3: gc, 4: gc, 5: ge, 6: ge, 7: ge}
    hops = {0: hop_a.at[0], 1: hop_a.at[1], 2: hop_b, 3: hop_c.at[0], 4: hop_c.at[1]}
    hops.update({5 + i: hop_e.at[i] for i in range(3)})

    def owner_at(way, k):
        return seq_at((p + NSEQ - k) % NSEQ) if way == 0 else seq_at((p + k) % NSEQ)

    def gather(n, k):
        for way, peer in enumerate((up, down)):
            block = weight[n].at[chunk(n, way, owner_at(way, k))]
            if not (isinstance(k, int) and k == 0):
                remote(block, block, ag_sems, (n, way, k - 1), d, peer).wait_recv()
            remote(block, block, ag_sems, (n, way, k), d, peer).start()

    def gather_end(n):
        for way, peer in enumerate((up, down)):
            block = weight[n].at[chunk(n, way, owner_at(way, 7))]
            remote(block, block, ag_sems, (n, way, 6), d, peer).wait_recv()

    def gather_sent(n):
        for way, peer in enumerate((up, down)):
            block = weight[n].at[chunk(n, way, s)]
            for k in range(7):
                remote(block, block, ag_sems, (n, way, k), d, peer).wait_send()

    def add_rows(into, other):
        def one(i, carry):
            at = pl.ds(aligned(i * 16, 16), 16)
            into[at] = (into[at].astype(f32) + other[at].astype(f32)).astype(bf)
            return carry

        lax.fori_loop(0, into.shape[0] // 16, one, 0)

    def reduce_(n, k):
        for way, peer in enumerate((up, down)):
            rows = chunk(n, way, seat[(7 - k) % NSEQ] if way == 0 else seat[(1 + k) % NSEQ])
            mine = grads[n].at[rows]
            if k == 0:
                src = mine
            else:
                src = hops[n].at[way, k - 1]
                remote(src, src, rs_sems, (n, way, k - 1), d, peer).wait_recv()
                add_rows(src, mine)
            remote(src, hops[n].at[way, k], rs_sems, (n, way, k), d, peer).start()

    def reduce_end(n, take):
        for way, peer in enumerate((up, down)):
            src = hops[n].at[way, 6]
            remote(src, src, rs_sems, (n, way, 6), d, peer).wait_recv()
            take(way, src[...].astype(f32) + grads[n][chunk(n, way, s)].astype(f32))

    def reduce_sent(n):
        for way, peer in enumerate((up, down)):
            for k in range(7):
                src = hops[n].at[way, k]
                remote(src, src, rs_sems, (n, way, k), d, peer).wait_send()

    ops = {}
    tree_slot, tree_core = z // 2, z % 2
    tree_owner = 2 * ((y + tree_slot + tree_core) % 2) + tree_core
    pending = []
    held = {}

    def stage(name):
        def keep(run):
            ops[name] = run
            return run

        return keep

    def launch(cp):
        cp.start()
        pending.append(cp)

    raws = [
        pltpu.make_async_copy(src, dst, loc.at[9 + n])
        for n, (src, dst) in enumerate(
            (
                (lengths, raw_lengths), (parents, raw_parents),
                (gain_a, raw_a), (gain_f, raw_f), (gain_q, raw_q), (gain_k, raw_k),
            )
        )
    ]
    pieces = (
        (wq, wa, 512, 0), (wk, wa, 256, 512), (wv, wa, 256, 768), (wg, wc, 768, 0), (wu, wc, 768, 768)
    )
    col_rows = lambda q: pl.ds(aligned(q * 256 + s * 32, 32), 32)

    def column_copy(n):
        src, dst, width, at = pieces[n]
        return pltpu.make_async_copy(
            src.at[:, pl.ds(aligned(d * width, 128), width)],
            dst.at[col_rows(d), pl.ds(at, width)],
            loc.at[2 + n],
        )

    def columns(n):
        src, dst, width, at = pieces[n]
        for i in range(1, NDP):
            q = (d + i) % NDP
            launch(
                remote(
                    src.at[:, pl.ds(aligned(q * width, 128), width)],
                    dst.at[col_rows(d), pl.ds(at, width)],
                    col_sems, (n, i), q, s,
                )
            )
        column_copy(n).start()

    def columns_in(n):
        _, dst, width, at = pieces[n]
        column_copy(n).wait()
        for i in range(1, NDP):
            place = dst.at[col_rows((d + NDP - i) % NDP), pl.ds(at, width)]
            remote(place, place, col_sems, (n, i), d, s).wait_recv()

    def row_copy(n, m, i):
        src, dst = ((tok, tree), (cot, tree_cot))[n]
        q = (d + i) % NDP
        return pltpu.make_async_remote_copy(
            src_ref=src.at[m, pl.ds(aligned(q * 32, 32), 32)],
            dst_ref=dst.at[s, q],
            send_sem=s_tok.at[n, m, i],
            recv_sem=r_tok.at[n],
            device_id=(q, tree_seat(d, m)),
            device_id_type=MESH,
        )

    def rows_out(n, half):
        src, dst = ((tok, tree), (cot, tree_cot))[n]
        for m in range(MICRO):
            if half == 0:
                target = tree_seat(d, m)

                @pl.when(target == s)
                def _():
                    piece = src.at[m, pl.ds(aligned(d * 32, 32), 32)]
                    pltpu.make_async_copy(piece, dst.at[s, d], r_tok.at[n]).start()

                @pl.when(target != s)
                def _():
                    row_copy(n, m, 0).start()

                row_copy(n, m, 1).start()
            else:
                row_copy(n, m, 2).start()
                row_copy(n, m, 3).start()

    def rows_in(dst, n):
        everything = dst.at[:, d]
        pltpu.make_async_copy(everything, everything, r_tok.at[n]).wait()

    fill_b = pltpu.make_async_copy(wo, wb.at[pl.ds(aligned(s * 64, 64), 64)], loc.at[7])
    fill_e = pltpu.make_async_copy(wd, we.at[pl.ds(aligned(s * 96, 16), 96)], loc.at[15])

    @stage(START)
    def _():
        for cp in raws:
            cp.start()
        greet_near(d, s, up, down)
        fill_b.start()
        fill_e.start()
        for n in range(3):
            columns(n)

    @stage(TOKENS)
    def _():
        rows_out(0, 0)
        rows_out(0, 1)

    for i in range(2):
        stage(COTANGENT + i)(functools.partial(rows_out, 1, i))


    @stage(SMALL_DP)
    def _():
        for cp in raws:
            cp.wait()
        for row, ref in enumerate((raw_a, raw_f, raw_q, raw_k)):
            count = ref.shape[0]
            line = ref[...].astype(f32).reshape(1, count)
            smalls[d, s, row : row + 1, :] = jnp.concatenate([line] * (128 // count), axis=1)
        smalls[d, s, 4:8, :] = jnp.zeros((4, 128), f32)
        smalls[d, s, 4:6, 0:nodes] = raw_lengths[0].astype(f32)
        smalls[d, s, 6:8, 0:nodes] = raw_parents[0].astype(f32)
        for i in range(1, NDP):
            launch(remote(smalls.at[d, s], smalls.at[d, s], small_sems, i, (d + i) % NDP, s))

    @stage(SMALL_SEQ)
    def _():
        for i in range(1, NDP):
            place = smalls.at[(d + NDP - i) % NDP, s]
            remote(place, place, small_sems, i, d, s).wait_recv()
        for i in range(1, NSEQ):
            launch(remote(smalls.at[:, s], smalls.at[:, s], small_sems, NDP + i, d, (s + i) % NSEQ))

    @stage(A_IN)
    def _():
        for n in range(3):
            columns_in(n)

    @stage(C_OUT)
    def _():
        for n in range(3, 5):
            columns(n)

    @stage(C_IN)
    def _():
        for n in range(3, 5):
            columns_in(n)

    streams = ((A0, 0), (A1, 1), (B, 2), (C0, 3), (C1, 4), (E0, 5), (E1, 6), (E2, 7))

    def ring_first(n):
        if n == 2:
            fill_b.wait()
        if n == 5:
            fill_e.wait()
        gather(n, 0)

    for label, n in streams:
        stage(label)(functools.partial(ring_first, n))
        stage(label + 7)(functools.partial(gather_end, n))
        for k in range(1, 7):
            stage(label + k)(functools.partial(gather, n, k))
        for k in range(7):
            stage(R_A0 + label + k)(functools.partial(reduce_, n, k))

    everything = pl.ds(0, NSEQ)
    spread_tree = Spread(tree, (s_tree, r_tree), lambda way, rows: (0, way), spot)
    spread_cot = Spread(tree_cot, (s_tree, r_tree), lambda way, rows: (1, way), spot)

    @stage(TREE_START)
    def _():
        rows_in(tree, 0)
        spread_tree.start(everything)

    @stage(COT_START)
    def _():
        rows_in(tree_cot, 1)
        spread_cot.start(everything)

    stage(TREE_MID)(lambda: spread_tree.mid(everything))
    stage(COT_MID)(lambda: spread_cot.mid(everything))
    stage(COT_END)(lambda: spread_cot.end(everything))
    own_rows = pltpu.make_async_copy(tree.at[:, d], tree_own, loc.at[8])

    @stage(TREE_END)
    def _():
        spread_tree.end(everything)
        own_rows.start()

    @stage(NODE)
    def _():
        ir = lax.broadcasted_iota(jnp.int32, (128, 128), 0)
        ic = lax.broadcasted_iota(jnp.int32, (128, 128), 1)
        block = smalls.at[tree_owner, s]
        length_row = block[pl.ds(4 + tree_slot, 1), :]
        parent_row = block[pl.ds(6 + tree_slot, 1), :]
        length_col = jnp.sum(jnp.where(ir == ic, length_row, 0.0), axis=1, keepdims=True)
        over = (parent_row == ir.astype(f32)) & (ic > 0) & (ic < nodes)
        above = jnp.where(over | (ir == ic), 1.0, 0.0)
        for _ in range(4):
            low = above.astype(bf)
            above = jnp.minimum(product(low, low), 1.0)
        start_row = jnp.sum(jnp.where(ir < ic, length_col, 0.0), axis=0, keepdims=True)
        base_row = jnp.sum(
            jnp.where((above > 0.5) & (ir != ic), length_col, 0.0), axis=0, keepdims=True
        )
        shut = jnp.where(above > 0.5, 0.0, BLOCKED).astype(bf)
        held["node"] = (start_row, start_row + length_row, base_row - start_row, shut)

    def tables(i, carry):
        start_row, end_row, offset_row, shut = held["node"]
        rows = pl.ds(aligned(i * QB, QB), QB)
        index = (lax.broadcasted_iota(jnp.int32, (QB, 128), 0) + i * QB).astype(f32)
        inside = (index >= start_row) & (index < end_row)
        position = index[:, :1] + jnp.sum(
            jnp.where(inside, offset_row, 0.0), axis=1, keepdims=True
        )
        hot = jnp.where(inside, 1.0, 0.0).astype(bf)
        member[rows] = hot
        hidden[rows] = against(hot, shut).astype(bf)
        angle = position * inv_freq[...]
        cosine[rows] = jnp.cos(angle)
        lane = lax.broadcasted_iota(jnp.int32, (QB, 128), 1)
        wave = jnp.sin(angle)
        sine[rows] = jnp.where(lane < 64, -wave, wave)
        return carry

    stage(TABLES + 0)(lambda: lax.fori_loop(0, 2, tables, 0))
    stage(TABLES + 1)(lambda: lax.fori_loop(2, 4, tables, 0))

    @stage(GAINS)
    def _():
        for i in range(1, NSEQ):
            place = smalls.at[:, (s + NSEQ - i) % NSEQ]
            remote(place, place, small_sems, NDP + i, d, s).wait_recv()
        lane = lax.broadcasted_iota(jnp.int32, (1, 128), 1)
        for row, dst in ((0, attn_g), (1, ffn_g)):
            for j in range(8):
                parts = [
                    smalls[(4 * j + i) // 8, (4 * j + i) % 8, row : row + 1, :] for i in range(4)
                ]
                dst[:, 128 * j : 128 * (j + 1)] = jnp.where(
                    lane < 64,
                    jnp.where(lane < 32, parts[0], parts[1]),
                    jnp.where(lane < 96, parts[2], parts[3]),
                )
        for row in (2, 3):
            joined = jnp.zeros((1, 128), f32)
            for i in range(32):
                joined = jnp.where(lane // 4 == i, smalls[i // 8, i % 8, row : row + 1, :], joined)
            head_g[row - 2 : row - 1, :] = joined
        pack_dp[d] = jnp.zeros((24, 128), f32)

    def norm_in(i, carry):
        rows = tree[i].reshape(128, D).astype(f32)
        scale = lax.rsqrt(jnp.mean(rows * rows, axis=-1, keepdims=True) + EPSILON)
        normed_in[pl.ds(aligned(i * 128, 128), 128)] = (rows * scale * attn_g[...]).astype(bf)
        return carry

    stage(NORM_IN + 0)(lambda: lax.fori_loop(0, 4, norm_in, 0))
    stage(NORM_IN + 1)(lambda: lax.fori_loop(4, 8, norm_in, 0))

    def unit_of(v):
        scale = lax.rsqrt(jnp.mean(v * v, axis=-1, keepdims=True) + EPSILON)
        return v * scale, scale

    def turn(v, gain, cos, sin):
        unit, _ = unit_of(v)
        lifted = unit * gain
        return lifted * cos + pltpu.roll(lifted, 64, 1) * sin

    def turn_back(dr, v, gain, cos, sin):
        d_lift = dr * cos + pltpu.roll(dr * sin, 64, 1)
        unit, scale = unit_of(v)
        d_unit = d_lift * gain
        return (
            scale * (d_unit - unit * jnp.mean(unit * d_unit, axis=-1, keepdims=True)),
            jnp.sum(d_lift * unit, axis=0, keepdims=True),
        )

    def project(i):
        rows = pl.ds(i * QB, QB)
        cos, sin = cosine[rows], sine[rows]

        def one(j, carry):
            lanes = pl.ds(aligned(j * 256, 256), 256)
            pair = product(normed_in[rows], wa[:, lanes])
            lin[rows, lanes] = pair
            gain = head_g[pl.ds(j // 2, 1), :]
            for i2 in range(2):
                turned = turn(pair[:, 128 * i2 : 128 * (i2 + 1)], gain, cos, sin)
                heads[2 * j + i2, rows] = turned.astype(bf)
            return carry

        lax.fori_loop(0, 3, one, 0)
        value[rows] = product(normed_in[rows], wa[:, 768:]).astype(bf)

    for i in range(4):
        stage(PROJECT + i)(functools.partial(project, i))

    def span(b):
        return pl.ds(b * QB, QB), (b + 1) * QB

    def weights_of(b, h, n):
        here = pl.ds(b * QB, QB)
        q = jnp.concatenate([heads[h, here], hidden[here]], axis=1)
        k = jnp.concatenate([heads[4 + h // 2, pl.ds(0, n)], member[pl.ds(0, n)]], axis=1)
        score = against(q, k) * SOFT
        row = lax.broadcasted_iota(jnp.int32, (QB, QB), 0)
        col = lax.broadcasted_iota(jnp.int32, (QB, QB), 1)
        diag = jnp.where(col <= row, score[:, n - QB :], NEGATIVE)
        score = diag if b == 0 else jnp.concatenate([score[:, : n - QB], diag], axis=1)
        grown = jnp.exp2(score)
        return grown, 1.0 / jnp.sum(grown, axis=-1, keepdims=True)

    def head_lanes(h):
        return pl.ds(aligned(h * HEAD_DIM, HEAD_DIM), HEAD_DIM)

    sum_sems, spread_sems = (s_sum, r_sum), (s_spread, r_spread)
    mixed_sum = Sum(part, near, sent, got, sum_sems, 0, spot)
    mid_sum = Sum(part, near, sent, got, sum_sems, 1, spot)
    out_sum = Sum(part_out, near_o, sent_o, got_o, sum_sems, 2, spot)
    in_sum = Sum(part, near, sent, got, sum_sems, 3, spot)
    pair_of = {b: pl.ds(2 * b, 2) for b in BLOCKS}
    spread_mid = Spread(normed_mid, spread_sems, lambda way, rows: (0, way, rows.start // 2), spot)
    spread_low = Spread(d_low, spread_sems, lambda way, rows: (1, way, rows.start // 2), spot)

    def attend(b):
        here, n = span(b)
        if b == BLOCKS[0]:
            own_rows.wait()

        def one(h, carry):
            grown, inverse = weights_of(b, h, n)
            mixed = product(grown.astype(bf), value[pl.ds(0, n), head_lanes(h // 2)])
            att[here, head_lanes(h)] = (mixed * inverse).astype(bf)
            return carry

        lax.fori_loop(0, HEADS // NDP, one, 0)
        rows = product(att[here], wb[...]).astype(bf)
        part[pair_of[b]] = rows.reshape(2, NDP, 32, D)
        mixed_sum.start(b)

    def to_middle(i, rows):
        rows = rows + tree_own[i].astype(f32)
        middle[i] = rows
        scale = lax.rsqrt(jnp.mean(rows * rows, axis=-1, keepdims=True) + EPSILON)
        normed_mid[i, d] = (rows * scale * ffn_g[...]).astype(bf)

    def close_mixed(b):
        mixed_sum.end(b, to_middle)
        spread_mid.start(pair_of[b])

    def lift(b):
        here = pl.ds(b * QB, QB)
        rows = normed_mid[pair_of[b]].reshape(QB, D)

        def one(t, carry):
            left = pl.ds(aligned(t * 256, 256), 256)
            right = pl.ds(aligned(768 + t * 256, 256), 256)
            gate = product(rows, wc[:, left])
            wide = product(rows, wc[:, right])
            sigma = 1.0 / (1.0 + jnp.exp(-gate))
            silu = gate * sigma
            act[here, left] = (silu * wide).astype(bf)
            both[here, left] = (wide * sigma * (1.0 + gate * (1.0 - sigma))).astype(bf)
            both[here, right] = silu.astype(bf)
            return carry

        lax.fori_loop(0, 3, one, 0)

    @stage(GRAD_DOWN)
    def _():
        def one(i, carry):
            cols = pl.ds(aligned(i * 256, 256), 256)
            ge[cols] = across(act[:, cols], tree_cot[...].reshape(NSEQ * 128, D)).astype(bf)
            return carry

        lax.fori_loop(0, 3, one, 0)

    def d_activate(b):
        here = pl.ds(b * QB, QB)
        cots = tree_cot[pair_of[b]].reshape(QB, D)

        def one(t, carry):
            left = pl.ds(aligned(t * 256, 256), 256)
            right = pl.ds(aligned(768 + t * 256, 256), 256)
            d_act = against(cots, we[left])
            both[here, left] = (d_act * both[here, left].astype(f32)).astype(bf)
            both[here, right] = (d_act * both[here, right].astype(f32)).astype(bf)
            return carry

        lax.fori_loop(0, 3, one, 0)

    def sink(b):
        here = pl.ds(b * QB, QB)
        part[pair_of[b]] = against(both[here], wc[...]).astype(bf).reshape(2, NDP, 32, D)
        mid_sum.start(b)

    def settle(b):
        here = pl.ds(b * QB, QB)
        part_out[pair_of[b]] = product(act[here], we[...]).astype(bf).reshape(2, NDP, 32, D)
        out_sum.start(b)

    def to_turn(i, rows):
        unit, scale = unit_of(middle[i])
        lifted = ffn_g[...] * rows
        term = jnp.sum(rows * unit, axis=0, keepdims=True)
        for j in range(8):
            pack_dp[d, 8 + j : 9 + j] += term[:, 128 * j : 128 * (j + 1)]
        d_mid = tree_cot[i, d].astype(f32) + scale * (
            lifted - unit * jnp.mean(unit * lifted, axis=-1, keepdims=True)
        )
        d_middle[i] = d_mid
        d_low[i, d] = d_mid.astype(bf)

    def close_mid(b):
        mid_sum.end(b, to_turn)
        spread_low.start(pair_of[b])

    def to_outs(i, rows):
        outs[i] = (middle[i] + rows).astype(bf)

    back_owner, back_slot = tree_owner, tree_slot
    back = ((outs, out_rows), (grad_low, grad_rows))

    def give_copy(n, j):
        src, dst = back[n]
        return pltpu.make_async_remote_copy(
            src_ref=src.at[j],
            dst_ref=dst.at[back_slot, pl.ds(aligned(d * 32, 32), 32)],
            send_sem=s_back.at[n, j],
            recv_sem=r_back.at[n],
            device_id=(back_owner, j),
            device_id_type=MESH,
        )

    def give(n):
        src, dst = back[n]

        def one(j, carry):
            same = (back_owner == d) & (s == j)

            @pl.when(same)
            def _():
                place = dst.at[back_slot, pl.ds(aligned(d * 32, 32), 32)]
                pltpu.make_async_copy(src.at[j], place, r_back.at[n]).start()

            @pl.when(jnp.logical_not(same))
            def _():
                give_copy(n, j).start()

            return carry

        lax.fori_loop(0, NSEQ, one, 0)

    def close_out(b):
        out_sum.end(b, to_outs)

    def grad_wide(sub):
        for i in (sub, 2 + sub):
            cols = pl.ds(i * 256, 256)

            rows = normed_mid[:, :, :, cols].reshape(NSEQ * 128, 256)
            gc[cols] = across(rows, both[...]).astype(bf)

    d_lin = tree

    def close_low(b):
        spread_low.end(pair_of[b])
        here = pl.ds(b * QB, QB)
        rows = d_low[pair_of[b]].reshape(QB, D)
        d_att[here] = against(rows, wb[...]).astype(bf)

    def attend_back(b):
        here, n = span(b)
        keys = pl.ds(0, n)
        if b == BLOCKS[0]:
            spread_tree.sent(everything)
            d_key[...] = jnp.zeros_like(d_key)
            d_value[...] = jnp.zeros_like(d_value)

        def one(h, carry):
            kv = h // 2
            grown, inverse = weights_of(b, h, n)
            d_out = d_att[here, head_lanes(h)]
            wide_out = d_out.astype(f32)
            d_prob = against(d_out, value[keys, head_lanes(kv)])
            delta = jnp.sum(wide_out * att[here, head_lanes(h)].astype(f32), axis=-1, keepdims=True)
            d_raw = (grown * (d_prob - delta)).astype(bf)
            factor = inverse * HEAD_DIM ** (-0.5)
            d_rot = product(d_raw, heads[4 + kv, keys]) * factor
            d_key[kv, keys] += across(d_raw, (heads[h, here].astype(f32) * factor).astype(bf))
            d_value[kv, keys] += across(grown.astype(bf), (wide_out * inverse).astype(bf))
            back, d_gain = turn_back(
                d_rot, lin[here, head_lanes(h)], head_g[0:1, :], cosine[here], sine[here]
            )
            pack_dp[d, 16:17] += d_gain
            d_lin[pair_of[b], :, :, head_lanes(h)] = back.astype(bf).reshape(2, NDP, 32, HEAD_DIM)
            return carry

        lax.fori_loop(0, HEADS // NDP, one, 0)
        for kv in range(KV_HEADS // NDP):
            at = 512 + 128 * kv
            back, d_gain = turn_back(
                d_key[kv, here], lin[here, pl.ds(at, 128)], head_g[1:2, :], cosine[here], sine[here]
            )
            pack_dp[d, 17:18] += d_gain
            d_lin[pair_of[b], :, :, pl.ds(at, 128)] = back.astype(bf).reshape(2, NDP, 32, 128)
            d_lin[pair_of[b], :, :, pl.ds(at + 256, 128)] = (
                d_value[kv, here].astype(bf).reshape(2, NDP, 32, 128)
            )

    def sink_in(b):
        rows = against(d_lin[pair_of[b]].reshape(QB, 1024), wa[...])
        part[pair_of[b]] = rows.astype(bf).reshape(2, NDP, 32, D)
        in_sum.start(b)

    @stage(GRAD_OUT)
    def _():
        gather_sent(2)
        for i in range(2):
            cols = pl.ds(256 * i, 256)
            wb[cols] = across(att[:, cols], d_low[...].reshape(NSEQ * 128, D)).astype(bf)

    def grad_attn(sub):
        gather_sent(sub)
        for i in (sub, 2 + sub):
            cols = pl.ds(i * 256, 256)

            wa[cols] = across(normed_in[:, cols], d_lin[...].reshape(NSEQ * 128, 1024)).astype(bf)

    def to_grad(i, rows):
        unit, scale = unit_of(tree_own[i].astype(f32))
        lifted = attn_g[...] * rows
        term = jnp.sum(rows * unit, axis=0, keepdims=True)
        for j in range(8):
            pack_dp[d, j : j + 1] += term[:, 128 * j : 128 * (j + 1)]
        grad = d_middle[i] + scale * (
            lifted - unit * jnp.mean(unit * lifted, axis=-1, keepdims=True)
        )
        grad_low[i] = grad.astype(bf)

    def close_in(b):
        in_sum.end(b, to_grad)

    per_block = (
        (ATTEND, attend), (MIX_MID, mixed_sum.mid), (MIX_END, close_mixed),
        (NORM_MID, lambda b: spread_mid.mid(pair_of[b])), (NORM_END, lambda b: spread_mid.end(pair_of[b])),
        (LIFT, lift), (D_ACT, d_activate), (SINK, sink), (TURN_MID, mid_sum.mid), (TURN_END, close_mid),
        (LOW_MID, lambda b: spread_low.mid(pair_of[b])), (LOW_END, close_low),
        (OUT_START, settle), (OUT_MID, out_sum.mid), (OUT_END, close_out),
        (ATTEND_BACK, attend_back), (IN_START, sink_in), (IN_MID, in_sum.mid), (IN_END, close_in),
    )
    for label, run in per_block:
        for b in BLOCKS:
            stage(label + b)(functools.partial(run, b))
    for sub in range(2):
        stage(GRAD_WIDE + sub)(functools.partial(grad_wide, sub))
        stage(GRAD_ATTN + sub)(functools.partial(grad_attn, sub))

    stage(GIVE_OUT)(functools.partial(give, 0))
    stage(GIVE_IN)(functools.partial(give, 1))

    pack_sems, fin_sems = (s_pack, r_pack), (s_fin, r_fin)

    @stage(PACK_DP)
    def _():
        for i in range(1, NDP):
            launch(remote(pack_dp.at[d], pack_dp.at[d], pack_sems, i, (d + i) % NDP, s))

    @stage(PACK_SEQ)
    def _():
        for i in range(1, NDP):
            place = pack_dp.at[(d + NDP - i) % NDP]
            remote(place, place, pack_sems, i, d, s).wait_recv()
        pack_seq[s] = (pack_dp[0] + pack_dp[1]) + (pack_dp[2] + pack_dp[3])
        for i in range(1, NSEQ):
            launch(remote(pack_seq.at[s], pack_seq.at[s], pack_sems, NDP + i, d, (s + i) % NSEQ))

    @stage(PACK_END)
    def _():
        for i in range(1, NSEQ):
            place = pack_seq.at[(s + NSEQ - i) % NSEQ]
            remote(place, place, pack_sems, NDP + i, d, s).wait_recv()
        total = pack_seq[0]
        for j in range(1, NSEQ):
            total = total + pack_seq[j]
        pack_sum[...] = total
        at = d * NSEQ + s
        for n, (row, count) in enumerate(
            ((at // 4, 32), (8 + at // 4, 32), (16, 4), (17, 4))
        ):
            line = pack_sum[pl.ds(row, 1), :]
            shift = (128 - (at * count) % 128) % 128
            pack_out[n : n + 1, :] = pltpu.roll(line, shift, 1)

    def close_cols(n, fin, landed, which):
        sub = (n + (n > 2)) % 2

        def take(way, total):
            fin[2 * way + sub] = total.astype(bf)

        reduce_end(n, take)
        for way in range(2):
            q = 2 * way + sub

            @pl.when(q == d)
            def _():
                pltpu.make_async_copy(fin.at[q], landed.at[d], loc.at[which]).start()

            @pl.when(q != d)
            def _():
                remote(fin.at[q], landed.at[d], fin_sems, (which, d), q, s).start()

    for label, n, fin, landed, which in (
        (A0, 0, fin_a, res_a, 0), (A1, 1, fin_a, res_a, 0),
        (C0, 3, fin_c, res_c, 1), (C1, 4, fin_c, res_c, 1),
    ):
        stage(R_A0 + label + 7)(functools.partial(close_cols, n, fin, landed, which))

    def land(landed, which):
        for i in range(1, NDP):
            q = (d + i) % NDP
            remote(landed.at[q], landed.at[q], fin_sems, (which, q), q, s).wait_recv()
        pltpu.make_async_copy(landed.at[d], landed.at[d], loc.at[which]).wait()

    stage(LAND_A)(lambda: land(res_a, 0))
    stage(LAND_C)(lambda: land(res_c, 1))

    def take_rows(dst, rows, at, way, total):
        dst[pl.ds(rows * way + at, total.shape[0])] = total

    stage(R_B + 7)(lambda: reduce_end(2, functools.partial(take_rows, g_output, 32, 0)))
    for label, n in streams[5:]:
        take = functools.partial(take_rows, g_down, 48, (n - 5) * 16)
        stage(R_A0 + label + 7)(functools.partial(reduce_end, n, take))

    @stage(DRAIN)
    def _():
        for n, (src, dst) in enumerate(back):
            pltpu.make_async_copy(dst, dst, r_back.at[n]).wait()

            def one(j, carry):
                @pl.when(jnp.logical_not((back_owner == d) & (s == j)))
                def _():
                    give_copy(n, j).wait_send()

                return carry

            lax.fori_loop(0, NSEQ, one, 0)
        for n, (fin, landed) in enumerate(((fin_a, res_a), (fin_c, res_c))):
            for i in range(1, NDP):
                q = (d + i) % NDP
                remote(fin.at[q], landed.at[d], fin_sems, (n, d), q, s).wait_send()
        for n in range(3, 8):
            gather_sent(n)
        for n in range(8):
            reduce_sent(n)
        spread_cot.sent(everything)
        for b in BLOCKS:
            spread_mid.sent(pair_of[b])
            spread_low.sent(pair_of[b])
        for cp in pending:
            cp.wait_send()
        for n in range(2):
            for m in range(MICRO):

                @pl.when(tree_seat(d, m) != s)
                def _():
                    row_copy(n, m, 0).wait_send()

                for i in range(1, NDP):
                    row_copy(n, m, i).wait_send()

    for name in ORDER:
        ops[name]()


def finish_kernel(
    out_rows, grad_rows, res_a, res_c, g_output, g_down, pack,
    outs, grads, g_query, g_key, g_value, out_output, g_gate, g_up, out_down, g_attn, g_ffn, g_qg, g_kg,
    low_rows, low_a, low_c, small, *rest,
):
    *held, sems = rest
    coming = [
        pltpu.make_async_copy(src, dst, sems.at[n])
        for n, (src, dst) in enumerate(
            (
                (grad_rows, low_rows), (res_a, low_a), (res_c, low_c), (pack, small),
                (out_rows, held[0]), (g_output, held[1]), (g_down, held[2]),
            )
        )
    ]
    for cp in coming:
        cp.start()
    leaving = [
        pltpu.make_async_copy(src, dst, sems.at[7 + n])
        for n, (src, dst) in enumerate(zip(held, (outs, out_output, out_down)))
    ]
    for came, goes in zip(coming[4:], leaving):
        came.wait()
        goes.start()
    coming[0].wait()
    grads[...] = low_rows[...].astype(jnp.float32)
    for cp in coming[1:4]:
        cp.wait()
    for src, cuts in (
        (low_a, ((0, 512, g_query), (512, 256, g_key), (768, 256, g_value))),
        (low_c, ((0, 768, g_gate), (768, 768, g_up))),
    ):
        for q in range(NDP):
            for at, width, dst in cuts:
                dst[:, width * q : width * (q + 1)] = src[q, :, at : at + width].astype(jnp.float32)
    for n, dst in enumerate((g_attn, g_ffn, g_qg, g_kg)):
        count = dst.shape[0]
        dst[...] = small[n : n + 1, 0:count].reshape(count)
    for cp in leaving:
        cp.wait()


def tree_shards(
    tokens, cotangent, node_lengths, parents, w_query, w_key, w_value, w_output, w_gate, w_up, w_down,
    attn_gain, ffn_gain, query_gain, key_gain,
):
    f32, bf = jnp.float32, jnp.bfloat16
    nodes = node_lengths.shape[2]
    half = np.arange(HEAD_DIM // 2, dtype=np.float64)
    inv_freq = THETA ** (-(half * (2.0 / HEAD_DIM)))
    inv_freq = np.concatenate([inv_freq, inv_freq])[None].astype(np.float32)
    shape, vmem, dma = jax.ShapeDtypeStruct, pltpu.VMEM, pltpu.SemaphoreType.DMA
    anywhere = pl.BlockSpec(memory_space=pl.ANY)
    here = pl.BlockSpec(memory_space=pltpu.VMEM)
    rows = NSEQ * 128
    quarter = (NSEQ, 32, D)
    twice = lambda *dims: [dma(dims), dma(dims)]
    results = pl.pallas_call(
        functools.partial(layer_kernel, nodes),
        out_shape=(
            shape((MICRO, 128, D), bf),
            shape((MICRO, 128, D), bf),
            shape((NDP, 32, 1024), bf),
            shape((NDP, 32, 1536), bf),
            shape((64, D), f32),
            shape((96, D), f32),
            shape((8, 128), f32),
        ),
        in_specs=[anywhere] * 8 + [here] + [anywhere] * 7,
        out_specs=[anywhere] * 4 + [here] * 3,
        scratch_shapes=[
            vmem(node_lengths.shape, jnp.int32), vmem(parents.shape, jnp.int32),
            *[vmem(gain.shape, bf) for gain in (attn_gain, ffn_gain, query_gain, key_gain)],
            vmem((NDP, NSEQ, 8, 128), f32),
            vmem((D, 1024), bf), vmem((512, D), bf), vmem((D, 1536), bf), vmem((768, D), bf),
            vmem((D, 1536), bf), vmem((768, D), bf),
            vmem((2, 2, 7, 32, 1024), bf), vmem((2, 7, 32, D), bf),
            vmem((2, 2, 7, 32, 1536), bf), vmem((3, 2, 7, 16, D), bf),
            vmem((NSEQ, NDP, 32, D), bf), vmem((NSEQ, NDP, 32, D), bf), vmem((rows, D), bf),
            vmem((NSEQ, NDP, 32, D), bf), vmem((NSEQ, NDP, 32, D), bf), vmem(quarter, bf),
            vmem((rows, 768), f32), vmem((6, rows, 128), bf),
            vmem((rows, 256), bf), vmem((rows, 128), bf), vmem((rows, 128), bf),
            vmem((rows, 128), f32), vmem((rows, 128), f32), vmem((rows, 512), bf), vmem((rows, 512), bf),
            vmem((NSEQ, NDP, 32, D), bf), vmem((NSEQ, NDP, 32, D), bf),
            vmem((2,) + quarter, bf), vmem(quarter, bf), vmem(quarter, bf),
            vmem((2,) + quarter, bf), vmem(quarter, bf), vmem(quarter, bf),
            vmem(quarter, f32), vmem(quarter, f32), vmem((rows, 768), bf), vmem((rows, 1536), bf),
            vmem((2, rows, 128), f32), vmem((2, rows, 128), f32), vmem(quarter, bf), vmem(quarter, bf),
            vmem((NDP, 32, 1024), bf), vmem((NDP, 32, 1536), bf),
            vmem((1, D), f32), vmem((1, D), f32), vmem((8, 128), f32),
            vmem((NDP, 24, 128), f32), vmem((NSEQ, 24, 128), f32), vmem((24, 128), f32),
            dma((16,)),
            *twice(12), *twice(5, NDP), dma((2, MICRO, NDP)), dma((2,)),
            *twice(8, 2, 7), *twice(8, 2, 7),
            *twice(4, 3, 4), *twice(2, 3), *twice(2, 3, 4),
            dma((2, NSEQ)), dma((2,)), *twice(2, NDP), *twice(12),
        ],
        compiler_params=pltpu.CompilerParams(
            collective_id=1, has_side_effects=True, vmem_limit_bytes=61 << 20
        ),
        name="layer",
    )(
        tokens[0], cotangent[0], node_lengths, parents, attn_gain, ffn_gain, query_gain, key_gain, inv_freq,
        w_query, w_key, w_value, w_output, w_gate, w_up, w_down,
    )
    full = lambda *dims: shape(dims, f32)
    finished = pl.pallas_call(
        finish_kernel,
        out_shape=(
            shape((MICRO, 128, D), bf), full(MICRO, 128, D),
            full(32, 2048), full(32, 1024), full(32, 1024), full(64, D),
            full(32, FF), full(32, FF), full(96, D),
            full(32), full(32), full(4), full(4),
        ),
        in_specs=[pl.BlockSpec(memory_space=pltpu.HBM)] * 7,
        out_specs=[anywhere, here, here, here, here, anywhere, here, here, anywhere] + [here] * 4,
        scratch_shapes=[
            vmem((MICRO, 128, D), bf), vmem((NDP, 32, 1024), bf), vmem((NDP, 32, 1536), bf),
            vmem((8, 128), f32), vmem((MICRO, 128, D), bf), vmem((64, D), f32), vmem((96, D), f32),
            dma((10,)),
        ],
        compiler_params=pltpu.CompilerParams(vmem_limit_bytes=61 << 20),
        name="finish",
    )(*results)
    return (finished[0][None], finished[1][None]) + tuple(finished[2:])


def solution(mesh):
    ring = mesh.shape["dp"] == NDP and mesh.shape["seq"] == NSEQ
    return jax.shard_map(
        tree_shards if ring else general_shards,
        mesh=mesh,
        in_specs=(
            P("dp", None, "seq", None),
            P("dp", None, "seq", None),
            P("dp", None, None),
            P("dp", None, None),
            P(("dp", "seq"), None),
            P(("dp", "seq"), None),
            P(("dp", "seq"), None),
            P(("dp", "seq"), None),
            P(("dp", "seq"), None),
            P(("dp", "seq"), None),
            P(("dp", "seq"), None),
            P(("dp", "seq")),
            P(("dp", "seq")),
            P(("dp", "seq")),
            P(("dp", "seq")),
        ),
        out_specs=(
            P("dp", None, "seq", None),
            P("dp", None, "seq", None),
            P(("dp", "seq"), None),
            P(("dp", "seq"), None),
            P(("dp", "seq"), None),
            P(("dp", "seq"), None),
            P(("dp", "seq"), None),
            P(("dp", "seq"), None),
            P(("dp", "seq"), None),
            P(("dp", "seq")),
            P(("dp", "seq")),
            P(("dp", "seq")),
            P(("dp", "seq")),
        ),
        check_vma=False,
    )
```

```python
import functools

import jax
import jax.numpy as jnp
import numpy as np
from jax import lax
from jax.experimental import pallas as pl
from jax.experimental.pallas import tpu as pltpu
from jax.sharding import PartitionSpec as P

D = 1024
HEADS = 16
KV_HEADS = 8
HEAD_DIM = 128
FF = 3072
MICRO = 2


EPSILON = 1e-06
THETA = 1000000.0
NEGATIVE = -1e30
PRECISE = lax.Precision.HIGHEST


def norm_rows(values, row_gain):
    return (
        values * lax.rsqrt(jnp.mean(values * values, axis=-1, keepdims=True) + EPSILON) * row_gain
    )


def rope_tables(position, head_dim):
    half_dim = head_dim // 2
    inv_freq = THETA ** (-(jnp.arange(half_dim, dtype=jnp.float32) * (2.0 / head_dim)))
    angles = position.astype(jnp.float32)[:, None] * inv_freq[None, :]
    cosine_table = jnp.cos(angles)
    sine_table = jnp.sin(angles)
    return (
        jnp.concatenate([cosine_table, cosine_table], axis=1),
        jnp.concatenate([sine_table, sine_table], axis=1),
    )


def rotate(values, cosine_table, sine_table):
    half_dim = values.shape[-1] // 2
    turned = jnp.concatenate([-values[..., half_dim:], values[..., :half_dim]], axis=-1)
    return values * cosine_table[:, None, :] + turned * sine_table[:, None, :]


def tree_tables(lengths, parent_row):
    node_count = lengths.shape[0]
    labels = jnp.arange(node_count, dtype=jnp.int32)
    parent_hot = ((parent_row[:, None] == labels[None, :]) & (labels[:, None] > 0)).astype(
        jnp.int32
    )

    def extend(depth_step, state_pair):
        reached, covered = state_pair
        reached = jnp.sum(reached[:, :, None] * parent_hot[None, :, :], axis=1)
        return (reached, covered + reached)

    reached, covered = lax.fori_loop(0, node_count, extend, (parent_hot, parent_hot))
    ancestry = (covered > 0).astype(jnp.float32)
    starts = jnp.cumsum(lengths) - lengths
    path_base = jnp.sum(jnp.where(covered > 0, lengths[None, :], 0), axis=1)
    return (labels, starts, path_base, ancestry)


def token_nodes(token_index, labels, starts, path_base):
    node_id = jnp.sum((token_index[:, None] >= starts[None, 1:]).astype(jnp.int32), axis=1)
    member = node_id[:, None] == labels[None, :]
    offset = jnp.sum(jnp.where(member, (path_base - starts)[None, :], 0), axis=1)
    return (member.astype(jnp.float32), token_index + offset)


def visible(query_member, query_index, key_member, key_index, ancestry):
    numbers = (((1,), (1,)), ((), ()))
    lifted = jnp.dot(query_member, ancestry, precision=PRECISE)
    above = lax.dot_general(lifted, key_member, numbers, precision=PRECISE)
    same_node = lax.dot_general(query_member, key_member, numbers, precision=PRECISE)
    return (above > 0.5) | (same_node > 0.5) & (key_index[None, :] <= query_index[:, None])


def product(left_side, right_side):
    return jnp.dot(left_side, right_side, preferred_element_type=jnp.float32)


def against(left_side, right_side):
    return lax.dot_general(
        left_side, right_side, (((1,), (1,)), ((), ())), preferred_element_type=jnp.float32
    )


def across(left_side, right_side):
    return lax.dot_general(
        left_side, right_side, (((0,), (0,)), ((), ())), preferred_element_type=jnp.float32
    )


def general_shards(
    tokens,
    cotangent,
    node_lengths,
    parents,
    w_query,
    w_key,
    w_value,
    w_output,
    w_gate,
    w_up,
    w_down,
    attn_gain,
    ffn_gain,
    query_gain,
    key_gain,
):
    rows_here = tokens.shape[2]
    length = lax.axis_size("seq") * rows_here
    group_size = HEADS // KV_HEADS
    pair_count = KV_HEADS // 2
    width_query = 2 * group_size * HEAD_DIM
    width_key = 2 * HEAD_DIM
    score_scale = HEAD_DIM ** (-0.5)
    local_index = lax.axis_index("seq") * rows_here + jnp.arange(rows_here, dtype=jnp.int32)
    full_index = jnp.arange(length, dtype=jnp.int32)
    pair_ids = jnp.arange(pair_count, dtype=jnp.int32)
    float_type = jnp.float32
    brain_type = jnp.bfloat16
    sums = (
        jnp.zeros((D, HEADS * HEAD_DIM), float_type),
        jnp.zeros((D, KV_HEADS * HEAD_DIM), float_type),
        jnp.zeros((D, KV_HEADS * HEAD_DIM), float_type),
        jnp.zeros((HEADS * HEAD_DIM, D), float_type),
        jnp.zeros((D, FF), float_type),
        jnp.zeros((D, FF), float_type),
        jnp.zeros((FF, D), float_type),
        jnp.zeros((D,), float_type),
        jnp.zeros((D,), float_type),
        jnp.zeros((HEAD_DIM,), float_type),
        jnp.zeros((HEAD_DIM,), float_type),
    )
    out_list = []
    grad_list = []
    for batch_index in range(MICRO):
        attn_fwd = (
            lax.all_gather(w_query, ("dp", "seq"), axis=0, tiled=True),
            lax.all_gather(w_key, ("dp", "seq"), axis=0, tiled=True),
            lax.all_gather(w_value, ("dp", "seq"), axis=0, tiled=True),
            lax.all_gather(w_output, ("dp", "seq"), axis=0, tiled=True),
            lax.all_gather(attn_gain, ("dp", "seq"), axis=0, tiled=True),
            lax.all_gather(query_gain, ("dp", "seq"), axis=0, tiled=True),
            lax.all_gather(key_gain, ("dp", "seq"), axis=0, tiled=True),
        )
        ffn_fwd = (
            lax.all_gather(w_gate, ("dp", "seq"), axis=0, tiled=True),
            lax.all_gather(w_up, ("dp", "seq"), axis=0, tiled=True),
            lax.all_gather(w_down, ("dp", "seq"), axis=0, tiled=True),
            lax.all_gather(ffn_gain, ("dp", "seq"), axis=0, tiled=True),
        )
        query_w, key_w, value_w, output_w, attn_g, query_g, key_g = attn_fwd
        gate_w, up_w, down_w, ffn_g = ffn_fwd
        labels, starts, path_base, ancestry = tree_tables(
            node_lengths[0, batch_index], parents[0, batch_index]
        )
        member_here, position = token_nodes(local_index, labels, starts, path_base)
        member_all, unused_position = token_nodes(full_index, labels, starts, path_base)
        keep_mask = visible(member_here, local_index, member_all, full_index, ancestry)
        cosine_table, sine_table = rope_tables(position, HEAD_DIM)
        rows_in = tokens[0, batch_index].astype(float_type)
        attn_g32 = attn_g.astype(float_type)
        query_g32 = query_g.astype(float_type)
        key_g32 = key_g.astype(float_type)
        normed_in = norm_rows(rows_in, attn_g32).astype(brain_type)
        query_heads = product(normed_in, query_w).reshape(rows_here, HEADS, HEAD_DIM)
        key_heads = product(normed_in, key_w).reshape(rows_here, KV_HEADS, HEAD_DIM)
        value_low = product(normed_in, value_w).astype(brain_type)
        query_rot = (
            rotate(norm_rows(query_heads, query_g32), cosine_table, sine_table)
            .astype(brain_type)
            .reshape(rows_here, HEADS * HEAD_DIM)
        )
        key_rot = (
            rotate(norm_rows(key_heads, key_g32), cosine_table, sine_table)
            .astype(brain_type)
            .reshape(rows_here, KV_HEADS * HEAD_DIM)
        )
        key_all, value_all = (
            lax.all_gather(key_rot, "seq", axis=0, tiled=True),
            lax.all_gather(value_low, "seq", axis=0, tiled=True),
        )

        def attend_pair(pair_id):
            query_pair = lax.dynamic_slice_in_dim(
                query_rot, pair_id * width_query, width_query, 1
            ).reshape(rows_here, 2, group_size, HEAD_DIM)
            key_pair = lax.dynamic_slice_in_dim(key_all, pair_id * width_key, width_key, 1).reshape(
                length, 2, HEAD_DIM
            )
            value_pair = lax.dynamic_slice_in_dim(
                value_all, pair_id * width_key, width_key, 1
            ).reshape(length, 2, HEAD_DIM)
            raw_score = jnp.einsum(
                "qhgd,khd->hgqk", query_pair, key_pair, preferred_element_type=jnp.float32
            )
            scores = jnp.where(keep_mask[None, None], raw_score * score_scale, NEGATIVE)
            row_top = jnp.max(scores, axis=-1, keepdims=True)
            weight = jnp.exp(scores - row_top)
            row_total = jnp.sum(weight, axis=-1, keepdims=True)
            soft_low = (weight / row_total).astype(jnp.bfloat16)
            mixed = jnp.einsum(
                "hgqk,khd->qhgd", soft_low, value_pair, preferred_element_type=jnp.float32
            )
            return (mixed, row_top + jnp.log(row_total))

        mixed_pairs, log_totals = lax.map(attend_pair, pair_ids)
        attended = (
            mixed_pairs.transpose(1, 0, 2, 3, 4)
            .reshape(rows_here, HEADS * HEAD_DIM)
            .astype(brain_type)
        )
        middle = rows_in + product(attended, output_w)
        ffn_g32 = ffn_g.astype(float_type)
        normed_mid = norm_rows(middle, ffn_g32).astype(brain_type)
        gate_lin = product(normed_mid, gate_w)
        up_lin = product(normed_mid, up_w)
        activated = (jax.nn.silu(gate_lin) * up_lin).astype(brain_type)
        out_list.append((middle + product(activated, down_w)).astype(brain_type))
        attn_back = (
            lax.all_gather(w_query, ("dp", "seq"), axis=0, tiled=True),
            lax.all_gather(w_key, ("dp", "seq"), axis=0, tiled=True),
            lax.all_gather(w_value, ("dp", "seq"), axis=0, tiled=True),
            lax.all_gather(w_output, ("dp", "seq"), axis=0, tiled=True),
            lax.all_gather(attn_gain, ("dp", "seq"), axis=0, tiled=True),
            lax.all_gather(query_gain, ("dp", "seq"), axis=0, tiled=True),
            lax.all_gather(key_gain, ("dp", "seq"), axis=0, tiled=True),
        )
        ffn_back = (
            lax.all_gather(w_gate, ("dp", "seq"), axis=0, tiled=True),
            lax.all_gather(w_up, ("dp", "seq"), axis=0, tiled=True),
            lax.all_gather(w_down, ("dp", "seq"), axis=0, tiled=True),
            lax.all_gather(ffn_gain, ("dp", "seq"), axis=0, tiled=True),
        )
        key_back, value_back = (
            lax.all_gather(key_rot, "seq", axis=0, tiled=True),
            lax.all_gather(value_low, "seq", axis=0, tiled=True),
        )
        query_wb, key_wb, value_wb, output_wb, attn_gb, query_gb, key_gb = attn_back
        gate_wb, up_wb, down_wb, ffn_gb = ffn_back
        cot_rows = cotangent[0, batch_index]
        grad_down = across(activated, cot_rows)
        d_activated = against(cot_rows, down_wb)
        sigma_gate = jax.nn.sigmoid(gate_lin)
        d_gate = (d_activated * up_lin * sigma_gate * (1.0 + gate_lin * (1.0 - sigma_gate))).astype(
            brain_type
        )
        d_up = (d_activated * gate_lin * sigma_gate).astype(brain_type)
        grad_gate = across(normed_mid, d_gate)
        grad_up = across(normed_mid, d_up)
        d_normed_mid = against(d_gate, gate_wb) + against(d_up, up_wb)
        unused_mid, pull_ffn = jax.vjp(norm_rows, middle, ffn_gb.astype(float_type))
        d_mid_norm, grad_ffn_gain = pull_ffn(d_normed_mid)
        d_middle = cot_rows.astype(float_type) + d_mid_norm
        d_middle_low = d_middle.astype(brain_type)
        grad_output = across(attended, d_middle_low)
        d_attended = against(d_middle_low, output_wb).astype(brain_type)

        def back_pair(pair_id):
            query_pair = lax.dynamic_slice_in_dim(
                query_rot, pair_id * width_query, width_query, 1
            ).reshape(rows_here, 2, group_size, HEAD_DIM)
            grad_pair = lax.dynamic_slice_in_dim(
                d_attended, pair_id * width_query, width_query, 1
            ).reshape(rows_here, 2, group_size, HEAD_DIM)
            key_pair = lax.dynamic_slice_in_dim(
                key_back, pair_id * width_key, width_key, 1
            ).reshape(length, 2, HEAD_DIM)
            value_pair = lax.dynamic_slice_in_dim(
                value_back, pair_id * width_key, width_key, 1
            ).reshape(length, 2, HEAD_DIM)
            raw_score = jnp.einsum(
                "qhgd,khd->hgqk", query_pair, key_pair, preferred_element_type=jnp.float32
            )
            scores = jnp.where(keep_mask[None, None], raw_score * score_scale, NEGATIVE)
            soft_prob = jnp.exp(scores - log_totals[pair_id])
            soft_low = soft_prob.astype(jnp.bfloat16)
            d_prob = jnp.einsum(
                "qhgd,khd->hgqk", grad_pair, value_pair, preferred_element_type=jnp.float32
            )
            d_score = soft_prob * (d_prob - jnp.sum(soft_prob * d_prob, axis=-1, keepdims=True))
            d_raw = (d_score * score_scale).astype(jnp.bfloat16)
            d_query = jnp.einsum(
                "hgqk,khd->qhgd", d_raw, key_pair, preferred_element_type=jnp.float32
            )
            d_key = jnp.einsum(
                "hgqk,qhgd->khd", d_raw, query_pair, preferred_element_type=jnp.float32
            )
            d_value = jnp.einsum(
                "hgqk,qhgd->khd", soft_low, grad_pair, preferred_element_type=jnp.float32
            )
            return (
                d_query,
                jnp.concatenate(
                    [d_key.reshape(length, width_key), d_value.reshape(length, width_key)], axis=1
                ),
            )

        d_query_pairs, kv_terms = lax.map(back_pair, pair_ids)
        kv_share = lax.psum_scatter(
            kv_terms.astype(jnp.bfloat16), "seq", scatter_dimension=1, tiled=True
        ).astype(jnp.float32)
        d_key_rot = (
            kv_share[:, :, :width_key]
            .reshape(pair_count, rows_here, 2, HEAD_DIM)
            .transpose(1, 0, 2, 3)
            .reshape(rows_here, KV_HEADS, HEAD_DIM)
        )
        d_value_low = (
            kv_share[:, :, width_key:]
            .transpose(1, 0, 2)
            .reshape(rows_here, KV_HEADS * HEAD_DIM)
            .astype(brain_type)
        )
        d_query_rot = d_query_pairs.transpose(1, 0, 2, 3, 4).reshape(rows_here, HEADS, HEAD_DIM)

        def turn_rows(heads_in, gain_in):
            return rotate(norm_rows(heads_in, gain_in), cosine_table, sine_table)

        unused_query, pull_query = jax.vjp(turn_rows, query_heads, query_gb.astype(float_type))
        d_query_heads, grad_query_gain = pull_query(d_query_rot)
        unused_key, pull_key = jax.vjp(turn_rows, key_heads, key_gb.astype(float_type))
        d_key_heads, grad_key_gain = pull_key(d_key_rot)
        d_query_low = d_query_heads.reshape(rows_here, HEADS * HEAD_DIM).astype(brain_type)
        d_key_low = d_key_heads.reshape(rows_here, KV_HEADS * HEAD_DIM).astype(brain_type)
        grad_query = across(normed_in, d_query_low)
        grad_key = across(normed_in, d_key_low)
        grad_value = across(normed_in, d_value_low)
        d_normed_in = (
            against(d_query_low, query_wb)
            + against(d_key_low, key_wb)
            + against(d_value_low, value_wb)
        )
        unused_in, pull_attn = jax.vjp(norm_rows, rows_in, attn_gb.astype(float_type))
        d_in_norm, grad_attn_gain = pull_attn(d_normed_in)
        grad_list.append(d_middle + d_in_norm)
        fresh = (
            grad_query,
            grad_key,
            grad_value,
            grad_output,
            grad_gate,
            grad_up,
            grad_down,
            grad_attn_gain,
            grad_ffn_gain,
            grad_query_gain,
            grad_key_gain,
        )
        sums = tuple((old + new for old, new in zip(sums, fresh)))
    attn_parts = (
        lax.psum_scatter(sums[0], ("dp", "seq"), scatter_dimension=0, tiled=True),
        lax.psum_scatter(sums[1], ("dp", "seq"), scatter_dimension=0, tiled=True),
        lax.psum_scatter(sums[2], ("dp", "seq"), scatter_dimension=0, tiled=True),
        lax.psum_scatter(sums[3], ("dp", "seq"), scatter_dimension=0, tiled=True),
        lax.psum_scatter(sums[7], ("dp", "seq"), scatter_dimension=0, tiled=True),
        lax.psum_scatter(sums[9], ("dp", "seq"), scatter_dimension=0, tiled=True),
        lax.psum_scatter(sums[10], ("dp", "seq"), scatter_dimension=0, tiled=True),
    )
    ffn_parts = (
        lax.psum_scatter(sums[4], ("dp", "seq"), scatter_dimension=0, tiled=True),
        lax.psum_scatter(sums[5], ("dp", "seq"), scatter_dimension=0, tiled=True),
        lax.psum_scatter(sums[6], ("dp", "seq"), scatter_dimension=0, tiled=True),
        lax.psum_scatter(sums[8], ("dp", "seq"), scatter_dimension=0, tiled=True),
    )
    outputs = jnp.stack(out_list)[None]
    input_grad = jnp.stack(grad_list)[None]
    return (
        outputs,
        input_grad,
        attn_parts[0],
        attn_parts[1],
        attn_parts[2],
        attn_parts[3],
        ffn_parts[0],
        ffn_parts[1],
        ffn_parts[2],
        attn_parts[4],
        ffn_parts[3],
        attn_parts[5],
        attn_parts[6],
    )


MESH = pl.DeviceIdType.MESH
NDP = 4
NSEQ = 8
BLOCKED = -65536.0
QB = 256
BLOCKS = (3, 2, 1, 0)
SOFT = HEAD_DIM ** (-0.5) * 1.4426950408889634

A0, A1, B, C0, C1, E0, E1, E2 = range(0, 80, 10)
R_A0, R_A1, R_B, R_C0, R_C1, R_E0, R_E1, R_E2 = range(80, 160, 10)
(
    ATTEND, MIX_MID, MIX_END, NORM_MID, NORM_END, LIFT, D_ACT, SINK, TURN_MID, TURN_END, LOW_MID,
    LOW_END, OUT_START, OUT_MID, OUT_END, ATTEND_BACK, IN_START, IN_MID, IN_END, PROJECT,
    GRAD_WIDE, GRAD_ATTN, TABLES, NORM_IN, COTANGENT,
) = range(200, 450, 10)
(
    START, TOKENS, SMALL_DP, SMALL_SEQ, A_IN, C_OUT, C_IN, TREE_START, COT_START, TREE_MID,
    COT_MID, COT_END, TREE_END, NODE, GAINS, GRAD_DOWN, GRAD_OUT, PACK_DP, PACK_SEQ, PACK_END,
    LAND_A, LAND_C, GIVE_OUT, GIVE_IN, DRAIN,
) = range(600, 625, 1)
ORDER = (
    START, B, E0, E1, E2, B + 1, A_IN, A0, A1, B + 2, A0 + 1, A1 + 1, C_OUT, B + 3, A0 + 2, SMALL_DP, A1 + 2,
    B + 4, TOKENS, A1 + 3, A0 + 3, SMALL_SEQ, TREE_START, C_IN, A1 + 4, A0 + 4, NODE, TABLES, B + 5,
    TABLES + 1, A1 + 5, A0 + 5, C1, A1 + 6, A0 + 6, GAINS, TREE_MID, B + 6, COTANGENT + 1, C0, COTANGENT,
    C1 + 1, A1 + 7, TREE_END, NORM_IN, NORM_IN + 1, A0 + 7, PROJECT, PROJECT + 1, PROJECT + 2, E2 + 1,
    PROJECT + 3, C0 + 1, B + 7, ATTEND + 3, COT_START, E1 + 1, E0 + 1, C1 + 2, ATTEND + 2, C0 + 2, E0 + 2,
    E2 + 2, MIX_MID + 3, MIX_MID + 2, C1 + 3, ATTEND + 1, C0 + 3, ATTEND, E1 + 2, C1 + 4, MIX_MID, C0 + 4,
    E0 + 3, MIX_END + 3, C1 + 5, C0 + 5, E1 + 3, COT_MID, E2 + 3, MIX_END, MIX_MID + 1, C1 + 6, C0 + 6,
    E0 + 4, NORM_MID + 3, MIX_END + 2, E1 + 4, COT_END, NORM_MID, C1 + 7, NORM_END + 3, E2 + 4, NORM_END,
    MIX_END + 1, C0 + 7, LIFT + 3, E0 + 5, E2 + 5, NORM_MID + 2, E1 + 5, LIFT, NORM_MID + 1, NORM_END + 2,
    LIFT + 2, NORM_END + 1, E0 + 6, E1 + 6, E2 + 6, LIFT + 1, GRAD_DOWN, R_E0, R_E2, E0 + 7, R_E1, E1 + 7,
    E2 + 7, D_ACT + 3, SINK + 3, R_E0 + 1, D_ACT + 2, R_E2 + 1, D_ACT, D_ACT + 1, TURN_MID + 3, R_E1 + 1,
    R_E0 + 2, R_E2 + 2, GRAD_WIDE + 1, R_C1, GRAD_WIDE, R_C0, TURN_END + 3, SINK + 2, R_E0 + 3, R_C1 + 1,
    R_E2 + 3, TURN_MID + 2, SINK, R_C0 + 1, OUT_START + 3, LOW_MID + 3, TURN_MID, R_C1 + 2, SINK + 1,
    R_E1 + 2, R_E0 + 4, TURN_END + 2, LOW_END + 3, TURN_MID + 1, R_C0 + 2, R_E2 + 4, TURN_END, R_C1 + 3,
    ATTEND_BACK + 3, R_E1 + 3, R_C0 + 3, LOW_MID + 2, TURN_END + 1, R_E2 + 5, R_E0 + 5, R_C1 + 4, LOW_END + 2,
    ATTEND_BACK + 2, R_C0 + 4, R_E1 + 4, LOW_MID + 1, LOW_MID, IN_START + 3, IN_START + 2, LOW_END, R_C1 + 5,
    LOW_END + 1, GRAD_OUT, R_B, R_C0 + 5, R_E0 + 6, R_E2 + 6, R_E1 + 5, ATTEND_BACK + 1, IN_START + 1,
    R_C1 + 6, R_B + 1, ATTEND_BACK, R_C0 + 6, IN_START, GRAD_ATTN + 1, R_A1, R_B + 2, GRAD_ATTN, R_A0,
    IN_MID + 1, IN_MID + 2, R_A1 + 1, OUT_START, R_B + 3, R_E0 + 7, IN_MID + 3, R_A0 + 1, IN_MID, OUT_MID,
    R_A1 + 2, OUT_MID + 3, R_B + 4, R_A0 + 2, R_C0 + 7, R_A1 + 3, R_B + 5, IN_END + 2, R_A0 + 3, IN_END,
    R_A1 + 4, IN_END + 3, R_B + 6, R_A0 + 4, IN_END + 1, GIVE_IN, PACK_DP, OUT_START + 2, R_A1 + 5,
    OUT_MID + 2, R_A0 + 5, OUT_START + 1, OUT_MID + 1, OUT_END, R_C1 + 7, PACK_SEQ, R_E2 + 7, OUT_END + 2,
    R_E1 + 6, OUT_END + 3, R_B + 7, R_A1 + 6, R_A0 + 6, OUT_END + 1, GIVE_OUT, PACK_END, R_E1 + 7, R_A1 + 7,
    LAND_C, R_A0 + 7, LAND_A, DRAIN,
)


def seq_at(position):
    half = position // 4
    z = position + half * (7 - 2 * position)
    return 2 * z + half


def tree_seat(d, m):
    x, c = d // 2, d % 2
    return 2 * (2 * m + c) + (m + c + x) % 2


def greet_near(d, s, up, down):
    barrier = pltpu.get_barrier_semaphore()
    near = [((d + i) % NDP, s) for i in range(1, NDP)] + [(d, up), (d, down)]
    for other in near:
        pl.semaphore_signal(barrier, inc=1, device_id=other, device_id_type=MESH)
    pl.semaphore_wait(barrier, len(near))


def remote(src, dst, sems, at, d, s):
    send, recv = sems
    return pltpu.make_async_remote_copy(
        src_ref=src,
        dst_ref=dst,
        send_sem=send.at[at],
        recv_sem=recv.at[at],
        device_id=(d, s),
        device_id_type=MESH,
    )


class Sum:
    def __init__(self, part, near, sent, got, sems, n, spot):
        self.part, self.near, self.sent, self.got = part, near, sent, got
        self.sems, self.n = sems, n
        d, self.s = spot
        x, c = d // 2, d % 2
        self.d, self.sib, self.far = d, 2 * x + 1 - c, 2 * (1 - x) + c
        self.far_sib = 2 * (1 - x) + 1 - c

    def copies(self, b):
        rows = pl.ds(2 * b, 2)
        return (
            remote(self.part.at[rows, self.far_sib], self.near.at[0, rows], self.sems, (self.n, 0, b), self.sib, self.s),
            remote(self.part.at[rows, self.sib], self.near.at[1, rows], self.sems, (self.n, 1, b), self.sib, self.s),
            remote(self.sent.at[rows], self.got.at[rows], self.sems, (self.n, 2, b), self.far, self.s),
        )

    def start(self, b):
        first, second, _ = self.copies(b)
        first.start()
        second.start()

    def mid(self, b):
        first, _, across_x = self.copies(b)
        first.wait_recv()

        def join(i, carry):
            self.sent[i] = (
                self.part[i, self.far].astype(jnp.float32) + self.near[0, i].astype(jnp.float32)
            ).astype(jnp.bfloat16)
            return carry

        lax.fori_loop(2 * b, 2 * b + 2, join, 0)
        across_x.start()

    def end(self, b, finish):
        first, second, across_x = self.copies(b)
        second.wait_recv()
        across_x.wait_recv()

        def close(i, carry):
            rows = self.part[i, self.d].astype(jnp.float32) + self.near[1, i].astype(jnp.float32)
            finish(i, rows + self.got[i].astype(jnp.float32))
            return carry

        lax.fori_loop(2 * b, 2 * b + 2, close, 0)
        first.wait_send()
        second.wait_send()
        across_x.wait_send()


class Spread:
    def __init__(self, out, sems, at, spot):
        self.out, self.sems, self.place = out, sems, at
        d, self.s = spot
        x, c = d // 2, d % 2
        self.d, self.sib, self.far = d, 2 * x + 1 - c, 2 * (1 - x) + c
        self.far_sib = 2 * (1 - x) + 1 - c

    def copy(self, rows, owner, way, to):
        block = self.out.at[rows, owner]
        return remote(block, block, self.sems, self.place(way, rows), to, self.s)

    def start(self, rows):
        self.copy(rows, self.d, 0, self.far).start()
        self.copy(rows, self.d, 1, self.sib).start()

    def mid(self, rows):
        self.copy(rows, self.far, 0, self.far).wait_recv()
        self.copy(rows, self.far, 2, self.sib).start()

    def end(self, rows):
        self.copy(rows, self.sib, 1, self.sib).wait_recv()
        self.copy(rows, self.far_sib, 2, self.sib).wait_recv()

    def sent(self, rows):
        self.copy(rows, self.d, 0, self.far).wait_send()
        self.copy(rows, self.d, 1, self.sib).wait_send()
        self.copy(rows, self.far, 2, self.sib).wait_send()


def layer_kernel(
    nodes,
    tok, cot, lengths, parents, gain_a, gain_f, gain_q, gain_k, inv_freq, wq, wk, wv, wo, wg, wu, wd,
    out_rows, grad_rows, res_a, res_c, g_output, g_down, pack_out,
    raw_lengths, raw_parents, raw_a, raw_f, raw_q, raw_k, smalls, wa, wb, wc, we, gc, ge, hop_a, hop_b, hop_c, hop_e,
    tree, tree_cot, normed_in, normed_mid, d_low, tree_own,
    lin, heads, value, hidden, member, cosine, sine, att, d_att,
    part, part_out, near, sent, got, near_o, sent_o, got_o,
    middle, d_middle, act, both, d_key, d_value, outs, grad_low,
    fin_a, fin_c, attn_g, ffn_g, head_g, packed, pack_dp, pack_seq, pack_sum, pack_cut,
    loc, s_small, r_small, s_col, r_col, s_tok, r_tok, s_ag, r_ag, s_rs, r_rs,
    s_sum, r_sum, s_tree, r_tree, s_spread, r_spread, s_back, r_back, s_fin, r_fin, s_pack, r_pack,
):
    f32, bf = jnp.float32, jnp.bfloat16
    d = lax.axis_index("dp")
    s = lax.axis_index("seq")
    z, y = s // 2, s % 2
    p = z + y * (7 - 2 * z)
    spot = (d, s)
    seat = [seq_at((p + i) % NSEQ) for i in range(NSEQ)]
    up, down = seat[1], seat[7]
    ag_sems, rs_sems = (s_ag, r_ag), (s_rs, r_rs)
    small_sems, col_sems, tok_sems = (s_small, r_small), (s_col, r_col), (s_tok, r_tok)

    def aligned(v, n):
        return pl.multiple_of(v, n)

    def chunk(n, way, j):
        if n in (0, 1, 3, 4):
            return pl.ds(aligned((2 * way + (n + (n > 2)) % 2) * 256 + j * 32, 32), 32)
        if n == 2:
            return pl.ds(aligned(j * 64 + way * 32, 32), 32)
        return pl.ds(aligned(j * 96 + way * 48 + (n - 5) * 16, 16), 16)

    weight = {0: wa, 1: wa, 2: wb, 3: wc, 4: wc, 5: we, 6: we, 7: we}
    grads = {0: wa, 1: wa, 2: wb, 3: gc, 4: gc, 5: ge, 6: ge, 7: ge}
    hops = {0: hop_a.at[0], 1: hop_a.at[1], 2: hop_b, 3: hop_c.at[0], 4: hop_c.at[1]}
    hops.update({5 + i: hop_e.at[i] for i in range(3)})

    def owner_at(way, k):
        return seq_at((p + NSEQ - k) % NSEQ) if way == 0 else seq_at((p + k) % NSEQ)

    def gather(n, k):
        for way, peer in enumerate((up, down)):
            block = weight[n].at[chunk(n, way, owner_at(way, k))]
            if not (isinstance(k, int) and k == 0):
                remote(block, block, ag_sems, (n, way, k - 1), d, peer).wait_recv()
            remote(block, block, ag_sems, (n, way, k), d, peer).start()

    def gather_end(n):
        for way, peer in enumerate((up, down)):
            block = weight[n].at[chunk(n, way, owner_at(way, 7))]
            remote(block, block, ag_sems, (n, way, 6), d, peer).wait_recv()

    def gather_sent(n):
        for way, peer in enumerate((up, down)):
            block = weight[n].at[chunk(n, way, s)]
            for k in range(7):
                remote(block, block, ag_sems, (n, way, k), d, peer).wait_send()

    def add_rows(into, other):
        def one(i, carry):
            at = pl.ds(aligned(i * 16, 16), 16)
            into[at] = (into[at].astype(f32) + other[at].astype(f32)).astype(bf)
            return carry

        lax.fori_loop(0, into.shape[0] // 16, one, 0)

    def reduce_(n, k):
        for way, peer in enumerate((up, down)):
            rows = chunk(n, way, seat[(7 - k) % NSEQ] if way == 0 else seat[(1 + k) % NSEQ])
            mine = grads[n].at[rows]
            if k == 0:
                src = mine
            else:
                src = hops[n].at[way, k - 1]
                remote(src, src, rs_sems, (n, way, k - 1), d, peer).wait_recv()
                add_rows(src, mine)
            remote(src, hops[n].at[way, k], rs_sems, (n, way, k), d, peer).start()

    def reduce_end(n, take):
        for way, peer in enumerate((up, down)):
            src = hops[n].at[way, 6]
            remote(src, src, rs_sems, (n, way, 6), d, peer).wait_recv()
            take(way, src[...].astype(f32) + grads[n][chunk(n, way, s)].astype(f32))

    def reduce_sent(n):
        for way, peer in enumerate((up, down)):
            for k in range(7):
                src = hops[n].at[way, k]
                remote(src, src, rs_sems, (n, way, k), d, peer).wait_send()

    ops = {}
    tree_slot, tree_core = z // 2, z % 2
    tree_owner = 2 * ((y + tree_slot + tree_core) % 2) + tree_core
    pending = []
    held = {}

    def stage(name):
        def keep(run):
            ops[name] = run
            return run

        return keep

    def launch(cp):
        cp.start()
        pending.append(cp)

    raws = [
        pltpu.make_async_copy(src, dst, loc.at[9 + n])
        for n, (src, dst) in enumerate(
            (
                (lengths, raw_lengths), (parents, raw_parents),
                (gain_a, raw_a), (gain_f, raw_f), (gain_q, raw_q), (gain_k, raw_k),
            )
        )
    ]
    pieces = (
        (wq, wa, 512, 0), (wk, wa, 256, 512), (wv, wa, 256, 768), (wg, wc, 768, 0), (wu, wc, 768, 768)
    )
    col_rows = lambda q: pl.ds(aligned(q * 256 + s * 32, 32), 32)

    def column_copy(n):
        src, dst, width, at = pieces[n]
        return pltpu.make_async_copy(
            src.at[:, pl.ds(aligned(d * width, 128), width)],
            dst.at[col_rows(d), pl.ds(at, width)],
            loc.at[2 + n],
        )

    def columns(n):
        src, dst, width, at = pieces[n]
        for i in range(1, NDP):
            q = (d + i) % NDP
            launch(
                remote(
                    src.at[:, pl.ds(aligned(q * width, 128), width)],
                    dst.at[col_rows(d), pl.ds(at, width)],
                    col_sems, (n, i), q, s,
                )
            )
        column_copy(n).start()

    def columns_in(n):
        _, dst, width, at = pieces[n]
        column_copy(n).wait()
        for i in range(1, NDP):
            place = dst.at[col_rows((d + NDP - i) % NDP), pl.ds(at, width)]
            remote(place, place, col_sems, (n, i), d, s).wait_recv()

    def row_copy(n, m, i):
        src, dst = ((tok, tree), (cot, tree_cot))[n]
        q = (d + i) % NDP
        return pltpu.make_async_remote_copy(
            src_ref=src.at[m, pl.ds(aligned(q * 32, 32), 32)],
            dst_ref=dst.at[s, q],
            send_sem=s_tok.at[n, m, i],
            recv_sem=r_tok.at[n],
            device_id=(q, tree_seat(d, m)),
            device_id_type=MESH,
        )

    def rows_out(n, half):
        src, dst = ((tok, tree), (cot, tree_cot))[n]
        for m in range(MICRO):
            if half == 0:
                target = tree_seat(d, m)

                @pl.when(target == s)
                def _():
                    piece = src.at[m, pl.ds(aligned(d * 32, 32), 32)]
                    pltpu.make_async_copy(piece, dst.at[s, d], r_tok.at[n]).start()

                @pl.when(target != s)
                def _():
                    row_copy(n, m, 0).start()

                row_copy(n, m, 1).start()
            else:
                row_copy(n, m, 2).start()
                row_copy(n, m, 3).start()

    def rows_in(dst, n):
        everything = dst.at[:, d]
        pltpu.make_async_copy(everything, everything, r_tok.at[n]).wait()

    fill_b = pltpu.make_async_copy(wo, wb.at[pl.ds(aligned(s * 64, 64), 64)], loc.at[7])
    fill_e = pltpu.make_async_copy(wd, we.at[pl.ds(aligned(s * 96, 16), 96)], loc.at[15])

    @stage(START)
    def _():
        for cp in raws:
            cp.start()
        greet_near(d, s, up, down)
        fill_b.start()
        fill_e.start()
        for n in range(3):
            columns(n)

    @stage(TOKENS)
    def _():
        rows_out(0, 0)
        rows_out(0, 1)

    for i in range(2):
        stage(COTANGENT + i)(functools.partial(rows_out, 1, i))


    @stage(SMALL_DP)
    def _():
        for cp in raws:
            cp.wait()
        for row, ref in enumerate((raw_a, raw_f, raw_q, raw_k)):
            count = ref.shape[0]
            line = ref[...].astype(f32).reshape(1, count)
            smalls[d, s, row : row + 1, :] = jnp.concatenate([line] * (128 // count), axis=1)
        smalls[d, s, 4:8, :] = jnp.zeros((4, 128), f32)
        smalls[d, s, 4:6, 0:nodes] = raw_lengths[0].astype(f32)
        smalls[d, s, 6:8, 0:nodes] = raw_parents[0].astype(f32)
        for i in range(1, NDP):
            launch(remote(smalls.at[d, s], smalls.at[d, s], small_sems, i, (d + i) % NDP, s))

    @stage(SMALL_SEQ)
    def _():
        for i in range(1, NDP):
            place = smalls.at[(d + NDP - i) % NDP, s]
            remote(place, place, small_sems, i, d, s).wait_recv()
        lane = lax.broadcasted_iota(jnp.int32, (1, 128), 1)
        for q in range(NDP):
            rows = [smalls[q, s, row : row + 1, :] for row in range(4)]
            tail = jnp.where(lane < 68, rows[2], rows[3])
            packed[s, q : q + 1, :] = jnp.where(lane < 32, rows[0], jnp.where(lane < 64, rows[1], tail))
            packed[s, q + 4 : q + 5, :] = jnp.zeros((1, 128), f32)
        for i in range(1, NSEQ):
            launch(remote(packed.at[s], packed.at[s], small_sems, NDP + i, d, (s + i) % NSEQ))

    @stage(A_IN)
    def _():
        for n in range(3):
            columns_in(n)

    @stage(C_OUT)
    def _():
        for n in range(3, 5):
            columns(n)

    @stage(C_IN)
    def _():
        for n in range(3, 5):
            columns_in(n)

    streams = ((A0, 0), (A1, 1), (B, 2), (C0, 3), (C1, 4), (E0, 5), (E1, 6), (E2, 7))

    def ring_first(n):
        if n == 2:
            fill_b.wait()
        if n == 5:
            fill_e.wait()
        gather(n, 0)

    for label, n in streams:
        stage(label)(functools.partial(ring_first, n))
        stage(label + 7)(functools.partial(gather_end, n))
        for k in range(1, 7):
            stage(label + k)(functools.partial(gather, n, k))
        for k in range(7):
            stage(R_A0 + label + k)(functools.partial(reduce_, n, k))

    everything = pl.ds(0, NSEQ)
    spread_tree = Spread(tree, (s_tree, r_tree), lambda way, rows: (0, way), spot)
    spread_cot = Spread(tree_cot, (s_tree, r_tree), lambda way, rows: (1, way), spot)

    @stage(TREE_START)
    def _():
        rows_in(tree, 0)
        spread_tree.start(everything)

    @stage(COT_START)
    def _():
        rows_in(tree_cot, 1)
        spread_cot.start(everything)

    stage(TREE_MID)(lambda: spread_tree.mid(everything))
    stage(COT_MID)(lambda: spread_cot.mid(everything))
    stage(COT_END)(lambda: spread_cot.end(everything))
    own_rows = pltpu.make_async_copy(tree.at[:, d], tree_own, loc.at[8])

    @stage(TREE_END)
    def _():
        spread_tree.end(everything)
        own_rows.start()

    @stage(NODE)
    def _():
        ir = lax.broadcasted_iota(jnp.int32, (128, 128), 0)
        ic = lax.broadcasted_iota(jnp.int32, (128, 128), 1)
        block = smalls.at[tree_owner, s]
        length_row = block[pl.ds(4 + tree_slot, 1), :]
        parent_row = block[pl.ds(6 + tree_slot, 1), :]
        length_col = jnp.sum(jnp.where(ir == ic, length_row, 0.0), axis=1, keepdims=True)
        over = (parent_row == ir.astype(f32)) & (ic > 0) & (ic < nodes)
        above = jnp.where(over | (ir == ic), 1.0, 0.0)
        for _ in range(4):
            low = above.astype(bf)
            above = jnp.minimum(product(low, low), 1.0)
        start_row = jnp.sum(jnp.where(ir < ic, length_col, 0.0), axis=0, keepdims=True)
        base_row = jnp.sum(
            jnp.where((above > 0.5) & (ir != ic), length_col, 0.0), axis=0, keepdims=True
        )
        shut = jnp.where(above > 0.5, 0.0, BLOCKED).astype(bf)
        held["node"] = (start_row, start_row + length_row, base_row - start_row, shut)

    def tables(i, carry):
        start_row, end_row, offset_row, shut = held["node"]
        rows = pl.ds(aligned(i * QB, QB), QB)
        index = (lax.broadcasted_iota(jnp.int32, (QB, 128), 0) + i * QB).astype(f32)
        inside = (index >= start_row) & (index < end_row)
        position = index[:, :1] + jnp.sum(
            jnp.where(inside, offset_row, 0.0), axis=1, keepdims=True
        )
        hot = jnp.where(inside, 1.0, 0.0).astype(bf)
        member[rows] = hot
        hidden[rows] = against(hot, shut).astype(bf)
        angle = position * inv_freq[...]
        cosine[rows] = jnp.cos(angle)
        lane = lax.broadcasted_iota(jnp.int32, (QB, 128), 1)
        wave = jnp.sin(angle)
        sine[rows] = jnp.where(lane < 64, -wave, wave)
        return carry

    stage(TABLES + 0)(lambda: lax.fori_loop(0, 2, tables, 0))
    stage(TABLES + 1)(lambda: lax.fori_loop(2, 4, tables, 0))

    @stage(GAINS)
    def _():
        for i in range(1, NSEQ):
            place = packed.at[(s + NSEQ - i) % NSEQ]
            remote(place, place, small_sems, NDP + i, d, s).wait_recv()
        lane = lax.broadcasted_iota(jnp.int32, (1, 128), 1)

        def moved(i, source, target):
            line = packed[i % NSEQ, i // NSEQ : i // NSEQ + 1, :]
            shift = (target - source) % 128
            return pltpu.roll(line, shift, 1) if shift else line

        for source, dst in ((0, attn_g), (32, ffn_g)):
            for j in range(8):
                parts = [moved(4 * j + i, source, 32 * i) for i in range(4)]
                dst[:, 128 * j : 128 * (j + 1)] = jnp.where(
                    lane < 64,
                    jnp.where(lane < 32, parts[0], parts[1]),
                    jnp.where(lane < 96, parts[2], parts[3]),
                )
        for row in range(2):
            joined = jnp.zeros((1, 128), f32)
            for i in range(32):
                joined = jnp.where(lane // 4 == i, moved(i, 64 + 4 * row, 4 * i), joined)
            head_g[row : row + 1, :] = joined
        pack_dp[d] = jnp.zeros((24, 128), f32)

    def norm_in(i, carry):
        rows = tree[i].reshape(128, D).astype(f32)
        scale = lax.rsqrt(jnp.mean(rows * rows, axis=-1, keepdims=True) + EPSILON)
        normed_in[pl.ds(aligned(i * 128, 128), 128)] = (rows * scale * attn_g[...]).astype(bf)
        return carry

    stage(NORM_IN + 0)(lambda: lax.fori_loop(0, 4, norm_in, 0))
    stage(NORM_IN + 1)(lambda: lax.fori_loop(4, 8, norm_in, 0))

    def unit_of(v):
        scale = lax.rsqrt(jnp.mean(v * v, axis=-1, keepdims=True) + EPSILON)
        return v * scale, scale

    def turn(v, gain, cos, sin):
        unit, _ = unit_of(v)
        lifted = unit * gain
        return lifted * cos + pltpu.roll(lifted, 64, 1) * sin

    def turn_back(dr, v, gain, cos, sin):
        d_lift = dr * cos + pltpu.roll(dr * sin, 64, 1)
        unit, scale = unit_of(v)
        d_unit = d_lift * gain
        return (
            scale * (d_unit - unit * jnp.mean(unit * d_unit, axis=-1, keepdims=True)),
            jnp.sum(d_lift * unit, axis=0, keepdims=True),
        )

    def project(i):
        rows = pl.ds(i * QB, QB)
        cos, sin = cosine[rows], sine[rows]

        def one(j, carry):
            lanes = pl.ds(aligned(j * 256, 256), 256)
            pair = product(normed_in[rows], wa[:, lanes])
            lin[rows, lanes] = pair
            gain = head_g[pl.ds(j // 2, 1), :]
            for i2 in range(2):
                turned = turn(pair[:, 128 * i2 : 128 * (i2 + 1)], gain, cos, sin)
                heads[2 * j + i2, rows] = turned.astype(bf)
            return carry

        lax.fori_loop(0, 3, one, 0)
        value[rows] = product(normed_in[rows], wa[:, 768:]).astype(bf)

    for i in range(4):
        stage(PROJECT + i)(functools.partial(project, i))

    def span(b):
        return pl.ds(b * QB, QB), (b + 1) * QB

    def weights_of(b, h, n):
        here = pl.ds(b * QB, QB)
        q = jnp.concatenate([heads[h, here], hidden[here]], axis=1)
        k = jnp.concatenate([heads[4 + h // 2, pl.ds(0, n)], member[pl.ds(0, n)]], axis=1)
        score = against(q, k) * SOFT
        row = lax.broadcasted_iota(jnp.int32, (QB, QB), 0)
        col = lax.broadcasted_iota(jnp.int32, (QB, QB), 1)
        diag = jnp.where(col <= row, score[:, n - QB :], NEGATIVE)
        score = diag if b == 0 else jnp.concatenate([score[:, : n - QB], diag], axis=1)
        grown = jnp.exp2(score)
        return grown, 1.0 / jnp.sum(grown, axis=-1, keepdims=True)

    def head_lanes(h):
        return pl.ds(aligned(h * HEAD_DIM, HEAD_DIM), HEAD_DIM)

    sum_sems, spread_sems = (s_sum, r_sum), (s_spread, r_spread)
    mixed_sum = Sum(part, near, sent, got, sum_sems, 0, spot)
    mid_sum = Sum(part, near, sent, got, sum_sems, 1, spot)
    out_sum = Sum(part_out, near_o, sent_o, got_o, sum_sems, 2, spot)
    in_sum = Sum(part, near, sent, got, sum_sems, 3, spot)
    pair_of = {b: pl.ds(2 * b, 2) for b in BLOCKS}
    spread_mid = Spread(normed_mid, spread_sems, lambda way, rows: (0, way, rows.start // 2), spot)
    spread_low = Spread(d_low, spread_sems, lambda way, rows: (1, way, rows.start // 2), spot)

    def attend(b):
        here, n = span(b)
        if b == BLOCKS[0]:
            own_rows.wait()

        def one(h, carry):
            grown, inverse = weights_of(b, h, n)
            mixed = product(grown.astype(bf), value[pl.ds(0, n), head_lanes(h // 2)])
            att[here, head_lanes(h)] = (mixed * inverse).astype(bf)
            return carry

        lax.fori_loop(0, HEADS // NDP, one, 0)
        rows = product(att[here], wb[...]).astype(bf)
        part[pair_of[b]] = rows.reshape(2, NDP, 32, D)
        mixed_sum.start(b)

    def to_middle(i, rows):
        rows = rows + tree_own[i].astype(f32)
        middle[i] = rows
        scale = lax.rsqrt(jnp.mean(rows * rows, axis=-1, keepdims=True) + EPSILON)
        normed_mid[i, d] = (rows * scale * ffn_g[...]).astype(bf)

    def close_mixed(b):
        mixed_sum.end(b, to_middle)
        spread_mid.start(pair_of[b])

    def lift(b):
        here = pl.ds(b * QB, QB)
        rows = normed_mid[pair_of[b]].reshape(QB, D)

        def one(t, carry):
            left = pl.ds(aligned(t * 256, 256), 256)
            right = pl.ds(aligned(768 + t * 256, 256), 256)
            gate = product(rows, wc[:, left])
            wide = product(rows, wc[:, right])
            sigma = 1.0 / (1.0 + jnp.exp(-gate))
            silu = gate * sigma
            act[here, left] = (silu * wide).astype(bf)
            both[here, left] = (wide * sigma * (1.0 + gate * (1.0 - sigma))).astype(bf)
            both[here, right] = silu.astype(bf)
            return carry

        lax.fori_loop(0, 3, one, 0)

    @stage(GRAD_DOWN)
    def _():
        def one(i, carry):
            cols = pl.ds(aligned(i * 256, 256), 256)
            ge[cols] = across(act[:, cols], tree_cot[...].reshape(NSEQ * 128, D)).astype(bf)
            return carry

        lax.fori_loop(0, 3, one, 0)

    def d_activate(b):
        here = pl.ds(b * QB, QB)
        cots = tree_cot[pair_of[b]].reshape(QB, D)

        def one(t, carry):
            left = pl.ds(aligned(t * 256, 256), 256)
            right = pl.ds(aligned(768 + t * 256, 256), 256)
            d_act = against(cots, we[left])
            both[here, left] = (d_act * both[here, left].astype(f32)).astype(bf)
            both[here, right] = (d_act * both[here, right].astype(f32)).astype(bf)
            return carry

        lax.fori_loop(0, 3, one, 0)

    def sink(b):
        here = pl.ds(b * QB, QB)
        part[pair_of[b]] = against(both[here], wc[...]).astype(bf).reshape(2, NDP, 32, D)
        mid_sum.start(b)

    def settle(b):
        here = pl.ds(b * QB, QB)
        part_out[pair_of[b]] = product(act[here], we[...]).astype(bf).reshape(2, NDP, 32, D)
        out_sum.start(b)

    def to_turn(i, rows):
        unit, scale = unit_of(middle[i])
        lifted = ffn_g[...] * rows
        term = jnp.sum(rows * unit, axis=0, keepdims=True)
        for j in range(8):
            pack_dp[d, 8 + j : 9 + j] += term[:, 128 * j : 128 * (j + 1)]
        d_mid = tree_cot[i, d].astype(f32) + scale * (
            lifted - unit * jnp.mean(unit * lifted, axis=-1, keepdims=True)
        )
        d_middle[i] = d_mid
        d_low[i, d] = d_mid.astype(bf)

    def close_mid(b):
        mid_sum.end(b, to_turn)
        spread_low.start(pair_of[b])

    def to_outs(i, rows):
        outs[i] = (middle[i] + rows).astype(bf)

    back_owner, back_slot = tree_owner, tree_slot
    back = ((outs, out_rows), (grad_low, grad_rows))

    def give_copy(n, j):
        src, dst = back[n]
        return pltpu.make_async_remote_copy(
            src_ref=src.at[j],
            dst_ref=dst.at[back_slot, pl.ds(aligned(d * 32, 32), 32)],
            send_sem=s_back.at[n, j],
            recv_sem=r_back.at[n],
            device_id=(back_owner, j),
            device_id_type=MESH,
        )

    def give(n):
        src, dst = back[n]

        def one(j, carry):
            same = (back_owner == d) & (s == j)

            @pl.when(same)
            def _():
                place = dst.at[back_slot, pl.ds(aligned(d * 32, 32), 32)]
                pltpu.make_async_copy(src.at[j], place, r_back.at[n]).start()

            @pl.when(jnp.logical_not(same))
            def _():
                give_copy(n, j).start()

            return carry

        lax.fori_loop(0, NSEQ, one, 0)

    def close_out(b):
        out_sum.end(b, to_outs)

    def grad_wide(sub):
        for i in (sub, 2 + sub):
            cols = pl.ds(i * 256, 256)

            rows = normed_mid[:, :, :, cols].reshape(NSEQ * 128, 256)
            gc[cols] = across(rows, both[...]).astype(bf)

    d_lin = tree

    def close_low(b):
        spread_low.end(pair_of[b])
        here = pl.ds(b * QB, QB)
        rows = d_low[pair_of[b]].reshape(QB, D)
        d_att[here] = against(rows, wb[...]).astype(bf)

    def attend_back(b):
        here, n = span(b)
        keys = pl.ds(0, n)
        if b == BLOCKS[0]:
            spread_tree.sent(everything)
            d_key[...] = jnp.zeros_like(d_key)
            d_value[...] = jnp.zeros_like(d_value)

        def one(h, carry):
            kv = h // 2
            grown, inverse = weights_of(b, h, n)
            d_out = d_att[here, head_lanes(h)]
            wide_out = d_out.astype(f32)
            d_prob = against(d_out, value[keys, head_lanes(kv)])
            delta = jnp.sum(wide_out * att[here, head_lanes(h)].astype(f32), axis=-1, keepdims=True)
            d_raw = (grown * (d_prob - delta)).astype(bf)
            factor = inverse * HEAD_DIM ** (-0.5)
            d_rot = product(d_raw, heads[4 + kv, keys]) * factor
            d_key[kv, keys] += across(d_raw, (heads[h, here].astype(f32) * factor).astype(bf))
            d_value[kv, keys] += across(grown.astype(bf), (wide_out * inverse).astype(bf))
            back, d_gain = turn_back(
                d_rot, lin[here, head_lanes(h)], head_g[0:1, :], cosine[here], sine[here]
            )
            pack_dp[d, 16:17] += d_gain
            d_lin[pair_of[b], :, :, head_lanes(h)] = back.astype(bf).reshape(2, NDP, 32, HEAD_DIM)
            return carry

        lax.fori_loop(0, HEADS // NDP, one, 0)
        for kv in range(KV_HEADS // NDP):
            at = 512 + 128 * kv
            back, d_gain = turn_back(
                d_key[kv, here], lin[here, pl.ds(at, 128)], head_g[1:2, :], cosine[here], sine[here]
            )
            pack_dp[d, 17:18] += d_gain
            d_lin[pair_of[b], :, :, pl.ds(at, 128)] = back.astype(bf).reshape(2, NDP, 32, 128)
            d_lin[pair_of[b], :, :, pl.ds(at + 256, 128)] = (
                d_value[kv, here].astype(bf).reshape(2, NDP, 32, 128)
            )

    def sink_in(b):
        rows = against(d_lin[pair_of[b]].reshape(QB, 1024), wa[...])
        part[pair_of[b]] = rows.astype(bf).reshape(2, NDP, 32, D)
        in_sum.start(b)

    @stage(GRAD_OUT)
    def _():
        gather_sent(2)
        for i in range(2):
            cols = pl.ds(256 * i, 256)
            wb[cols] = across(att[:, cols], d_low[...].reshape(NSEQ * 128, D)).astype(bf)

    def grad_attn(sub):
        gather_sent(sub)
        for i in (sub, 2 + sub):
            cols = pl.ds(i * 256, 256)

            wa[cols] = across(normed_in[:, cols], d_lin[...].reshape(NSEQ * 128, 1024)).astype(bf)

    def to_grad(i, rows):
        unit, scale = unit_of(tree_own[i].astype(f32))
        lifted = attn_g[...] * rows
        term = jnp.sum(rows * unit, axis=0, keepdims=True)
        for j in range(8):
            pack_dp[d, j : j + 1] += term[:, 128 * j : 128 * (j + 1)]
        grad = d_middle[i] + scale * (
            lifted - unit * jnp.mean(unit * lifted, axis=-1, keepdims=True)
        )
        grad_low[i] = grad.astype(bf)

    def close_in(b):
        in_sum.end(b, to_grad)

    per_block = (
        (ATTEND, attend), (MIX_MID, mixed_sum.mid), (MIX_END, close_mixed),
        (NORM_MID, lambda b: spread_mid.mid(pair_of[b])), (NORM_END, lambda b: spread_mid.end(pair_of[b])),
        (LIFT, lift), (D_ACT, d_activate), (SINK, sink), (TURN_MID, mid_sum.mid), (TURN_END, close_mid),
        (LOW_MID, lambda b: spread_low.mid(pair_of[b])), (LOW_END, close_low),
        (OUT_START, settle), (OUT_MID, out_sum.mid), (OUT_END, close_out),
        (ATTEND_BACK, attend_back), (IN_START, sink_in), (IN_MID, in_sum.mid), (IN_END, close_in),
    )
    for label, run in per_block:
        for b in BLOCKS:
            stage(label + b)(functools.partial(run, b))
    for sub in range(2):
        stage(GRAD_WIDE + sub)(functools.partial(grad_wide, sub))
        stage(GRAD_ATTN + sub)(functools.partial(grad_attn, sub))

    stage(GIVE_OUT)(functools.partial(give, 0))
    stage(GIVE_IN)(functools.partial(give, 1))

    pack_sems, fin_sems = (s_pack, r_pack), (s_fin, r_fin)

    @stage(PACK_DP)
    def _():
        for i in range(1, NDP):
            launch(remote(pack_dp.at[d], pack_dp.at[d], pack_sems, i, (d + i) % NDP, s))

    @stage(PACK_SEQ)
    def _():
        for i in range(1, NDP):
            place = pack_dp.at[(d + NDP - i) % NDP]
            remote(place, place, pack_sems, i, d, s).wait_recv()
        pack_sum[...] = (pack_dp[0] + pack_dp[1]) + (pack_dp[2] + pack_dp[3])
        for j in range(NSEQ):
            block = 2 * d + j // 4
            wide = (128 - 32 * (j % 4)) % 128
            thin = (256 - 32 * d - 4 * j) % 128
            pack_cut[j] = jnp.zeros((8, 128), f32)
            for n, (row, shift) in enumerate(((block, wide), (8 + block, wide), (16, thin), (17, thin))):
                pack_cut[j, n : n + 1, :] = pltpu.roll(pack_sum[pl.ds(row, 1), :], shift, 1)
        pack_seq[s] = pack_cut[s]
        for i in range(1, NSEQ):
            j = (s + i) % NSEQ
            launch(remote(pack_cut.at[j], pack_seq.at[s], pack_sems, NDP + i, d, j))

    @stage(PACK_END)
    def _():
        for i in range(1, NSEQ):
            place = pack_seq.at[(s + NSEQ - i) % NSEQ]
            remote(place, place, pack_sems, NDP + i, d, s).wait_recv()
        total = pack_seq[0]
        for j in range(1, NSEQ):
            total = total + pack_seq[j]
        pack_out[...] = total

    def close_cols(n, fin, landed, which):
        sub = (n + (n > 2)) % 2

        def take(way, total):
            fin[2 * way + sub] = total.astype(bf)

        reduce_end(n, take)
        for way in range(2):
            q = 2 * way + sub

            @pl.when(q == d)
            def _():
                pltpu.make_async_copy(fin.at[q], landed.at[d], loc.at[which]).start()

            @pl.when(q != d)
            def _():
                remote(fin.at[q], landed.at[d], fin_sems, (which, d), q, s).start()

    for label, n, fin, landed, which in (
        (A0, 0, fin_a, res_a, 0), (A1, 1, fin_a, res_a, 0),
        (C0, 3, fin_c, res_c, 1), (C1, 4, fin_c, res_c, 1),
    ):
        stage(R_A0 + label + 7)(functools.partial(close_cols, n, fin, landed, which))

    def land(landed, which):
        for i in range(1, NDP):
            q = (d + i) % NDP
            remote(landed.at[q], landed.at[q], fin_sems, (which, q), q, s).wait_recv()
        pltpu.make_async_copy(landed.at[d], landed.at[d], loc.at[which]).wait()

    stage(LAND_A)(lambda: land(res_a, 0))
    stage(LAND_C)(lambda: land(res_c, 1))

    def take_rows(dst, rows, at, way, total):
        dst[pl.ds(rows * way + at, total.shape[0])] = total

    stage(R_B + 7)(lambda: reduce_end(2, functools.partial(take_rows, g_output, 32, 0)))
    for label, n in streams[5:]:
        take = functools.partial(take_rows, g_down, 48, (n - 5) * 16)
        stage(R_A0 + label + 7)(functools.partial(reduce_end, n, take))

    @stage(DRAIN)
    def _():
        for n, (src, dst) in enumerate(back):
            pltpu.make_async_copy(dst, dst, r_back.at[n]).wait()

            def one(j, carry):
                @pl.when(jnp.logical_not((back_owner == d) & (s == j)))
                def _():
                    give_copy(n, j).wait_send()

                return carry

            lax.fori_loop(0, NSEQ, one, 0)
        for n, (fin, landed) in enumerate(((fin_a, res_a), (fin_c, res_c))):
            for i in range(1, NDP):
                q = (d + i) % NDP
                remote(fin.at[q], landed.at[d], fin_sems, (n, d), q, s).wait_send()
        for n in range(3, 8):
            gather_sent(n)
        for n in range(8):
            reduce_sent(n)
        spread_cot.sent(everything)
        for b in BLOCKS:
            spread_mid.sent(pair_of[b])
            spread_low.sent(pair_of[b])
        for cp in pending:
            cp.wait_send()
        for n in range(2):
            for m in range(MICRO):

                @pl.when(tree_seat(d, m) != s)
                def _():
                    row_copy(n, m, 0).wait_send()

                for i in range(1, NDP):
                    row_copy(n, m, i).wait_send()

    for name in ORDER:
        ops[name]()


def finish_kernel(
    out_rows, grad_rows, res_a, res_c, g_output, g_down, pack,
    outs, grads, g_query, g_key, g_value, out_output, g_gate, g_up, out_down, g_attn, g_ffn, g_qg, g_kg,
    low_rows, low_a, low_c, small, *rest,
):
    *held, sems = rest
    coming = [
        pltpu.make_async_copy(src, dst, sems.at[n])
        for n, (src, dst) in enumerate(
            (
                (grad_rows, low_rows), (res_a, low_a), (res_c, low_c), (pack, small),
                (out_rows, held[0]), (g_output, held[1]), (g_down, held[2]),
            )
        )
    ]
    for cp in coming:
        cp.start()
    leaving = [
        pltpu.make_async_copy(src, dst, sems.at[7 + n])
        for n, (src, dst) in enumerate(zip(held, (outs, out_output, out_down)))
    ]
    for came, goes in zip(coming[4:], leaving):
        came.wait()
        goes.start()
    coming[0].wait()
    grads[...] = low_rows[...].astype(jnp.float32)
    for cp in coming[1:4]:
        cp.wait()
    for src, cuts in (
        (low_a, ((0, 512, g_query), (512, 256, g_key), (768, 256, g_value))),
        (low_c, ((0, 768, g_gate), (768, 768, g_up))),
    ):
        for q in range(NDP):
            for at, width, dst in cuts:
                dst[:, width * q : width * (q + 1)] = src[q, :, at : at + width].astype(jnp.float32)
    for n, dst in enumerate((g_attn, g_ffn, g_qg, g_kg)):
        count = dst.shape[0]
        dst[...] = small[n : n + 1, 0:count].reshape(count)
    for cp in leaving:
        cp.wait()


def tree_shards(
    tokens, cotangent, node_lengths, parents, w_query, w_key, w_value, w_output, w_gate, w_up, w_down,
    attn_gain, ffn_gain, query_gain, key_gain,
):
    f32, bf = jnp.float32, jnp.bfloat16
    nodes = node_lengths.shape[2]
    half = np.arange(HEAD_DIM // 2, dtype=np.float64)
    inv_freq = THETA ** (-(half * (2.0 / HEAD_DIM)))
    inv_freq = np.concatenate([inv_freq, inv_freq])[None].astype(np.float32)
    shape, vmem, dma = jax.ShapeDtypeStruct, pltpu.VMEM, pltpu.SemaphoreType.DMA
    anywhere = pl.BlockSpec(memory_space=pl.ANY)
    here = pl.BlockSpec(memory_space=pltpu.VMEM)
    rows = NSEQ * 128
    quarter = (NSEQ, 32, D)
    twice = lambda *dims: [dma(dims), dma(dims)]
    results = pl.pallas_call(
        functools.partial(layer_kernel, nodes),
        out_shape=(
            shape((MICRO, 128, D), bf),
            shape((MICRO, 128, D), bf),
            shape((NDP, 32, 1024), bf),
            shape((NDP, 32, 1536), bf),
            shape((64, D), f32),
            shape((96, D), f32),
            shape((8, 128), f32),
        ),
        in_specs=[anywhere] * 8 + [here] + [anywhere] * 7,
        out_specs=[anywhere] * 4 + [here] * 3,
        scratch_shapes=[
            vmem(node_lengths.shape, jnp.int32), vmem(parents.shape, jnp.int32),
            *[vmem(gain.shape, bf) for gain in (attn_gain, ffn_gain, query_gain, key_gain)],
            vmem((NDP, NSEQ, 8, 128), f32),
            vmem((D, 1024), bf), vmem((512, D), bf), vmem((D, 1536), bf), vmem((768, D), bf),
            vmem((D, 1536), bf), vmem((768, D), bf),
            vmem((2, 2, 7, 32, 1024), bf), vmem((2, 7, 32, D), bf),
            vmem((2, 2, 7, 32, 1536), bf), vmem((3, 2, 7, 16, D), bf),
            vmem((NSEQ, NDP, 32, D), bf), vmem((NSEQ, NDP, 32, D), bf), vmem((rows, D), bf),
            vmem((NSEQ, NDP, 32, D), bf), vmem((NSEQ, NDP, 32, D), bf), vmem(quarter, bf),
            vmem((rows, 768), f32), vmem((6, rows, 128), bf),
            vmem((rows, 256), bf), vmem((rows, 128), bf), vmem((rows, 128), bf),
            vmem((rows, 128), f32), vmem((rows, 128), f32), vmem((rows, 512), bf), vmem((rows, 512), bf),
            vmem((NSEQ, NDP, 32, D), bf), vmem((NSEQ, NDP, 32, D), bf),
            vmem((2,) + quarter, bf), vmem(quarter, bf), vmem(quarter, bf),
            vmem((2,) + quarter, bf), vmem(quarter, bf), vmem(quarter, bf),
            vmem(quarter, f32), vmem(quarter, f32), vmem((rows, 768), bf), vmem((rows, 1536), bf),
            vmem((2, rows, 128), f32), vmem((2, rows, 128), f32), vmem(quarter, bf), vmem(quarter, bf),
            vmem((NDP, 32, 1024), bf), vmem((NDP, 32, 1536), bf),
            vmem((1, D), f32), vmem((1, D), f32), vmem((8, 128), f32),
            vmem((NSEQ, 8, 128), f32), vmem((NDP, 24, 128), f32), vmem((NSEQ, 8, 128), f32),
            vmem((24, 128), f32), vmem((NSEQ, 8, 128), f32),
            dma((16,)),
            *twice(12), *twice(5, NDP), dma((2, MICRO, NDP)), dma((2,)),
            *twice(8, 2, 7), *twice(8, 2, 7),
            *twice(4, 3, 4), *twice(2, 3), *twice(2, 3, 4),
            dma((2, NSEQ)), dma((2,)), *twice(2, NDP), *twice(12),
        ],
        compiler_params=pltpu.CompilerParams(
            collective_id=1, has_side_effects=True, vmem_limit_bytes=61 << 20
        ),
        name="layer",
    )(
        tokens[0], cotangent[0], node_lengths, parents, attn_gain, ffn_gain, query_gain, key_gain, inv_freq,
        w_query, w_key, w_value, w_output, w_gate, w_up, w_down,
    )
    full = lambda *dims: shape(dims, f32)
    finished = pl.pallas_call(
        finish_kernel,
        out_shape=(
            shape((MICRO, 128, D), bf), full(MICRO, 128, D),
            full(32, 2048), full(32, 1024), full(32, 1024), full(64, D),
            full(32, FF), full(32, FF), full(96, D),
            full(32), full(32), full(4), full(4),
        ),
        in_specs=[pl.BlockSpec(memory_space=pltpu.HBM)] * 7,
        out_specs=[anywhere, here, here, here, here, anywhere, here, here, anywhere] + [here] * 4,
        scratch_shapes=[
            vmem((MICRO, 128, D), bf), vmem((NDP, 32, 1024), bf), vmem((NDP, 32, 1536), bf),
            vmem((8, 128), f32), vmem((MICRO, 128, D), bf), vmem((64, D), f32), vmem((96, D), f32),
            dma((10,)),
        ],
        compiler_params=pltpu.CompilerParams(vmem_limit_bytes=61 << 20),
        name="finish",
    )(*results)
    return (finished[0][None], finished[1][None]) + tuple(finished[2:])


def solution(mesh):
    ring = mesh.shape["dp"] == NDP and mesh.shape["seq"] == NSEQ
    return jax.shard_map(
        tree_shards if ring else general_shards,
        mesh=mesh,
        in_specs=(
            P("dp", None, "seq", None),
            P("dp", None, "seq", None),
            P("dp", None, None),
            P("dp", None, None),
            P(("dp", "seq"), None),
            P(("dp", "seq"), None),
            P(("dp", "seq"), None),
            P(("dp", "seq"), None),
            P(("dp", "seq"), None),
            P(("dp", "seq"), None),
            P(("dp", "seq"), None),
            P(("dp", "seq")),
            P(("dp", "seq")),
            P(("dp", "seq")),
            P(("dp", "seq")),
        ),
        out_specs=(
            P("dp", None, "seq", None),
            P("dp", None, "seq", None),
            P(("dp", "seq"), None),
            P(("dp", "seq"), None),
            P(("dp", "seq"), None),
            P(("dp", "seq"), None),
            P(("dp", "seq"), None),
            P(("dp", "seq"), None),
            P(("dp", "seq"), None),
            P(("dp", "seq")),
            P(("dp", "seq")),
            P(("dp", "seq")),
            P(("dp", "seq")),
        ),
        check_vma=False,
    )
```

```python
import functools

import jax
import jax.numpy as jnp
import numpy as np
from jax import lax
from jax.experimental import pallas as pl
from jax.experimental.pallas import tpu as pltpu
from jax.sharding import PartitionSpec as P

D = 1024
HEADS = 16
KV_HEADS = 8
HEAD_DIM = 128
FF = 3072
MICRO = 2


EPSILON = 1e-06
THETA = 1000000.0
NEGATIVE = -1e30
PRECISE = lax.Precision.HIGHEST


def norm_rows(values, row_gain):
    return (
        values * lax.rsqrt(jnp.mean(values * values, axis=-1, keepdims=True) + EPSILON) * row_gain
    )


def rope_tables(position, head_dim):
    half_dim = head_dim // 2
    inv_freq = THETA ** (-(jnp.arange(half_dim, dtype=jnp.float32) * (2.0 / head_dim)))
    angles = position.astype(jnp.float32)[:, None] * inv_freq[None, :]
    cosine_table = jnp.cos(angles)
    sine_table = jnp.sin(angles)
    return (
        jnp.concatenate([cosine_table, cosine_table], axis=1),
        jnp.concatenate([sine_table, sine_table], axis=1),
    )


def rotate(values, cosine_table, sine_table):
    half_dim = values.shape[-1] // 2
    turned = jnp.concatenate([-values[..., half_dim:], values[..., :half_dim]], axis=-1)
    return values * cosine_table[:, None, :] + turned * sine_table[:, None, :]


def tree_tables(lengths, parent_row):
    node_count = lengths.shape[0]
    labels = jnp.arange(node_count, dtype=jnp.int32)
    parent_hot = ((parent_row[:, None] == labels[None, :]) & (labels[:, None] > 0)).astype(
        jnp.int32
    )

    def extend(depth_step, state_pair):
        reached, covered = state_pair
        reached = jnp.sum(reached[:, :, None] * parent_hot[None, :, :], axis=1)
        return (reached, covered + reached)

    reached, covered = lax.fori_loop(0, node_count, extend, (parent_hot, parent_hot))
    ancestry = (covered > 0).astype(jnp.float32)
    starts = jnp.cumsum(lengths) - lengths
    path_base = jnp.sum(jnp.where(covered > 0, lengths[None, :], 0), axis=1)
    return (labels, starts, path_base, ancestry)


def token_nodes(token_index, labels, starts, path_base):
    node_id = jnp.sum((token_index[:, None] >= starts[None, 1:]).astype(jnp.int32), axis=1)
    member = node_id[:, None] == labels[None, :]
    offset = jnp.sum(jnp.where(member, (path_base - starts)[None, :], 0), axis=1)
    return (member.astype(jnp.float32), token_index + offset)


def visible(query_member, query_index, key_member, key_index, ancestry):
    numbers = (((1,), (1,)), ((), ()))
    lifted = jnp.dot(query_member, ancestry, precision=PRECISE)
    above = lax.dot_general(lifted, key_member, numbers, precision=PRECISE)
    same_node = lax.dot_general(query_member, key_member, numbers, precision=PRECISE)
    return (above > 0.5) | (same_node > 0.5) & (key_index[None, :] <= query_index[:, None])


def product(left_side, right_side):
    return jnp.dot(left_side, right_side, preferred_element_type=jnp.float32)


def against(left_side, right_side):
    return lax.dot_general(
        left_side, right_side, (((1,), (1,)), ((), ())), preferred_element_type=jnp.float32
    )


def across(left_side, right_side):
    return lax.dot_general(
        left_side, right_side, (((0,), (0,)), ((), ())), preferred_element_type=jnp.float32
    )


def general_shards(
    tokens,
    cotangent,
    node_lengths,
    parents,
    w_query,
    w_key,
    w_value,
    w_output,
    w_gate,
    w_up,
    w_down,
    attn_gain,
    ffn_gain,
    query_gain,
    key_gain,
):
    rows_here = tokens.shape[2]
    length = lax.axis_size("seq") * rows_here
    group_size = HEADS // KV_HEADS
    pair_count = KV_HEADS // 2
    width_query = 2 * group_size * HEAD_DIM
    width_key = 2 * HEAD_DIM
    score_scale = HEAD_DIM ** (-0.5)
    local_index = lax.axis_index("seq") * rows_here + jnp.arange(rows_here, dtype=jnp.int32)
    full_index = jnp.arange(length, dtype=jnp.int32)
    pair_ids = jnp.arange(pair_count, dtype=jnp.int32)
    float_type = jnp.float32
    brain_type = jnp.bfloat16
    sums = (
        jnp.zeros((D, HEADS * HEAD_DIM), float_type),
        jnp.zeros((D, KV_HEADS * HEAD_DIM), float_type),
        jnp.zeros((D, KV_HEADS * HEAD_DIM), float_type),
        jnp.zeros((HEADS * HEAD_DIM, D), float_type),
        jnp.zeros((D, FF), float_type),
        jnp.zeros((D, FF), float_type),
        jnp.zeros((FF, D), float_type),
        jnp.zeros((D,), float_type),
        jnp.zeros((D,), float_type),
        jnp.zeros((HEAD_DIM,), float_type),
        jnp.zeros((HEAD_DIM,), float_type),
    )
    out_list = []
    grad_list = []
    for batch_index in range(MICRO):
        attn_fwd = (
            lax.all_gather(w_query, ("dp", "seq"), axis=0, tiled=True),
            lax.all_gather(w_key, ("dp", "seq"), axis=0, tiled=True),
            lax.all_gather(w_value, ("dp", "seq"), axis=0, tiled=True),
            lax.all_gather(w_output, ("dp", "seq"), axis=0, tiled=True),
            lax.all_gather(attn_gain, ("dp", "seq"), axis=0, tiled=True),
            lax.all_gather(query_gain, ("dp", "seq"), axis=0, tiled=True),
            lax.all_gather(key_gain, ("dp", "seq"), axis=0, tiled=True),
        )
        ffn_fwd = (
            lax.all_gather(w_gate, ("dp", "seq"), axis=0, tiled=True),
            lax.all_gather(w_up, ("dp", "seq"), axis=0, tiled=True),
            lax.all_gather(w_down, ("dp", "seq"), axis=0, tiled=True),
            lax.all_gather(ffn_gain, ("dp", "seq"), axis=0, tiled=True),
        )
        query_w, key_w, value_w, output_w, attn_g, query_g, key_g = attn_fwd
        gate_w, up_w, down_w, ffn_g = ffn_fwd
        labels, starts, path_base, ancestry = tree_tables(
            node_lengths[0, batch_index], parents[0, batch_index]
        )
        member_here, position = token_nodes(local_index, labels, starts, path_base)
        member_all, unused_position = token_nodes(full_index, labels, starts, path_base)
        keep_mask = visible(member_here, local_index, member_all, full_index, ancestry)
        cosine_table, sine_table = rope_tables(position, HEAD_DIM)
        rows_in = tokens[0, batch_index].astype(float_type)
        attn_g32 = attn_g.astype(float_type)
        query_g32 = query_g.astype(float_type)
        key_g32 = key_g.astype(float_type)
        normed_in = norm_rows(rows_in, attn_g32).astype(brain_type)
        query_heads = product(normed_in, query_w).reshape(rows_here, HEADS, HEAD_DIM)
        key_heads = product(normed_in, key_w).reshape(rows_here, KV_HEADS, HEAD_DIM)
        value_low = product(normed_in, value_w).astype(brain_type)
        query_rot = (
            rotate(norm_rows(query_heads, query_g32), cosine_table, sine_table)
            .astype(brain_type)
            .reshape(rows_here, HEADS * HEAD_DIM)
        )
        key_rot = (
            rotate(norm_rows(key_heads, key_g32), cosine_table, sine_table)
            .astype(brain_type)
            .reshape(rows_here, KV_HEADS * HEAD_DIM)
        )
        key_all, value_all = (
            lax.all_gather(key_rot, "seq", axis=0, tiled=True),
            lax.all_gather(value_low, "seq", axis=0, tiled=True),
        )

        def attend_pair(pair_id):
            query_pair = lax.dynamic_slice_in_dim(
                query_rot, pair_id * width_query, width_query, 1
            ).reshape(rows_here, 2, group_size, HEAD_DIM)
            key_pair = lax.dynamic_slice_in_dim(key_all, pair_id * width_key, width_key, 1).reshape(
                length, 2, HEAD_DIM
            )
            value_pair = lax.dynamic_slice_in_dim(
                value_all, pair_id * width_key, width_key, 1
            ).reshape(length, 2, HEAD_DIM)
            raw_score = jnp.einsum(
                "qhgd,khd->hgqk", query_pair, key_pair, preferred_element_type=jnp.float32
            )
            scores = jnp.where(keep_mask[None, None], raw_score * score_scale, NEGATIVE)
            row_top = jnp.max(scores, axis=-1, keepdims=True)
            weight = jnp.exp(scores - row_top)
            row_total = jnp.sum(weight, axis=-1, keepdims=True)
            soft_low = (weight / row_total).astype(jnp.bfloat16)
            mixed = jnp.einsum(
                "hgqk,khd->qhgd", soft_low, value_pair, preferred_element_type=jnp.float32
            )
            return (mixed, row_top + jnp.log(row_total))

        mixed_pairs, log_totals = lax.map(attend_pair, pair_ids)
        attended = (
            mixed_pairs.transpose(1, 0, 2, 3, 4)
            .reshape(rows_here, HEADS * HEAD_DIM)
            .astype(brain_type)
        )
        middle = rows_in + product(attended, output_w)
        ffn_g32 = ffn_g.astype(float_type)
        normed_mid = norm_rows(middle, ffn_g32).astype(brain_type)
        gate_lin = product(normed_mid, gate_w)
        up_lin = product(normed_mid, up_w)
        activated = (jax.nn.silu(gate_lin) * up_lin).astype(brain_type)
        out_list.append((middle + product(activated, down_w)).astype(brain_type))
        attn_back = (
            lax.all_gather(w_query, ("dp", "seq"), axis=0, tiled=True),
            lax.all_gather(w_key, ("dp", "seq"), axis=0, tiled=True),
            lax.all_gather(w_value, ("dp", "seq"), axis=0, tiled=True),
            lax.all_gather(w_output, ("dp", "seq"), axis=0, tiled=True),
            lax.all_gather(attn_gain, ("dp", "seq"), axis=0, tiled=True),
            lax.all_gather(query_gain, ("dp", "seq"), axis=0, tiled=True),
            lax.all_gather(key_gain, ("dp", "seq"), axis=0, tiled=True),
        )
        ffn_back = (
            lax.all_gather(w_gate, ("dp", "seq"), axis=0, tiled=True),
            lax.all_gather(w_up, ("dp", "seq"), axis=0, tiled=True),
            lax.all_gather(w_down, ("dp", "seq"), axis=0, tiled=True),
            lax.all_gather(ffn_gain, ("dp", "seq"), axis=0, tiled=True),
        )
        key_back, value_back = (
            lax.all_gather(key_rot, "seq", axis=0, tiled=True),
            lax.all_gather(value_low, "seq", axis=0, tiled=True),
        )
        query_wb, key_wb, value_wb, output_wb, attn_gb, query_gb, key_gb = attn_back
        gate_wb, up_wb, down_wb, ffn_gb = ffn_back
        cot_rows = cotangent[0, batch_index]
        grad_down = across(activated, cot_rows)
        d_activated = against(cot_rows, down_wb)
        sigma_gate = jax.nn.sigmoid(gate_lin)
        d_gate = (d_activated * up_lin * sigma_gate * (1.0 + gate_lin * (1.0 - sigma_gate))).astype(
            brain_type
        )
        d_up = (d_activated * gate_lin * sigma_gate).astype(brain_type)
        grad_gate = across(normed_mid, d_gate)
        grad_up = across(normed_mid, d_up)
        d_normed_mid = against(d_gate, gate_wb) + against(d_up, up_wb)
        unused_mid, pull_ffn = jax.vjp(norm_rows, middle, ffn_gb.astype(float_type))
        d_mid_norm, grad_ffn_gain = pull_ffn(d_normed_mid)
        d_middle = cot_rows.astype(float_type) + d_mid_norm
        d_middle_low = d_middle.astype(brain_type)
        grad_output = across(attended, d_middle_low)
        d_attended = against(d_middle_low, output_wb).astype(brain_type)

        def back_pair(pair_id):
            query_pair = lax.dynamic_slice_in_dim(
                query_rot, pair_id * width_query, width_query, 1
            ).reshape(rows_here, 2, group_size, HEAD_DIM)
            grad_pair = lax.dynamic_slice_in_dim(
                d_attended, pair_id * width_query, width_query, 1
            ).reshape(rows_here, 2, group_size, HEAD_DIM)
            key_pair = lax.dynamic_slice_in_dim(
                key_back, pair_id * width_key, width_key, 1
            ).reshape(length, 2, HEAD_DIM)
            value_pair = lax.dynamic_slice_in_dim(
                value_back, pair_id * width_key, width_key, 1
            ).reshape(length, 2, HEAD_DIM)
            raw_score = jnp.einsum(
                "qhgd,khd->hgqk", query_pair, key_pair, preferred_element_type=jnp.float32
            )
            scores = jnp.where(keep_mask[None, None], raw_score * score_scale, NEGATIVE)
            soft_prob = jnp.exp(scores - log_totals[pair_id])
            soft_low = soft_prob.astype(jnp.bfloat16)
            d_prob = jnp.einsum(
                "qhgd,khd->hgqk", grad_pair, value_pair, preferred_element_type=jnp.float32
            )
            d_score = soft_prob * (d_prob - jnp.sum(soft_prob * d_prob, axis=-1, keepdims=True))
            d_raw = (d_score * score_scale).astype(jnp.bfloat16)
            d_query = jnp.einsum(
                "hgqk,khd->qhgd", d_raw, key_pair, preferred_element_type=jnp.float32
            )
            d_key = jnp.einsum(
                "hgqk,qhgd->khd", d_raw, query_pair, preferred_element_type=jnp.float32
            )
            d_value = jnp.einsum(
                "hgqk,qhgd->khd", soft_low, grad_pair, preferred_element_type=jnp.float32
            )
            return (
                d_query,
                jnp.concatenate(
                    [d_key.reshape(length, width_key), d_value.reshape(length, width_key)], axis=1
                ),
            )

        d_query_pairs, kv_terms = lax.map(back_pair, pair_ids)
        kv_share = lax.psum_scatter(
            kv_terms.astype(jnp.bfloat16), "seq", scatter_dimension=1, tiled=True
        ).astype(jnp.float32)
        d_key_rot = (
            kv_share[:, :, :width_key]
            .reshape(pair_count, rows_here, 2, HEAD_DIM)
            .transpose(1, 0, 2, 3)
            .reshape(rows_here, KV_HEADS, HEAD_DIM)
        )
        d_value_low = (
            kv_share[:, :, width_key:]
            .transpose(1, 0, 2)
            .reshape(rows_here, KV_HEADS * HEAD_DIM)
            .astype(brain_type)
        )
        d_query_rot = d_query_pairs.transpose(1, 0, 2, 3, 4).reshape(rows_here, HEADS, HEAD_DIM)

        def turn_rows(heads_in, gain_in):
            return rotate(norm_rows(heads_in, gain_in), cosine_table, sine_table)

        unused_query, pull_query = jax.vjp(turn_rows, query_heads, query_gb.astype(float_type))
        d_query_heads, grad_query_gain = pull_query(d_query_rot)
        unused_key, pull_key = jax.vjp(turn_rows, key_heads, key_gb.astype(float_type))
        d_key_heads, grad_key_gain = pull_key(d_key_rot)
        d_query_low = d_query_heads.reshape(rows_here, HEADS * HEAD_DIM).astype(brain_type)
        d_key_low = d_key_heads.reshape(rows_here, KV_HEADS * HEAD_DIM).astype(brain_type)
        grad_query = across(normed_in, d_query_low)
        grad_key = across(normed_in, d_key_low)
        grad_value = across(normed_in, d_value_low)
        d_normed_in = (
            against(d_query_low, query_wb)
            + against(d_key_low, key_wb)
            + against(d_value_low, value_wb)
        )
        unused_in, pull_attn = jax.vjp(norm_rows, rows_in, attn_gb.astype(float_type))
        d_in_norm, grad_attn_gain = pull_attn(d_normed_in)
        grad_list.append(d_middle + d_in_norm)
        fresh = (
            grad_query,
            grad_key,
            grad_value,
            grad_output,
            grad_gate,
            grad_up,
            grad_down,
            grad_attn_gain,
            grad_ffn_gain,
            grad_query_gain,
            grad_key_gain,
        )
        sums = tuple((old + new for old, new in zip(sums, fresh)))
    attn_parts = (
        lax.psum_scatter(sums[0], ("dp", "seq"), scatter_dimension=0, tiled=True),
        lax.psum_scatter(sums[1], ("dp", "seq"), scatter_dimension=0, tiled=True),
        lax.psum_scatter(sums[2], ("dp", "seq"), scatter_dimension=0, tiled=True),
        lax.psum_scatter(sums[3], ("dp", "seq"), scatter_dimension=0, tiled=True),
        lax.psum_scatter(sums[7], ("dp", "seq"), scatter_dimension=0, tiled=True),
        lax.psum_scatter(sums[9], ("dp", "seq"), scatter_dimension=0, tiled=True),
        lax.psum_scatter(sums[10], ("dp", "seq"), scatter_dimension=0, tiled=True),
    )
    ffn_parts = (
        lax.psum_scatter(sums[4], ("dp", "seq"), scatter_dimension=0, tiled=True),
        lax.psum_scatter(sums[5], ("dp", "seq"), scatter_dimension=0, tiled=True),
        lax.psum_scatter(sums[6], ("dp", "seq"), scatter_dimension=0, tiled=True),
        lax.psum_scatter(sums[8], ("dp", "seq"), scatter_dimension=0, tiled=True),
    )
    outputs = jnp.stack(out_list)[None]
    input_grad = jnp.stack(grad_list)[None]
    return (
        outputs,
        input_grad,
        attn_parts[0],
        attn_parts[1],
        attn_parts[2],
        attn_parts[3],
        ffn_parts[0],
        ffn_parts[1],
        ffn_parts[2],
        attn_parts[4],
        ffn_parts[3],
        attn_parts[5],
        attn_parts[6],
    )


MESH = pl.DeviceIdType.MESH
NDP = 4
NSEQ = 8
BLOCKED = -65536.0
QB = 256
BLOCKS = (3, 2, 1, 0)
SOFT = HEAD_DIM ** (-0.5) * 1.4426950408889634

A0, A1, B, C0, C1, E0, E1, E2 = range(0, 80, 10)
R_A0, R_A1, R_B, R_C0, R_C1, R_E0, R_E1, R_E2 = range(80, 160, 10)
(
    ATTEND, MIX_MID, MIX_END, NORM_MID, NORM_END, LIFT, D_ACT, SINK, TURN_MID, TURN_END, LOW_MID,
    LOW_END, OUT_START, OUT_MID, OUT_END, ATTEND_BACK, IN_START, IN_MID, IN_END, PROJECT,
    GRAD_WIDE, GRAD_ATTN, TABLES, NORM_IN, COTANGENT,
) = range(200, 450, 10)
(
    START, TOKENS, SMALL_DP, SMALL_SEQ, A_IN, C_OUT, C_IN, TREE_START, COT_START, TREE_MID,
    COT_MID, COT_END, TREE_END, NODE, GAINS, GRAD_DOWN, GRAD_OUT, PACK_DP, PACK_SEQ, PACK_END,
    LAND_A, LAND_C, GIVE_OUT, GIVE_IN, DRAIN,
) = range(600, 625, 1)
ORDER = (
    START, B, SMALL_DP, E0, E2, E1, B + 1, E0 + 1, A_IN, A0, A1, B + 2, A0 + 1, A1 + 1, B + 3, A0 + 2, A1 + 2,
    B + 4, TOKENS, A1 + 3, C_OUT, A0 + 3, B + 5, TREE_START, A1 + 4, A0 + 4, B + 6, A1 + 5, SMALL_SEQ, A0 + 5,
    NODE, C_IN, C0, TABLES, TABLES + 1, A1 + 6, A0 + 6, E2 + 1, C1, GAINS, TREE_MID, C0 + 1, B + 7, COTANGENT,
    COTANGENT + 1, A1 + 7, TREE_END, NORM_IN, A0 + 7, NORM_IN + 1, PROJECT, PROJECT + 1, E2 + 2, PROJECT + 2,
    PROJECT + 3, ATTEND + 3, C1 + 1, ATTEND + 2, C0 + 2, MIX_MID + 3, MIX_MID + 2, E1 + 1, ATTEND + 1, C1 + 2,
    E0 + 2, E2 + 3, MIX_MID + 1, MIX_END + 3, C0 + 3, ATTEND, C1 + 3, E1 + 2, MIX_MID, MIX_END + 2, C0 + 4,
    C1 + 4, NORM_MID + 3, E1 + 3, MIX_END + 1, MIX_END, C0 + 5, C1 + 5, COT_START, E0 + 3, NORM_MID + 1,
    C0 + 6, C1 + 6, NORM_MID + 2, E1 + 4, E2 + 4, NORM_END + 2, NORM_MID, NORM_END + 1, NORM_END,
    NORM_END + 3, E0 + 4, C0 + 7, C1 + 7, LIFT + 2, E1 + 5, E2 + 5, E0 + 5, LIFT, LIFT + 1, E1 + 6, COT_MID,
    E0 + 6, E2 + 6, LIFT + 3, COT_END, GRAD_DOWN, R_E0, E2 + 7, E1 + 7, R_E2, R_E1, E0 + 7, D_ACT + 1,
    D_ACT + 2, R_E2 + 1, D_ACT + 3, R_E0 + 1, R_E1 + 1, D_ACT, GRAD_WIDE, R_C0, SINK + 3, R_E2 + 2, SINK + 2,
    TURN_MID + 3, R_E0 + 2, R_E1 + 2, SINK, R_C0 + 1, TURN_MID + 2, R_E2 + 3, GRAD_WIDE + 1, R_C1,
    TURN_END + 3, R_C0 + 2, R_E1 + 3, SINK + 1, TURN_MID, TURN_END + 2, R_C1 + 1, OUT_START + 3, R_E0 + 3,
    OUT_START + 2, R_E2 + 4, LOW_MID + 3, R_C0 + 3, TURN_MID + 1, R_E1 + 4, LOW_END + 3, TURN_END, R_C1 + 2,
    ATTEND_BACK + 3, R_E2 + 5, LOW_MID + 2, R_C0 + 4, R_E1 + 5, TURN_END + 1, R_E0 + 4, R_C1 + 3, LOW_END + 2,
    ATTEND_BACK + 2, R_C0 + 5, LOW_MID + 1, LOW_MID, R_E0 + 5, R_E2 + 6, IN_START + 2, IN_START + 3,
    OUT_MID + 2, LOW_END + 1, R_C1 + 4, LOW_END, GRAD_OUT, R_B, R_C0 + 6, ATTEND_BACK + 1, R_C1 + 5,
    IN_START + 1, R_E1 + 6, R_E0 + 6, R_B + 1, ATTEND_BACK, R_C1 + 6, IN_START, GRAD_ATTN + 1, R_A1,
    GRAD_ATTN, R_A0, IN_MID + 3, R_B + 2, R_C1 + 7, R_A1 + 1, IN_MID, R_A0 + 1, R_B + 3, R_A1 + 2, IN_MID + 1,
    R_A0 + 2, OUT_START + 1, R_B + 4, IN_MID + 2, OUT_START, R_A1 + 3, OUT_MID + 3, OUT_MID + 1, R_A0 + 3,
    R_B + 5, OUT_MID, R_A1 + 4, IN_END, R_A0 + 4, IN_END + 3, R_B + 6, IN_END + 2, R_E1 + 7, R_A1 + 5,
    IN_END + 1, R_A0 + 5, PACK_DP, GIVE_IN, R_A1 + 6, OUT_END + 2, PACK_SEQ, R_C0 + 7, R_B + 7, OUT_END,
    LAND_C, R_E0 + 7, OUT_END + 1, R_A0 + 6, OUT_END + 3, GIVE_OUT, R_A1 + 7, R_A0 + 7, R_E2 + 7, PACK_END,
    LAND_A, DRAIN,
)


def seq_at(position):
    half = position // 4
    z = position + half * (7 - 2 * position)
    return 2 * z + half


def tree_seat(d, m):
    x, c = d // 2, d % 2
    return 2 * (2 * m + c) + (m + c + x) % 2


def greet_near(d, s, up, down):
    barrier = pltpu.get_barrier_semaphore()
    near = [((d + i) % NDP, s) for i in range(1, NDP)] + [(d, up), (d, down)]
    for other in near:
        pl.semaphore_signal(barrier, inc=1, device_id=other, device_id_type=MESH)
    pl.semaphore_wait(barrier, len(near))


def remote(src, dst, sems, at, d, s):
    send, recv = sems
    return pltpu.make_async_remote_copy(
        src_ref=src,
        dst_ref=dst,
        send_sem=send.at[at],
        recv_sem=recv.at[at],
        device_id=(d, s),
        device_id_type=MESH,
    )


class Sum:
    def __init__(self, part, near, sent, got, sems, n, spot):
        self.part, self.near, self.sent, self.got = part, near, sent, got
        self.sems, self.n = sems, n
        d, self.s = spot
        x, c = d // 2, d % 2
        self.d, self.sib, self.far = d, 2 * x + 1 - c, 2 * (1 - x) + c
        self.far_sib = 2 * (1 - x) + 1 - c

    def copies(self, b):
        rows = pl.ds(2 * b, 2)
        return (
            remote(self.part.at[rows, self.far_sib], self.near.at[0, rows], self.sems, (self.n, 0, b), self.sib, self.s),
            remote(self.part.at[rows, self.sib], self.near.at[1, rows], self.sems, (self.n, 1, b), self.sib, self.s),
            remote(self.sent.at[rows], self.got.at[rows], self.sems, (self.n, 2, b), self.far, self.s),
        )

    def start(self, b):
        first, second, _ = self.copies(b)
        first.start()
        second.start()

    def mid(self, b):
        first, _, across_x = self.copies(b)
        first.wait_recv()

        def join(i, carry):
            self.sent[i] = (
                self.part[i, self.far].astype(jnp.float32) + self.near[0, i].astype(jnp.float32)
            ).astype(jnp.bfloat16)
            return carry

        lax.fori_loop(2 * b, 2 * b + 2, join, 0)
        across_x.start()

    def end(self, b, finish):
        first, second, across_x = self.copies(b)
        second.wait_recv()
        across_x.wait_recv()

        def close(i, carry):
            rows = self.part[i, self.d].astype(jnp.float32) + self.near[1, i].astype(jnp.float32)
            finish(i, rows + self.got[i].astype(jnp.float32))
            return carry

        lax.fori_loop(2 * b, 2 * b + 2, close, 0)
        first.wait_send()
        second.wait_send()
        across_x.wait_send()


class Spread:
    def __init__(self, out, sems, at, spot):
        self.out, self.sems, self.place = out, sems, at
        d, self.s = spot
        x, c = d // 2, d % 2
        self.d, self.sib, self.far = d, 2 * x + 1 - c, 2 * (1 - x) + c
        self.far_sib = 2 * (1 - x) + 1 - c

    def copy(self, rows, owner, way, to):
        block = self.out.at[rows, owner]
        return remote(block, block, self.sems, self.place(way, rows), to, self.s)

    def start(self, rows):
        self.copy(rows, self.d, 0, self.far).start()
        self.copy(rows, self.d, 1, self.sib).start()

    def mid(self, rows):
        self.copy(rows, self.far, 0, self.far).wait_recv()
        self.copy(rows, self.far, 2, self.sib).start()

    def end(self, rows):
        self.copy(rows, self.sib, 1, self.sib).wait_recv()
        self.copy(rows, self.far_sib, 2, self.sib).wait_recv()

    def sent(self, rows):
        self.copy(rows, self.d, 0, self.far).wait_send()
        self.copy(rows, self.d, 1, self.sib).wait_send()
        self.copy(rows, self.far, 2, self.sib).wait_send()


def layer_kernel(
    nodes,
    tok, cot, lengths, parents, gain_a, gain_f, gain_q, gain_k, inv_freq, wq, wk, wv, wo, wg, wu, wd,
    out_rows, grad_rows, res_a, res_c, g_output, g_down, pack_out,
    raw_lengths, raw_parents, raw_a, raw_f, raw_q, raw_k, smalls, wa, wb, wc, we, gc, ge, hop_a, hop_b, hop_c, hop_e,
    tree, tree_cot, normed_in, normed_mid, d_low, tree_own,
    lin, heads, value, hidden, member, cosine, sine, att, d_att,
    part, part_out, near, sent, got, near_o, sent_o, got_o,
    middle, d_middle, act, both, d_key, d_value, outs, grad_low,
    fin_a, fin_c, attn_g, ffn_g, head_g, packed, pack_dp, pack_seq, pack_sum, pack_cut,
    loc, s_small, r_small, s_col, r_col, s_tok, r_tok, s_ag, r_ag, s_rs, r_rs,
    s_sum, r_sum, s_tree, r_tree, s_spread, r_spread, s_back, r_back, s_fin, r_fin, s_pack, r_pack,
):
    f32, bf = jnp.float32, jnp.bfloat16
    d = lax.axis_index("dp")
    s = lax.axis_index("seq")
    z, y = s // 2, s % 2
    p = z + y * (7 - 2 * z)
    spot = (d, s)
    seat = [seq_at((p + i) % NSEQ) for i in range(NSEQ)]
    up, down = seat[1], seat[7]
    ag_sems, rs_sems = (s_ag, r_ag), (s_rs, r_rs)
    small_sems, col_sems, tok_sems = (s_small, r_small), (s_col, r_col), (s_tok, r_tok)

    def aligned(v, n):
        return pl.multiple_of(v, n)

    def chunk(n, way, j):
        if n in (0, 1, 3, 4):
            return pl.ds(aligned((2 * way + (n + (n > 2)) % 2) * 256 + j * 32, 32), 32)
        if n == 2:
            return pl.ds(aligned(j * 64 + way * 32, 32), 32)
        return pl.ds(aligned(j * 96 + way * 48 + (n - 5) * 16, 16), 16)

    weight = {0: wa, 1: wa, 2: wb, 3: wc, 4: wc, 5: we, 6: we, 7: we}
    grads = {0: wa, 1: wa, 2: wb, 3: gc, 4: gc, 5: ge, 6: ge, 7: ge}
    hops = {0: hop_a.at[0], 1: hop_a.at[1], 2: hop_b, 3: hop_c.at[0], 4: hop_c.at[1]}
    hops.update({5 + i: hop_e.at[i] for i in range(3)})

    def owner_at(way, k):
        return seq_at((p + NSEQ - k) % NSEQ) if way == 0 else seq_at((p + k) % NSEQ)

    def gather(n, k):
        for way, peer in enumerate((up, down)):
            block = weight[n].at[chunk(n, way, owner_at(way, k))]
            if not (isinstance(k, int) and k == 0):
                remote(block, block, ag_sems, (n, way, k - 1), d, peer).wait_recv()
            remote(block, block, ag_sems, (n, way, k), d, peer).start()

    def gather_end(n):
        for way, peer in enumerate((up, down)):
            block = weight[n].at[chunk(n, way, owner_at(way, 7))]
            remote(block, block, ag_sems, (n, way, 6), d, peer).wait_recv()

    def gather_sent(n):
        for way, peer in enumerate((up, down)):
            block = weight[n].at[chunk(n, way, s)]
            for k in range(7):
                remote(block, block, ag_sems, (n, way, k), d, peer).wait_send()

    def add_rows(into, other):
        def one(i, carry):
            at = pl.ds(aligned(i * 16, 16), 16)
            into[at] = (into[at].astype(f32) + other[at].astype(f32)).astype(bf)
            return carry

        lax.fori_loop(0, into.shape[0] // 16, one, 0)

    def reduce_(n, k):
        for way, peer in enumerate((up, down)):
            rows = chunk(n, way, seat[(7 - k) % NSEQ] if way == 0 else seat[(1 + k) % NSEQ])
            mine = grads[n].at[rows]
            if k == 0:
                src = mine
            else:
                src = hops[n].at[way, k - 1]
                remote(src, src, rs_sems, (n, way, k - 1), d, peer).wait_recv()
                add_rows(src, mine)
            remote(src, hops[n].at[way, k], rs_sems, (n, way, k), d, peer).start()

    def reduce_end(n, take):
        for way, peer in enumerate((up, down)):
            src = hops[n].at[way, 6]
            remote(src, src, rs_sems, (n, way, 6), d, peer).wait_recv()
            take(way, src[...].astype(f32) + grads[n][chunk(n, way, s)].astype(f32))

    def reduce_sent(n):
        for way, peer in enumerate((up, down)):
            for k in range(7):
                src = hops[n].at[way, k]
                remote(src, src, rs_sems, (n, way, k), d, peer).wait_send()

    ops = {}
    tree_slot, tree_core = z // 2, z % 2
    tree_owner = 2 * ((y + tree_slot + tree_core) % 2) + tree_core
    pending = []
    held = {}

    def stage(name):
        def keep(run):
            ops[name] = run
            return run

        return keep

    def launch(cp):
        cp.start()
        pending.append(cp)

    raws = [
        pltpu.make_async_copy(src, dst, loc.at[9 + n])
        for n, (src, dst) in enumerate(
            (
                (lengths, raw_lengths), (parents, raw_parents),
                (gain_a, raw_a), (gain_f, raw_f), (gain_q, raw_q), (gain_k, raw_k),
            )
        )
    ]
    pieces = (
        (wq, wa, 512, 0), (wk, wa, 256, 512), (wv, wa, 256, 768), (wg, wc, 768, 0), (wu, wc, 768, 768)
    )
    col_rows = lambda q: pl.ds(aligned(q * 256 + s * 32, 32), 32)

    def column_copy(n):
        src, dst, width, at = pieces[n]
        return pltpu.make_async_copy(
            src.at[:, pl.ds(aligned(d * width, 128), width)],
            dst.at[col_rows(d), pl.ds(at, width)],
            loc.at[2 + n],
        )

    def columns(n):
        src, dst, width, at = pieces[n]
        for i in range(1, NDP):
            q = (d + i) % NDP
            launch(
                remote(
                    src.at[:, pl.ds(aligned(q * width, 128), width)],
                    dst.at[col_rows(d), pl.ds(at, width)],
                    col_sems, (n, i), q, s,
                )
            )
        column_copy(n).start()

    def columns_in(n):
        _, dst, width, at = pieces[n]
        column_copy(n).wait()
        for i in range(1, NDP):
            place = dst.at[col_rows((d + NDP - i) % NDP), pl.ds(at, width)]
            remote(place, place, col_sems, (n, i), d, s).wait_recv()

    def row_copy(n, m, i):
        src, dst = ((tok, tree), (cot, tree_cot))[n]
        q = (d + i) % NDP
        return pltpu.make_async_remote_copy(
            src_ref=src.at[m, pl.ds(aligned(q * 32, 32), 32)],
            dst_ref=dst.at[s, q],
            send_sem=s_tok.at[n, m, i],
            recv_sem=r_tok.at[n],
            device_id=(q, tree_seat(d, m)),
            device_id_type=MESH,
        )

    def rows_out(n, half):
        src, dst = ((tok, tree), (cot, tree_cot))[n]
        for m in range(MICRO):
            if half == 0:
                target = tree_seat(d, m)

                @pl.when(target == s)
                def _():
                    piece = src.at[m, pl.ds(aligned(d * 32, 32), 32)]
                    pltpu.make_async_copy(piece, dst.at[s, d], r_tok.at[n]).start()

                @pl.when(target != s)
                def _():
                    row_copy(n, m, 0).start()

                row_copy(n, m, 1).start()
            else:
                row_copy(n, m, 2).start()
                row_copy(n, m, 3).start()

    def rows_in(dst, n):
        everything = dst.at[:, d]
        pltpu.make_async_copy(everything, everything, r_tok.at[n]).wait()

    fill_b = pltpu.make_async_copy(wo, wb.at[pl.ds(aligned(s * 64, 64), 64)], loc.at[7])
    fill_e = pltpu.make_async_copy(wd, we.at[pl.ds(aligned(s * 96, 16), 96)], loc.at[15])

    @stage(START)
    def _():
        for cp in raws:
            cp.start()
        greet_near(d, s, up, down)
        fill_b.start()
        fill_e.start()
        for n in range(3):
            columns(n)

    @stage(TOKENS)
    def _():
        rows_out(0, 0)
        rows_out(0, 1)

    for i in range(2):
        stage(COTANGENT + i)(functools.partial(rows_out, 1, i))


    @stage(SMALL_DP)
    def _():
        for cp in raws:
            cp.wait()
        for row, ref in enumerate((raw_a, raw_f, raw_q, raw_k)):
            count = ref.shape[0]
            line = ref[...].astype(f32).reshape(1, count)
            smalls[d, s, row : row + 1, :] = jnp.concatenate([line] * (128 // count), axis=1)
        smalls[d, s, 4:8, :] = jnp.zeros((4, 128), f32)
        smalls[d, s, 4:6, 0:nodes] = raw_lengths[0].astype(f32)
        smalls[d, s, 6:8, 0:nodes] = raw_parents[0].astype(f32)
        for i in range(1, NDP):
            launch(remote(smalls.at[d, s], smalls.at[d, s], small_sems, i, (d + i) % NDP, s))

    @stage(SMALL_SEQ)
    def _():
        for i in range(1, NDP):
            place = smalls.at[(d + NDP - i) % NDP, s]
            remote(place, place, small_sems, i, d, s).wait_recv()
        lane = lax.broadcasted_iota(jnp.int32, (1, 128), 1)
        for q in range(NDP):
            rows = [smalls[q, s, row : row + 1, :] for row in range(4)]
            tail = jnp.where(lane < 68, rows[2], rows[3])
            packed[s, q : q + 1, :] = jnp.where(lane < 32, rows[0], jnp.where(lane < 64, rows[1], tail))
            packed[s, q + 4 : q + 5, :] = jnp.zeros((1, 128), f32)
        for i in range(1, NSEQ):
            launch(remote(packed.at[s], packed.at[s], small_sems, NDP + i, d, (s + i) % NSEQ))

    @stage(A_IN)
    def _():
        for n in range(3):
            columns_in(n)

    @stage(C_OUT)
    def _():
        for n in range(3, 5):
            columns(n)

    @stage(C_IN)
    def _():
        for n in range(3, 5):
            columns_in(n)

    streams = ((A0, 0), (A1, 1), (B, 2), (C0, 3), (C1, 4), (E0, 5), (E1, 6), (E2, 7))

    def ring_first(n):
        if n == 2:
            fill_b.wait()
        if n == 5:
            fill_e.wait()
        gather(n, 0)

    for label, n in streams:
        stage(label)(functools.partial(ring_first, n))
        stage(label + 7)(functools.partial(gather_end, n))
        for k in range(1, 7):
            stage(label + k)(functools.partial(gather, n, k))
        for k in range(7):
            stage(R_A0 + label + k)(functools.partial(reduce_, n, k))

    everything = pl.ds(0, NSEQ)
    spread_tree = Spread(tree, (s_tree, r_tree), lambda way, rows: (0, way), spot)
    spread_cot = Spread(tree_cot, (s_tree, r_tree), lambda way, rows: (1, way), spot)

    @stage(TREE_START)
    def _():
        rows_in(tree, 0)
        spread_tree.start(everything)

    @stage(COT_START)
    def _():
        rows_in(tree_cot, 1)
        spread_cot.start(everything)

    stage(TREE_MID)(lambda: spread_tree.mid(everything))
    stage(COT_MID)(lambda: spread_cot.mid(everything))
    stage(COT_END)(lambda: spread_cot.end(everything))
    own_rows = pltpu.make_async_copy(tree.at[:, d], tree_own, loc.at[8])

    @stage(TREE_END)
    def _():
        spread_tree.end(everything)
        own_rows.start()

    @stage(NODE)
    def _():
        ir = lax.broadcasted_iota(jnp.int32, (128, 128), 0)
        ic = lax.broadcasted_iota(jnp.int32, (128, 128), 1)
        block = smalls.at[tree_owner, s]
        length_row = block[pl.ds(4 + tree_slot, 1), :]
        parent_row = block[pl.ds(6 + tree_slot, 1), :]
        length_col = jnp.sum(jnp.where(ir == ic, length_row, 0.0), axis=1, keepdims=True)
        over = (parent_row == ir.astype(f32)) & (ic > 0) & (ic < nodes)
        above = jnp.where(over | (ir == ic), 1.0, 0.0)
        for _ in range(4):
            low = above.astype(bf)
            above = jnp.minimum(product(low, low), 1.0)
        start_row = jnp.sum(jnp.where(ir < ic, length_col, 0.0), axis=0, keepdims=True)
        base_row = jnp.sum(
            jnp.where((above > 0.5) & (ir != ic), length_col, 0.0), axis=0, keepdims=True
        )
        shut = jnp.where(above > 0.5, 0.0, BLOCKED).astype(bf)
        held["node"] = (start_row, start_row + length_row, base_row - start_row, shut)

    def tables(i, carry):
        start_row, end_row, offset_row, shut = held["node"]
        rows = pl.ds(aligned(i * QB, QB), QB)
        index = (lax.broadcasted_iota(jnp.int32, (QB, 128), 0) + i * QB).astype(f32)
        inside = (index >= start_row) & (index < end_row)
        position = index[:, :1] + jnp.sum(
            jnp.where(inside, offset_row, 0.0), axis=1, keepdims=True
        )
        hot = jnp.where(inside, 1.0, 0.0).astype(bf)
        member[rows] = hot
        hidden[rows] = against(hot, shut).astype(bf)
        angle = position * inv_freq[...]
        cosine[rows] = jnp.cos(angle)
        lane = lax.broadcasted_iota(jnp.int32, (QB, 128), 1)
        wave = jnp.sin(angle)
        sine[rows] = jnp.where(lane < 64, -wave, wave)
        return carry

    stage(TABLES + 0)(lambda: lax.fori_loop(0, 2, tables, 0))
    stage(TABLES + 1)(lambda: lax.fori_loop(2, 4, tables, 0))

    @stage(GAINS)
    def _():
        for i in range(1, NSEQ):
            place = packed.at[(s + NSEQ - i) % NSEQ]
            remote(place, place, small_sems, NDP + i, d, s).wait_recv()
        lane = lax.broadcasted_iota(jnp.int32, (1, 128), 1)

        def moved(i, source, target):
            line = packed[i % NSEQ, i // NSEQ : i // NSEQ + 1, :]
            shift = (target - source) % 128
            return pltpu.roll(line, shift, 1) if shift else line

        for source, dst in ((0, attn_g), (32, ffn_g)):
            for j in range(8):
                parts = [moved(4 * j + i, source, 32 * i) for i in range(4)]
                dst[:, 128 * j : 128 * (j + 1)] = jnp.where(
                    lane < 64,
                    jnp.where(lane < 32, parts[0], parts[1]),
                    jnp.where(lane < 96, parts[2], parts[3]),
                )
        for row in range(2):
            joined = jnp.zeros((1, 128), f32)
            for i in range(32):
                joined = jnp.where(lane // 4 == i, moved(i, 64 + 4 * row, 4 * i), joined)
            head_g[row : row + 1, :] = joined
        pack_dp[d] = jnp.zeros((24, 128), f32)

    def norm_in(i, carry):
        rows = tree[i].reshape(128, D).astype(f32)
        scale = lax.rsqrt(jnp.mean(rows * rows, axis=-1, keepdims=True) + EPSILON)
        normed_in[pl.ds(aligned(i * 128, 128), 128)] = (rows * scale * attn_g[...]).astype(bf)
        return carry

    stage(NORM_IN + 0)(lambda: lax.fori_loop(0, 4, norm_in, 0))
    stage(NORM_IN + 1)(lambda: lax.fori_loop(4, 8, norm_in, 0))

    def unit_of(v):
        scale = lax.rsqrt(jnp.mean(v * v, axis=-1, keepdims=True) + EPSILON)
        return v * scale, scale

    def turn(v, gain, cos, sin):
        unit, _ = unit_of(v)
        lifted = unit * gain
        return lifted * cos + pltpu.roll(lifted, 64, 1) * sin

    def turn_back(dr, v, gain, cos, sin):
        d_lift = dr * cos + pltpu.roll(dr * sin, 64, 1)
        unit, scale = unit_of(v)
        d_unit = d_lift * gain
        return (
            scale * (d_unit - unit * jnp.mean(unit * d_unit, axis=-1, keepdims=True)),
            jnp.sum(d_lift * unit, axis=0, keepdims=True),
        )

    def project(i):
        rows = pl.ds(i * QB, QB)
        cos, sin = cosine[rows], sine[rows]

        def one(j, carry):
            lanes = pl.ds(aligned(j * 256, 256), 256)
            pair = product(normed_in[rows], wa[:, lanes])
            lin[rows, lanes] = pair
            gain = head_g[pl.ds(j // 2, 1), :]
            for i2 in range(2):
                turned = turn(pair[:, 128 * i2 : 128 * (i2 + 1)], gain, cos, sin)
                heads[2 * j + i2, rows] = turned.astype(bf)
            return carry

        lax.fori_loop(0, 3, one, 0)
        value[rows] = product(normed_in[rows], wa[:, 768:]).astype(bf)

    for i in range(4):
        stage(PROJECT + i)(functools.partial(project, i))

    def span(b):
        return pl.ds(b * QB, QB), (b + 1) * QB

    def weights_of(b, h, n):
        here = pl.ds(b * QB, QB)
        q = jnp.concatenate([heads[h, here], hidden[here]], axis=1)
        k = jnp.concatenate([heads[4 + h // 2, pl.ds(0, n)], member[pl.ds(0, n)]], axis=1)
        score = against(q, k) * SOFT
        row = lax.broadcasted_iota(jnp.int32, (QB, QB), 0)
        col = lax.broadcasted_iota(jnp.int32, (QB, QB), 1)
        diag = jnp.where(col <= row, score[:, n - QB :], NEGATIVE)
        score = diag if b == 0 else jnp.concatenate([score[:, : n - QB], diag], axis=1)
        grown = jnp.exp2(score)
        return grown, 1.0 / jnp.sum(grown, axis=-1, keepdims=True)

    def head_lanes(h):
        return pl.ds(aligned(h * HEAD_DIM, HEAD_DIM), HEAD_DIM)

    sum_sems, spread_sems = (s_sum, r_sum), (s_spread, r_spread)
    mixed_sum = Sum(part, near, sent, got, sum_sems, 0, spot)
    mid_sum = Sum(part, near, sent, got, sum_sems, 1, spot)
    out_sum = Sum(part_out, near_o, sent_o, got_o, sum_sems, 2, spot)
    in_sum = Sum(part, near, sent, got, sum_sems, 3, spot)
    pair_of = {b: pl.ds(2 * b, 2) for b in BLOCKS}
    spread_mid = Spread(normed_mid, spread_sems, lambda way, rows: (0, way, rows.start // 2), spot)
    spread_low = Spread(d_low, spread_sems, lambda way, rows: (1, way, rows.start // 2), spot)

    def attend(b):
        here, n = span(b)
        if b == BLOCKS[0]:
            own_rows.wait()

        def one(h, carry):
            grown, inverse = weights_of(b, h, n)
            mixed = product(grown.astype(bf), value[pl.ds(0, n), head_lanes(h // 2)])
            att[here, head_lanes(h)] = (mixed * inverse).astype(bf)
            return carry

        lax.fori_loop(0, HEADS // NDP, one, 0)
        rows = product(att[here], wb[...]).astype(bf)
        part[pair_of[b]] = rows.reshape(2, NDP, 32, D)
        mixed_sum.start(b)

    def to_middle(i, rows):
        rows = rows + tree_own[i].astype(f32)
        middle[i] = rows
        scale = lax.rsqrt(jnp.mean(rows * rows, axis=-1, keepdims=True) + EPSILON)
        normed_mid[i, d] = (rows * scale * ffn_g[...]).astype(bf)

    def close_mixed(b):
        mixed_sum.end(b, to_middle)
        spread_mid.start(pair_of[b])

    def lift(b):
        here = pl.ds(b * QB, QB)
        rows = normed_mid[pair_of[b]].reshape(QB, D)

        def one(t, carry):
            left = pl.ds(aligned(t * 256, 256), 256)
            right = pl.ds(aligned(768 + t * 256, 256), 256)
            gate = product(rows, wc[:, left])
            wide = product(rows, wc[:, right])
            sigma = 0.5 + 0.5 * jnp.tanh(0.5 * gate)
            silu = gate * sigma
            act[here, left] = (silu * wide).astype(bf)
            both[here, left] = (wide * sigma * (1.0 + gate * (1.0 - sigma))).astype(bf)
            both[here, right] = silu.astype(bf)
            return carry

        lax.fori_loop(0, 3, one, 0)

    @stage(GRAD_DOWN)
    def _():
        def one(i, carry):
            cols = pl.ds(aligned(i * 256, 256), 256)
            ge[cols] = across(act[:, cols], tree_cot[...].reshape(NSEQ * 128, D)).astype(bf)
            return carry

        lax.fori_loop(0, 3, one, 0)

    def d_activate(b):
        here = pl.ds(b * QB, QB)
        cots = tree_cot[pair_of[b]].reshape(QB, D)

        def one(t, carry):
            left = pl.ds(aligned(t * 256, 256), 256)
            right = pl.ds(aligned(768 + t * 256, 256), 256)
            d_act = against(cots, we[left])
            both[here, left] = (d_act * both[here, left].astype(f32)).astype(bf)
            both[here, right] = (d_act * both[here, right].astype(f32)).astype(bf)
            return carry

        lax.fori_loop(0, 3, one, 0)

    def sink(b):
        here = pl.ds(b * QB, QB)
        part[pair_of[b]] = against(both[here], wc[...]).astype(bf).reshape(2, NDP, 32, D)
        mid_sum.start(b)

    def settle(b):
        here = pl.ds(b * QB, QB)
        part_out[pair_of[b]] = product(act[here], we[...]).astype(bf).reshape(2, NDP, 32, D)
        out_sum.start(b)

    def to_turn(i, rows):
        unit, scale = unit_of(middle[i])
        lifted = ffn_g[...] * rows
        term = jnp.sum(rows * unit, axis=0, keepdims=True)
        for j in range(8):
            pack_dp[d, 8 + j : 9 + j] += term[:, 128 * j : 128 * (j + 1)]
        d_mid = tree_cot[i, d].astype(f32) + scale * (
            lifted - unit * jnp.mean(unit * lifted, axis=-1, keepdims=True)
        )
        d_middle[i] = d_mid
        d_low[i, d] = d_mid.astype(bf)

    def close_mid(b):
        mid_sum.end(b, to_turn)
        spread_low.start(pair_of[b])

    def to_outs(i, rows):
        outs[i] = (middle[i] + rows).astype(bf)

    back_owner, back_slot = tree_owner, tree_slot
    back = ((outs, out_rows), (grad_low, grad_rows))

    def give_copy(n, j):
        src, dst = back[n]
        return pltpu.make_async_remote_copy(
            src_ref=src.at[j],
            dst_ref=dst.at[back_slot, pl.ds(aligned(d * 32, 32), 32)],
            send_sem=s_back.at[n, j],
            recv_sem=r_back.at[n],
            device_id=(back_owner, j),
            device_id_type=MESH,
        )

    def give(n):
        src, dst = back[n]

        def one(j, carry):
            same = (back_owner == d) & (s == j)

            @pl.when(same)
            def _():
                place = dst.at[back_slot, pl.ds(aligned(d * 32, 32), 32)]
                pltpu.make_async_copy(src.at[j], place, r_back.at[n]).start()

            @pl.when(jnp.logical_not(same))
            def _():
                give_copy(n, j).start()

            return carry

        lax.fori_loop(0, NSEQ, one, 0)

    def close_out(b):
        out_sum.end(b, to_outs)

    def grad_wide(sub):
        for i in (sub, 2 + sub):
            cols = pl.ds(i * 256, 256)

            rows = normed_mid[:, :, :, cols].reshape(NSEQ * 128, 256)
            gc[cols] = across(rows, both[...]).astype(bf)

    d_lin = tree

    def close_low(b):
        spread_low.end(pair_of[b])
        here = pl.ds(b * QB, QB)
        rows = d_low[pair_of[b]].reshape(QB, D)
        d_att[here] = against(rows, wb[...]).astype(bf)

    def attend_back(b):
        here, n = span(b)
        keys = pl.ds(0, n)
        if b == BLOCKS[0]:
            spread_tree.sent(everything)
            d_key[...] = jnp.zeros_like(d_key)
            d_value[...] = jnp.zeros_like(d_value)

        def one(h, carry):
            kv = h // 2
            grown, inverse = weights_of(b, h, n)
            d_out = d_att[here, head_lanes(h)]
            wide_out = d_out.astype(f32)
            d_prob = against(d_out, value[keys, head_lanes(kv)])
            delta = jnp.sum(wide_out * att[here, head_lanes(h)].astype(f32), axis=-1, keepdims=True)
            d_raw = (grown * (d_prob - delta)).astype(bf)
            factor = inverse * HEAD_DIM ** (-0.5)
            d_rot = product(d_raw, heads[4 + kv, keys]) * factor
            d_key[kv, keys] += across(d_raw, (heads[h, here].astype(f32) * factor).astype(bf))
            d_value[kv, keys] += across(grown.astype(bf), (wide_out * inverse).astype(bf))
            back, d_gain = turn_back(
                d_rot, lin[here, head_lanes(h)], head_g[0:1, :], cosine[here], sine[here]
            )
            pack_dp[d, 16:17] += d_gain
            d_lin[pair_of[b], :, :, head_lanes(h)] = back.astype(bf).reshape(2, NDP, 32, HEAD_DIM)
            return carry

        lax.fori_loop(0, HEADS // NDP, one, 0)
        for kv in range(KV_HEADS // NDP):
            at = 512 + 128 * kv
            back, d_gain = turn_back(
                d_key[kv, here], lin[here, pl.ds(at, 128)], head_g[1:2, :], cosine[here], sine[here]
            )
            pack_dp[d, 17:18] += d_gain
            d_lin[pair_of[b], :, :, pl.ds(at, 128)] = back.astype(bf).reshape(2, NDP, 32, 128)
            d_lin[pair_of[b], :, :, pl.ds(at + 256, 128)] = (
                d_value[kv, here].astype(bf).reshape(2, NDP, 32, 128)
            )

    def sink_in(b):
        rows = against(d_lin[pair_of[b]].reshape(QB, 1024), wa[...])
        part[pair_of[b]] = rows.astype(bf).reshape(2, NDP, 32, D)
        in_sum.start(b)

    @stage(GRAD_OUT)
    def _():
        gather_sent(2)
        for i in range(2):
            cols = pl.ds(256 * i, 256)
            wb[cols] = across(att[:, cols], d_low[...].reshape(NSEQ * 128, D)).astype(bf)

    def grad_attn(sub):
        gather_sent(sub)
        for i in (sub, 2 + sub):
            cols = pl.ds(i * 256, 256)

            wa[cols] = across(normed_in[:, cols], d_lin[...].reshape(NSEQ * 128, 1024)).astype(bf)

    def to_grad(i, rows):
        unit, scale = unit_of(tree_own[i].astype(f32))
        lifted = attn_g[...] * rows
        term = jnp.sum(rows * unit, axis=0, keepdims=True)
        for j in range(8):
            pack_dp[d, j : j + 1] += term[:, 128 * j : 128 * (j + 1)]
        grad = d_middle[i] + scale * (
            lifted - unit * jnp.mean(unit * lifted, axis=-1, keepdims=True)
        )
        grad_low[i] = grad.astype(bf)

    def close_in(b):
        in_sum.end(b, to_grad)

    per_block = (
        (ATTEND, attend), (MIX_MID, mixed_sum.mid), (MIX_END, close_mixed),
        (NORM_MID, lambda b: spread_mid.mid(pair_of[b])), (NORM_END, lambda b: spread_mid.end(pair_of[b])),
        (LIFT, lift), (D_ACT, d_activate), (SINK, sink), (TURN_MID, mid_sum.mid), (TURN_END, close_mid),
        (LOW_MID, lambda b: spread_low.mid(pair_of[b])), (LOW_END, close_low),
        (OUT_START, settle), (OUT_MID, out_sum.mid), (OUT_END, close_out),
        (ATTEND_BACK, attend_back), (IN_START, sink_in), (IN_MID, in_sum.mid), (IN_END, close_in),
    )
    for label, run in per_block:
        for b in BLOCKS:
            stage(label + b)(functools.partial(run, b))
    for sub in range(2):
        stage(GRAD_WIDE + sub)(functools.partial(grad_wide, sub))
        stage(GRAD_ATTN + sub)(functools.partial(grad_attn, sub))

    stage(GIVE_OUT)(functools.partial(give, 0))
    stage(GIVE_IN)(functools.partial(give, 1))

    pack_sems, fin_sems = (s_pack, r_pack), (s_fin, r_fin)

    @stage(PACK_DP)
    def _():
        for i in range(1, NDP):
            launch(remote(pack_dp.at[d], pack_dp.at[d], pack_sems, i, (d + i) % NDP, s))

    @stage(PACK_SEQ)
    def _():
        for i in range(1, NDP):
            place = pack_dp.at[(d + NDP - i) % NDP]
            remote(place, place, pack_sems, i, d, s).wait_recv()
        pack_sum[...] = (pack_dp[0] + pack_dp[1]) + (pack_dp[2] + pack_dp[3])
        for j in range(NSEQ):
            block = 2 * d + j // 4
            wide = (128 - 32 * (j % 4)) % 128
            thin = (256 - 32 * d - 4 * j) % 128
            pack_cut[j] = jnp.zeros((8, 128), f32)
            for n, (row, shift) in enumerate(((block, wide), (8 + block, wide), (16, thin), (17, thin))):
                pack_cut[j, n : n + 1, :] = pltpu.roll(pack_sum[pl.ds(row, 1), :], shift, 1)
        pack_seq[s] = pack_cut[s]
        for i in range(1, NSEQ):
            j = (s + i) % NSEQ
            launch(remote(pack_cut.at[j], pack_seq.at[s], pack_sems, NDP + i, d, j))

    @stage(PACK_END)
    def _():
        for i in range(1, NSEQ):
            place = pack_seq.at[(s + NSEQ - i) % NSEQ]
            remote(place, place, pack_sems, NDP + i, d, s).wait_recv()
        total = pack_seq[0]
        for j in range(1, NSEQ):
            total = total + pack_seq[j]
        pack_out[...] = total

    def close_cols(n, fin, landed, which):
        sub = (n + (n > 2)) % 2

        def take(way, total):
            fin[2 * way + sub] = total.astype(bf)

        reduce_end(n, take)
        for way in range(2):
            q = 2 * way + sub

            @pl.when(q == d)
            def _():
                pltpu.make_async_copy(fin.at[q], landed.at[d], loc.at[which]).start()

            @pl.when(q != d)
            def _():
                remote(fin.at[q], landed.at[d], fin_sems, (which, d), q, s).start()

    for label, n, fin, landed, which in (
        (A0, 0, fin_a, res_a, 0), (A1, 1, fin_a, res_a, 0),
        (C0, 3, fin_c, res_c, 1), (C1, 4, fin_c, res_c, 1),
    ):
        stage(R_A0 + label + 7)(functools.partial(close_cols, n, fin, landed, which))

    def land(landed, which):
        for i in range(1, NDP):
            q = (d + i) % NDP
            remote(landed.at[q], landed.at[q], fin_sems, (which, q), q, s).wait_recv()
        pltpu.make_async_copy(landed.at[d], landed.at[d], loc.at[which]).wait()

    stage(LAND_A)(lambda: land(res_a, 0))
    stage(LAND_C)(lambda: land(res_c, 1))

    def take_rows(dst, rows, at, way, total):
        dst[pl.ds(rows * way + at, total.shape[0])] = total

    stage(R_B + 7)(lambda: reduce_end(2, functools.partial(take_rows, g_output, 32, 0)))
    for label, n in streams[5:]:
        take = functools.partial(take_rows, g_down, 48, (n - 5) * 16)
        stage(R_A0 + label + 7)(functools.partial(reduce_end, n, take))

    @stage(DRAIN)
    def _():
        for n, (src, dst) in enumerate(back):
            pltpu.make_async_copy(dst, dst, r_back.at[n]).wait()

            def one(j, carry):
                @pl.when(jnp.logical_not((back_owner == d) & (s == j)))
                def _():
                    give_copy(n, j).wait_send()

                return carry

            lax.fori_loop(0, NSEQ, one, 0)
        for n, (fin, landed) in enumerate(((fin_a, res_a), (fin_c, res_c))):
            for i in range(1, NDP):
                q = (d + i) % NDP
                remote(fin.at[q], landed.at[d], fin_sems, (n, d), q, s).wait_send()
        for n in range(3, 8):
            gather_sent(n)
        for n in range(8):
            reduce_sent(n)
        spread_cot.sent(everything)
        for b in BLOCKS:
            spread_mid.sent(pair_of[b])
            spread_low.sent(pair_of[b])
        for cp in pending:
            cp.wait_send()
        for n in range(2):
            for m in range(MICRO):

                @pl.when(tree_seat(d, m) != s)
                def _():
                    row_copy(n, m, 0).wait_send()

                for i in range(1, NDP):
                    row_copy(n, m, i).wait_send()

    for name in ORDER:
        ops[name]()


def finish_kernel(
    out_rows, grad_rows, res_a, res_c, g_output, g_down, pack,
    outs, grads, g_query, g_key, g_value, out_output, g_gate, g_up, out_down, g_attn, g_ffn, g_qg, g_kg,
    low_rows, low_a, low_c, small, *rest,
):
    *held, sems = rest
    coming = [
        pltpu.make_async_copy(src, dst, sems.at[n])
        for n, (src, dst) in enumerate(
            (
                (grad_rows, low_rows), (res_a, low_a), (res_c, low_c), (pack, small),
                (out_rows, held[0]), (g_output, held[1]), (g_down, held[2]),
            )
        )
    ]
    for cp in coming:
        cp.start()
    leaving = [
        pltpu.make_async_copy(src, dst, sems.at[7 + n])
        for n, (src, dst) in enumerate(zip(held, (outs, out_output, out_down)))
    ]
    for came, goes in zip(coming[4:], leaving):
        came.wait()
        goes.start()
    coming[0].wait()
    grads[...] = low_rows[...].astype(jnp.float32)
    for cp in coming[1:4]:
        cp.wait()
    for src, cuts in (
        (low_a, ((0, 512, g_query), (512, 256, g_key), (768, 256, g_value))),
        (low_c, ((0, 768, g_gate), (768, 768, g_up))),
    ):
        for q in range(NDP):
            for at, width, dst in cuts:
                dst[:, width * q : width * (q + 1)] = src[q, :, at : at + width].astype(jnp.float32)
    for n, dst in enumerate((g_attn, g_ffn, g_qg, g_kg)):
        count = dst.shape[0]
        dst[...] = small[n : n + 1, 0:count].reshape(count)
    for cp in leaving:
        cp.wait()


def tree_shards(
    tokens, cotangent, node_lengths, parents, w_query, w_key, w_value, w_output, w_gate, w_up, w_down,
    attn_gain, ffn_gain, query_gain, key_gain,
):
    f32, bf = jnp.float32, jnp.bfloat16
    nodes = node_lengths.shape[2]
    half = np.arange(HEAD_DIM // 2, dtype=np.float64)
    inv_freq = THETA ** (-(half * (2.0 / HEAD_DIM)))
    inv_freq = np.concatenate([inv_freq, inv_freq])[None].astype(np.float32)
    shape, vmem, dma = jax.ShapeDtypeStruct, pltpu.VMEM, pltpu.SemaphoreType.DMA
    anywhere = pl.BlockSpec(memory_space=pl.ANY)
    here = pl.BlockSpec(memory_space=pltpu.VMEM)
    rows = NSEQ * 128
    quarter = (NSEQ, 32, D)
    twice = lambda *dims: [dma(dims), dma(dims)]
    results = pl.pallas_call(
        functools.partial(layer_kernel, nodes),
        out_shape=(
            shape((MICRO, 128, D), bf),
            shape((MICRO, 128, D), bf),
            shape((NDP, 32, 1024), bf),
            shape((NDP, 32, 1536), bf),
            shape((64, D), f32),
            shape((96, D), f32),
            shape((8, 128), f32),
        ),
        in_specs=[anywhere] * 8 + [here] + [anywhere] * 7,
        out_specs=[anywhere] * 4 + [here] * 3,
        scratch_shapes=[
            vmem(node_lengths.shape, jnp.int32), vmem(parents.shape, jnp.int32),
            *[vmem(gain.shape, bf) for gain in (attn_gain, ffn_gain, query_gain, key_gain)],
            vmem((NDP, NSEQ, 8, 128), f32),
            vmem((D, 1024), bf), vmem((512, D), bf), vmem((D, 1536), bf), vmem((768, D), bf),
            vmem((D, 1536), bf), vmem((768, D), bf),
            vmem((2, 2, 7, 32, 1024), bf), vmem((2, 7, 32, D), bf),
            vmem((2, 2, 7, 32, 1536), bf), vmem((3, 2, 7, 16, D), bf),
            vmem((NSEQ, NDP, 32, D), bf), vmem((NSEQ, NDP, 32, D), bf), vmem((rows, D), bf),
            vmem((NSEQ, NDP, 32, D), bf), vmem((NSEQ, NDP, 32, D), bf), vmem(quarter, bf),
            vmem((rows, 768), f32), vmem((6, rows, 128), bf),
            vmem((rows, 256), bf), vmem((rows, 128), bf), vmem((rows, 128), bf),
            vmem((rows, 128), f32), vmem((rows, 128), f32), vmem((rows, 512), bf), vmem((rows, 512), bf),
            vmem((NSEQ, NDP, 32, D), bf), vmem((NSEQ, NDP, 32, D), bf),
            vmem((2,) + quarter, bf), vmem(quarter, bf), vmem(quarter, bf),
            vmem((2,) + quarter, bf), vmem(quarter, bf), vmem(quarter, bf),
            vmem(quarter, f32), vmem(quarter, f32), vmem((rows, 768), bf), vmem((rows, 1536), bf),
            vmem((2, rows, 128), f32), vmem((2, rows, 128), f32), vmem(quarter, bf), vmem(quarter, bf),
            vmem((NDP, 32, 1024), bf), vmem((NDP, 32, 1536), bf),
            vmem((1, D), f32), vmem((1, D), f32), vmem((8, 128), f32),
            vmem((NSEQ, 8, 128), f32), vmem((NDP, 24, 128), f32), vmem((NSEQ, 8, 128), f32),
            vmem((24, 128), f32), vmem((NSEQ, 8, 128), f32),
            dma((16,)),
            *twice(12), *twice(5, NDP), dma((2, MICRO, NDP)), dma((2,)),
            *twice(8, 2, 7), *twice(8, 2, 7),
            *twice(4, 3, 4), *twice(2, 3), *twice(2, 3, 4),
            dma((2, NSEQ)), dma((2,)), *twice(2, NDP), *twice(12),
        ],
        compiler_params=pltpu.CompilerParams(
            collective_id=1, has_side_effects=True, vmem_limit_bytes=61 << 20
        ),
        name="layer",
    )(
        tokens[0], cotangent[0], node_lengths, parents, attn_gain, ffn_gain, query_gain, key_gain, inv_freq,
        w_query, w_key, w_value, w_output, w_gate, w_up, w_down,
    )
    full = lambda *dims: shape(dims, f32)
    finished = pl.pallas_call(
        finish_kernel,
        out_shape=(
            shape((MICRO, 128, D), bf), full(MICRO, 128, D),
            full(32, 2048), full(32, 1024), full(32, 1024), full(64, D),
            full(32, FF), full(32, FF), full(96, D),
            full(32), full(32), full(4), full(4),
        ),
        in_specs=[pl.BlockSpec(memory_space=pltpu.HBM)] * 7,
        out_specs=[anywhere, here, here, here, here, anywhere, here, here, anywhere] + [here] * 4,
        scratch_shapes=[
            vmem((MICRO, 128, D), bf), vmem((NDP, 32, 1024), bf), vmem((NDP, 32, 1536), bf),
            vmem((8, 128), f32), vmem((MICRO, 128, D), bf), vmem((64, D), f32), vmem((96, D), f32),
            dma((10,)),
        ],
        compiler_params=pltpu.CompilerParams(vmem_limit_bytes=61 << 20),
        name="finish",
    )(*results)
    return (finished[0][None], finished[1][None]) + tuple(finished[2:])


def solution(mesh):
    ring = mesh.shape["dp"] == NDP and mesh.shape["seq"] == NSEQ
    return jax.shard_map(
        tree_shards if ring else general_shards,
        mesh=mesh,
        in_specs=(
            P("dp", None, "seq", None),
            P("dp", None, "seq", None),
            P("dp", None, None),
            P("dp", None, None),
            P(("dp", "seq"), None),
            P(("dp", "seq"), None),
            P(("dp", "seq"), None),
            P(("dp", "seq"), None),
            P(("dp", "seq"), None),
            P(("dp", "seq"), None),
            P(("dp", "seq"), None),
            P(("dp", "seq")),
            P(("dp", "seq")),
            P(("dp", "seq")),
            P(("dp", "seq")),
        ),
        out_specs=(
            P("dp", None, "seq", None),
            P("dp", None, "seq", None),
            P(("dp", "seq"), None),
            P(("dp", "seq"), None),
            P(("dp", "seq"), None),
            P(("dp", "seq"), None),
            P(("dp", "seq"), None),
            P(("dp", "seq"), None),
            P(("dp", "seq"), None),
            P(("dp", "seq")),
            P(("dp", "seq")),
            P(("dp", "seq")),
            P(("dp", "seq")),
        ),
        check_vma=False,
    )
```
